32 devices in a mesh: cp: 2 (over core), sp: 4 (over y, x), fsdp: 4 (over z).
Axes of the slice: x: 2, y: 2, z: 4, core: 2. Of those that a mesh axis runs over, the one named last changes fastest.
Arguments:
- tokens: bfloat16 [4, 2048, 1536], P('fsdp', ('cp', 'sp')), may hold values from -6 to 6
- out_cotangent: bfloat16 [4, 2048, 1536], P('fsdp', ('cp', 'sp')), may hold values from -6 to 6
- seq_lengths: int32 [4, 8], P('fsdp'), may hold values from 1 to 1024, 2048 in all within a row
- slab_place: int32 [4, 4], P('fsdp'), may hold values from 0 to 3, as said below
- attn_gain: float32 [1536], replicated, may hold values from 0.25 to 1.75
- query_weight: bfloat16 [1536, 1536], P('fsdp'), may hold values from -0.15625 to 0.15625
- key_weight: bfloat16 [1536, 1536], P('fsdp'), may hold values from -0.15625 to 0.15625
- value_weight: bfloat16 [1536, 1536], P('fsdp'), may hold values from -0.15625 to 0.15625
- outgate_weight: bfloat16 [1536, 1536], P('fsdp'), may hold values from -0.15625 to 0.15625
- forget_weight: bfloat16 [1536, 24], P('fsdp'), may hold values from -0.15625 to 0.15625
- forget_bias: float32 [24], replicated, may hold values from 3 to 9
- output_weight: bfloat16 [1536, 1536], P('fsdp'), may hold values from -1.25 to 1.25
- mlp_gain: float32 [1536], replicated, may hold values from 0.25 to 1.75
- gate_weight: bfloat16 [1536, 4096], P('fsdp'), may hold values from -0.15625 to 0.15625
- up_weight: bfloat16 [1536, 4096], P('fsdp'), may hold values from -0.15625 to 0.15625
- down_weight: bfloat16 [1536, 4096], P('fsdp'), may hold values from -0.09375 to 0.09375
Outputs:
- block_out: bfloat16 [4, 2048, 1536], P('fsdp', ('cp', 'sp'))
- tokens_grad: float32 [4, 2048, 1536], P('fsdp', ('cp', 'sp'))
- attn_gain_grad: float32 [1536], replicated
- query_grad: float32 [1536, 1536], P(('cp', 'sp', 'fsdp'))
- key_grad: float32 [1536, 1536], P(('cp', 'sp', 'fsdp'))
- value_grad: float32 [1536, 1536], P(('cp', 'sp', 'fsdp'))
- outgate_grad: float32 [1536, 1536], P(('cp', 'sp', 'fsdp'))
- forget_grad: float32 [1536, 24], P(('cp', 'sp', 'fsdp'))
- forget_bias_grad: float32 [24], replicated
- output_weight_grad: float32 [1536, 1536], P(('cp', 'sp', 'fsdp'))
- mlp_gain_grad: float32 [1536], replicated
- gate_grad: float32 [1536, 4096], P(('cp', 'sp', 'fsdp'))
- up_grad: float32 [1536, 4096], P(('cp', 'sp', 'fsdp'))
- down_grad: float32 [1536, 4096], P(('cp', 'sp', 'fsdp'))
The draws below stay inside these ranges and needn't reach their ends.
Inputs may be any that keep to these rules, and one draw needn't show every extreme that they name: `seq_lengths`: each row sums to 2048, and its largest entry is exactly 1024. `slab_place`: each row is a permutation of 0 to 3 in which entries 2 * c and 2 * c + 1 sum to 3.
All inputs are finite; a program needn't handle non-finite values.
Results may differ from the reference program's by a relative error of at most 0.017.
Values may be sent and summed in bfloat16 or wider, within the bound.
A program may use at most 320 MiB of HBM per device.

```python
import math
import jax
import jax.numpy as jnp
import numpy as np
from jax import lax

D = 1536
H = 24
HD = 64
FF = 4096
NSEQ = 8
GROUP = 2048
SLAB = 512
NSLAB = 4
MOST = 1024
N_FSDP = 4


def draw_slab_place(key, part):
    row_keys = jax.random.split(key, N_FSDP)

    def one_row(row_key):
        pair_key, flip_key = jax.random.split(row_key)
        pairs = jax.random.permutation(pair_key, NSLAB // 2).astype(jnp.int32)
        flips = jax.random.randint(flip_key, (NSLAB // 2,), 0, 2).astype(jnp.int32)
        first = jnp.where(flips == 0, pairs, NSLAB - 1 - pairs)
        second = NSLAB - 1 - first
        return jnp.stack([first, second], axis=1).reshape(NSLAB).astype(jnp.int32)
    return jax.vmap(one_row)(row_keys)


def shard_levels(stream_key, extent, shards, smallest, largest):
    def one(dim, shards_of):
        draws = jax.random.uniform(jax.random.fold_in(jax.random.fold_in(stream_key, 6), dim), (shards_of,), jnp.float32, smallest / len(shards), largest / len(shards))
        return jnp.repeat(jnp.exp(draws), extent[dim] // shards_of).reshape((-1,) + (1,) * (len(extent) - dim - 1))

    loudness = one(*shards[0])
    for cut in shards[1:]:
        loudness = loudness * one(*cut)
    return loudness


def split_up(amount, total, limit, skew):
    weights = [(1 << 20) // math.isqrt(rank ** skew) + 1 for rank in range(2, amount + 1)]
    spare, given = total - limit - (amount - 1), [1] * (amount - 1)
    while spare > 0:
        free = [i for i in range(amount - 1) if given[i] < limit]
        pool, remaining = sum([weights[i] for i in free]), spare
        for i in free:
            more = min(limit - given[i], max(1, remaining * weights[i] // pool), spare)
            given[i] = given[i] + more
            spare = spare - more
    return np.array([limit] + given)


def ragged_sizes(stream_key, count, total, most, lean):
    if count == 2:
        one = jax.random.randint(stream_key, (), max(1, total - most), min(most, total - 1) + 1)
        return jnp.stack([one, total - one])
    lengths = jnp.asarray(split_up(count, total, most, lean), jnp.int32)
    pairs = (count - 1) // 2
    source_of, sink = lengths[1:1 + 2 * pairs:2], lengths[2:2 + 2 * pairs:2]
    room = jnp.minimum(source_of - 1, most - sink)
    passed = jax.random.randint(jax.random.fold_in(stream_key, 1), (pairs,), 0, 1 << 20) % (room + 1)
    lengths = lengths.at[1:1 + 2 * pairs:2].set(source_of - passed).at[2:2 + 2 * pairs:2].set(sink + passed)
    return lengths[jax.random.permutation(jax.random.fold_in(stream_key, 2), count)]


def centred(own_key, dims, deviation, limit, pieces=(), kind=jnp.bfloat16):
    gain = shard_levels(own_key, dims, pieces, -0.22, 0.18) if pieces else 1.0
    array = jax.random.normal(own_key, dims, jnp.float32) * deviation * gain
    return jnp.minimum(jnp.maximum(array, -limit), limit).astype(kind)


def setup_inputs(seed: int = 0) -> dict:
    arg_keys = jax.random.split(jax.random.key(seed), 17)
    tokens = centred(arg_keys[0], (N_FSDP, GROUP, D), 1.0, 6.0, ((0, 4), (1, 8)))
    out_cotangent = centred(arg_keys[1], (N_FSDP, GROUP, D), 1.0, 6.0, ((0, 4), (1, 8)))
    seq_lengths = jax.vmap(lambda own: ragged_sizes(own, NSEQ, GROUP, MOST, 1))(jax.random.split(arg_keys[2], N_FSDP)).reshape((N_FSDP, NSEQ)).astype(jnp.int32)
    slab_place = draw_slab_place(jax.random.fold_in(arg_keys[16], 71), 0)
    attn_gain = jnp.clip(1.0 + 0.15 * jax.random.normal(arg_keys[4], (D,), jnp.float32), 0.25, 1.75)
    query_weight = centred(arg_keys[5], (D, D), D ** -0.5, 0.15625, ((0, 4),))
    key_weight = centred(arg_keys[6], (D, D), D ** -0.5, 0.15625, ((0, 4),))
    value_weight = centred(arg_keys[7], (D, D), D ** -0.5, 0.15625, ((0, 4),))
    outgate_weight = centred(arg_keys[8], (D, D), D ** -0.5, 0.15625, ((0, 4),))
    forget_weight = centred(arg_keys[9], (D, H), D ** -0.5, 0.15625, ((0, 4),))
    forget_bias = jnp.clip(jax.random.uniform(arg_keys[10], (H,), jnp.float32, 3.0, 9.0), 3.0, 9.0)
    output_weight = centred(arg_keys[11], (D, D), (D // 64) ** -0.5, 1.25, ((0, 4),))
    mlp_gain = jnp.clip(1.0 + 0.15 * jax.random.normal(arg_keys[12], (D,), jnp.float32), 0.25, 1.75)
    gate_weight = centred(arg_keys[13], (D, FF), D ** -0.5, 0.15625, ((0, 4),))
    up_weight = centred(arg_keys[14], (D, FF), D ** -0.5, 0.15625, ((0, 4),))
    down_weight = centred(arg_keys[15], (D, FF), FF ** -0.5, 0.09375, ((0, 4),))
    return {"tokens": tokens, "out_cotangent": out_cotangent, "seq_lengths": seq_lengths, "slab_place": slab_place, "attn_gain": attn_gain, "query_weight": query_weight, "key_weight": key_weight, "value_weight": value_weight, "outgate_weight": outgate_weight, "forget_weight": forget_weight, "forget_bias": forget_bias, "output_weight": output_weight, "mlp_gain": mlp_gain, "gate_weight": gate_weight, "up_weight": up_weight, "down_weight": down_weight}


epsilon = 1e-06
very_low = -1e+30

@jax.custom_vjp
def low(v):
    return lax.optimization_barrier(v.astype(jnp.bfloat16)).astype(jnp.float32)

@jax.custom_vjp
def low_back(v):
    return v

def low_keep(v):
    return (low(v), None)

def low_pass(kept, grad):
    return (grad,)

def back_keep(v):
    return (v, None)

def back_low(kept, grad):
    return (low(grad),)
low.defvjp(low_keep, low_pass)
low_back.defvjp(back_keep, back_low)

def rms_inverse(values):
    return lax.rsqrt(lax.optimization_barrier(jnp.mean(values * values, axis=-1, keepdims=True)) + epsilon)

def matmul(left, right):
    return jnp.dot(left, right, preferred_element_type=jnp.float32, precision=lax.Precision.HIGHEST)

def layout(lens_row, place_row):
    rows = jnp.arange(GROUP, dtype=jnp.int32)
    position = place_row[rows // SLAB].astype(jnp.int32) * SLAB + rows % SLAB
    ends = jnp.cumsum(lens_row).astype(jnp.int32)
    segment = lax.optimization_barrier(jnp.sum((position[:, None] >= ends[None, :]).astype(jnp.int32), axis=1))
    storage = jnp.zeros((NSLAB,), jnp.int32).at[place_row].set(jnp.arange(NSLAB, dtype=jnp.int32))
    row_of = storage[rows // SLAB] * SLAB + rows % SLAB
    return (position, segment, row_of)

def attend_rows(queries, query_pos, query_seg, query_prefix, keys, values, position, segment, prefix):
    raw = jnp.einsum('qhd,khd->hqk', queries, keys, precision=lax.Precision.HIGHEST) * HD ** (-0.5)
    raw = raw + query_prefix.T[:, :, None] - prefix.T[:, None, :]
    raw = low_back(raw)
    allowed = (query_pos[:, None] >= position[None, :]) & (query_seg[:, None] == segment[None, :])
    masked = jnp.where(allowed[None], raw, very_low)
    weights = low(jax.nn.softmax(masked, axis=-1))
    return jnp.einsum('hqk,khd->qhd', weights, values, precision=lax.Precision.HIGHEST)

def attention(queries, keys, values, position, segment, prefix):
    block_rows = min(512, GROUP)
    blocks = GROUP // block_rows
    block_fn = jax.checkpoint(attend_rows)

    def one_block(args):
        query_blk, pos_blk, seg_blk, prefix_blk = args
        return block_fn(query_blk, pos_blk, seg_blk, prefix_blk, keys, values, position, segment, prefix)
    results = lax.map(one_block, (queries.reshape(blocks, block_rows, H, HD), position.reshape(blocks, block_rows), segment.reshape(blocks, block_rows), prefix.reshape(blocks, block_rows, H)))
    return results.reshape(GROUP, H, HD)

def group_forward(params, tokens_g, lens_row, place_row):
    attn_gain, w_query, w_key, w_value, w_outgate, w_forget, forget_bias, w_output, mlp_gain, w_gate, w_up, w_down = params
    position, segment, row_of = layout(lens_row, place_row)
    normed = low(tokens_g * rms_inverse(tokens_g) * attn_gain)
    queries = low(low_back(matmul(normed, w_query)))
    keys = low(low_back(matmul(normed, w_key)))
    values = low(low_back(matmul(normed, w_value)))
    out_gate = jax.nn.sigmoid(low_back(matmul(normed, w_outgate)))
    forget_pre = low_back(matmul(normed, w_forget) + forget_bias)
    log_forget = low(low_back(jax.nn.log_sigmoid(forget_pre)))
    prefix = jnp.cumsum(log_forget[row_of], axis=0)[position]
    attended = attention(queries.reshape(GROUP, H, HD), keys.reshape(GROUP, H, HD), values.reshape(GROUP, H, HD), position, segment, prefix).reshape(GROUP, D)
    attended = low(low_back(attended))
    gated = low(attended * out_gate)
    mid = tokens_g + low_back(matmul(gated, w_output))
    normed_mlp = low(mid * rms_inverse(mid) * mlp_gain)
    gate_lin = low_back(matmul(normed_mlp, w_gate))
    up_lin = low_back(matmul(normed_mlp, w_up))
    hidden = low(jax.nn.silu(gate_lin) * up_lin)
    return mid + matmul(hidden, w_down.T)

def reference(tokens, out_cotangent, seq_lengths, slab_place, attn_gain, query_weight, key_weight, value_weight, outgate_weight, forget_weight, forget_bias, output_weight, mlp_gain, gate_weight, up_weight, down_weight):
    params = tuple((item.astype(jnp.float32) for item in (attn_gain, query_weight, key_weight, value_weight, outgate_weight, forget_weight, forget_bias, output_weight, mlp_gain, gate_weight, up_weight, down_weight)))
    group_fn = jax.checkpoint(group_forward)

    def forward(weights, inputs):

        def one_group(args):
            tokens_g, lens_row, place_row = args
            return group_fn(weights, tokens_g, lens_row, place_row)
        return lax.map(one_group, (inputs, seq_lengths, slab_place))
    block_out, pullback = jax.vjp(forward, params, tokens.astype(jnp.float32))
    grads, tokens_grad = pullback(out_cotangent.astype(jnp.float32))
    return (block_out.astype(jnp.bfloat16), tokens_grad, grads[0], grads[1], grads[2], grads[3], grads[4], grads[5], grads[6], grads[7], grads[8], grads[9], grads[10], grads[11])
```

```python
import functools

import jax
import jax.numpy as jnp
from jax import lax
from jax.experimental import pallas as pl
from jax.experimental.pallas import tpu as pltpu
from jax.sharding import PartitionSpec as P

epsilon = 1e-06
very_low = -1e30
MESH = pl.DeviceIdType.MESH
BF = jnp.bfloat16
F32 = jnp.float32
REMOTE = pltpu.make_async_remote_copy
VMEM_BYTES = 60 * 1024 * 1024


def matmul(left, right):
    return jnp.dot(left, right, preferred_element_type=jnp.float32)


def matmul_right_t(left, right):
    return lax.dot_general(
        left, right, (((1,), (1,)), ((), ())), preferred_element_type=jnp.float32
    )


def matmul_left_t(left, right):
    return lax.dot_general(
        left, right, (((0,), (0,)), ((), ())), preferred_element_type=jnp.float32
    )


def rms_inverse(values):
    return lax.rsqrt(jnp.mean(values * values, axis=1, keepdims=True) + epsilon)


def norm_back(upstream, values, inverse, gain):
    weighted = upstream * gain
    return inverse * weighted - values * inverse**3 * jnp.mean(
        weighted * values, axis=1, keepdims=True
    )


def row_layout(place_row, lens_row, count, slab_rows):
    rows = jnp.arange(count, dtype=jnp.int32)
    slab_index = rows // slab_rows
    table = (
        slab_index[:, None] == jnp.arange(place_row.shape[0], dtype=jnp.int32)[None, :]
    ).astype(jnp.int32)
    position = jnp.sum(table * place_row[None, :], axis=1) * slab_rows + rows % slab_rows
    ends = jnp.cumsum(lens_row)
    segment = jnp.sum((position[:, None] >= ends[None, :]).astype(jnp.int32), axis=1)
    return (position, segment)


def forget_prefix(log_all, place_row, slab_rows):
    slabs = place_row.shape[0]
    steps = log_all.astype(jnp.float32).reshape(slabs, slab_rows, -1)
    inside = jnp.cumsum(steps, axis=1)
    totals = inside[:, -1, :]
    earlier = (place_row[None, :] < place_row[:, None]).astype(jnp.float32)
    offsets = jnp.dot(earlier, totals, precision=lax.Precision.HIGHEST)
    return (inside + offsets[:, None, :]).reshape(slabs * slab_rows, -1)


def prefix_back(grad_prefix, place_row, slab_rows):
    slabs = place_row.shape[0]
    steps = grad_prefix.reshape(slabs, slab_rows, -1)
    inside = jnp.flip(jnp.cumsum(jnp.flip(steps, 1), axis=1), 1)
    totals = inside[:, 0, :]
    later = (place_row[None, :] > place_row[:, None]).astype(jnp.float32)
    offsets = jnp.dot(later, totals, precision=lax.Precision.HIGHEST)
    return (inside + offsets[:, None, :]).reshape(slabs * slab_rows, -1)


def local(
    tokens,
    out_cotangent,
    seq_lengths,
    slab_place,
    attn_gain,
    query_weight,
    key_weight,
    value_weight,
    outgate_weight,
    forget_weight,
    forget_bias,
    output_weight,
    mlp_gain,
    gate_weight,
    up_weight,
    down_weight,
):
    seq_devices = lax.axis_size("sp")
    ctx_devices = lax.axis_size("cp")
    ctx_index = lax.axis_index("cp")
    tok_rows = tokens.shape[1]
    model_width = tokens.shape[2]
    head_count = forget_weight.shape[1]
    local_heads = head_count // seq_devices
    head_size = model_width // head_count
    ctx_rows = tok_rows * seq_devices
    group_rows = ctx_rows * ctx_devices
    slab_rows = ctx_rows // 2
    key_block = min(512, group_rows)
    key_blocks = group_rows // key_block
    score_scale = head_size ** (-0.5)
    place_row = slab_place[0]
    lens_row = seq_lengths[0]
    ctx_start = ctx_index * ctx_rows
    inputs = tokens[0]
    input_f = inputs.astype(jnp.float32)
    weights_attn = (
        lax.all_gather(query_weight, "fsdp", axis=0, tiled=True),
        lax.all_gather(key_weight, "fsdp", axis=0, tiled=True),
        lax.all_gather(value_weight, "fsdp", axis=0, tiled=True),
        lax.all_gather(outgate_weight, "fsdp", axis=0, tiled=True),
        lax.all_gather(forget_weight, "fsdp", axis=0, tiled=True),
        lax.all_gather(output_weight, "fsdp", axis=0, tiled=True),
    )
    full_query, full_key, full_value, full_outgate, full_forget, full_output = weights_attn
    inv_first = rms_inverse(input_f)
    normed = (input_f * inv_first * attn_gain).astype(jnp.bfloat16)
    queries = matmul(normed, full_query).astype(jnp.bfloat16)
    keys = matmul(normed, full_key).astype(jnp.bfloat16)
    values = matmul(normed, full_value).astype(jnp.bfloat16)
    out_gate = jax.nn.sigmoid(matmul(normed, full_outgate))
    forget_pre = matmul(normed, full_forget) + forget_bias
    log_forget = jax.nn.log_sigmoid(forget_pre).astype(jnp.bfloat16)
    head_query, head_key, head_value, head_forget = (
        lax.all_to_all(queries, "sp", split_axis=1, concat_axis=0, tiled=True),
        lax.all_to_all(keys, "sp", split_axis=1, concat_axis=0, tiled=True),
        lax.all_to_all(values, "sp", split_axis=1, concat_axis=0, tiled=True),
        lax.all_to_all(log_forget, "sp", split_axis=1, concat_axis=0, tiled=True),
    )
    keys_all, values_all, forget_all = (
        lax.all_gather(head_key, "cp", axis=0, tiled=True),
        lax.all_gather(head_value, "cp", axis=0, tiled=True),
        lax.all_gather(head_forget, "cp", axis=0, tiled=True),
    )
    prefix_all = forget_prefix(forget_all, place_row, slab_rows)
    pos_all, seg_all = row_layout(place_row, lens_row, group_rows, slab_rows)
    query_pos = lax.dynamic_slice_in_dim(pos_all, ctx_start, ctx_rows, 0)
    query_seg = lax.dynamic_slice_in_dim(seg_all, ctx_start, ctx_rows, 0)
    query_prefix = lax.dynamic_slice_in_dim(prefix_all, ctx_start, ctx_rows, 0)
    query_three = head_query.reshape(ctx_rows, local_heads, head_size)
    query_pos_top = jnp.max(query_pos)
    query_seg_low = jnp.min(query_seg)
    query_seg_top = jnp.max(query_seg)
    key_pieces = (
        keys_all.reshape(key_blocks, key_block, local_heads, head_size),
        values_all.reshape(key_blocks, key_block, local_heads, head_size),
        prefix_all.reshape(key_blocks, key_block, local_heads),
        pos_all.reshape(key_blocks, key_block),
        seg_all.reshape(key_blocks, key_block),
    )

    def block_live(key_pos, key_seg):
        return (
            (query_pos_top >= jnp.min(key_pos))
            & (query_seg_top >= jnp.min(key_seg))
            & (jnp.max(key_seg) >= query_seg_low)
        )

    def block_scores(key_piece, key_prefix, key_pos, key_seg):
        raw = (
            jnp.einsum("qhd,khd->hqk", query_three, key_piece, preferred_element_type=jnp.float32)
            * score_scale
        )
        raw = raw + query_prefix.T[:, :, None] - key_prefix.T[:, None, :]
        allowed = (query_pos[:, None] >= key_pos[None, :]) & (
            query_seg[:, None] == key_seg[None, :]
        )
        return (raw, allowed[None, :, :])

    def total_work(carry, piece):
        running_max, running_sum = carry
        key_piece, value_piece, key_prefix, key_pos, key_seg = piece
        raw, allowed = block_scores(key_piece, key_prefix, key_pos, key_seg)
        new_max = jnp.maximum(running_max, jnp.max(jnp.where(allowed, raw, very_low), axis=2))
        terms = jnp.where(allowed, jnp.exp(raw - new_max[:, :, None]), 0.0)
        new_sum = running_sum * jnp.exp(running_max - new_max) + jnp.sum(terms, axis=2)
        return (new_max, new_sum)

    def total_step(carry, piece):
        live = block_live(piece[3], piece[4])
        return (lax.cond(live, total_work, lambda held, unused: held, carry, piece), None)

    start_max = jnp.full((local_heads, ctx_rows), very_low, jnp.float32)
    start_sum = jnp.zeros((local_heads, ctx_rows), jnp.float32)
    (final_max, final_sum), _ = lax.scan(total_step, (start_max, start_sum), key_pieces)
    log_total = final_max + jnp.log(final_sum)

    def output_work(carry, piece):
        coarse, fine = carry
        key_piece, value_piece, key_prefix, key_pos, key_seg = piece
        raw, allowed = block_scores(key_piece, key_prefix, key_pos, key_seg)
        probs = jnp.where(allowed, jnp.exp(raw - log_total[:, :, None]), 0.0)
        rounded = probs.astype(jnp.bfloat16)
        rest = (probs - rounded.astype(jnp.float32)).astype(jnp.bfloat16)
        coarse = coarse + jnp.einsum(
            "hqk,khd->qhd", rounded, value_piece, preferred_element_type=jnp.float32
        )
        fine = fine + jnp.einsum(
            "hqk,khd->qhd", rest, value_piece, preferred_element_type=jnp.float32
        )
        return (coarse, fine)

    def output_step(carry, piece):
        live = block_live(piece[3], piece[4])
        return (lax.cond(live, output_work, lambda held, unused: held, carry, piece), None)

    zero_out = jnp.zeros((ctx_rows, local_heads, head_size), jnp.float32)
    (coarse_out, fine_out), _ = lax.scan(output_step, (zero_out, zero_out), key_pieces)
    exact_out = coarse_out + fine_out
    head_out = coarse_out.reshape(ctx_rows, local_heads * head_size).astype(jnp.bfloat16)
    token_out = lax.all_to_all(head_out, "sp", split_axis=0, concat_axis=1, tiled=True)
    token_out_f = token_out.astype(jnp.float32)
    gated = (token_out_f * out_gate).astype(jnp.bfloat16)
    mid = input_f + matmul(gated, full_output)
    weights_mlp = (
        lax.all_gather(gate_weight, "fsdp", axis=0, tiled=True),
        lax.all_gather(up_weight, "fsdp", axis=0, tiled=True),
        lax.all_gather(down_weight, "fsdp", axis=0, tiled=True),
    )
    full_gate, full_up, full_down = weights_mlp
    inv_second = rms_inverse(mid)
    normed_mlp = (mid * inv_second * mlp_gain).astype(jnp.bfloat16)
    gate_lin = matmul(normed_mlp, full_gate)
    up_lin = matmul(normed_mlp, full_up)
    gate_sig = jax.nn.sigmoid(gate_lin)
    activated = gate_lin * gate_sig
    hidden = (activated * up_lin).astype(jnp.bfloat16)
    block_out = (mid + matmul_right_t(hidden, full_down)).astype(jnp.bfloat16)
    cotangent = out_cotangent[0]
    grad_hidden = matmul(cotangent, full_down)
    grad_gate_lin = (grad_hidden * up_lin * gate_sig * (1.0 + gate_lin * (1.0 - gate_sig))).astype(
        jnp.bfloat16
    )
    grad_up_lin = (grad_hidden * activated).astype(jnp.bfloat16)
    grad_normed_mlp = matmul_right_t(grad_gate_lin, full_gate) + matmul_right_t(
        grad_up_lin, full_up
    )
    mlp_gain_term = jnp.sum(grad_normed_mlp * mid * inv_second, axis=0)
    grad_mid = cotangent.astype(jnp.float32) + norm_back(grad_normed_mlp, mid, inv_second, mlp_gain)
    gate_term = matmul_left_t(normed_mlp, grad_gate_lin)
    up_term = matmul_left_t(normed_mlp, grad_up_lin)
    down_term = matmul_left_t(cotangent, hidden)
    grad_branch = grad_mid.astype(jnp.bfloat16)
    grad_gated = matmul_right_t(grad_branch, full_output)
    grad_attended = (grad_gated * out_gate).astype(jnp.bfloat16)
    grad_gate_pre = (grad_gated * token_out_f * out_gate * (1.0 - out_gate)).astype(jnp.bfloat16)
    head_grad = lax.all_to_all(grad_attended, "sp", split_axis=1, concat_axis=0, tiled=True)
    grad_three = head_grad.reshape(ctx_rows, local_heads, head_size)
    delta = jnp.sum(grad_three.astype(jnp.float32) * exact_out, axis=2).T

    def back_work(carry, piece):
        grad_query_acc, grad_prefix_acc = carry
        key_piece, value_piece, key_prefix, key_pos, key_seg = piece
        raw, allowed = block_scores(key_piece, key_prefix, key_pos, key_seg)
        probs = jnp.where(allowed, jnp.exp(raw - log_total[:, :, None]), 0.0)
        rounded = probs.astype(jnp.bfloat16)
        grad_probs = jnp.einsum(
            "qhd,khd->hqk", grad_three, value_piece, preferred_element_type=jnp.float32
        )
        grad_scores = (probs * (grad_probs - delta[:, :, None])).astype(jnp.bfloat16)
        grad_query_acc = (
            grad_query_acc
            + jnp.einsum("hqk,khd->qhd", grad_scores, key_piece, preferred_element_type=jnp.float32)
            * score_scale
        )
        key_term = (
            jnp.einsum("hqk,qhd->khd", grad_scores, query_three, preferred_element_type=jnp.float32)
            * score_scale
        )
        value_term = jnp.einsum(
            "hqk,qhd->khd", rounded, grad_three, preferred_element_type=jnp.float32
        )
        score_f = grad_scores.astype(jnp.float32)
        grad_prefix_acc = grad_prefix_acc + jnp.sum(score_f, axis=2)
        prefix_term = -jnp.sum(score_f, axis=1)
        return ((grad_query_acc, grad_prefix_acc), (key_term, value_term, prefix_term))

    def back_skip(carry, piece):
        empty_kv = jnp.zeros((key_block, local_heads, head_size), jnp.float32)
        empty_prefix = jnp.zeros((local_heads, key_block), jnp.float32)
        return (carry, (empty_kv, empty_kv, empty_prefix))

    def back_step(carry, piece):
        live = block_live(piece[3], piece[4])
        return lax.cond(live, back_work, back_skip, carry, piece)

    start_prefix = jnp.zeros((local_heads, ctx_rows), jnp.float32)
    (grad_query_acc, grad_prefix_q), (key_terms, value_terms, prefix_terms) = lax.scan(
        back_step, (zero_out, start_prefix), key_pieces
    )
    keys_grad_all = key_terms.reshape(group_rows, local_heads * head_size)
    values_grad_all = value_terms.reshape(group_rows, local_heads * head_size)
    prefix_grad_all = jnp.transpose(prefix_terms, (0, 2, 1)).reshape(group_rows, local_heads)
    own_prefix = lax.dynamic_slice_in_dim(prefix_grad_all, ctx_start, ctx_rows, 0)
    prefix_grad_all = lax.dynamic_update_slice_in_dim(
        prefix_grad_all, own_prefix + grad_prefix_q.T, ctx_start, 0
    )
    forget_grad_term = prefix_back(prefix_grad_all, place_row, slab_rows)
    key_sum, value_sum, forget_sum = (
        lax.psum_scatter(keys_grad_all, "cp", scatter_dimension=0, tiled=True),
        lax.psum_scatter(values_grad_all, "cp", scatter_dimension=0, tiled=True),
        lax.psum_scatter(forget_grad_term, "cp", scatter_dimension=0, tiled=True),
    )
    grad_query_head = grad_query_acc.reshape(ctx_rows, local_heads * head_size).astype(jnp.bfloat16)
    grad_query_tok, grad_key_tok, grad_value_tok, grad_forget_tok = (
        lax.all_to_all(grad_query_head, "sp", split_axis=0, concat_axis=1, tiled=True),
        lax.all_to_all(key_sum.astype(jnp.bfloat16), "sp", split_axis=0, concat_axis=1, tiled=True),
        lax.all_to_all(
            value_sum.astype(jnp.bfloat16), "sp", split_axis=0, concat_axis=1, tiled=True
        ),
        lax.all_to_all(
            forget_sum.astype(jnp.bfloat16), "sp", split_axis=0, concat_axis=1, tiled=True
        ),
    )
    grad_forget_pre = (grad_forget_tok.astype(jnp.float32) * jax.nn.sigmoid(-forget_pre)).astype(
        jnp.bfloat16
    )
    grad_normed = (
        matmul_right_t(grad_query_tok, full_query)
        + matmul_right_t(grad_key_tok, full_key)
        + matmul_right_t(grad_value_tok, full_value)
        + matmul_right_t(grad_gate_pre, full_outgate)
        + matmul_right_t(grad_forget_pre, full_forget)
    )
    attn_gain_term = jnp.sum(grad_normed * input_f * inv_first, axis=0)
    bias_term = jnp.sum(grad_forget_pre.astype(jnp.float32), axis=0)
    tokens_grad = grad_mid + norm_back(grad_normed, input_f, inv_first, attn_gain)
    query_term = matmul_left_t(normed, grad_query_tok)
    key_term_w = matmul_left_t(normed, grad_key_tok)
    value_term_w = matmul_left_t(normed, grad_value_tok)
    outgate_term = matmul_left_t(normed, grad_gate_pre)
    forget_term = matmul_left_t(normed, grad_forget_pre)
    output_term = matmul_left_t(gated, grad_branch)
    (
        query_grad,
        key_grad,
        value_grad,
        outgate_grad,
        forget_grad,
        output_weight_grad,
        gate_grad,
        up_grad,
        down_grad,
    ) = (
        lax.psum_scatter(query_term, ("cp", "sp", "fsdp"), scatter_dimension=0, tiled=True),
        lax.psum_scatter(key_term_w, ("cp", "sp", "fsdp"), scatter_dimension=0, tiled=True),
        lax.psum_scatter(value_term_w, ("cp", "sp", "fsdp"), scatter_dimension=0, tiled=True),
        lax.psum_scatter(outgate_term, ("cp", "sp", "fsdp"), scatter_dimension=0, tiled=True),
        lax.psum_scatter(forget_term, ("cp", "sp", "fsdp"), scatter_dimension=0, tiled=True),
        lax.psum_scatter(output_term, ("cp", "sp", "fsdp"), scatter_dimension=0, tiled=True),
        lax.psum_scatter(gate_term, ("cp", "sp", "fsdp"), scatter_dimension=0, tiled=True),
        lax.psum_scatter(up_term, ("cp", "sp", "fsdp"), scatter_dimension=0, tiled=True),
        lax.psum_scatter(down_term, ("cp", "sp", "fsdp"), scatter_dimension=0, tiled=True),
    )
    attn_gain_grad, mlp_gain_grad, forget_bias_grad = lax.psum(
        (attn_gain_term, mlp_gain_term, bias_term), ("cp", "sp", "fsdp")
    )
    return (
        block_out[None],
        tokens_grad[None],
        attn_gain_grad,
        query_grad,
        key_grad,
        value_grad,
        outgate_grad,
        forget_grad,
        forget_bias_grad,
        output_weight_grad,
        mlp_gain_grad,
        gate_grad,
        up_grad,
        down_grad,
    )


def here():
    return (lax.axis_index("cp"), lax.axis_index("sp"), lax.axis_index("fsdp"))


def flip(s, k):
    if k == 1:
        return s + 1 - 2 * lax.rem(s, 2)
    if k == 2:
        return lax.rem(s + 2, 4)
    return 3 - s


def greet(devices):
    sem = pltpu.get_barrier_semaphore()
    for device in devices:
        pl.semaphore_signal(sem, inc=1, device_id=device, device_id_type=MESH)
    pl.semaphore_wait(sem, len(devices))


def rows_of(index, count):
    return pl.ds(pl.multiple_of(index * count, count), count)


def row_loop(total, step, body):
    def one(i, carry):
        return body(rows_of(i, step), carry)

    return one, total // step


class Gather:
    sems = 13

    def __init__(self, src, out, send, recv):
        c, s, f = here()
        self.src, self.out, self.send, self.recv = src, out, send, recv
        self.c, self.s, self.rows = c, s, src.shape[0]
        self.x, self.y, self.sib = (c, flip(s, 1), f), (c, flip(s, 2), f), (1 - c, s, f)
        self.made = []

    def block(self, k, half=None):
        index = self.c * 4 + (self.s if k == 0 else flip(self.s, k))
        n = self.rows
        if half is None:
            return self.out.at[pl.ds(pl.multiple_of(index * n, n), n)]
        return self.out.at[pl.ds(pl.multiple_of(index * n + half * (n // 2), n // 2), n // 2)]

    def copy(self, src, dst, k, device):
        made = REMOTE(src, dst, self.send.at[k], self.recv.at[k], device, MESH)
        made.start()
        self.made.append(made)
        return made

    def start(self):
        half = self.rows // 2
        low, high = self.src.at[pl.ds(0, half)], self.src.at[pl.ds(half, half)]
        self.a = [
            self.copy(low, self.block(0, 0), 0, self.x),
            self.copy(high, self.block(0, 1), 1, self.y),
            self.copy(high, self.block(0, 1), 2, self.x),
            self.copy(low, self.block(0, 0), 3, self.y),
        ]
        self.g = [self.copy(self.src, self.block(0), 4, self.sib)]

    def pass_on(self, ref, k):
        self.g.append(self.copy(ref, ref, k, self.sib))

    def relay(self):
        self.a[0].wait_recv()
        self.b0 = self.copy(self.block(1, 0), self.block(1, 0), 5, self.y)
        self.a[1].wait_recv()
        self.b1 = self.copy(self.block(2, 1), self.block(2, 1), 6, self.x)
        self.pass_on(self.block(1, 0), 7)
        self.pass_on(self.block(2, 1), 8)
        self.a[2].wait_recv()
        self.pass_on(self.block(1, 1), 9)
        self.a[3].wait_recv()
        self.pass_on(self.block(2, 0), 10)

    def finish(self):
        self.b0.wait_recv()
        self.pass_on(self.block(3, 0), 11)
        self.b1.wait_recv()
        self.pass_on(self.block(3, 1), 12)
        for made in self.g:
            made.wait_recv()
        for made in self.made:
            made.wait_send()


class Reduce:
    sems = 10

    @staticmethod
    def scratch(n, w):
        return [
            pltpu.VMEM((4, n, w), BF),
            pltpu.VMEM((4, n, w), BF),
            pltpu.VMEM((4, n, w // 2), BF),
            pltpu.VMEM((2, n, w // 2), BF),
        ]

    def __init__(self, part, refs, send, recv):
        c, s, f = here()
        self.part, self.send, self.recv = part, send, recv
        self.near, self.sums, self.far, self.last = refs
        self.c, self.s = c, s
        self.n, self.w = self.sums.shape[1], self.sums.shape[2]
        self.x, self.y, self.sib = (c, flip(s, 1), f), (c, flip(s, 2), f), (1 - c, s, f)
        self.made = []

    def copy(self, src, dst, k, device):
        made = REMOTE(src, dst, self.send.at[k], self.recv.at[k], device, MESH)
        made.start()
        self.made.append(made)
        return made

    def own(self, k, core):
        index = core * 4 + (self.s if k == 0 else flip(self.s, k))
        return index * self.n

    def start(self):
        self.a = {}
        for sem, k in enumerate((3, 1, 2, 0)):
            src = self.part.at[pl.ds(pl.multiple_of(self.own(k, 1 - self.c), self.n), self.n)]
            self.a[k] = self.copy(src, self.near.at[k], sem, self.sib)

    def chip_sum(self, k):
        self.a[k].wait_recv()
        base = self.own(k, self.c)

        def body(i, carry):
            r = rows_of(i, 32)
            p = self.part[pl.ds(pl.multiple_of(base + i * 32, 32), 32), :].astype(F32)
            self.sums[k, r, :] = (p + self.near[k, r, :].astype(F32)).astype(BF)
            return carry

        lax.fori_loop(0, self.n // 32, body, 0)

    def add(self, k, cols, slot):
        def body(i, carry):
            r = rows_of(i, 32)
            total = self.sums[k, r, cols].astype(F32) + self.far[slot, r, :].astype(F32)
            self.sums[k, r, cols] = total.astype(BF)
            return carry

        lax.fori_loop(0, self.n // 32, body, 0)

    def run(self):
        left, right = pl.ds(0, self.w // 2), pl.ds(self.w // 2, self.w // 2)
        self.chip_sum(3)
        fx = self.copy(self.sums.at[3, :, left], self.far.at[1], 4, self.x)
        fy = self.copy(self.sums.at[3, :, right], self.far.at[3], 5, self.y)
        self.chip_sum(1)
        self.nx = self.copy(self.sums.at[1, :, left], self.far.at[0], 6, self.x)
        self.chip_sum(2)
        self.ny = self.copy(self.sums.at[2, :, right], self.far.at[2], 7, self.y)
        fx.wait_recv()
        self.add(2, left, 1)
        self.by = self.copy(self.sums.at[2, :, left], self.last.at[0], 8, self.y)
        fy.wait_recv()
        self.add(1, right, 3)
        self.bx = self.copy(self.sums.at[1, :, right], self.last.at[1], 9, self.x)
        self.a[0].wait_recv()

    def arrive(self):
        for made in (self.nx, self.ny, self.by, self.bx):
            made.wait_recv()

    def total(self, i, step):
        r = rows_of(i, step)
        base = self.own(0, self.c)
        p = self.part[pl.ds(pl.multiple_of(base + i * step, step), step), :].astype(F32)
        p = p + self.near[0, r, :].astype(F32)
        far = jnp.concatenate([self.far[0, r, :], self.far[2, r, :]], axis=1).astype(F32)
        last = jnp.concatenate([self.last[0, r, :], self.last[1, r, :]], axis=1).astype(F32)
        return p + far + last

    def finish(self):
        for made in self.made:
            made.wait_send()


def partners():
    c, s, f = here()
    return [(c, flip(s, 1), f), (c, flip(s, 2), f), (1 - c, s, f)]


STEP = 32


def mean_square_inverse(values):
    return lax.rsqrt(jnp.mean(values * values, axis=1, keepdims=True) + epsilon)


def enter_kernel(tok_ref, dy_ref, gain_ref, normed_ref, dy_all_ref, mine, s0, r0, s1, r1, l0):
    greet(partners())
    c, s, f = here()
    n = tok_ref.shape[0]

    def body(i, carry):
        r = rows_of(i, STEP)
        v = tok_ref[r, :].astype(F32)
        mine[r, :] = (v * mean_square_inverse(v) * gain_ref[...]).astype(BF)
        return carry

    lax.fori_loop(0, n // STEP, body, 0)
    first = Gather(mine, normed_ref, s0, r0)
    second = Gather(dy_ref, dy_all_ref, s1, r1)
    first.start()
    second.start()
    keep = [
        pltpu.make_async_copy(mine, first.block(0), l0.at[0]),
        pltpu.make_async_copy(dy_ref, second.block(0), l0.at[1]),
    ]
    for made in keep:
        made.start()
    first.relay()
    first.finish()
    second.relay()
    second.finish()
    for made in keep:
        made.wait()


def enter(tokens, cotangent, gain):
    n, w = tokens.shape
    whole = jax.ShapeDtypeStruct((8 * n, w), BF)
    dma = pltpu.SemaphoreType.DMA((Gather.sems,))
    return pl.pallas_call(
        enter_kernel,
        name="enter",
        out_shape=(whole, whole),
        in_specs=[pl.BlockSpec(memory_space=pltpu.VMEM)] * 3,
        out_specs=[pl.BlockSpec(memory_space=pl.ANY)] * 2,
        scratch_shapes=[pltpu.VMEM((n, w), BF), dma, dma, dma, dma, pltpu.SemaphoreType.DMA((2,))],
        compiler_params=pltpu.CompilerParams(
            collective_id=1, has_side_effects=True, vmem_limit_bytes=VMEM_BYTES
        ),
        cost_estimate=pl.CostEstimate(
            flops=50_000_000, bytes_accessed=4 * 8 * n * w * 2, transcendentals=0
        ),
    )(tokens, cotangent, gain[None])


def middle_kernel(
    part_ref, tok_ref, gain_ref, mid_ref, normed_ref,
    near, sums, far, last, mine, s0, r0, s1, r1, l0,
):
    greet(partners())
    reduce = Reduce(part_ref, (near, sums, far, last), s0, r0)
    reduce.start()
    reduce.run()
    reduce.arrive()

    def body(i, carry):
        r = rows_of(i, STEP)
        mid = tok_ref[r, :].astype(F32) + reduce.total(i, STEP)
        mid_ref[r, :] = mid
        mine[r, :] = (mid * mean_square_inverse(mid) * gain_ref[...]).astype(BF)
        return carry

    lax.fori_loop(0, mine.shape[0] // STEP, body, 0)
    gather = Gather(mine, normed_ref, s1, r1)
    gather.start()
    keep = pltpu.make_async_copy(mine, gather.block(0), l0.at[0])
    keep.start()
    reduce.finish()
    gather.relay()
    gather.finish()
    keep.wait()


def middle(part, tokens, gain):
    n, w = tokens.shape
    dma = pltpu.SemaphoreType.DMA((16,))
    vmem = pl.BlockSpec(memory_space=pltpu.VMEM)
    return pl.pallas_call(
        middle_kernel,
        name="middle",
        out_shape=(jax.ShapeDtypeStruct((n, w), F32), jax.ShapeDtypeStruct((8 * n, w), BF)),
        in_specs=[vmem] * 3,
        out_specs=[vmem, pl.BlockSpec(memory_space=pl.ANY)],
        scratch_shapes=Reduce.scratch(n, w)
        + [pltpu.VMEM((n, w), BF), dma, dma, dma, dma, pltpu.SemaphoreType.DMA((2,))],
        compiler_params=pltpu.CompilerParams(
            collective_id=2, has_side_effects=True, vmem_limit_bytes=VMEM_BYTES
        ),
        cost_estimate=pl.CostEstimate(
            flops=50_000_000, bytes_accessed=4 * 8 * n * w * 2, transcendentals=0
        ),
    )(part, tokens, gain[None])


def turn_kernel(
    part_ref, dy_ref, mid_ref, gain_ref, grad_mid_ref, gain_term_ref, branch_ref,
    near, sums, far, last, mine, s0, r0, s1, r1, l0,
):
    greet(partners())
    reduce = Reduce(part_ref, (near, sums, far, last), s0, r0)
    reduce.start()
    reduce.run()
    reduce.arrive()

    def body(i, carry):
        r = rows_of(i, STEP)
        grad = reduce.total(i, STEP)
        mid = mid_ref[r, :]
        inverse = mean_square_inverse(mid)
        weighted = grad * gain_ref[...]
        back = inverse * weighted - mid * inverse**3 * jnp.mean(
            weighted * mid, axis=1, keepdims=True
        )
        grad_mid = dy_ref[r, :].astype(F32) + back
        grad_mid_ref[r, :] = grad_mid
        mine[r, :] = grad_mid.astype(BF)
        return carry + jnp.sum(grad * mid * inverse, axis=0, keepdims=True)

    n, w = mine.shape
    gain_term_ref[...] = lax.fori_loop(0, n // STEP, body, jnp.zeros((1, w), F32))
    gather = Gather(mine, branch_ref, s1, r1)
    gather.start()
    keep = pltpu.make_async_copy(mine, gather.block(0), l0.at[0])
    keep.start()
    reduce.finish()
    gather.relay()
    gather.finish()
    keep.wait()


def turn(part, cotangent, mid, gain):
    n, w = mid.shape
    dma = pltpu.SemaphoreType.DMA((16,))
    vmem = pl.BlockSpec(memory_space=pltpu.VMEM)
    return pl.pallas_call(
        turn_kernel,
        name="turn",
        out_shape=(
            jax.ShapeDtypeStruct((n, w), F32),
            jax.ShapeDtypeStruct((1, w), F32),
            jax.ShapeDtypeStruct((8 * n, w), BF),
        ),
        in_specs=[vmem] * 4,
        out_specs=[vmem, vmem, pl.BlockSpec(memory_space=pl.ANY)],
        scratch_shapes=Reduce.scratch(n, w)
        + [pltpu.VMEM((n, w), BF), dma, dma, dma, dma, pltpu.SemaphoreType.DMA((2,))],
        compiler_params=pltpu.CompilerParams(
            collective_id=3, has_side_effects=True, vmem_limit_bytes=VMEM_BYTES
        ),
        cost_estimate=pl.CostEstimate(
            flops=50_000_000, bytes_accessed=4 * 8 * n * w * 2, transcendentals=0
        ),
    )(part, cotangent, mid, gain[None])


def leave_kernel(
    part_ref, down_ref, tok_ref, grad_mid_ref, mid_ref, gain_ref,
    grad_ref, gain_term_ref, out_ref,
    near, sums, far, last, near2, sums2, far2, last2, s0, r0, s1, r1,
):
    greet(partners())
    reduce = Reduce(part_ref, (near, sums, far, last), s0, r0)
    other = Reduce(down_ref, (near2, sums2, far2, last2), s1, r1)
    reduce.start()
    other.start()
    reduce.run()
    other.run()
    reduce.arrive()

    def body(i, carry):
        r = rows_of(i, STEP)
        grad = reduce.total(i, STEP)
        tok = tok_ref[r, :].astype(F32)
        inverse = mean_square_inverse(tok)
        weighted = grad * gain_ref[...]
        back = inverse * weighted - tok * inverse**3 * jnp.mean(
            weighted * tok, axis=1, keepdims=True
        )
        grad_ref[r, :] = grad_mid_ref[r, :] + back
        return carry + jnp.sum(grad * tok * inverse, axis=0, keepdims=True)

    n, w = tok_ref.shape
    gain_term_ref[...] = lax.fori_loop(0, n // STEP, body, jnp.zeros((1, w), F32))
    other.arrive()

    def body2(i, carry):
        r = rows_of(i, STEP)
        out_ref[r, :] = (mid_ref[r, :] + other.total(i, STEP)).astype(BF)
        return carry

    lax.fori_loop(0, n // STEP, body2, 0)
    reduce.finish()
    other.finish()


def leave(part, down_part, tokens, grad_mid, mid, gain):
    n, w = mid.shape
    dma = pltpu.SemaphoreType.DMA((16,))
    vmem = pl.BlockSpec(memory_space=pltpu.VMEM)
    return pl.pallas_call(
        leave_kernel,
        name="leave",
        out_shape=(
            jax.ShapeDtypeStruct((n, w), F32),
            jax.ShapeDtypeStruct((1, w), F32),
            jax.ShapeDtypeStruct((n, w), BF),
        ),
        in_specs=[vmem] * 6,
        out_specs=[vmem] * 3,
        scratch_shapes=Reduce.scratch(n, w) + Reduce.scratch(n, w) + [dma, dma, dma, dma],
        compiler_params=pltpu.CompilerParams(
            collective_id=4, has_side_effects=True, vmem_limit_bytes=VMEM_BYTES
        ),
        cost_estimate=pl.CostEstimate(
            flops=50_000_000, bytes_accessed=4 * 8 * n * w * 2, transcendentals=0
        ),
    )(part, down_part, tokens, grad_mid, mid, gain[None])


BQ = 256
BK = 256
AUG = 128


def dot(a, b, ca, cb):
    return lax.dot_general(a, b, (((ca,), (cb,)), ((), ())), preferred_element_type=F32)


def three_parts(v):
    hi = v.astype(BF).astype(F32)
    mid = (v - hi).astype(BF).astype(F32)
    low = (v - hi - mid).astype(BF).astype(F32)
    return hi, mid, low


def triangle(n, suffix):
    a = lax.broadcasted_iota(jnp.int32, (n, n), 0)
    b = lax.broadcasted_iota(jnp.int32, (n, n), 1)
    return jnp.where(a >= b if suffix else a <= b, 1.0, 0.0).astype(BF)


def log_sigmoid(v):
    return jnp.minimum(v, 0.0) - jnp.log1p(jnp.exp(-jnp.abs(v)))


def doc_starts(ends_ref, pos):
    start = jnp.zeros_like(pos)
    for n in range(ends_ref.shape[0]):
        end = ends_ref[n]
        start = jnp.where(pos >= end, jnp.maximum(start, end), start)
    return start


def first_block(ends_ref, pos):
    start = jnp.int32(0)
    for n in range(ends_ref.shape[0]):
        end = ends_ref[n]
        start = jnp.where(pos >= end, jnp.maximum(start, end), start)
    return start // BK


def extend(prefix_row, sign_first):
    hi, mid, low = three_parts(prefix_row)
    r = lax.broadcasted_iota(jnp.int32, (16, prefix_row.shape[1]), 0)
    base = 0 if sign_first else 3
    sign = 1.0 if sign_first else -1.0
    ones = (r >= 3) & (r < 6) if sign_first else r < 3
    out = jnp.where(ones, 1.0, 0.0)
    out = jnp.where(r == base, sign * hi, out)
    out = jnp.where(r == base + 1, sign * mid, out)
    return jnp.where(r == base + 2, sign * low, out)


def lay_out(place_ref, cat_ref, prefix_ref, heads, hd, slab, qa, ka, kta):
    hw = heads * hd
    slabs = cat_ref.shape[1] // slab
    for p in range(slabs):
        src = pl.ds(pl.multiple_of(place_ref[p] * slab, slab), slab)
        dst = pl.ds(p * slab, slab)
        for h in range(heads):
            q = cat_ref[h * hd : (h + 1) * hd, src].astype(BF).astype(F32)
            row = prefix_ref[h : h + 1, dst]
            rest = jnp.zeros((AUG - hd - 16, slab), F32)
            qe = jnp.concatenate([q * hd**-0.5, extend(row, True), rest], axis=0)
            qa[h, :, dst] = qe.astype(BF)
            k = cat_ref[hw + h * hd : hw + (h + 1) * hd, src].astype(BF).astype(F32)
            ke = jnp.concatenate([k, extend(row, False), rest], axis=0)
            if kta is not None:
                kta[h, :, dst] = ke.astype(BF)
            ka[h, dst, :] = ke.T.astype(BF)


def attention_kernel(
    place_ref, ends_ref, cat_ref, bias_ref,
    gated_ref, att_ref, exact_ref, lse_ref, prefix_ref,
    qa, ka, va, *, heads, hd, slab,
):
    hw = heads * hd
    tokens = cat_ref.shape[1]
    slabs = tokens // slab
    tri = triangle(slab, False)
    carry = jnp.zeros((16, 1), F32)
    for p in range(slabs):
        src = pl.ds(pl.multiple_of(place_ref[p] * slab, slab), slab)
        pre = cat_ref[4 * hw : 4 * hw + 16, src] + bias_ref[:, 0:1]
        steps = log_sigmoid(pre).astype(BF)
        part = dot(steps, tri, 1, 0) + carry
        prefix_ref[:, p * slab : (p + 1) * slab] = part
        carry = part[:, slab - 1 : slab]
        for h in range(heads):
            va[h, :, p * slab : (p + 1) * slab] = cat_ref[
                2 * hw + h * hd : 2 * hw + (h + 1) * hd, src
            ].astype(BF)
    lay_out(place_ref, cat_ref, prefix_ref, heads, hd, slab, qa, ka, None)
    per = slab // BQ

    def one_query_block(qb, unused):
        q0 = pl.multiple_of(qb * BQ, BQ)
        pos = q0 + lax.broadcasted_iota(jnp.int32, (1, BQ), 1)
        start = doc_starts(ends_ref, pos)
        low = first_block(ends_ref, q0)
        inside = lax.broadcasted_iota(jnp.int32, (BK, BQ), 0)

        def one_key_block(kb, held):
            k0 = pl.multiple_of(kb * BK, BK)
            allowed = (inside <= pos - k0) & (inside >= start - k0)
            out = []
            for h in range(heads):
                m, l, acc = held[h]
                st = dot(ka[h, pl.ds(k0, BK), :], qa[h, :, pl.ds(q0, BQ)], 1, 0)
                st = jnp.where(allowed, st, very_low)
                new = jnp.maximum(m, jnp.max(st, axis=0, keepdims=True))
                p = jnp.exp(st - new)
                scale = jnp.exp(m - new)
                l = l * scale + jnp.sum(p, axis=0, keepdims=True)
                acc = acc * scale + dot(va[h, :, pl.ds(k0, BK)], p.astype(BF), 1, 0)
                out.append((new, l, acc))
            return tuple(out)

        begin = tuple(
            (jnp.full((1, BQ), very_low, F32), jnp.zeros((1, BQ), F32), jnp.zeros((hd, BQ), F32))
            for _ in range(heads)
        )
        done = lax.fori_loop(low, qb + 1, one_key_block, begin)
        dst = pl.ds(pl.multiple_of(place_ref[qb // per] * slab + lax.rem(qb, per) * BQ, BQ), BQ)
        for h in range(heads):
            m, l, acc = done[h]
            lse_ref[h : h + 1, pl.ds(q0, BQ)] = m + jnp.log(l)
            exact = acc / l
            rounded = exact.astype(BF)
            exact_ref[h * hd : (h + 1) * hd, dst] = exact
            att_ref[h * hd : (h + 1) * hd, dst] = rounded
            gate = jax.nn.sigmoid(cat_ref[3 * hw + h * hd : 3 * hw + (h + 1) * hd, dst])
            gated_ref[h * hd : (h + 1) * hd, dst] = (rounded.astype(F32) * gate).astype(BF)
        return unused

    lse_ref[...] = jnp.zeros_like(lse_ref)
    lax.fori_loop(0, tokens // BQ, one_query_block, 0)


def attention(place, ends, cat, bias, heads, hd, slab):
    tokens = cat.shape[1]
    hw = heads * hd
    vmem = pl.BlockSpec(memory_space=pltpu.VMEM)
    smem = pl.BlockSpec(memory_space=pltpu.SMEM)
    return pl.pallas_call(
        functools.partial(attention_kernel, heads=heads, hd=hd, slab=slab),
        name="attention",
        out_shape=(
            jax.ShapeDtypeStruct((hw, tokens), BF),
            jax.ShapeDtypeStruct((hw, tokens), BF),
            jax.ShapeDtypeStruct((hw, tokens), F32),
            jax.ShapeDtypeStruct((8, tokens), F32),
            jax.ShapeDtypeStruct((16, tokens), F32),
        ),
        in_specs=[smem, smem, vmem, vmem],
        out_specs=[vmem] * 5,
        scratch_shapes=[
            pltpu.VMEM((heads, AUG, tokens), BF),
            pltpu.VMEM((heads, tokens, AUG), BF),
            pltpu.VMEM((heads, hd, tokens), BF),
        ],
        compiler_params=pltpu.CompilerParams(vmem_limit_bytes=VMEM_BYTES),
        cost_estimate=pl.CostEstimate(
            flops=8 * heads * tokens * tokens * hd, bytes_accessed=cat.size * 4,
            transcendentals=heads * tokens * tokens // 2,
        ),
    )(place, ends, cat, bias)


def attention_back_kernel(
    place_ref, ends_ref, cat_ref, bias_ref, gg_ref, att_ref, exact_ref, lse_ref, prefix_ref,
    out_ref, bias_grad_ref,
    qa, ka, kta, va, do, delta_ref, dk, dv, gp, *, heads, hd, slab,
):
    hw = heads * hd
    tokens = cat_ref.shape[1]
    slabs = tokens // slab
    per = slab // BQ
    lay_out(place_ref, cat_ref, prefix_ref, heads, hd, slab, qa, ka, kta)
    delta_ref[...] = jnp.zeros_like(delta_ref)
    gp[...] = jnp.zeros_like(gp)
    dk[...] = jnp.zeros_like(dk)
    dv[...] = jnp.zeros_like(dv)
    out_ref[4 * hw :, :] = jnp.zeros((out_ref.shape[0] - 4 * hw, tokens), BF)
    for p in range(slabs):
        src = pl.ds(pl.multiple_of(place_ref[p] * slab, slab), slab)
        dst = pl.ds(p * slab, slab)
        for h in range(heads):
            rows = slice(h * hd, (h + 1) * hd)
            gate = jax.nn.sigmoid(cat_ref[3 * hw + h * hd : 3 * hw + (h + 1) * hd, src])
            gg = gg_ref[rows, src]
            low = (gg * gate).astype(BF)
            do[h, :, dst] = low
            delta_ref[h : h + 1, dst] = jnp.sum(
                low.astype(F32) * exact_ref[rows, src], axis=0, keepdims=True
            )
            gate_grad = gg * att_ref[rows, src].astype(F32) * gate * (1.0 - gate)
            out_ref[3 * hw + h * hd : 3 * hw + (h + 1) * hd, src] = gate_grad.astype(BF)
            v = cat_ref[2 * hw + h * hd : 2 * hw + (h + 1) * hd, src]
            va[h, dst, :] = v.T.astype(BF)

    def one_query_block(qb, unused):
        q0 = pl.multiple_of(qb * BQ, BQ)
        pos = q0 + lax.broadcasted_iota(jnp.int32, (1, BQ), 1)
        start = doc_starts(ends_ref, pos)
        low = first_block(ends_ref, q0)
        inside = lax.broadcasted_iota(jnp.int32, (BK, BQ), 0)

        def one_key_block(kb, held):
            k0 = pl.multiple_of(kb * BK, BK)
            keys = pl.ds(k0, BK)
            allowed = (inside <= pos - k0) & (inside >= start - k0)
            out = []
            for h in range(heads):
                queries = qa[h, :, pl.ds(q0, BQ)]
                grads = do[h, :, pl.ds(q0, BQ)]
                st = dot(ka[h, keys, :], queries, 1, 0) - lse_ref[h : h + 1, pl.ds(q0, BQ)]
                p = jnp.exp(jnp.where(allowed, st, very_low))
                dp = dot(va[h, keys, :], grads, 1, 0) - delta_ref[h : h + 1, pl.ds(q0, BQ)]
                ds = (p * dp).astype(BF)
                out.append(held[h] + dot(kta[h, :, keys], ds, 1, 0))
                dk[h, :, keys] += dot(queries, ds, 1, 1)
                dv[h, :, keys] += dot(grads, p.astype(BF), 1, 1)
            return tuple(out)

        begin = tuple(jnp.zeros((AUG, BQ), F32) for _ in range(heads))
        done = lax.fori_loop(low, qb + 1, one_key_block, begin)
        dst = pl.ds(pl.multiple_of(place_ref[qb // per] * slab + lax.rem(qb, per) * BQ, BQ), BQ)
        for h in range(heads):
            out_ref[h * hd : (h + 1) * hd, dst] = (done[h][0:hd, :] * hd**-0.5).astype(BF)
            gp[h : h + 1, pl.ds(q0, BQ)] = done[h][hd : hd + 1, :]
        return unused

    lax.fori_loop(0, tokens // BQ, one_query_block, 0)
    tri = triangle(slab, True)
    carry = jnp.zeros((16, 1), F32)
    bias_grad = jnp.zeros((16, 1), F32)
    for p in reversed(range(slabs)):
        src = pl.ds(pl.multiple_of(place_ref[p] * slab, slab), slab)
        dst = pl.ds(p * slab, slab)
        for h in range(heads):
            out_ref[hw + h * hd : hw + (h + 1) * hd, src] = dk[h, 0:hd, dst].astype(BF)
            out_ref[2 * hw + h * hd : 2 * hw + (h + 1) * hd, src] = dv[h, :, dst].astype(BF)
            gp[h : h + 1, dst] = gp[h : h + 1, dst] - dk[h, hd + 3 : hd + 4, dst]
        grad = gp[:, dst]
        total = carry
        for piece in three_parts(grad):
            total = total + dot(piece.astype(BF), tri, 1, 0)
        carry = total[:, 0:1]
        pre = cat_ref[4 * hw : 4 * hw + 16, src] + bias_ref[:, 0:1]
        low = (total.astype(BF).astype(F32) * jax.nn.sigmoid(-pre)).astype(BF)
        out_ref[4 * hw : 4 * hw + 16, src] = low
        bias_grad = bias_grad + jnp.sum(low.astype(F32), axis=1, keepdims=True)
    bias_grad_ref[...] = jnp.broadcast_to(bias_grad, bias_grad_ref.shape)


def attention_back(place, ends, cat, bias, gg, att, exact, lse, prefix, heads, hd, slab):
    tokens = cat.shape[1]
    vmem = pl.BlockSpec(memory_space=pltpu.VMEM)
    smem = pl.BlockSpec(memory_space=pltpu.SMEM)
    return pl.pallas_call(
        functools.partial(attention_back_kernel, heads=heads, hd=hd, slab=slab),
        name="attention_back",
        out_shape=(
            jax.ShapeDtypeStruct(cat.shape, BF),
            jax.ShapeDtypeStruct((16, 128), F32),
        ),
        in_specs=[smem, smem] + [vmem] * 7,
        out_specs=[vmem] * 2,
        scratch_shapes=[
            pltpu.VMEM((heads, AUG, tokens), BF),
            pltpu.VMEM((heads, tokens, AUG), BF),
            pltpu.VMEM((heads, AUG, tokens), BF),
            pltpu.VMEM((heads, tokens, hd), BF),
            pltpu.VMEM((heads, hd, tokens), BF),
            pltpu.VMEM((8, tokens), F32),
            pltpu.VMEM((heads, AUG, tokens), F32),
            pltpu.VMEM((heads, hd, tokens), F32),
            pltpu.VMEM((16, tokens), F32),
        ],
        compiler_params=pltpu.CompilerParams(vmem_limit_bytes=VMEM_BYTES),
        cost_estimate=pl.CostEstimate(
            flops=20 * heads * tokens * tokens * hd, bytes_accessed=cat.size * 8,
            transcendentals=heads * tokens * tokens // 2,
        ),
    )(place, ends, cat, bias, gg, att, exact, lse, prefix)


def spread_rows(grad, plane, depth):
    rows, cols = grad.shape
    part = rows // (plane * depth)
    return grad.reshape(plane, depth, part, cols).transpose(1, 0, 2, 3).reshape(rows, cols)


def local_plane(
    tokens, out_cotangent, seq_lengths, slab_place, attn_gain, query_weight, key_weight,
    value_weight, outgate_weight, forget_weight, forget_bias, output_weight, mlp_gain,
    gate_weight, up_weight, down_weight,
):
    plane_axes = ("cp", "sp")
    plane = lax.axis_size("cp") * lax.axis_size("sp")
    depth = lax.axis_size("fsdp")
    place = lax.axis_index("cp") * lax.axis_size("sp") + lax.axis_index("sp")
    head_count = forget_weight.shape[1]
    width = tokens.shape[2]
    hd = width // head_count
    heads = head_count // plane
    hw = heads * hd
    fw = gate_weight.shape[1] // plane
    shard = query_weight.shape[0]
    group_rows = tokens.shape[1] * plane
    slab = group_rows // slab_place.shape[1]

    def columns(weight, count):
        return lax.dynamic_slice_in_dim(weight, place * count, count, 1)

    inputs, cotangent = tokens[0], out_cotangent[0]
    slabs = slab_place.shape[1]
    order = jnp.arange(slabs, dtype=jnp.int32)
    storage = jnp.sum(
        jnp.where(slab_place[0][None, :] == order[:, None], order[None, :], 0), axis=1
    )
    ends = jnp.cumsum(seq_lengths[0])

    forget_part = jnp.pad(columns(forget_weight, heads), ((0, 0), (0, 128 - heads)))
    own_attn = jnp.concatenate(
        [
            columns(query_weight, hw),
            columns(key_weight, hw),
            columns(value_weight, hw),
            columns(outgate_weight, hw),
            forget_part,
        ],
        axis=1,
    )
    own_out = columns(output_weight, hw)
    own_mlp = jnp.concatenate(
        [columns(gate_weight, fw), columns(up_weight, fw), columns(down_weight, fw)], axis=1
    )
    w_attn = lax.all_gather(own_attn, "fsdp", axis=0, tiled=True)
    w_out_cols = lax.all_gather(own_out, "fsdp", axis=0, tiled=True)
    w_mlp = lax.all_gather(own_mlp, "fsdp", axis=0, tiled=True)
    w_out = lax.all_to_all(w_out_cols, plane_axes, split_axis=0, concat_axis=1, tiled=True)

    normed, cotangent_all = enter(inputs, cotangent, attn_gain)
    cat = dot(w_attn, normed, 0, 1)
    bias_own = lax.dynamic_slice_in_dim(forget_bias, place * heads, heads, 0)
    bias = jnp.broadcast_to(jnp.pad(bias_own, (0, 16 - heads))[:, None], (16, 128))
    gated, att, exact, lse, prefix = attention(storage, ends, cat, bias, heads, hd, slab)
    mid_part = dot(gated, w_out, 0, 0).astype(BF)
    mid, normed_mlp = middle(mid_part, inputs, mlp_gain)

    w_gate, w_up, w_down = w_mlp[:, :fw], w_mlp[:, fw : 2 * fw], w_mlp[:, 2 * fw :]
    gate_lin = matmul(normed_mlp, w_gate)
    up_lin = matmul(normed_mlp, w_up)
    gate_sig = jax.nn.sigmoid(gate_lin)
    activated = gate_lin * gate_sig
    hidden = (activated * up_lin).astype(BF)
    grad_hidden = matmul(cotangent_all, w_down)
    grad_gate_lin = (grad_hidden * up_lin * gate_sig * (1.0 + gate_lin * (1.0 - gate_sig))).astype(
        BF
    )
    grad_up_lin = (grad_hidden * activated).astype(BF)
    mlp_part = (
        matmul_right_t(grad_gate_lin, w_gate) + matmul_right_t(grad_up_lin, w_up)
    ).astype(BF)
    down_part = matmul_right_t(hidden, w_down).astype(BF)
    mlp_terms = jnp.concatenate(
        [
            matmul_left_t(normed_mlp, grad_gate_lin).astype(BF),
            matmul_left_t(normed_mlp, grad_up_lin).astype(BF),
            matmul_left_t(cotangent_all, hidden).astype(BF),
        ],
        axis=1,
    )
    mlp_grad = lax.psum_scatter(
        spread_rows(mlp_terms, plane, depth), "fsdp", scatter_dimension=0, tiled=True
    )
    grad_mid, mlp_gain_term, branch = turn(mlp_part, cotangent, mid, mlp_gain)

    grad_gated = dot(w_out, branch, 1, 1)
    grad_cat, bias_grad = attention_back(
        storage, ends, cat, bias, grad_gated, att, exact, lse, prefix, heads, hd, slab
    )
    out_term = dot(gated, branch, 1, 0).astype(BF)
    attn_term = dot(normed, grad_cat, 0, 1).astype(BF)
    attn_part = dot(grad_cat, w_attn, 0, 1).astype(BF)
    attn_grad = lax.psum_scatter(
        spread_rows(attn_term, plane, depth), "fsdp", scatter_dimension=0, tiled=True
    )
    output_weight_grad = lax.psum_scatter(out_term, "fsdp", scatter_dimension=0, tiled=True)
    tokens_grad, attn_gain_term, block_out = leave(
        attn_part, down_part, inputs, grad_mid, mid, attn_gain
    )

    def to_rows(grad):
        part = grad.shape[0] // plane
        got = lax.all_to_all(
            grad.reshape(plane, part, -1), plane_axes, split_axis=0, concat_axis=0, tiled=True
        )
        return got.astype(F32)

    mlp_rows = to_rows(mlp_grad)
    attn_rows = to_rows(attn_grad)

    def pick(rows, begin, count):
        part = rows[:, :, begin : begin + count].transpose(1, 0, 2)
        return part.reshape(part.shape[0], -1)

    gate_grad, up_grad, down_grad = (pick(mlp_rows, i * fw, fw) for i in range(3))
    query_grad, key_grad, value_grad, outgate_grad = (
        pick(attn_rows, i * hw, hw) for i in range(4)
    )
    forget_grad = pick(attn_rows, 4 * hw, heads)
    bias_term = lax.dynamic_update_slice_in_dim(
        jnp.zeros((head_count,), F32), bias_grad[:heads, 0], place * heads, 0
    )
    attn_gain_grad, mlp_gain_grad, forget_bias_grad = lax.psum(
        (attn_gain_term[0], mlp_gain_term[0], bias_term), ("cp", "sp", "fsdp")
    )
    return (
        block_out[None],
        tokens_grad[None],
        attn_gain_grad,
        query_grad,
        key_grad,
        value_grad,
        outgate_grad,
        forget_grad,
        forget_bias_grad,
        output_weight_grad.astype(F32),
        mlp_gain_grad,
        gate_grad,
        up_grad,
        down_grad,
    )


def fits_plane(mesh, tokens, slab_place, forget_weight, gate_weight):
    sizes = dict(mesh.shape)
    if (sizes["cp"], sizes["sp"]) != (2, 4):
        return False
    plane = sizes["cp"] * sizes["sp"]
    width = tokens.shape[2]
    head_count = forget_weight.shape[1]
    group_rows = tokens.shape[1]
    slab = group_rows // slab_place.shape[1]
    heads = head_count // plane
    return (
        head_count % plane == 0
        and heads <= 8
        and width // head_count == 64
        and slab % 256 == 0
        and group_rows <= 2048
        and width % 256 == 0
        and gate_weight.shape[1] % (128 * plane) == 0
        and width % (16 * plane * sizes["fsdp"]) == 0
        and (group_rows // plane) % 64 == 0
    )


def shard(mesh, fn):
    return jax.shard_map(
        fn,
        mesh=mesh,
        in_specs=(
            P("fsdp", ("cp", "sp"), None),
            P("fsdp", ("cp", "sp"), None),
            P("fsdp", None),
            P("fsdp", None),
            P(),
            P("fsdp", None),
            P("fsdp", None),
            P("fsdp", None),
            P("fsdp", None),
            P("fsdp", None),
            P(),
            P("fsdp", None),
            P(),
            P("fsdp", None),
            P("fsdp", None),
            P("fsdp", None),
        ),
        out_specs=(
            P("fsdp", ("cp", "sp"), None),
            P("fsdp", ("cp", "sp"), None),
            P(),
            P(("cp", "sp", "fsdp"), None),
            P(("cp", "sp", "fsdp"), None),
            P(("cp", "sp", "fsdp"), None),
            P(("cp", "sp", "fsdp"), None),
            P(("cp", "sp", "fsdp"), None),
            P(),
            P(("cp", "sp", "fsdp"), None),
            P(),
            P(("cp", "sp", "fsdp"), None),
            P(("cp", "sp", "fsdp"), None),
            P(("cp", "sp", "fsdp"), None),
        ),
        check_vma=False,
    )


def solution(mesh):
    def run(*args):
        fast = fits_plane(mesh, args[0], args[3], args[9], args[13])
        return shard(mesh, local_plane if fast else local)(*args)

    return run
```

```python
import functools

import jax
import jax.numpy as jnp
from jax import lax
from jax.experimental import pallas as pl
from jax.experimental.pallas import tpu as pltpu
from jax.sharding import PartitionSpec as P

epsilon = 1e-06
very_low = -1e30
MESH = pl.DeviceIdType.MESH
BF = jnp.bfloat16
F32 = jnp.float32
REMOTE = pltpu.make_async_remote_copy
VMEM_BYTES = 60 * 1024 * 1024


def matmul(left, right):
    return jnp.dot(left, right, preferred_element_type=jnp.float32)


def matmul_right_t(left, right):
    return lax.dot_general(
        left, right, (((1,), (1,)), ((), ())), preferred_element_type=jnp.float32
    )


def matmul_left_t(left, right):
    return lax.dot_general(
        left, right, (((0,), (0,)), ((), ())), preferred_element_type=jnp.float32
    )


def rms_inverse(values):
    return lax.rsqrt(jnp.mean(values * values, axis=1, keepdims=True) + epsilon)


def norm_back(upstream, values, inverse, gain):
    weighted = upstream * gain
    return inverse * weighted - values * inverse**3 * jnp.mean(
        weighted * values, axis=1, keepdims=True
    )


def row_layout(place_row, lens_row, count, slab_rows):
    rows = jnp.arange(count, dtype=jnp.int32)
    slab_index = rows // slab_rows
    table = (
        slab_index[:, None] == jnp.arange(place_row.shape[0], dtype=jnp.int32)[None, :]
    ).astype(jnp.int32)
    position = jnp.sum(table * place_row[None, :], axis=1) * slab_rows + rows % slab_rows
    ends = jnp.cumsum(lens_row)
    segment = jnp.sum((position[:, None] >= ends[None, :]).astype(jnp.int32), axis=1)
    return (position, segment)


def forget_prefix(log_all, place_row, slab_rows):
    slabs = place_row.shape[0]
    steps = log_all.astype(jnp.float32).reshape(slabs, slab_rows, -1)
    inside = jnp.cumsum(steps, axis=1)
    totals = inside[:, -1, :]
    earlier = (place_row[None, :] < place_row[:, None]).astype(jnp.float32)
    offsets = jnp.dot(earlier, totals, precision=lax.Precision.HIGHEST)
    return (inside + offsets[:, None, :]).reshape(slabs * slab_rows, -1)


def prefix_back(grad_prefix, place_row, slab_rows):
    slabs = place_row.shape[0]
    steps = grad_prefix.reshape(slabs, slab_rows, -1)
    inside = jnp.flip(jnp.cumsum(jnp.flip(steps, 1), axis=1), 1)
    totals = inside[:, 0, :]
    later = (place_row[None, :] > place_row[:, None]).astype(jnp.float32)
    offsets = jnp.dot(later, totals, precision=lax.Precision.HIGHEST)
    return (inside + offsets[:, None, :]).reshape(slabs * slab_rows, -1)


def local(
    tokens,
    out_cotangent,
    seq_lengths,
    slab_place,
    attn_gain,
    query_weight,
    key_weight,
    value_weight,
    outgate_weight,
    forget_weight,
    forget_bias,
    output_weight,
    mlp_gain,
    gate_weight,
    up_weight,
    down_weight,
):
    seq_devices = lax.axis_size("sp")
    ctx_devices = lax.axis_size("cp")
    ctx_index = lax.axis_index("cp")
    tok_rows = tokens.shape[1]
    model_width = tokens.shape[2]
    head_count = forget_weight.shape[1]
    local_heads = head_count // seq_devices
    head_size = model_width // head_count
    ctx_rows = tok_rows * seq_devices
    group_rows = ctx_rows * ctx_devices
    slab_rows = ctx_rows // 2
    key_block = min(512, group_rows)
    key_blocks = group_rows // key_block
    score_scale = head_size ** (-0.5)
    place_row = slab_place[0]
    lens_row = seq_lengths[0]
    ctx_start = ctx_index * ctx_rows
    inputs = tokens[0]
    input_f = inputs.astype(jnp.float32)
    weights_attn = (
        lax.all_gather(query_weight, "fsdp", axis=0, tiled=True),
        lax.all_gather(key_weight, "fsdp", axis=0, tiled=True),
        lax.all_gather(value_weight, "fsdp", axis=0, tiled=True),
        lax.all_gather(outgate_weight, "fsdp", axis=0, tiled=True),
        lax.all_gather(forget_weight, "fsdp", axis=0, tiled=True),
        lax.all_gather(output_weight, "fsdp", axis=0, tiled=True),
    )
    full_query, full_key, full_value, full_outgate, full_forget, full_output = weights_attn
    inv_first = rms_inverse(input_f)
    normed = (input_f * inv_first * attn_gain).astype(jnp.bfloat16)
    queries = matmul(normed, full_query).astype(jnp.bfloat16)
    keys = matmul(normed, full_key).astype(jnp.bfloat16)
    values = matmul(normed, full_value).astype(jnp.bfloat16)
    out_gate = jax.nn.sigmoid(matmul(normed, full_outgate))
    forget_pre = matmul(normed, full_forget) + forget_bias
    log_forget = jax.nn.log_sigmoid(forget_pre).astype(jnp.bfloat16)
    head_query, head_key, head_value, head_forget = (
        lax.all_to_all(queries, "sp", split_axis=1, concat_axis=0, tiled=True),
        lax.all_to_all(keys, "sp", split_axis=1, concat_axis=0, tiled=True),
        lax.all_to_all(values, "sp", split_axis=1, concat_axis=0, tiled=True),
        lax.all_to_all(log_forget, "sp", split_axis=1, concat_axis=0, tiled=True),
    )
    keys_all, values_all, forget_all = (
        lax.all_gather(head_key, "cp", axis=0, tiled=True),
        lax.all_gather(head_value, "cp", axis=0, tiled=True),
        lax.all_gather(head_forget, "cp", axis=0, tiled=True),
    )
    prefix_all = forget_prefix(forget_all, place_row, slab_rows)
    pos_all, seg_all = row_layout(place_row, lens_row, group_rows, slab_rows)
    query_pos = lax.dynamic_slice_in_dim(pos_all, ctx_start, ctx_rows, 0)
    query_seg = lax.dynamic_slice_in_dim(seg_all, ctx_start, ctx_rows, 0)
    query_prefix = lax.dynamic_slice_in_dim(prefix_all, ctx_start, ctx_rows, 0)
    query_three = head_query.reshape(ctx_rows, local_heads, head_size)
    query_pos_top = jnp.max(query_pos)
    query_seg_low = jnp.min(query_seg)
    query_seg_top = jnp.max(query_seg)
    key_pieces = (
        keys_all.reshape(key_blocks, key_block, local_heads, head_size),
        values_all.reshape(key_blocks, key_block, local_heads, head_size),
        prefix_all.reshape(key_blocks, key_block, local_heads),
        pos_all.reshape(key_blocks, key_block),
        seg_all.reshape(key_blocks, key_block),
    )

    def block_live(key_pos, key_seg):
        return (
            (query_pos_top >= jnp.min(key_pos))
            & (query_seg_top >= jnp.min(key_seg))
            & (jnp.max(key_seg) >= query_seg_low)
        )

    def block_scores(key_piece, key_prefix, key_pos, key_seg):
        raw = (
            jnp.einsum("qhd,khd->hqk", query_three, key_piece, preferred_element_type=jnp.float32)
            * score_scale
        )
        raw = raw + query_prefix.T[:, :, None] - key_prefix.T[:, None, :]
        allowed = (query_pos[:, None] >= key_pos[None, :]) & (
            query_seg[:, None] == key_seg[None, :]
        )
        return (raw, allowed[None, :, :])

    def total_work(carry, piece):
        running_max, running_sum = carry
        key_piece, value_piece, key_prefix, key_pos, key_seg = piece
        raw, allowed = block_scores(key_piece, key_prefix, key_pos, key_seg)
        new_max = jnp.maximum(running_max, jnp.max(jnp.where(allowed, raw, very_low), axis=2))
        terms = jnp.where(allowed, jnp.exp(raw - new_max[:, :, None]), 0.0)
        new_sum = running_sum * jnp.exp(running_max - new_max) + jnp.sum(terms, axis=2)
        return (new_max, new_sum)

    def total_step(carry, piece):
        live = block_live(piece[3], piece[4])
        return (lax.cond(live, total_work, lambda held, unused: held, carry, piece), None)

    start_max = jnp.full((local_heads, ctx_rows), very_low, jnp.float32)
    start_sum = jnp.zeros((local_heads, ctx_rows), jnp.float32)
    (final_max, final_sum), _ = lax.scan(total_step, (start_max, start_sum), key_pieces)
    log_total = final_max + jnp.log(final_sum)

    def output_work(carry, piece):
        coarse, fine = carry
        key_piece, value_piece, key_prefix, key_pos, key_seg = piece
        raw, allowed = block_scores(key_piece, key_prefix, key_pos, key_seg)
        probs = jnp.where(allowed, jnp.exp(raw - log_total[:, :, None]), 0.0)
        rounded = probs.astype(jnp.bfloat16)
        rest = (probs - rounded.astype(jnp.float32)).astype(jnp.bfloat16)
        coarse = coarse + jnp.einsum(
            "hqk,khd->qhd", rounded, value_piece, preferred_element_type=jnp.float32
        )
        fine = fine + jnp.einsum(
            "hqk,khd->qhd", rest, value_piece, preferred_element_type=jnp.float32
        )
        return (coarse, fine)

    def output_step(carry, piece):
        live = block_live(piece[3], piece[4])
        return (lax.cond(live, output_work, lambda held, unused: held, carry, piece), None)

    zero_out = jnp.zeros((ctx_rows, local_heads, head_size), jnp.float32)
    (coarse_out, fine_out), _ = lax.scan(output_step, (zero_out, zero_out), key_pieces)
    exact_out = coarse_out + fine_out
    head_out = coarse_out.reshape(ctx_rows, local_heads * head_size).astype(jnp.bfloat16)
    token_out = lax.all_to_all(head_out, "sp", split_axis=0, concat_axis=1, tiled=True)
    token_out_f = token_out.astype(jnp.float32)
    gated = (token_out_f * out_gate).astype(jnp.bfloat16)
    mid = input_f + matmul(gated, full_output)
    weights_mlp = (
        lax.all_gather(gate_weight, "fsdp", axis=0, tiled=True),
        lax.all_gather(up_weight, "fsdp", axis=0, tiled=True),
        lax.all_gather(down_weight, "fsdp", axis=0, tiled=True),
    )
    full_gate, full_up, full_down = weights_mlp
    inv_second = rms_inverse(mid)
    normed_mlp = (mid * inv_second * mlp_gain).astype(jnp.bfloat16)
    gate_lin = matmul(normed_mlp, full_gate)
    up_lin = matmul(normed_mlp, full_up)
    gate_sig = jax.nn.sigmoid(gate_lin)
    activated = gate_lin * gate_sig
    hidden = (activated * up_lin).astype(jnp.bfloat16)
    block_out = (mid + matmul_right_t(hidden, full_down)).astype(jnp.bfloat16)
    cotangent = out_cotangent[0]
    grad_hidden = matmul(cotangent, full_down)
    grad_gate_lin = (grad_hidden * up_lin * gate_sig * (1.0 + gate_lin * (1.0 - gate_sig))).astype(
        jnp.bfloat16
    )
    grad_up_lin = (grad_hidden * activated).astype(jnp.bfloat16)
    grad_normed_mlp = matmul_right_t(grad_gate_lin, full_gate) + matmul_right_t(
        grad_up_lin, full_up
    )
    mlp_gain_term = jnp.sum(grad_normed_mlp * mid * inv_second, axis=0)
    grad_mid = cotangent.astype(jnp.float32) + norm_back(grad_normed_mlp, mid, inv_second, mlp_gain)
    gate_term = matmul_left_t(normed_mlp, grad_gate_lin)
    up_term = matmul_left_t(normed_mlp, grad_up_lin)
    down_term = matmul_left_t(cotangent, hidden)
    grad_branch = grad_mid.astype(jnp.bfloat16)
    grad_gated = matmul_right_t(grad_branch, full_output)
    grad_attended = (grad_gated * out_gate).astype(jnp.bfloat16)
    grad_gate_pre = (grad_gated * token_out_f * out_gate * (1.0 - out_gate)).astype(jnp.bfloat16)
    head_grad = lax.all_to_all(grad_attended, "sp", split_axis=1, concat_axis=0, tiled=True)
    grad_three = head_grad.reshape(ctx_rows, local_heads, head_size)
    delta = jnp.sum(grad_three.astype(jnp.float32) * exact_out, axis=2).T

    def back_work(carry, piece):
        grad_query_acc, grad_prefix_acc = carry
        key_piece, value_piece, key_prefix, key_pos, key_seg = piece
        raw, allowed = block_scores(key_piece, key_prefix, key_pos, key_seg)
        probs = jnp.where(allowed, jnp.exp(raw - log_total[:, :, None]), 0.0)
        rounded = probs.astype(jnp.bfloat16)
        grad_probs = jnp.einsum(
            "qhd,khd->hqk", grad_three, value_piece, preferred_element_type=jnp.float32
        )
        grad_scores = (probs * (grad_probs - delta[:, :, None])).astype(jnp.bfloat16)
        grad_query_acc = (
            grad_query_acc
            + jnp.einsum("hqk,khd->qhd", grad_scores, key_piece, preferred_element_type=jnp.float32)
            * score_scale
        )
        key_term = (
            jnp.einsum("hqk,qhd->khd", grad_scores, query_three, preferred_element_type=jnp.float32)
            * score_scale
        )
        value_term = jnp.einsum(
            "hqk,qhd->khd", rounded, grad_three, preferred_element_type=jnp.float32
        )
        score_f = grad_scores.astype(jnp.float32)
        grad_prefix_acc = grad_prefix_acc + jnp.sum(score_f, axis=2)
        prefix_term = -jnp.sum(score_f, axis=1)
        return ((grad_query_acc, grad_prefix_acc), (key_term, value_term, prefix_term))

    def back_skip(carry, piece):
        empty_kv = jnp.zeros((key_block, local_heads, head_size), jnp.float32)
        empty_prefix = jnp.zeros((local_heads, key_block), jnp.float32)
        return (carry, (empty_kv, empty_kv, empty_prefix))

    def back_step(carry, piece):
        live = block_live(piece[3], piece[4])
        return lax.cond(live, back_work, back_skip, carry, piece)

    start_prefix = jnp.zeros((local_heads, ctx_rows), jnp.float32)
    (grad_query_acc, grad_prefix_q), (key_terms, value_terms, prefix_terms) = lax.scan(
        back_step, (zero_out, start_prefix), key_pieces
    )
    keys_grad_all = key_terms.reshape(group_rows, local_heads * head_size)
    values_grad_all = value_terms.reshape(group_rows, local_heads * head_size)
    prefix_grad_all = jnp.transpose(prefix_terms, (0, 2, 1)).reshape(group_rows, local_heads)
    own_prefix = lax.dynamic_slice_in_dim(prefix_grad_all, ctx_start, ctx_rows, 0)
    prefix_grad_all = lax.dynamic_update_slice_in_dim(
        prefix_grad_all, own_prefix + grad_prefix_q.T, ctx_start, 0
    )
    forget_grad_term = prefix_back(prefix_grad_all, place_row, slab_rows)
    key_sum, value_sum, forget_sum = (
        lax.psum_scatter(keys_grad_all, "cp", scatter_dimension=0, tiled=True),
        lax.psum_scatter(values_grad_all, "cp", scatter_dimension=0, tiled=True),
        lax.psum_scatter(forget_grad_term, "cp", scatter_dimension=0, tiled=True),
    )
    grad_query_head = grad_query_acc.reshape(ctx_rows, local_heads * head_size).astype(jnp.bfloat16)
    grad_query_tok, grad_key_tok, grad_value_tok, grad_forget_tok = (
        lax.all_to_all(grad_query_head, "sp", split_axis=0, concat_axis=1, tiled=True),
        lax.all_to_all(key_sum.astype(jnp.bfloat16), "sp", split_axis=0, concat_axis=1, tiled=True),
        lax.all_to_all(
            value_sum.astype(jnp.bfloat16), "sp", split_axis=0, concat_axis=1, tiled=True
        ),
        lax.all_to_all(
            forget_sum.astype(jnp.bfloat16), "sp", split_axis=0, concat_axis=1, tiled=True
        ),
    )
    grad_forget_pre = (grad_forget_tok.astype(jnp.float32) * jax.nn.sigmoid(-forget_pre)).astype(
        jnp.bfloat16
    )
    grad_normed = (
        matmul_right_t(grad_query_tok, full_query)
        + matmul_right_t(grad_key_tok, full_key)
        + matmul_right_t(grad_value_tok, full_value)
        + matmul_right_t(grad_gate_pre, full_outgate)
        + matmul_right_t(grad_forget_pre, full_forget)
    )
    attn_gain_term = jnp.sum(grad_normed * input_f * inv_first, axis=0)
    bias_term = jnp.sum(grad_forget_pre.astype(jnp.float32), axis=0)
    tokens_grad = grad_mid + norm_back(grad_normed, input_f, inv_first, attn_gain)
    query_term = matmul_left_t(normed, grad_query_tok)
    key_term_w = matmul_left_t(normed, grad_key_tok)
    value_term_w = matmul_left_t(normed, grad_value_tok)
    outgate_term = matmul_left_t(normed, grad_gate_pre)
    forget_term = matmul_left_t(normed, grad_forget_pre)
    output_term = matmul_left_t(gated, grad_branch)
    (
        query_grad,
        key_grad,
        value_grad,
        outgate_grad,
        forget_grad,
        output_weight_grad,
        gate_grad,
        up_grad,
        down_grad,
    ) = (
        lax.psum_scatter(query_term, ("cp", "sp", "fsdp"), scatter_dimension=0, tiled=True),
        lax.psum_scatter(key_term_w, ("cp", "sp", "fsdp"), scatter_dimension=0, tiled=True),
        lax.psum_scatter(value_term_w, ("cp", "sp", "fsdp"), scatter_dimension=0, tiled=True),
        lax.psum_scatter(outgate_term, ("cp", "sp", "fsdp"), scatter_dimension=0, tiled=True),
        lax.psum_scatter(forget_term, ("cp", "sp", "fsdp"), scatter_dimension=0, tiled=True),
        lax.psum_scatter(output_term, ("cp", "sp", "fsdp"), scatter_dimension=0, tiled=True),
        lax.psum_scatter(gate_term, ("cp", "sp", "fsdp"), scatter_dimension=0, tiled=True),
        lax.psum_scatter(up_term, ("cp", "sp", "fsdp"), scatter_dimension=0, tiled=True),
        lax.psum_scatter(down_term, ("cp", "sp", "fsdp"), scatter_dimension=0, tiled=True),
    )
    attn_gain_grad, mlp_gain_grad, forget_bias_grad = lax.psum(
        (attn_gain_term, mlp_gain_term, bias_term), ("cp", "sp", "fsdp")
    )
    return (
        block_out[None],
        tokens_grad[None],
        attn_gain_grad,
        query_grad,
        key_grad,
        value_grad,
        outgate_grad,
        forget_grad,
        forget_bias_grad,
        output_weight_grad,
        mlp_gain_grad,
        gate_grad,
        up_grad,
        down_grad,
    )


def here():
    return (lax.axis_index("cp"), lax.axis_index("sp"), lax.axis_index("fsdp"))


def flip(s, k):
    if k == 1:
        return s + 1 - 2 * lax.rem(s, 2)
    if k == 2:
        return lax.rem(s + 2, 4)
    return 3 - s


def greet(devices):
    sem = pltpu.get_barrier_semaphore()
    for device in devices:
        pl.semaphore_signal(sem, inc=1, device_id=device, device_id_type=MESH)
    pl.semaphore_wait(sem, len(devices))


def rows_of(index, count):
    return pl.ds(pl.multiple_of(index * count, count), count)


def row_loop(total, step, body):
    def one(i, carry):
        return body(rows_of(i, step), carry)

    return one, total // step


class Gather:
    sems = 13

    def __init__(self, src, out, send, recv):
        c, s, f = here()
        self.src, self.out, self.send, self.recv = src, out, send, recv
        self.c, self.s, self.rows = c, s, src.shape[0]
        self.x, self.y, self.sib = (c, flip(s, 1), f), (c, flip(s, 2), f), (1 - c, s, f)
        self.made = []

    def block(self, k, half=None):
        index = self.c * 4 + (self.s if k == 0 else flip(self.s, k))
        n = self.rows
        if half is None:
            return self.out.at[pl.ds(pl.multiple_of(index * n, n), n)]
        return self.out.at[pl.ds(pl.multiple_of(index * n + half * (n // 2), n // 2), n // 2)]

    def copy(self, src, dst, k, device):
        made = REMOTE(src, dst, self.send.at[k], self.recv.at[k], device, MESH)
        made.start()
        self.made.append(made)
        return made

    def start(self):
        half = self.rows // 2
        low, high = self.src.at[pl.ds(0, half)], self.src.at[pl.ds(half, half)]
        self.a = [
            self.copy(low, self.block(0, 0), 0, self.x),
            self.copy(high, self.block(0, 1), 1, self.y),
            self.copy(high, self.block(0, 1), 2, self.x),
            self.copy(low, self.block(0, 0), 3, self.y),
        ]
        self.g = [self.copy(self.src, self.block(0), 4, self.sib)]

    def pass_on(self, ref, k):
        self.g.append(self.copy(ref, ref, k, self.sib))

    def relay(self):
        self.a[0].wait_recv()
        self.b0 = self.copy(self.block(1, 0), self.block(1, 0), 5, self.y)
        self.a[1].wait_recv()
        self.b1 = self.copy(self.block(2, 1), self.block(2, 1), 6, self.x)
        self.pass_on(self.block(1, 0), 7)
        self.pass_on(self.block(2, 1), 8)
        self.a[2].wait_recv()
        self.pass_on(self.block(1, 1), 9)
        self.a[3].wait_recv()
        self.pass_on(self.block(2, 0), 10)

    def finish(self):
        self.b0.wait_recv()
        self.pass_on(self.block(3, 0), 11)
        self.b1.wait_recv()
        self.pass_on(self.block(3, 1), 12)
        for made in self.g:
            made.wait_recv()
        for made in self.made:
            made.wait_send()


class Reduce:
    sems = 10

    @staticmethod
    def scratch(n, w):
        return [
            pltpu.VMEM((4, n, w), BF),
            pltpu.VMEM((4, n, w), BF),
            pltpu.VMEM((4, n, w // 2), BF),
            pltpu.VMEM((2, n, w // 2), BF),
        ]

    def __init__(self, part, refs, send, recv):
        c, s, f = here()
        self.part, self.send, self.recv = part, send, recv
        self.near, self.sums, self.far, self.last = refs
        self.c, self.s = c, s
        self.n, self.w = self.sums.shape[1], self.sums.shape[2]
        self.x, self.y, self.sib = (c, flip(s, 1), f), (c, flip(s, 2), f), (1 - c, s, f)
        self.made = []

    def copy(self, src, dst, k, device):
        made = REMOTE(src, dst, self.send.at[k], self.recv.at[k], device, MESH)
        made.start()
        self.made.append(made)
        return made

    def own(self, k, core):
        index = core * 4 + (self.s if k == 0 else flip(self.s, k))
        return index * self.n

    def start(self):
        self.a = {}
        for sem, k in enumerate((3, 1, 2, 0)):
            src = self.part.at[pl.ds(pl.multiple_of(self.own(k, 1 - self.c), self.n), self.n)]
            self.a[k] = self.copy(src, self.near.at[k], sem, self.sib)

    def chip_sum(self, k):
        self.a[k].wait_recv()
        base = self.own(k, self.c)

        def body(i, carry):
            r = rows_of(i, 32)
            p = self.part[pl.ds(pl.multiple_of(base + i * 32, 32), 32), :].astype(F32)
            self.sums[k, r, :] = (p + self.near[k, r, :].astype(F32)).astype(BF)
            return carry

        lax.fori_loop(0, self.n // 32, body, 0)

    def add(self, k, cols, slot):
        def body(i, carry):
            r = rows_of(i, 32)
            total = self.sums[k, r, cols].astype(F32) + self.far[slot, r, :].astype(F32)
            self.sums[k, r, cols] = total.astype(BF)
            return carry

        lax.fori_loop(0, self.n // 32, body, 0)

    def run(self):
        left, right = pl.ds(0, self.w // 2), pl.ds(self.w // 2, self.w // 2)
        self.chip_sum(3)
        fx = self.copy(self.sums.at[3, :, left], self.far.at[1], 4, self.x)
        fy = self.copy(self.sums.at[3, :, right], self.far.at[3], 5, self.y)
        self.chip_sum(1)
        self.nx = self.copy(self.sums.at[1, :, left], self.far.at[0], 6, self.x)
        self.chip_sum(2)
        self.ny = self.copy(self.sums.at[2, :, right], self.far.at[2], 7, self.y)
        fx.wait_recv()
        self.add(2, left, 1)
        self.by = self.copy(self.sums.at[2, :, left], self.last.at[0], 8, self.y)
        fy.wait_recv()
        self.add(1, right, 3)
        self.bx = self.copy(self.sums.at[1, :, right], self.last.at[1], 9, self.x)
        self.a[0].wait_recv()

    def arrive(self):
        for made in (self.nx, self.ny, self.by, self.bx):
            made.wait_recv()

    def total(self, i, step):
        r = rows_of(i, step)
        base = self.own(0, self.c)
        p = self.part[pl.ds(pl.multiple_of(base + i * step, step), step), :].astype(F32)
        p = p + self.near[0, r, :].astype(F32)
        far = jnp.concatenate([self.far[0, r, :], self.far[2, r, :]], axis=1).astype(F32)
        last = jnp.concatenate([self.last[0, r, :], self.last[1, r, :]], axis=1).astype(F32)
        return p + far + last

    def finish(self):
        for made in self.made:
            made.wait_send()


def partners():
    c, s, f = here()
    return [(c, flip(s, 1), f), (c, flip(s, 2), f), (1 - c, s, f)]


STEP = 32


def mean_square_inverse(values):
    return lax.rsqrt(jnp.mean(values * values, axis=1, keepdims=True) + epsilon)


class Line:
    def __init__(self, own, slot, send, recv, depth):
        self.own, self.slot, self.send, self.recv, self.depth = own, slot, send, recv, depth
        self.c, self.s, self.f = here()

    def copy(self, i, distance, up):
        owner = self.f - (distance - 1) if up else self.f + (distance - 1)
        to = lax.rem(self.f + (1 if up else self.depth - 1), self.depth)
        src = self.own[i] if distance == 1 else self.slot(i, owner)
        k = 0 if up else 1
        return REMOTE(
            src,
            self.slot(i, owner),
            self.send.at[k, distance - 1, i],
            self.recv.at[k, distance - 1, i],
            (self.c, self.s, to),
            MESH,
        )

    def may_send(self, distance, up):
        if up:
            return (self.f < self.depth - 1) & (self.f >= distance - 1)
        return (self.f > 0) & (self.f + distance <= self.depth)

    def gets(self, distance, up):
        return self.f >= distance if up else self.f + distance < self.depth

    def start(self):
        for i in range(len(self.own)):
            for up in (True, False):
                pl.when(self.may_send(1, up))(self.copy(i, 1, up).start)

    def pass_on(self, distance):
        for i in range(len(self.own)):
            for up in (True, False):
                pl.when(self.gets(distance, up))(self.got(i, distance, up).wait_recv)
                if distance < self.depth - 1:
                    pl.when(self.may_send(distance + 1, up))(self.copy(i, distance + 1, up).start)

    def got(self, i, distance, up):
        owner = self.f - distance if up else self.f + distance
        k = 0 if up else 1
        place = self.slot(i, owner)
        return REMOTE(
            place,
            place,
            self.send.at[k, distance - 1, i],
            self.recv.at[k, distance - 1, i],
            (self.c, self.s, lax.rem(self.f + (self.depth - 1 if up else 1), self.depth)),
            MESH,
        )

    def finish(self):
        for distance in range(1, self.depth):
            for i in range(len(self.own)):
                for up in (True, False):
                    pl.when(self.may_send(distance, up))(self.copy(i, distance, up).wait_send)


class Spread:
    def __init__(self, src, dst, origin, send, recv, depth, pieces):
        self.c, self.s, self.f = here()
        self.src, self.dst, self.origin, self.depth = src, dst, origin, depth
        self.send, self.recv, self.pieces = send, recv, pieces
        self.n = dst.shape[0] // pieces

    def part(self, ref, i):
        return ref.at[pl.ds(i * self.n, self.n)]

    def copy(self, i, up, first):
        k = 0 if up else 1
        return REMOTE(
            self.part(self.src if first else self.dst, i),
            self.part(self.dst, i),
            self.send.at[k, i],
            self.recv.at[i],
            (self.c, self.s, lax.rem(self.f + (1 if up else self.depth - 1), self.depth)),
            MESH,
        )

    def above(self):
        return (self.f > self.origin) & (self.f < self.depth - 1)

    def below(self):
        return (self.f < self.origin) & (self.f > 0)

    def start(self, local):
        first = self.f == self.origin

        @pl.when(first)
        def _():
            pltpu.make_async_copy(self.src, self.dst, local).start()

        for i in range(self.pieces):
            pl.when(first & (self.f < self.depth - 1))(self.copy(i, True, True).start)
            pl.when(first & (self.f > 0))(self.copy(i, False, True).start)

    def pass_on(self):
        for i in range(self.pieces):
            pl.when(self.f != self.origin)(self.copy(i, True, False).wait_recv)
            pl.when(self.above())(self.copy(i, True, False).start)
            pl.when(self.below())(self.copy(i, False, False).start)

    def finish(self, local):
        first = self.f == self.origin

        @pl.when(first)
        def _():
            pltpu.make_async_copy(self.src, self.dst, local).wait()

        for i in range(self.pieces):
            pl.when((first & (self.f < self.depth - 1)) | self.above())(
                self.copy(i, True, False).wait_send
            )
            pl.when((first & (self.f > 0)) | self.below())(self.copy(i, False, False).wait_send)


WEIGHT_PIECES = 4
OUT_PIECES = 2


def enter_kernel(
    tok_ref, dy_ref, gain_ref, attn_ref, forget_ref, out_w_ref,
    normed_ref, dy_all_ref, w_attn_ref, w_out_ref,
    mine, forget_all, s0, r0, s1, r1, sz, rz, so, ro, l0, *, depth,
):
    c, s, f = here()
    lines = [(c, s, lax.rem(f + 1, depth)), (c, s, lax.rem(f + depth - 1, depth))]
    greet(partners() + lines)
    n = tok_ref.shape[0]
    shard, cols = attn_ref.shape
    step = shard // WEIGHT_PIECES
    own = [attn_ref.at[pl.ds(i * step, step)] for i in range(WEIGHT_PIECES)] + [forget_ref]

    def slot(i, owner):
        if i == WEIGHT_PIECES:
            return forget_all.at[owner]
        rows = pl.ds(pl.multiple_of(owner * shard + i * step, step), step)
        return w_attn_ref.at[rows, pl.ds(0, cols)]

    line = Line(own, slot, sz, rz, depth)
    line.start()
    heads_rows = w_out_ref.shape[0]
    t = c * 4 + s
    origin = (t * heads_rows) // shard
    spread = Spread(
        out_w_ref.at[pl.ds(pl.multiple_of(t * heads_rows - origin * shard, heads_rows), heads_rows)],
        w_out_ref, origin, so, ro, depth, OUT_PIECES,
    )
    keep = [
        pltpu.make_async_copy(
            attn_ref,
            w_attn_ref.at[pl.ds(pl.multiple_of(f * shard, shard), shard), pl.ds(0, cols)],
            l0.at[2],
        ),
        pltpu.make_async_copy(forget_ref, forget_all.at[f], l0.at[3]),
    ]

    def body(i, carry):
        r = rows_of(i, STEP)
        v = tok_ref[r, :].astype(F32)
        mine[r, :] = (v * mean_square_inverse(v) * gain_ref[...]).astype(BF)
        return carry

    lax.fori_loop(0, n // STEP, body, 0)
    first = Gather(mine, normed_ref, s0, r0)
    second = Gather(dy_ref, dy_all_ref, s1, r1)
    keep += [
        pltpu.make_async_copy(mine, first.block(0), l0.at[0]),
        pltpu.make_async_copy(dy_ref, second.block(0), l0.at[1]),
    ]
    first.start()
    for made in keep:
        made.start()
    line.pass_on(1)
    spread.start(l0.at[4])
    first.relay()
    second.start()
    line.pass_on(2)
    first.finish()
    second.relay()
    spread.pass_on()
    line.pass_on(3)
    second.finish()
    line.finish()
    for made in keep:
        made.wait()
    spread.finish(l0.at[4])
    for owner in range(depth):
        small = forget_all[owner].astype(F32)
        tall = jnp.concatenate([small, jnp.zeros((128 - small.shape[0], shard), F32)], axis=0)
        w_attn_ref[owner * shard : (owner + 1) * shard, cols:] = tall.T.astype(BF)


def enter(tokens, cotangent, gain, own_attn, own_forget, output_weight, depth, heads_rows):
    n, w = tokens.shape
    shard, cols = own_attn.shape
    whole = jax.ShapeDtypeStruct((8 * n, w), BF)
    dma = pltpu.SemaphoreType.DMA((Gather.sems,))
    line = pltpu.SemaphoreType.DMA((2, depth - 1, WEIGHT_PIECES + 1))
    vmem = pl.BlockSpec(memory_space=pltpu.VMEM)
    anywhere = pl.BlockSpec(memory_space=pl.ANY)
    return pl.pallas_call(
        functools.partial(enter_kernel, depth=depth),
        name="enter",
        out_shape=(
            whole,
            whole,
            jax.ShapeDtypeStruct((depth * shard, cols + 128), BF),
            jax.ShapeDtypeStruct((heads_rows, w), BF),
        ),
        in_specs=[vmem] * 5 + [anywhere],
        out_specs=[anywhere, anywhere, vmem, anywhere],
        scratch_shapes=[
            pltpu.VMEM((n, w), BF),
            pltpu.VMEM((depth,) + own_forget.shape, BF),
            dma, dma, dma, dma, line, line,
            pltpu.SemaphoreType.DMA((2, OUT_PIECES)),
            pltpu.SemaphoreType.DMA((OUT_PIECES,)),
            pltpu.SemaphoreType.DMA((5,)),
        ],
        compiler_params=pltpu.CompilerParams(
            collective_id=1, has_side_effects=True, vmem_limit_bytes=VMEM_BYTES
        ),
        cost_estimate=pl.CostEstimate(
            flops=50_000_000, bytes_accessed=4 * 8 * n * w * 2, transcendentals=0
        ),
    )(tokens, cotangent, gain[None], own_attn, own_forget, output_weight)


def middle_kernel(
    part_ref, tok_ref, gain_ref, mid_ref, normed_ref,
    near, sums, far, last, mine, s0, r0, s1, r1, l0,
):
    greet(partners())
    reduce = Reduce(part_ref, (near, sums, far, last), s0, r0)
    reduce.start()
    reduce.run()
    reduce.arrive()

    def body(i, carry):
        r = rows_of(i, STEP)
        mid = tok_ref[r, :].astype(F32) + reduce.total(i, STEP)
        mid_ref[r, :] = mid
        mine[r, :] = (mid * mean_square_inverse(mid) * gain_ref[...]).astype(BF)
        return carry

    lax.fori_loop(0, mine.shape[0] // STEP, body, 0)
    gather = Gather(mine, normed_ref, s1, r1)
    gather.start()
    keep = pltpu.make_async_copy(mine, gather.block(0), l0.at[0])
    keep.start()
    reduce.finish()
    gather.relay()
    gather.finish()
    keep.wait()


def middle(part, tokens, gain):
    n, w = tokens.shape
    dma = pltpu.SemaphoreType.DMA((16,))
    vmem = pl.BlockSpec(memory_space=pltpu.VMEM)
    return pl.pallas_call(
        middle_kernel,
        name="middle",
        out_shape=(jax.ShapeDtypeStruct((n, w), F32), jax.ShapeDtypeStruct((8 * n, w), BF)),
        in_specs=[vmem] * 3,
        out_specs=[vmem, pl.BlockSpec(memory_space=pl.ANY)],
        scratch_shapes=Reduce.scratch(n, w)
        + [pltpu.VMEM((n, w), BF), dma, dma, dma, dma, pltpu.SemaphoreType.DMA((2,))],
        compiler_params=pltpu.CompilerParams(
            collective_id=2, has_side_effects=True, vmem_limit_bytes=VMEM_BYTES
        ),
        cost_estimate=pl.CostEstimate(
            flops=50_000_000, bytes_accessed=4 * 8 * n * w * 2, transcendentals=0
        ),
    )(part, tokens, gain[None])


def turn_kernel(
    part_ref, dy_ref, mid_ref, gain_ref, grad_mid_ref, gain_term_ref, branch_ref,
    near, sums, far, last, mine, s0, r0, s1, r1, l0,
):
    greet(partners())
    reduce = Reduce(part_ref, (near, sums, far, last), s0, r0)
    reduce.start()
    reduce.run()
    reduce.arrive()

    def body(i, carry):
        r = rows_of(i, STEP)
        grad = reduce.total(i, STEP)
        mid = mid_ref[r, :]
        inverse = mean_square_inverse(mid)
        weighted = grad * gain_ref[...]
        back = inverse * weighted - mid * inverse**3 * jnp.mean(
            weighted * mid, axis=1, keepdims=True
        )
        grad_mid = dy_ref[r, :].astype(F32) + back
        grad_mid_ref[r, :] = grad_mid
        mine[r, :] = grad_mid.astype(BF)
        return carry + jnp.sum(grad * mid * inverse, axis=0, keepdims=True)

    n, w = mine.shape
    gain_term_ref[...] = lax.fori_loop(0, n // STEP, body, jnp.zeros((1, w), F32))
    gather = Gather(mine, branch_ref, s1, r1)
    gather.start()
    keep = pltpu.make_async_copy(mine, gather.block(0), l0.at[0])
    keep.start()
    reduce.finish()
    gather.relay()
    gather.finish()
    keep.wait()


def turn(part, cotangent, mid, gain):
    n, w = mid.shape
    dma = pltpu.SemaphoreType.DMA((16,))
    vmem = pl.BlockSpec(memory_space=pltpu.VMEM)
    return pl.pallas_call(
        turn_kernel,
        name="turn",
        out_shape=(
            jax.ShapeDtypeStruct((n, w), F32),
            jax.ShapeDtypeStruct((1, w), F32),
            jax.ShapeDtypeStruct((8 * n, w), BF),
        ),
        in_specs=[vmem] * 4,
        out_specs=[vmem, vmem, pl.BlockSpec(memory_space=pl.ANY)],
        scratch_shapes=Reduce.scratch(n, w)
        + [pltpu.VMEM((n, w), BF), dma, dma, dma, dma, pltpu.SemaphoreType.DMA((2,))],
        compiler_params=pltpu.CompilerParams(
            collective_id=3, has_side_effects=True, vmem_limit_bytes=VMEM_BYTES
        ),
        cost_estimate=pl.CostEstimate(
            flops=50_000_000, bytes_accessed=4 * 8 * n * w * 2, transcendentals=0
        ),
    )(part, cotangent, mid, gain[None])


def leave_kernel(
    part_ref, down_ref, tok_ref, grad_mid_ref, mid_ref, gain_ref, small_ref,
    grad_ref, small_sum_ref, out_ref,
    near, sums, far, last, near2, sums2, far2, last2, small, plane_small, line_small,
    s0, r0, s1, r1, s2, r2, *, depth,
):
    c, s, f = here()
    plane_peers = [
        (core, flip(s, k) if k else s, f, k + 4 * i)
        for i, core in enumerate((c, 1 - c))
        for k in range(4)
        if i or k
    ]
    line_peers = [(c, s, lax.rem(f + k, depth), k) for k in range(1, depth)]
    greet([p[:3] for p in plane_peers + line_peers])
    reduce = Reduce(part_ref, (near, sums, far, last), s0, r0)
    other = Reduce(down_ref, (near2, sums2, far2, last2), s1, r1)
    reduce.start()
    other.start()
    reduce.run()
    other.run()
    reduce.arrive()

    def body(i, carry):
        r = rows_of(i, STEP)
        grad = reduce.total(i, STEP)
        tok = tok_ref[r, :].astype(F32)
        inverse = mean_square_inverse(tok)
        weighted = grad * gain_ref[...]
        back = inverse * weighted - tok * inverse**3 * jnp.mean(
            weighted * tok, axis=1, keepdims=True
        )
        grad_ref[r, :] = grad_mid_ref[r, :] + back
        return carry + jnp.sum(grad * tok * inverse, axis=0, keepdims=True)

    n, w = tok_ref.shape
    small[...] = small_ref[...]
    small[0:1, :] = lax.fori_loop(0, n // STEP, body, jnp.zeros((1, w), F32))
    place = c * 4 + s
    plane_small[pl.ds(place, 1)] = small[...][None]
    sent = []
    for core, other_s, other_f, k in plane_peers:
        made = REMOTE(
            small, plane_small.at[place], s2.at[k - 1], r2.at[k - 1], (core, other_s, other_f), MESH
        )
        made.start()
        sent.append(made)
    other.arrive()

    def body2(i, carry):
        r = rows_of(i, STEP)
        out_ref[r, :] = (mid_ref[r, :] + other.total(i, STEP)).astype(BF)
        return carry

    lax.fori_loop(0, n // STEP, body2, 0)
    for made in sent:
        made.wait()
    total = plane_small[0]
    for i in range(1, 8):
        total = total + plane_small[i]
    small[...] = total
    line_small[pl.ds(f, 1)] = total[None]
    sent = []
    for core, other_s, other_f, k in line_peers:
        made = REMOTE(
            small, line_small.at[f], s2.at[6 + k], r2.at[6 + k], (core, other_s, other_f), MESH
        )
        made.start()
        sent.append(made)
    reduce.finish()
    other.finish()
    for made in sent:
        made.wait()
    total = line_small[0]
    for i in range(1, depth):
        total = total + line_small[i]
    small_sum_ref[...] = total


def leave(part, down_part, tokens, grad_mid, mid, gain, small, depth):
    n, w = mid.shape
    sems = pltpu.SemaphoreType.DMA((6 + depth,))
    dma = pltpu.SemaphoreType.DMA((16,))
    vmem = pl.BlockSpec(memory_space=pltpu.VMEM)
    return pl.pallas_call(
        functools.partial(leave_kernel, depth=depth),
        name="leave",
        out_shape=(
            jax.ShapeDtypeStruct((n, w), F32),
            jax.ShapeDtypeStruct((8, w), F32),
            jax.ShapeDtypeStruct((n, w), BF),
        ),
        in_specs=[vmem] * 7,
        out_specs=[vmem] * 3,
        scratch_shapes=Reduce.scratch(n, w)
        + Reduce.scratch(n, w)
        + [
            pltpu.VMEM((8, w), F32),
            pltpu.VMEM((8, 8, w), F32),
            pltpu.VMEM((depth, 8, w), F32),
            dma, dma, dma, dma, sems, sems,
        ],
        compiler_params=pltpu.CompilerParams(
            collective_id=4, has_side_effects=True, vmem_limit_bytes=VMEM_BYTES
        ),
        cost_estimate=pl.CostEstimate(
            flops=50_000_000, bytes_accessed=4 * 8 * n * w * 2, transcendentals=0
        ),
    )(part, down_part, tokens, grad_mid, mid, gain[None], small)


BQ = 256
BK = 256
AUG = 128


def dot(a, b, ca, cb):
    return lax.dot_general(a, b, (((ca,), (cb,)), ((), ())), preferred_element_type=F32)


def three_parts(v):
    hi = v.astype(BF).astype(F32)
    mid = (v - hi).astype(BF).astype(F32)
    low = (v - hi - mid).astype(BF).astype(F32)
    return hi, mid, low


def triangle(n, suffix):
    a = lax.broadcasted_iota(jnp.int32, (n, n), 0)
    b = lax.broadcasted_iota(jnp.int32, (n, n), 1)
    return jnp.where(a >= b if suffix else a <= b, 1.0, 0.0).astype(BF)


def log_sigmoid(v):
    return jnp.minimum(v, 0.0) - jnp.log1p(jnp.exp(-jnp.abs(v)))


def doc_starts(ends_ref, pos):
    start = jnp.zeros_like(pos)
    for n in range(ends_ref.shape[0]):
        end = ends_ref[n]
        start = jnp.where(pos >= end, jnp.maximum(start, end), start)
    return start


def first_block(ends_ref, pos):
    start = jnp.int32(0)
    for n in range(ends_ref.shape[0]):
        end = ends_ref[n]
        start = jnp.where(pos >= end, jnp.maximum(start, end), start)
    return start // BK


def extend(prefix_row, sign_first):
    hi, mid, low = three_parts(prefix_row)
    r = lax.broadcasted_iota(jnp.int32, (16, prefix_row.shape[1]), 0)
    base = 0 if sign_first else 3
    sign = 1.0 if sign_first else -1.0
    ones = (r >= 3) & (r < 6) if sign_first else r < 3
    out = jnp.where(ones, 1.0, 0.0)
    out = jnp.where(r == base, sign * hi, out)
    out = jnp.where(r == base + 1, sign * mid, out)
    return jnp.where(r == base + 2, sign * low, out)


def lay_out(place_ref, cat_ref, prefix_ref, heads, hd, slab, qa, ka, kta):
    hw = heads * hd
    slabs = cat_ref.shape[1] // slab
    for p in range(slabs):
        src = pl.ds(pl.multiple_of(place_ref[p] * slab, slab), slab)
        dst = pl.ds(p * slab, slab)
        for h in range(heads):
            q = cat_ref[h * hd : (h + 1) * hd, src].astype(BF).astype(F32)
            row = prefix_ref[h : h + 1, dst]
            rest = jnp.zeros((AUG - hd - 16, slab), F32)
            qe = jnp.concatenate([q * hd**-0.5, extend(row, True), rest], axis=0)
            qa[h, :, dst] = qe.astype(BF)
            k = cat_ref[hw + h * hd : hw + (h + 1) * hd, src].astype(BF).astype(F32)
            ke = jnp.concatenate([k, extend(row, False), rest], axis=0)
            if kta is not None:
                kta[h, :, dst] = ke.astype(BF)
            ka[h, dst, :] = ke.T.astype(BF)


def attention_kernel(
    place_ref, ends_ref, cat_ref, bias_ref,
    gated_ref, att_ref, exact_ref, lse_ref, prefix_ref,
    qa, ka, va, *, heads, hd, slab,
):
    hw = heads * hd
    tokens = cat_ref.shape[1]
    slabs = tokens // slab
    tri = triangle(slab, False)
    carry = jnp.zeros((16, 1), F32)
    for p in range(slabs):
        src = pl.ds(pl.multiple_of(place_ref[p] * slab, slab), slab)
        pre = cat_ref[4 * hw : 4 * hw + 16, src] + bias_ref[:, 0:1]
        steps = log_sigmoid(pre).astype(BF)
        part = dot(steps, tri, 1, 0) + carry
        prefix_ref[:, p * slab : (p + 1) * slab] = part
        carry = part[:, slab - 1 : slab]
        for h in range(heads):
            va[h, :, p * slab : (p + 1) * slab] = cat_ref[
                2 * hw + h * hd : 2 * hw + (h + 1) * hd, src
            ].astype(BF)
    lay_out(place_ref, cat_ref, prefix_ref, heads, hd, slab, qa, ka, None)
    per = slab // BQ

    def one_query_block(qb, unused):
        q0 = pl.multiple_of(qb * BQ, BQ)
        pos = q0 + lax.broadcasted_iota(jnp.int32, (1, BQ), 1)
        start = doc_starts(ends_ref, pos)
        low = first_block(ends_ref, q0)
        inside = lax.broadcasted_iota(jnp.int32, (BK, BQ), 0)

        def one_key_block(kb, held):
            k0 = pl.multiple_of(kb * BK, BK)
            allowed = (inside <= pos - k0) & (inside >= start - k0)
            out = []
            for h in range(heads):
                m, l, acc = held[h]
                st = dot(ka[h, pl.ds(k0, BK), :], qa[h, :, pl.ds(q0, BQ)], 1, 0)
                st = jnp.where(allowed, st, very_low)
                new = jnp.maximum(m, jnp.max(st, axis=0, keepdims=True))
                p = jnp.exp(st - new)
                scale = jnp.exp(m - new)
                l = l * scale + jnp.sum(p, axis=0, keepdims=True)
                acc = acc * scale + dot(va[h, :, pl.ds(k0, BK)], p.astype(BF), 1, 0)
                out.append((new, l, acc))
            return tuple(out)

        begin = tuple(
            (jnp.full((1, BQ), very_low, F32), jnp.zeros((1, BQ), F32), jnp.zeros((hd, BQ), F32))
            for _ in range(heads)
        )
        done = lax.fori_loop(low, qb + 1, one_key_block, begin)
        dst = pl.ds(pl.multiple_of(place_ref[qb // per] * slab + lax.rem(qb, per) * BQ, BQ), BQ)
        for h in range(heads):
            m, l, acc = done[h]
            lse_ref[h : h + 1, pl.ds(q0, BQ)] = m + jnp.log(l)
            exact = acc / l
            rounded = exact.astype(BF)
            exact_ref[h * hd : (h + 1) * hd, dst] = exact
            att_ref[h * hd : (h + 1) * hd, dst] = rounded
            gate = jax.nn.sigmoid(cat_ref[3 * hw + h * hd : 3 * hw + (h + 1) * hd, dst])
            gated_ref[h * hd : (h + 1) * hd, dst] = (rounded.astype(F32) * gate).astype(BF)
        return unused

    lse_ref[...] = jnp.zeros_like(lse_ref)
    lax.fori_loop(0, tokens // BQ, one_query_block, 0)


def attention(place, ends, cat, bias, heads, hd, slab):
    tokens = cat.shape[1]
    hw = heads * hd
    vmem = pl.BlockSpec(memory_space=pltpu.VMEM)
    smem = pl.BlockSpec(memory_space=pltpu.SMEM)
    return pl.pallas_call(
        functools.partial(attention_kernel, heads=heads, hd=hd, slab=slab),
        name="attention",
        out_shape=(
            jax.ShapeDtypeStruct((hw, tokens), BF),
            jax.ShapeDtypeStruct((hw, tokens), BF),
            jax.ShapeDtypeStruct((hw, tokens), F32),
            jax.ShapeDtypeStruct((8, tokens), F32),
            jax.ShapeDtypeStruct((16, tokens), F32),
        ),
        in_specs=[smem, smem, vmem, vmem],
        out_specs=[vmem] * 5,
        scratch_shapes=[
            pltpu.VMEM((heads, AUG, tokens), BF),
            pltpu.VMEM((heads, tokens, AUG), BF),
            pltpu.VMEM((heads, hd, tokens), BF),
        ],
        compiler_params=pltpu.CompilerParams(vmem_limit_bytes=VMEM_BYTES),
        cost_estimate=pl.CostEstimate(
            flops=8 * heads * tokens * tokens * hd, bytes_accessed=cat.size * 4,
            transcendentals=heads * tokens * tokens // 2,
        ),
    )(place, ends, cat, bias)


def attention_back_kernel(
    place_ref, ends_ref, cat_ref, bias_ref, gg_ref, att_ref, exact_ref, lse_ref, prefix_ref,
    out_ref, bias_grad_ref,
    qa, ka, kta, va, do, delta_ref, dk, dv, gp, *, heads, hd, slab,
):
    hw = heads * hd
    tokens = cat_ref.shape[1]
    slabs = tokens // slab
    per = slab // BQ
    lay_out(place_ref, cat_ref, prefix_ref, heads, hd, slab, qa, ka, kta)
    delta_ref[...] = jnp.zeros_like(delta_ref)
    gp[...] = jnp.zeros_like(gp)
    dk[...] = jnp.zeros_like(dk)
    dv[...] = jnp.zeros_like(dv)
    out_ref[4 * hw :, :] = jnp.zeros((out_ref.shape[0] - 4 * hw, tokens), BF)
    for p in range(slabs):
        src = pl.ds(pl.multiple_of(place_ref[p] * slab, slab), slab)
        dst = pl.ds(p * slab, slab)
        for h in range(heads):
            rows = slice(h * hd, (h + 1) * hd)
            gate = jax.nn.sigmoid(cat_ref[3 * hw + h * hd : 3 * hw + (h + 1) * hd, src])
            gg = gg_ref[rows, src]
            low = (gg * gate).astype(BF)
            do[h, :, dst] = low
            delta_ref[h : h + 1, dst] = jnp.sum(
                low.astype(F32) * exact_ref[rows, src], axis=0, keepdims=True
            )
            gate_grad = gg * att_ref[rows, src].astype(F32) * gate * (1.0 - gate)
            out_ref[3 * hw + h * hd : 3 * hw + (h + 1) * hd, src] = gate_grad.astype(BF)
            v = cat_ref[2 * hw + h * hd : 2 * hw + (h + 1) * hd, src]
            va[h, dst, :] = v.T.astype(BF)

    def one_query_block(qb, unused):
        q0 = pl.multiple_of(qb * BQ, BQ)
        pos = q0 + lax.broadcasted_iota(jnp.int32, (1, BQ), 1)
        start = doc_starts(ends_ref, pos)
        low = first_block(ends_ref, q0)
        inside = lax.broadcasted_iota(jnp.int32, (BK, BQ), 0)

        def one_key_block(kb, held):
            k0 = pl.multiple_of(kb * BK, BK)
            keys = pl.ds(k0, BK)
            allowed = (inside <= pos - k0) & (inside >= start - k0)
            out = []
            for h in range(heads):
                queries = qa[h, :, pl.ds(q0, BQ)]
                grads = do[h, :, pl.ds(q0, BQ)]
                st = dot(ka[h, keys, :], queries, 1, 0) - lse_ref[h : h + 1, pl.ds(q0, BQ)]
                p = jnp.exp(jnp.where(allowed, st, very_low))
                dp = dot(va[h, keys, :], grads, 1, 0) - delta_ref[h : h + 1, pl.ds(q0, BQ)]
                ds = (p * dp).astype(BF)
                out.append(held[h] + dot(kta[h, :, keys], ds, 1, 0))
                dk[h, :, keys] += dot(queries, ds, 1, 1)
                dv[h, :, keys] += dot(grads, p.astype(BF), 1, 1)
            return tuple(out)

        begin = tuple(jnp.zeros((AUG, BQ), F32) for _ in range(heads))
        done = lax.fori_loop(low, qb + 1, one_key_block, begin)
        dst = pl.ds(pl.multiple_of(place_ref[qb // per] * slab + lax.rem(qb, per) * BQ, BQ), BQ)
        for h in range(heads):
            out_ref[h * hd : (h + 1) * hd, dst] = (done[h][0:hd, :] * hd**-0.5).astype(BF)
            gp[h : h + 1, pl.ds(q0, BQ)] = done[h][hd : hd + 1, :]
        return unused

    lax.fori_loop(0, tokens // BQ, one_query_block, 0)
    tri = triangle(slab, True)
    carry = jnp.zeros((16, 1), F32)
    bias_grad = jnp.zeros((16, 1), F32)
    for p in reversed(range(slabs)):
        src = pl.ds(pl.multiple_of(place_ref[p] * slab, slab), slab)
        dst = pl.ds(p * slab, slab)
        for h in range(heads):
            out_ref[hw + h * hd : hw + (h + 1) * hd, src] = dk[h, 0:hd, dst].astype(BF)
            out_ref[2 * hw + h * hd : 2 * hw + (h + 1) * hd, src] = dv[h, :, dst].astype(BF)
            gp[h : h + 1, dst] = gp[h : h + 1, dst] - dk[h, hd + 3 : hd + 4, dst]
        grad = gp[:, dst]
        total = carry
        for piece in three_parts(grad):
            total = total + dot(piece.astype(BF), tri, 1, 0)
        carry = total[:, 0:1]
        pre = cat_ref[4 * hw : 4 * hw + 16, src] + bias_ref[:, 0:1]
        low = (total.astype(BF).astype(F32) * jax.nn.sigmoid(-pre)).astype(BF)
        out_ref[4 * hw : 4 * hw + 16, src] = low
        bias_grad = bias_grad + jnp.sum(low.astype(F32), axis=1, keepdims=True)
    bias_grad_ref[...] = jnp.broadcast_to(bias_grad, bias_grad_ref.shape)


def attention_back(place, ends, cat, bias, gg, att, exact, lse, prefix, heads, hd, slab):
    tokens = cat.shape[1]
    vmem = pl.BlockSpec(memory_space=pltpu.VMEM)
    smem = pl.BlockSpec(memory_space=pltpu.SMEM)
    return pl.pallas_call(
        functools.partial(attention_back_kernel, heads=heads, hd=hd, slab=slab),
        name="attention_back",
        out_shape=(
            jax.ShapeDtypeStruct(cat.shape, BF),
            jax.ShapeDtypeStruct((16, 128), F32),
        ),
        in_specs=[smem, smem] + [vmem] * 7,
        out_specs=[vmem] * 2,
        scratch_shapes=[
            pltpu.VMEM((heads, AUG, tokens), BF),
            pltpu.VMEM((heads, tokens, AUG), BF),
            pltpu.VMEM((heads, AUG, tokens), BF),
            pltpu.VMEM((heads, tokens, hd), BF),
            pltpu.VMEM((heads, hd, tokens), BF),
            pltpu.VMEM((8, tokens), F32),
            pltpu.VMEM((heads, AUG, tokens), F32),
            pltpu.VMEM((heads, hd, tokens), F32),
            pltpu.VMEM((16, tokens), F32),
        ],
        compiler_params=pltpu.CompilerParams(vmem_limit_bytes=VMEM_BYTES),
        cost_estimate=pl.CostEstimate(
            flops=20 * heads * tokens * tokens * hd, bytes_accessed=cat.size * 8,
            transcendentals=heads * tokens * tokens // 2,
        ),
    )(place, ends, cat, bias, gg, att, exact, lse, prefix)


def spread_rows(grad, plane, depth):
    rows, cols = grad.shape
    part = rows // (plane * depth)
    return grad.reshape(plane, depth, part, cols).transpose(1, 0, 2, 3).reshape(rows, cols)


def local_plane(
    tokens, out_cotangent, seq_lengths, slab_place, attn_gain, query_weight, key_weight,
    value_weight, outgate_weight, forget_weight, forget_bias, output_weight, mlp_gain,
    gate_weight, up_weight, down_weight,
):
    plane_axes = ("cp", "sp")
    plane = lax.axis_size("cp") * lax.axis_size("sp")
    depth = lax.axis_size("fsdp")
    place = lax.axis_index("cp") * lax.axis_size("sp") + lax.axis_index("sp")
    head_count = forget_weight.shape[1]
    width = tokens.shape[2]
    hd = width // head_count
    heads = head_count // plane
    hw = heads * hd
    fw = gate_weight.shape[1] // plane
    shard = query_weight.shape[0]
    group_rows = tokens.shape[1] * plane
    slab = group_rows // slab_place.shape[1]

    def columns(weight, count):
        return lax.dynamic_slice_in_dim(weight, place * count, count, 1)

    inputs, cotangent = tokens[0], out_cotangent[0]
    slabs = slab_place.shape[1]
    order = jnp.arange(slabs, dtype=jnp.int32)
    storage = jnp.sum(
        jnp.where(slab_place[0][None, :] == order[:, None], order[None, :], 0), axis=1
    )
    ends = jnp.cumsum(seq_lengths[0])

    own_attn = jnp.concatenate(
        [columns(w, hw) for w in (query_weight, key_weight, value_weight, outgate_weight)], axis=1
    )
    own_forget = jnp.pad(columns(forget_weight, heads).T, ((0, 16 - heads), (0, 0)))
    own_mlp = jnp.concatenate(
        [columns(gate_weight, fw), columns(up_weight, fw), columns(down_weight, fw)], axis=1
    )
    normed, cotangent_all, w_attn, w_out = enter(
        inputs, cotangent, attn_gain, own_attn, own_forget, output_weight, depth, hw
    )
    own_mlp, w_attn = lax.optimization_barrier((own_mlp, w_attn))
    w_mlp = lax.all_gather(own_mlp, "fsdp", axis=0, tiled=True)
    cat = dot(w_attn, normed, 0, 1)
    bias_own = lax.dynamic_slice_in_dim(forget_bias, place * heads, heads, 0)
    bias = jnp.broadcast_to(jnp.pad(bias_own, (0, 16 - heads))[:, None], (16, 128))
    gated, att, exact, lse, prefix = attention(storage, ends, cat, bias, heads, hd, slab)
    mid_part = dot(gated, w_out, 0, 0).astype(BF)
    mid, normed_mlp = middle(mid_part, inputs, mlp_gain)

    w_gate, w_up, w_down = w_mlp[:, :fw], w_mlp[:, fw : 2 * fw], w_mlp[:, 2 * fw :]
    gate_lin = matmul(normed_mlp, w_gate)
    up_lin = matmul(normed_mlp, w_up)
    gate_sig = jax.nn.sigmoid(gate_lin)
    activated = gate_lin * gate_sig
    hidden = (activated * up_lin).astype(BF)
    grad_hidden = matmul(cotangent_all, w_down)
    grad_gate_lin = (grad_hidden * up_lin * gate_sig * (1.0 + gate_lin * (1.0 - gate_sig))).astype(
        BF
    )
    grad_up_lin = (grad_hidden * activated).astype(BF)
    mlp_part = (
        matmul_right_t(grad_gate_lin, w_gate) + matmul_right_t(grad_up_lin, w_up)
    ).astype(BF)
    down_part = matmul_right_t(hidden, w_down).astype(BF)
    mlp_terms = jnp.concatenate(
        [
            matmul_left_t(normed_mlp, grad_gate_lin).astype(BF),
            matmul_left_t(normed_mlp, grad_up_lin).astype(BF),
            matmul_left_t(cotangent_all, hidden).astype(BF),
        ],
        axis=1,
    )
    mlp_part, mlp_spread = lax.optimization_barrier(
        (mlp_part, spread_rows(mlp_terms, plane, depth))
    )
    grad_mid, mlp_gain_term, branch = turn(mlp_part, cotangent, mid, mlp_gain)
    mlp_grad = lax.psum_scatter(mlp_spread, "fsdp", scatter_dimension=0, tiled=True)

    grad_gated = dot(w_out, branch, 1, 1)
    grad_cat, bias_grad = attention_back(
        storage, ends, cat, bias, grad_gated, att, exact, lse, prefix, heads, hd, slab
    )
    out_term = dot(gated, branch, 1, 0).astype(BF)
    attn_term = dot(normed, grad_cat, 0, 1).astype(BF)
    grad_cat, attn_spread = lax.optimization_barrier(
        (grad_cat, spread_rows(attn_term, plane, depth))
    )
    out_term, mlp_grad = lax.optimization_barrier((out_term, mlp_grad))
    output_weight_grad = lax.psum_scatter(out_term, "fsdp", scatter_dimension=0, tiled=True)
    attn_spread, output_weight_grad = lax.optimization_barrier((attn_spread, output_weight_grad))
    attn_grad = lax.psum_scatter(attn_spread, "fsdp", scatter_dimension=0, tiled=True)
    attn_part = dot(grad_cat, w_attn, 0, 1).astype(BF)
    bias_row = lax.dynamic_update_slice_in_dim(
        jnp.zeros((width,), F32), bias_grad[:heads, 0], place * heads, 0
    )
    small = jnp.concatenate(
        [jnp.zeros((1, width), F32), mlp_gain_term, bias_row[None], jnp.zeros((5, width), F32)]
    )
    tokens_grad, small_sum, block_out = leave(
        attn_part, down_part, inputs, grad_mid, mid, attn_gain, small, depth
    )
    attn_grad, tokens_grad = lax.optimization_barrier((attn_grad, tokens_grad))

    def to_rows(grad):
        part = grad.shape[0] // plane
        got = lax.all_to_all(
            grad.reshape(plane, part, -1), plane_axes, split_axis=0, concat_axis=0, tiled=True
        )
        return got.astype(F32)

    mlp_rows = to_rows(mlp_grad)
    attn_rows = to_rows(attn_grad)

    def pick(rows, begin, count):
        part = rows[:, :, begin : begin + count].transpose(1, 0, 2)
        return part.reshape(part.shape[0], -1)

    gate_grad, up_grad, down_grad = (pick(mlp_rows, i * fw, fw) for i in range(3))
    query_grad, key_grad, value_grad, outgate_grad = (
        pick(attn_rows, i * hw, hw) for i in range(4)
    )
    forget_grad = pick(attn_rows, 4 * hw, heads)
    attn_gain_grad, mlp_gain_grad = small_sum[0], small_sum[1]
    forget_bias_grad = small_sum[2, :head_count]
    return (
        block_out[None],
        tokens_grad[None],
        attn_gain_grad,
        query_grad,
        key_grad,
        value_grad,
        outgate_grad,
        forget_grad,
        forget_bias_grad,
        output_weight_grad.astype(F32),
        mlp_gain_grad,
        gate_grad,
        up_grad,
        down_grad,
    )


def fits_plane(mesh, tokens, slab_place, forget_weight, gate_weight):
    sizes = dict(mesh.shape)
    if (sizes["cp"], sizes["sp"]) != (2, 4):
        return False
    plane = sizes["cp"] * sizes["sp"]
    width = tokens.shape[2]
    head_count = forget_weight.shape[1]
    group_rows = tokens.shape[1]
    slab = group_rows // slab_place.shape[1]
    heads = head_count // plane
    return (
        head_count % plane == 0
        and heads <= 8
        and width // head_count == 64
        and slab % 256 == 0
        and group_rows <= 2048
        and width % 256 == 0
        and gate_weight.shape[1] % (128 * plane) == 0
        and width % (16 * plane * sizes["fsdp"]) == 0
        and (group_rows // plane) % 64 == 0
    )


def shard(mesh, fn):
    return jax.shard_map(
        fn,
        mesh=mesh,
        in_specs=(
            P("fsdp", ("cp", "sp"), None),
            P("fsdp", ("cp", "sp"), None),
            P("fsdp", None),
            P("fsdp", None),
            P(),
            P("fsdp", None),
            P("fsdp", None),
            P("fsdp", None),
            P("fsdp", None),
            P("fsdp", None),
            P(),
            P("fsdp", None),
            P(),
            P("fsdp", None),
            P("fsdp", None),
            P("fsdp", None),
        ),
        out_specs=(
            P("fsdp", ("cp", "sp"), None),
            P("fsdp", ("cp", "sp"), None),
            P(),
            P(("cp", "sp", "fsdp"), None),
            P(("cp", "sp", "fsdp"), None),
            P(("cp", "sp", "fsdp"), None),
            P(("cp", "sp", "fsdp"), None),
            P(("cp", "sp", "fsdp"), None),
            P(),
            P(("cp", "sp", "fsdp"), None),
            P(),
            P(("cp", "sp", "fsdp"), None),
            P(("cp", "sp", "fsdp"), None),
            P(("cp", "sp", "fsdp"), None),
        ),
        check_vma=False,
    )


def solution(mesh):
    def run(*args):
        fast = fits_plane(mesh, args[0], args[3], args[9], args[13])
        return shard(mesh, local_plane if fast else local)(*args)

    return run
```

```python
import functools

import jax
import jax.numpy as jnp
from jax import lax
from jax.experimental import pallas as pl
from jax.experimental.pallas import tpu as pltpu
from jax.sharding import PartitionSpec as P

epsilon = 1e-06
very_low = -1e30
MESH = pl.DeviceIdType.MESH
BF = jnp.bfloat16
F32 = jnp.float32
REMOTE = pltpu.make_async_remote_copy
VMEM_BYTES = 60 * 1024 * 1024


def matmul(left, right):
    return jnp.dot(left, right, preferred_element_type=jnp.float32)


def matmul_right_t(left, right):
    return lax.dot_general(
        left, right, (((1,), (1,)), ((), ())), preferred_element_type=jnp.float32
    )


def matmul_left_t(left, right):
    return lax.dot_general(
        left, right, (((0,), (0,)), ((), ())), preferred_element_type=jnp.float32
    )


def rms_inverse(values):
    return lax.rsqrt(jnp.mean(values * values, axis=1, keepdims=True) + epsilon)


def norm_back(upstream, values, inverse, gain):
    weighted = upstream * gain
    return inverse * weighted - values * inverse**3 * jnp.mean(
        weighted * values, axis=1, keepdims=True
    )


def row_layout(place_row, lens_row, count, slab_rows):
    rows = jnp.arange(count, dtype=jnp.int32)
    slab_index = rows // slab_rows
    table = (
        slab_index[:, None] == jnp.arange(place_row.shape[0], dtype=jnp.int32)[None, :]
    ).astype(jnp.int32)
    position = jnp.sum(table * place_row[None, :], axis=1) * slab_rows + rows % slab_rows
    ends = jnp.cumsum(lens_row)
    segment = jnp.sum((position[:, None] >= ends[None, :]).astype(jnp.int32), axis=1)
    return (position, segment)


def forget_prefix(log_all, place_row, slab_rows):
    slabs = place_row.shape[0]
    steps = log_all.astype(jnp.float32).reshape(slabs, slab_rows, -1)
    inside = jnp.cumsum(steps, axis=1)
    totals = inside[:, -1, :]
    earlier = (place_row[None, :] < place_row[:, None]).astype(jnp.float32)
    offsets = jnp.dot(earlier, totals, precision=lax.Precision.HIGHEST)
    return (inside + offsets[:, None, :]).reshape(slabs * slab_rows, -1)


def prefix_back(grad_prefix, place_row, slab_rows):
    slabs = place_row.shape[0]
    steps = grad_prefix.reshape(slabs, slab_rows, -1)
    inside = jnp.flip(jnp.cumsum(jnp.flip(steps, 1), axis=1), 1)
    totals = inside[:, 0, :]
    later = (place_row[None, :] > place_row[:, None]).astype(jnp.float32)
    offsets = jnp.dot(later, totals, precision=lax.Precision.HIGHEST)
    return (inside + offsets[:, None, :]).reshape(slabs * slab_rows, -1)


def local(
    tokens,
    out_cotangent,
    seq_lengths,
    slab_place,
    attn_gain,
    query_weight,
    key_weight,
    value_weight,
    outgate_weight,
    forget_weight,
    forget_bias,
    output_weight,
    mlp_gain,
    gate_weight,
    up_weight,
    down_weight,
):
    seq_devices = lax.axis_size("sp")
    ctx_devices = lax.axis_size("cp")
    ctx_index = lax.axis_index("cp")
    tok_rows = tokens.shape[1]
    model_width = tokens.shape[2]
    head_count = forget_weight.shape[1]
    local_heads = head_count // seq_devices
    head_size = model_width // head_count
    ctx_rows = tok_rows * seq_devices
    group_rows = ctx_rows * ctx_devices
    slab_rows = ctx_rows // 2
    key_block = min(512, group_rows)
    key_blocks = group_rows // key_block
    score_scale = head_size ** (-0.5)
    place_row = slab_place[0]
    lens_row = seq_lengths[0]
    ctx_start = ctx_index * ctx_rows
    inputs = tokens[0]
    input_f = inputs.astype(jnp.float32)
    weights_attn = (
        lax.all_gather(query_weight, "fsdp", axis=0, tiled=True),
        lax.all_gather(key_weight, "fsdp", axis=0, tiled=True),
        lax.all_gather(value_weight, "fsdp", axis=0, tiled=True),
        lax.all_gather(outgate_weight, "fsdp", axis=0, tiled=True),
        lax.all_gather(forget_weight, "fsdp", axis=0, tiled=True),
        lax.all_gather(output_weight, "fsdp", axis=0, tiled=True),
    )
    full_query, full_key, full_value, full_outgate, full_forget, full_output = weights_attn
    inv_first = rms_inverse(input_f)
    normed = (input_f * inv_first * attn_gain).astype(jnp.bfloat16)
    queries = matmul(normed, full_query).astype(jnp.bfloat16)
    keys = matmul(normed, full_key).astype(jnp.bfloat16)
    values = matmul(normed, full_value).astype(jnp.bfloat16)
    out_gate = jax.nn.sigmoid(matmul(normed, full_outgate))
    forget_pre = matmul(normed, full_forget) + forget_bias
    log_forget = jax.nn.log_sigmoid(forget_pre).astype(jnp.bfloat16)
    head_query, head_key, head_value, head_forget = (
        lax.all_to_all(queries, "sp", split_axis=1, concat_axis=0, tiled=True),
        lax.all_to_all(keys, "sp", split_axis=1, concat_axis=0, tiled=True),
        lax.all_to_all(values, "sp", split_axis=1, concat_axis=0, tiled=True),
        lax.all_to_all(log_forget, "sp", split_axis=1, concat_axis=0, tiled=True),
    )
    keys_all, values_all, forget_all = (
        lax.all_gather(head_key, "cp", axis=0, tiled=True),
        lax.all_gather(head_value, "cp", axis=0, tiled=True),
        lax.all_gather(head_forget, "cp", axis=0, tiled=True),
    )
    prefix_all = forget_prefix(forget_all, place_row, slab_rows)
    pos_all, seg_all = row_layout(place_row, lens_row, group_rows, slab_rows)
    query_pos = lax.dynamic_slice_in_dim(pos_all, ctx_start, ctx_rows, 0)
    query_seg = lax.dynamic_slice_in_dim(seg_all, ctx_start, ctx_rows, 0)
    query_prefix = lax.dynamic_slice_in_dim(prefix_all, ctx_start, ctx_rows, 0)
    query_three = head_query.reshape(ctx_rows, local_heads, head_size)
    query_pos_top = jnp.max(query_pos)
    query_seg_low = jnp.min(query_seg)
    query_seg_top = jnp.max(query_seg)
    key_pieces = (
        keys_all.reshape(key_blocks, key_block, local_heads, head_size),
        values_all.reshape(key_blocks, key_block, local_heads, head_size),
        prefix_all.reshape(key_blocks, key_block, local_heads),
        pos_all.reshape(key_blocks, key_block),
        seg_all.reshape(key_blocks, key_block),
    )

    def block_live(key_pos, key_seg):
        return (
            (query_pos_top >= jnp.min(key_pos))
            & (query_seg_top >= jnp.min(key_seg))
            & (jnp.max(key_seg) >= query_seg_low)
        )

    def block_scores(key_piece, key_prefix, key_pos, key_seg):
        raw = (
            jnp.einsum("qhd,khd->hqk", query_three, key_piece, preferred_element_type=jnp.float32)
            * score_scale
        )
        raw = raw + query_prefix.T[:, :, None] - key_prefix.T[:, None, :]
        allowed = (query_pos[:, None] >= key_pos[None, :]) & (
            query_seg[:, None] == key_seg[None, :]
        )
        return (raw, allowed[None, :, :])

    def total_work(carry, piece):
        running_max, running_sum = carry
        key_piece, value_piece, key_prefix, key_pos, key_seg = piece
        raw, allowed = block_scores(key_piece, key_prefix, key_pos, key_seg)
        new_max = jnp.maximum(running_max, jnp.max(jnp.where(allowed, raw, very_low), axis=2))
        terms = jnp.where(allowed, jnp.exp(raw - new_max[:, :, None]), 0.0)
        new_sum = running_sum * jnp.exp(running_max - new_max) + jnp.sum(terms, axis=2)
        return (new_max, new_sum)

    def total_step(carry, piece):
        live = block_live(piece[3], piece[4])
        return (lax.cond(live, total_work, lambda held, unused: held, carry, piece), None)

    start_max = jnp.full((local_heads, ctx_rows), very_low, jnp.float32)
    start_sum = jnp.zeros((local_heads, ctx_rows), jnp.float32)
    (final_max, final_sum), _ = lax.scan(total_step, (start_max, start_sum), key_pieces)
    log_total = final_max + jnp.log(final_sum)

    def output_work(carry, piece):
        coarse, fine = carry
        key_piece, value_piece, key_prefix, key_pos, key_seg = piece
        raw, allowed = block_scores(key_piece, key_prefix, key_pos, key_seg)
        probs = jnp.where(allowed, jnp.exp(raw - log_total[:, :, None]), 0.0)
        rounded = probs.astype(jnp.bfloat16)
        rest = (probs - rounded.astype(jnp.float32)).astype(jnp.bfloat16)
        coarse = coarse + jnp.einsum(
            "hqk,khd->qhd", rounded, value_piece, preferred_element_type=jnp.float32
        )
        fine = fine + jnp.einsum(
            "hqk,khd->qhd", rest, value_piece, preferred_element_type=jnp.float32
        )
        return (coarse, fine)

    def output_step(carry, piece):
        live = block_live(piece[3], piece[4])
        return (lax.cond(live, output_work, lambda held, unused: held, carry, piece), None)

    zero_out = jnp.zeros((ctx_rows, local_heads, head_size), jnp.float32)
    (coarse_out, fine_out), _ = lax.scan(output_step, (zero_out, zero_out), key_pieces)
    exact_out = coarse_out + fine_out
    head_out = coarse_out.reshape(ctx_rows, local_heads * head_size).astype(jnp.bfloat16)
    token_out = lax.all_to_all(head_out, "sp", split_axis=0, concat_axis=1, tiled=True)
    token_out_f = token_out.astype(jnp.float32)
    gated = (token_out_f * out_gate).astype(jnp.bfloat16)
    mid = input_f + matmul(gated, full_output)
    weights_mlp = (
        lax.all_gather(gate_weight, "fsdp", axis=0, tiled=True),
        lax.all_gather(up_weight, "fsdp", axis=0, tiled=True),
        lax.all_gather(down_weight, "fsdp", axis=0, tiled=True),
    )
    full_gate, full_up, full_down = weights_mlp
    inv_second = rms_inverse(mid)
    normed_mlp = (mid * inv_second * mlp_gain).astype(jnp.bfloat16)
    gate_lin = matmul(normed_mlp, full_gate)
    up_lin = matmul(normed_mlp, full_up)
    gate_sig = jax.nn.sigmoid(gate_lin)
    activated = gate_lin * gate_sig
    hidden = (activated * up_lin).astype(jnp.bfloat16)
    block_out = (mid + matmul_right_t(hidden, full_down)).astype(jnp.bfloat16)
    cotangent = out_cotangent[0]
    grad_hidden = matmul(cotangent, full_down)
    grad_gate_lin = (grad_hidden * up_lin * gate_sig * (1.0 + gate_lin * (1.0 - gate_sig))).astype(
        jnp.bfloat16
    )
    grad_up_lin = (grad_hidden * activated).astype(jnp.bfloat16)
    grad_normed_mlp = matmul_right_t(grad_gate_lin, full_gate) + matmul_right_t(
        grad_up_lin, full_up
    )
    mlp_gain_term = jnp.sum(grad_normed_mlp * mid * inv_second, axis=0)
    grad_mid = cotangent.astype(jnp.float32) + norm_back(grad_normed_mlp, mid, inv_second, mlp_gain)
    gate_term = matmul_left_t(normed_mlp, grad_gate_lin)
    up_term = matmul_left_t(normed_mlp, grad_up_lin)
    down_term = matmul_left_t(cotangent, hidden)
    grad_branch = grad_mid.astype(jnp.bfloat16)
    grad_gated = matmul_right_t(grad_branch, full_output)
    grad_attended = (grad_gated * out_gate).astype(jnp.bfloat16)
    grad_gate_pre = (grad_gated * token_out_f * out_gate * (1.0 - out_gate)).astype(jnp.bfloat16)
    head_grad = lax.all_to_all(grad_attended, "sp", split_axis=1, concat_axis=0, tiled=True)
    grad_three = head_grad.reshape(ctx_rows, local_heads, head_size)
    delta = jnp.sum(grad_three.astype(jnp.float32) * exact_out, axis=2).T

    def back_work(carry, piece):
        grad_query_acc, grad_prefix_acc = carry
        key_piece, value_piece, key_prefix, key_pos, key_seg = piece
        raw, allowed = block_scores(key_piece, key_prefix, key_pos, key_seg)
        probs = jnp.where(allowed, jnp.exp(raw - log_total[:, :, None]), 0.0)
        rounded = probs.astype(jnp.bfloat16)
        grad_probs = jnp.einsum(
            "qhd,khd->hqk", grad_three, value_piece, preferred_element_type=jnp.float32
        )
        grad_scores = (probs * (grad_probs - delta[:, :, None])).astype(jnp.bfloat16)
        grad_query_acc = (
            grad_query_acc
            + jnp.einsum("hqk,khd->qhd", grad_scores, key_piece, preferred_element_type=jnp.float32)
            * score_scale
        )
        key_term = (
            jnp.einsum("hqk,qhd->khd", grad_scores, query_three, preferred_element_type=jnp.float32)
            * score_scale
        )
        value_term = jnp.einsum(
            "hqk,qhd->khd", rounded, grad_three, preferred_element_type=jnp.float32
        )
        score_f = grad_scores.astype(jnp.float32)
        grad_prefix_acc = grad_prefix_acc + jnp.sum(score_f, axis=2)
        prefix_term = -jnp.sum(score_f, axis=1)
        return ((grad_query_acc, grad_prefix_acc), (key_term, value_term, prefix_term))

    def back_skip(carry, piece):
        empty_kv = jnp.zeros((key_block, local_heads, head_size), jnp.float32)
        empty_prefix = jnp.zeros((local_heads, key_block), jnp.float32)
        return (carry, (empty_kv, empty_kv, empty_prefix))

    def back_step(carry, piece):
        live = block_live(piece[3], piece[4])
        return lax.cond(live, back_work, back_skip, carry, piece)

    start_prefix = jnp.zeros((local_heads, ctx_rows), jnp.float32)
    (grad_query_acc, grad_prefix_q), (key_terms, value_terms, prefix_terms) = lax.scan(
        back_step, (zero_out, start_prefix), key_pieces
    )
    keys_grad_all = key_terms.reshape(group_rows, local_heads * head_size)
    values_grad_all = value_terms.reshape(group_rows, local_heads * head_size)
    prefix_grad_all = jnp.transpose(prefix_terms, (0, 2, 1)).reshape(group_rows, local_heads)
    own_prefix = lax.dynamic_slice_in_dim(prefix_grad_all, ctx_start, ctx_rows, 0)
    prefix_grad_all = lax.dynamic_update_slice_in_dim(
        prefix_grad_all, own_prefix + grad_prefix_q.T, ctx_start, 0
    )
    forget_grad_term = prefix_back(prefix_grad_all, place_row, slab_rows)
    key_sum, value_sum, forget_sum = (
        lax.psum_scatter(keys_grad_all, "cp", scatter_dimension=0, tiled=True),
        lax.psum_scatter(values_grad_all, "cp", scatter_dimension=0, tiled=True),
        lax.psum_scatter(forget_grad_term, "cp", scatter_dimension=0, tiled=True),
    )
    grad_query_head = grad_query_acc.reshape(ctx_rows, local_heads * head_size).astype(jnp.bfloat16)
    grad_query_tok, grad_key_tok, grad_value_tok, grad_forget_tok = (
        lax.all_to_all(grad_query_head, "sp", split_axis=0, concat_axis=1, tiled=True),
        lax.all_to_all(key_sum.astype(jnp.bfloat16), "sp", split_axis=0, concat_axis=1, tiled=True),
        lax.all_to_all(
            value_sum.astype(jnp.bfloat16), "sp", split_axis=0, concat_axis=1, tiled=True
        ),
        lax.all_to_all(
            forget_sum.astype(jnp.bfloat16), "sp", split_axis=0, concat_axis=1, tiled=True
        ),
    )
    grad_forget_pre = (grad_forget_tok.astype(jnp.float32) * jax.nn.sigmoid(-forget_pre)).astype(
        jnp.bfloat16
    )
    grad_normed = (
        matmul_right_t(grad_query_tok, full_query)
        + matmul_right_t(grad_key_tok, full_key)
        + matmul_right_t(grad_value_tok, full_value)
        + matmul_right_t(grad_gate_pre, full_outgate)
        + matmul_right_t(grad_forget_pre, full_forget)
    )
    attn_gain_term = jnp.sum(grad_normed * input_f * inv_first, axis=0)
    bias_term = jnp.sum(grad_forget_pre.astype(jnp.float32), axis=0)
    tokens_grad = grad_mid + norm_back(grad_normed, input_f, inv_first, attn_gain)
    query_term = matmul_left_t(normed, grad_query_tok)
    key_term_w = matmul_left_t(normed, grad_key_tok)
    value_term_w = matmul_left_t(normed, grad_value_tok)
    outgate_term = matmul_left_t(normed, grad_gate_pre)
    forget_term = matmul_left_t(normed, grad_forget_pre)
    output_term = matmul_left_t(gated, grad_branch)
    (
        query_grad,
        key_grad,
        value_grad,
        outgate_grad,
        forget_grad,
        output_weight_grad,
        gate_grad,
        up_grad,
        down_grad,
    ) = (
        lax.psum_scatter(query_term, ("cp", "sp", "fsdp"), scatter_dimension=0, tiled=True),
        lax.psum_scatter(key_term_w, ("cp", "sp", "fsdp"), scatter_dimension=0, tiled=True),
        lax.psum_scatter(value_term_w, ("cp", "sp", "fsdp"), scatter_dimension=0, tiled=True),
        lax.psum_scatter(outgate_term, ("cp", "sp", "fsdp"), scatter_dimension=0, tiled=True),
        lax.psum_scatter(forget_term, ("cp", "sp", "fsdp"), scatter_dimension=0, tiled=True),
        lax.psum_scatter(output_term, ("cp", "sp", "fsdp"), scatter_dimension=0, tiled=True),
        lax.psum_scatter(gate_term, ("cp", "sp", "fsdp"), scatter_dimension=0, tiled=True),
        lax.psum_scatter(up_term, ("cp", "sp", "fsdp"), scatter_dimension=0, tiled=True),
        lax.psum_scatter(down_term, ("cp", "sp", "fsdp"), scatter_dimension=0, tiled=True),
    )
    attn_gain_grad, mlp_gain_grad, forget_bias_grad = lax.psum(
        (attn_gain_term, mlp_gain_term, bias_term), ("cp", "sp", "fsdp")
    )
    return (
        block_out[None],
        tokens_grad[None],
        attn_gain_grad,
        query_grad,
        key_grad,
        value_grad,
        outgate_grad,
        forget_grad,
        forget_bias_grad,
        output_weight_grad,
        mlp_gain_grad,
        gate_grad,
        up_grad,
        down_grad,
    )


def here():
    return (lax.axis_index("cp"), lax.axis_index("sp"), lax.axis_index("fsdp"))


def flip(s, k):
    if k == 1:
        return s + 1 - 2 * lax.rem(s, 2)
    if k == 2:
        return lax.rem(s + 2, 4)
    return 3 - s


def greet(devices):
    sem = pltpu.get_barrier_semaphore()
    for device in devices:
        pl.semaphore_signal(sem, inc=1, device_id=device, device_id_type=MESH)
    pl.semaphore_wait(sem, len(devices))


def rows_of(index, count):
    return pl.ds(pl.multiple_of(index * count, count), count)


def row_loop(total, step, body):
    def one(i, carry):
        return body(rows_of(i, step), carry)

    return one, total // step


class Gather:
    sems = 13

    def __init__(self, src, out, send, recv):
        c, s, f = here()
        self.src, self.out, self.send, self.recv = src, out, send, recv
        self.c, self.s, self.rows = c, s, src.shape[0]
        self.x, self.y, self.sib = (c, flip(s, 1), f), (c, flip(s, 2), f), (1 - c, s, f)
        self.made = []

    def block(self, k, half=None):
        index = self.c * 4 + (self.s if k == 0 else flip(self.s, k))
        n = self.rows
        if half is None:
            return self.out.at[pl.ds(pl.multiple_of(index * n, n), n)]
        return self.out.at[pl.ds(pl.multiple_of(index * n + half * (n // 2), n // 2), n // 2)]

    def copy(self, src, dst, k, device):
        made = REMOTE(src, dst, self.send.at[k], self.recv.at[k], device, MESH)
        made.start()
        self.made.append(made)
        return made

    def start(self):
        half = self.rows // 2
        low, high = self.src.at[pl.ds(0, half)], self.src.at[pl.ds(half, half)]
        self.a = [
            self.copy(low, self.block(0, 0), 0, self.x),
            self.copy(high, self.block(0, 1), 1, self.y),
            self.copy(high, self.block(0, 1), 2, self.x),
            self.copy(low, self.block(0, 0), 3, self.y),
        ]
        self.g = [self.copy(self.src, self.block(0), 4, self.sib)]

    def pass_on(self, ref, k):
        self.g.append(self.copy(ref, ref, k, self.sib))

    def relay(self):
        self.a[0].wait_recv()
        self.b0 = self.copy(self.block(1, 0), self.block(1, 0), 5, self.y)
        self.a[1].wait_recv()
        self.b1 = self.copy(self.block(2, 1), self.block(2, 1), 6, self.x)
        self.pass_on(self.block(1, 0), 7)
        self.pass_on(self.block(2, 1), 8)
        self.a[2].wait_recv()
        self.pass_on(self.block(1, 1), 9)
        self.a[3].wait_recv()
        self.pass_on(self.block(2, 0), 10)

    def finish(self):
        self.b0.wait_recv()
        self.pass_on(self.block(3, 0), 11)
        self.b1.wait_recv()
        self.pass_on(self.block(3, 1), 12)
        for made in self.g:
            made.wait_recv()
        for made in self.made:
            made.wait_send()


class Reduce:
    sems = 10

    @staticmethod
    def scratch(n, w):
        return [
            pltpu.VMEM((4, n, w), BF),
            pltpu.VMEM((4, n, w), BF),
            pltpu.VMEM((4, n, w // 2), BF),
            pltpu.VMEM((2, n, w // 2), BF),
        ]

    def __init__(self, part, refs, send, recv):
        c, s, f = here()
        self.part, self.send, self.recv = part, send, recv
        self.near, self.sums, self.far, self.last = refs
        self.c, self.s = c, s
        self.n, self.w = self.sums.shape[1], self.sums.shape[2]
        self.x, self.y, self.sib = (c, flip(s, 1), f), (c, flip(s, 2), f), (1 - c, s, f)
        self.made = []

    def copy(self, src, dst, k, device):
        made = REMOTE(src, dst, self.send.at[k], self.recv.at[k], device, MESH)
        made.start()
        self.made.append(made)
        return made

    def own(self, k, core):
        index = core * 4 + (self.s if k == 0 else flip(self.s, k))
        return index * self.n

    def start(self):
        self.a = {}
        for sem, k in enumerate((3, 1, 2, 0)):
            src = self.part.at[pl.ds(pl.multiple_of(self.own(k, 1 - self.c), self.n), self.n)]
            self.a[k] = self.copy(src, self.near.at[k], sem, self.sib)

    def chip_sum(self, k):
        self.a[k].wait_recv()
        base = self.own(k, self.c)

        def body(i, carry):
            r = rows_of(i, 32)
            p = self.part[pl.ds(pl.multiple_of(base + i * 32, 32), 32), :].astype(F32)
            self.sums[k, r, :] = (p + self.near[k, r, :].astype(F32)).astype(BF)
            return carry

        lax.fori_loop(0, self.n // 32, body, 0)

    def add(self, k, cols, slot):
        def body(i, carry):
            r = rows_of(i, 32)
            total = self.sums[k, r, cols].astype(F32) + self.far[slot, r, :].astype(F32)
            self.sums[k, r, cols] = total.astype(BF)
            return carry

        lax.fori_loop(0, self.n // 32, body, 0)

    def halves(self):
        return pl.ds(0, self.w // 2), pl.ds(self.w // 2, self.w // 2)

    def run(self):
        self.first()
        self.second()

    def first(self):
        left, right = self.halves()
        self.chip_sum(3)
        self.fx = self.copy(self.sums.at[3, :, left], self.far.at[1], 4, self.x)
        self.fy = self.copy(self.sums.at[3, :, right], self.far.at[3], 5, self.y)
        self.chip_sum(1)
        self.nx = self.copy(self.sums.at[1, :, left], self.far.at[0], 6, self.x)
        self.chip_sum(2)
        self.ny = self.copy(self.sums.at[2, :, right], self.far.at[2], 7, self.y)

    def second(self):
        left, right = self.halves()
        self.fx.wait_recv()
        self.add(2, left, 1)
        self.by = self.copy(self.sums.at[2, :, left], self.last.at[0], 8, self.y)
        self.fy.wait_recv()
        self.add(1, right, 3)
        self.bx = self.copy(self.sums.at[1, :, right], self.last.at[1], 9, self.x)
        self.a[0].wait_recv()

    def arrive(self):
        for made in (self.nx, self.ny, self.by, self.bx):
            made.wait_recv()

    def total(self, i, step):
        r = rows_of(i, step)
        base = self.own(0, self.c)
        p = self.part[pl.ds(pl.multiple_of(base + i * step, step), step), :].astype(F32)
        p = p + self.near[0, r, :].astype(F32)
        far = jnp.concatenate([self.far[0, r, :], self.far[2, r, :]], axis=1).astype(F32)
        last = jnp.concatenate([self.last[0, r, :], self.last[1, r, :]], axis=1).astype(F32)
        return p + far + last

    def finish(self):
        for made in self.made:
            made.wait_send()


def partners():
    c, s, f = here()
    return [(c, flip(s, 1), f), (c, flip(s, 2), f), (1 - c, s, f)]


STEP = 32


def mean_square_inverse(values):
    return lax.rsqrt(jnp.mean(values * values, axis=1, keepdims=True) + epsilon)


class Line:
    def __init__(self, own, slot, send, recv, depth):
        self.own, self.slot, self.send, self.recv, self.depth = own, slot, send, recv, depth
        self.c, self.s, self.f = here()

    def copy(self, i, distance, up):
        owner = self.f - (distance - 1) if up else self.f + (distance - 1)
        to = lax.rem(self.f + (1 if up else self.depth - 1), self.depth)
        src = self.own[i] if distance == 1 else self.slot(i, owner)
        k = 0 if up else 1
        return REMOTE(
            src,
            self.slot(i, owner),
            self.send.at[k, distance - 1, i],
            self.recv.at[k, distance - 1, i],
            (self.c, self.s, to),
            MESH,
        )

    def may_send(self, distance, up):
        if up:
            return (self.f < self.depth - 1) & (self.f >= distance - 1)
        return (self.f > 0) & (self.f + distance <= self.depth)

    def gets(self, distance, up):
        return self.f >= distance if up else self.f + distance < self.depth

    def start(self):
        for i in range(len(self.own)):
            for up in (True, False):
                pl.when(self.may_send(1, up))(self.copy(i, 1, up).start)

    def pass_on(self, distance):
        for i in range(len(self.own)):
            for up in (True, False):
                pl.when(self.gets(distance, up))(self.got(i, distance, up).wait_recv)
                if distance < self.depth - 1:
                    pl.when(self.may_send(distance + 1, up))(self.copy(i, distance + 1, up).start)

    def got(self, i, distance, up):
        owner = self.f - distance if up else self.f + distance
        k = 0 if up else 1
        place = self.slot(i, owner)
        return REMOTE(
            place,
            place,
            self.send.at[k, distance - 1, i],
            self.recv.at[k, distance - 1, i],
            (self.c, self.s, lax.rem(self.f + (self.depth - 1 if up else 1), self.depth)),
            MESH,
        )

    def finish(self):
        for distance in range(1, self.depth):
            for i in range(len(self.own)):
                for up in (True, False):
                    pl.when(self.may_send(distance, up))(self.copy(i, distance, up).wait_send)


class Spread:
    def __init__(self, src, dst, origin, send, recv, depth, pieces):
        self.c, self.s, self.f = here()
        self.src, self.dst, self.origin, self.depth = src, dst, origin, depth
        self.send, self.recv, self.pieces = send, recv, pieces
        self.n = dst.shape[0] // pieces

    def part(self, ref, i):
        return ref.at[pl.ds(i * self.n, self.n)]

    def copy(self, i, up, first):
        k = 0 if up else 1
        return REMOTE(
            self.part(self.src if first else self.dst, i),
            self.part(self.dst, i),
            self.send.at[k, i],
            self.recv.at[i],
            (self.c, self.s, lax.rem(self.f + (1 if up else self.depth - 1), self.depth)),
            MESH,
        )

    def above(self):
        return (self.f > self.origin) & (self.f < self.depth - 1)

    def below(self):
        return (self.f < self.origin) & (self.f > 0)

    def start(self, local):
        first = self.f == self.origin

        @pl.when(first)
        def _():
            pltpu.make_async_copy(self.src, self.dst, local).start()

        for i in range(self.pieces):
            pl.when(first & (self.f < self.depth - 1))(self.copy(i, True, True).start)
            pl.when(first & (self.f > 0))(self.copy(i, False, True).start)

    def pass_on(self):
        for i in range(self.pieces):
            pl.when(self.f != self.origin)(self.copy(i, True, False).wait_recv)
            pl.when(self.above())(self.copy(i, True, False).start)
            pl.when(self.below())(self.copy(i, False, False).start)

    def finish(self, local):
        first = self.f == self.origin

        @pl.when(first)
        def _():
            pltpu.make_async_copy(self.src, self.dst, local).wait()

        for i in range(self.pieces):
            pl.when((first & (self.f < self.depth - 1)) | self.above())(
                self.copy(i, True, False).wait_send
            )
            pl.when((first & (self.f > 0)) | self.below())(self.copy(i, False, False).wait_send)


WEIGHT_PIECES = 4
OUT_PIECES = 2


def enter_kernel(
    tok_ref, dy_ref, gain_ref, attn_ref, forget_ref, out_w_ref,
    normed_ref, dy_all_ref, w_attn_ref, w_out_ref,
    mine, forget_all, s0, r0, s1, r1, sz, rz, so, ro, l0, *, depth,
):
    c, s, f = here()
    lines = [(c, s, lax.rem(f + 1, depth)), (c, s, lax.rem(f + depth - 1, depth))]
    greet(partners() + lines)
    n = tok_ref.shape[0]
    shard, cols = attn_ref.shape
    step = shard // WEIGHT_PIECES
    own = [attn_ref.at[pl.ds(i * step, step)] for i in range(WEIGHT_PIECES)] + [forget_ref]

    def slot(i, owner):
        if i == WEIGHT_PIECES:
            return forget_all.at[owner]
        rows = pl.ds(pl.multiple_of(owner * shard + i * step, step), step)
        return w_attn_ref.at[rows, pl.ds(0, cols)]

    line = Line(own, slot, sz, rz, depth)
    line.start()
    heads_rows = w_out_ref.shape[0]
    t = c * 4 + s
    origin = (t * heads_rows) // shard
    spread = Spread(
        out_w_ref.at[pl.ds(pl.multiple_of(t * heads_rows - origin * shard, heads_rows), heads_rows)],
        w_out_ref, origin, so, ro, depth, OUT_PIECES,
    )
    keep = [
        pltpu.make_async_copy(
            attn_ref,
            w_attn_ref.at[pl.ds(pl.multiple_of(f * shard, shard), shard), pl.ds(0, cols)],
            l0.at[2],
        ),
        pltpu.make_async_copy(forget_ref, forget_all.at[f], l0.at[3]),
    ]

    def body(i, carry):
        r = rows_of(i, STEP)
        v = tok_ref[r, :].astype(F32)
        mine[r, :] = (v * mean_square_inverse(v) * gain_ref[...]).astype(BF)
        return carry

    lax.fori_loop(0, n // STEP, body, 0)
    first = Gather(mine, normed_ref, s0, r0)
    second = Gather(dy_ref, dy_all_ref, s1, r1)
    keep += [
        pltpu.make_async_copy(mine, first.block(0), l0.at[0]),
        pltpu.make_async_copy(dy_ref, second.block(0), l0.at[1]),
    ]
    first.start()
    for made in keep:
        made.start()
    line.pass_on(1)
    spread.start(l0.at[4])
    first.relay()
    second.start()
    line.pass_on(2)
    first.finish()
    second.relay()
    spread.pass_on()
    line.pass_on(3)
    second.finish()
    line.finish()
    for made in keep:
        made.wait()
    spread.finish(l0.at[4])
    for owner in range(depth):
        small = forget_all[owner].astype(F32)
        tall = jnp.concatenate([small, jnp.zeros((128 - small.shape[0], shard), F32)], axis=0)
        w_attn_ref[owner * shard : (owner + 1) * shard, cols:] = tall.T.astype(BF)


def enter(tokens, cotangent, gain, own_attn, own_forget, output_weight, depth, heads_rows):
    n, w = tokens.shape
    shard, cols = own_attn.shape
    whole = jax.ShapeDtypeStruct((8 * n, w), BF)
    dma = pltpu.SemaphoreType.DMA((Gather.sems,))
    line = pltpu.SemaphoreType.DMA((2, depth - 1, WEIGHT_PIECES + 1))
    vmem = pl.BlockSpec(memory_space=pltpu.VMEM)
    anywhere = pl.BlockSpec(memory_space=pl.ANY)
    return pl.pallas_call(
        functools.partial(enter_kernel, depth=depth),
        name="enter",
        out_shape=(
            whole,
            whole,
            jax.ShapeDtypeStruct((depth * shard, cols + 128), BF),
            jax.ShapeDtypeStruct((heads_rows, w), BF),
        ),
        in_specs=[vmem] * 5 + [anywhere],
        out_specs=[anywhere, anywhere, vmem, anywhere],
        scratch_shapes=[
            pltpu.VMEM((n, w), BF),
            pltpu.VMEM((depth,) + own_forget.shape, BF),
            dma, dma, dma, dma, line, line,
            pltpu.SemaphoreType.DMA((2, OUT_PIECES)),
            pltpu.SemaphoreType.DMA((OUT_PIECES,)),
            pltpu.SemaphoreType.DMA((5,)),
        ],
        compiler_params=pltpu.CompilerParams(
            collective_id=1, has_side_effects=True, vmem_limit_bytes=VMEM_BYTES
        ),
        cost_estimate=pl.CostEstimate(
            flops=50_000_000, bytes_accessed=4 * 8 * n * w * 2, transcendentals=0
        ),
    )(tokens, cotangent, gain[None], own_attn, own_forget, output_weight)


def middle_kernel(
    part_ref, tok_ref, gain_ref, mid_ref, normed_ref,
    near, sums, far, last, mine, s0, r0, s1, r1, l0,
):
    greet(partners())
    reduce = Reduce(part_ref, (near, sums, far, last), s0, r0)
    reduce.start()
    reduce.run()
    reduce.arrive()

    def body(i, carry):
        r = rows_of(i, STEP)
        mid = tok_ref[r, :].astype(F32) + reduce.total(i, STEP)
        mid_ref[r, :] = mid
        mine[r, :] = (mid * mean_square_inverse(mid) * gain_ref[...]).astype(BF)
        return carry

    lax.fori_loop(0, mine.shape[0] // STEP, body, 0)
    gather = Gather(mine, normed_ref, s1, r1)
    gather.start()
    keep = pltpu.make_async_copy(mine, gather.block(0), l0.at[0])
    keep.start()
    reduce.finish()
    gather.relay()
    gather.finish()
    keep.wait()


def middle(part, tokens, gain):
    n, w = tokens.shape
    dma = pltpu.SemaphoreType.DMA((16,))
    vmem = pl.BlockSpec(memory_space=pltpu.VMEM)
    return pl.pallas_call(
        middle_kernel,
        name="middle",
        out_shape=(jax.ShapeDtypeStruct((n, w), F32), jax.ShapeDtypeStruct((8 * n, w), BF)),
        in_specs=[vmem] * 3,
        out_specs=[vmem, pl.BlockSpec(memory_space=pl.ANY)],
        scratch_shapes=Reduce.scratch(n, w)
        + [pltpu.VMEM((n, w), BF), dma, dma, dma, dma, pltpu.SemaphoreType.DMA((2,))],
        compiler_params=pltpu.CompilerParams(
            collective_id=2, has_side_effects=True, vmem_limit_bytes=VMEM_BYTES
        ),
        cost_estimate=pl.CostEstimate(
            flops=50_000_000, bytes_accessed=4 * 8 * n * w * 2, transcendentals=0
        ),
    )(part, tokens, gain[None])


TERM_PIECES = 4


class LineSum:
    def __init__(self, term, got, send, recv, depth):
        self.term, self.got, self.send, self.recv, self.depth = term, got, send, recv, depth
        self.c, self.s, self.f = here()
        self.n = term.shape[0] // TERM_PIECES

    def source(self, i, g):
        return self.term.at[pl.ds(i * self.n, self.n), g]

    def copy(self, k, g, i, src):
        to = lax.rem(self.f + (1 if k == 0 else self.depth - 1), self.depth)
        return REMOTE(
            src,
            self.got.at[k, g, pl.ds(i * self.n, self.n)],
            self.send.at[k, g, i],
            self.recv.at[k, g, i],
            (self.c, self.s, to),
            MESH,
        )

    def targets(self, k):
        return range(self.depth - 1, 0, -1) if k == 0 else range(self.depth - 1)

    def is_end(self, k):
        return self.f == (0 if k == 0 else self.depth - 1)

    def start(self):
        for i in range(TERM_PIECES):
            self.start_piece(i)

    def start_piece(self, i):
        for n in range(self.depth - 1):
            for k in (0, 1):
                g = self.targets(k)[n]
                pl.when(self.is_end(k))(self.copy(k, g, i, self.source(i, g)).start)

    def add(self, k, g, i):
        rows = pl.ds(i * self.n, self.n)
        total = self.got[k, g, rows].astype(F32) + self.term[rows, g].astype(F32)
        self.got[k, g, rows] = total.astype(BF)

    def pass_on(self, i):
        for n in range(self.depth - 2):
            for k in (0, 1):
                g = self.targets(k)[n]
                beyond = self.f < g if k == 0 else self.f > g

                @pl.when(beyond & jnp.logical_not(self.is_end(k)))
                def _(k=k, g=g):
                    made = self.copy(k, g, i, self.got.at[k, g, pl.ds(i * self.n, self.n)])
                    made.wait_recv()
                    self.add(k, g, i)
                    made.start()

    def collect(self, out):
        for i in range(TERM_PIECES):
            rows = pl.ds(i * self.n, self.n)
            for g in range(self.depth):

                @pl.when(self.f == g)
                def _(g=g, i=i, rows=rows):
                    total = self.term[rows, g].astype(F32)
                    for k in (0, 1):
                        if g != (0 if k == 0 else self.depth - 1):
                            self.copy(k, g, i, self.source(i, g)).wait_recv()
                            total = total + self.got[k, g, rows].astype(F32)
                    out[rows] = total.astype(BF)

    def finish(self):
        for k in (0, 1):
            for g in self.targets(k):
                beyond = self.f < g if k == 0 else self.f > g
                for i in range(TERM_PIECES):
                    pl.when(beyond)(self.copy(k, g, i, self.source(i, g)).wait_send)


class Exchange:
    def __init__(self, rows, out, send, recv, peers):
        c, s, f = here()
        self.place = c * 4 + s
        self.made = [
            REMOTE(rows.at[core * 4 + other], out.at[self.place], send.at[k], recv.at[k], (core, other, f), MESH)
            for core, other, f, k in peers
        ]
        self.keep = pltpu.make_async_copy(rows.at[self.place], out.at[self.place], send.at[0])

    def start(self):
        for made in self.made:
            made.start()
        self.keep.start()

    def finish(self):
        for made in self.made:
            made.wait()
        self.keep.wait()


FFN_TILE = 256


def ffn_kernel(
    nm_ref, dy_all_ref, w_ref, dy_ref, mid_ref, gain_ref,
    grad_mid_ref, gain_term_ref, branch_ref, down_part_ref, gu_rows_ref, low_term_ref,
    nm, dy, w, grads, own, near, out, far, last, term, got, mine, stage,
    l0, l1, s0, r0, s1, r1, s2, r2, *, depth,
):
    c, s, f = here()
    n, width = dy_ref.shape
    fw = w.shape[1] // 3
    x, y, sib = partners()
    loads = []
    w_load = pltpu.make_async_copy(w_ref, w, l0.at[8])
    w_load.start()
    for i, k in enumerate((3, 1, 2, 0)):
        chip = flip(s, k) if k else s
        pair = []
        for half, core in enumerate((1 - c, c)):
            src = pl.ds(pl.multiple_of((core * 4 + chip) * n, n), n)
            dst = pl.ds((2 * i + half) * n, n)
            pair.append(pltpu.make_async_copy(nm_ref.at[src], nm.at[dst], l0.at[2 * i + half]))
            pair.append(pltpu.make_async_copy(dy_all_ref.at[src], dy.at[dst], l1.at[2 * i + half]))
        for made in pair:
            made.start()
        loads.append(pair)
    greet(partners() + [
        (c, s, lax.rem(f + 1, depth)), (c, s, lax.rem(f + depth - 1, depth))
    ])
    left, right = pl.ds(0, width // 2), pl.ds(width // 2, width // 2)

    def send(src, dst, k, device):
        return REMOTE(src, dst, s0.at[k], r0.at[k], device, MESH)

    def to_sibling(i):
        return send(out.at[lax.rem(i, 2)], near.at[i], i, sib)

    fx = send(own.at[0, :, left], far.at[1], 4, x)
    fy = send(own.at[0, :, right], far.at[3], 5, y)
    nx = send(own.at[1, :, left], far.at[0], 6, x)
    ny = send(own.at[2, :, right], far.at[2], 7, y)
    by = send(own.at[2, :, left], last.at[0], 8, y)
    bx = send(own.at[1, :, right], last.at[1], 9, x)
    w_load.wait()

    def one_pair(i, unused):
        rows = rows_of(i, 2 * n)
        for at, pair in enumerate(loads):

            @pl.when(i == at)
            def _(pair=pair):
                for made in pair:
                    made.wait()

        for t in range(fw // FFN_TILE):
            cols = pl.ds(t * FFN_TILE, FFN_TILE)
            ups = pl.ds(fw + t * FFN_TILE, FFN_TILE)
            downs = pl.ds(2 * fw + t * FFN_TILE, FFN_TILE)
            gate_lin = dot(nm[rows, :], w[:, cols], 1, 0)
            up_lin = dot(nm[rows, :], w[:, ups], 1, 0)
            grad_hidden = dot(dy[rows, :], w[:, downs], 1, 0)
            sig = jax.nn.sigmoid(gate_lin)
            active = gate_lin * sig
            grads[rows, downs] = (active * up_lin).astype(BF)
            grads[rows, cols] = (
                grad_hidden * up_lin * sig * (1.0 + gate_lin * (1.0 - sig))
            ).astype(BF)
            grads[rows, ups] = (grad_hidden * active).astype(BF)

        @pl.when(i >= 1)
        def _():
            to_sibling(i - 1).wait_recv()

            def body(j, carry):
                r = rows_of(j, 32)
                total = own[i - 1, r, :].astype(F32) + near[i - 1, r, :].astype(F32)
                own[i - 1, r, :] = total.astype(BF)
                return carry

            lax.fori_loop(0, n // 32, body, 0)

        @pl.when(i == 1)
        def _():
            fx.start()
            fy.start()

        pl.when(i == 2)(nx.start)
        pl.when(i == 3)(ny.start)

        @pl.when(i >= 2)
        def _():
            to_sibling(i - 2).wait_send()

        for t in range(width // FFN_TILE):
            feats = pl.ds(t * FFN_TILE, FFN_TILE)
            part = dot(grads[rows, 0 : 2 * fw], w[feats, 0 : 2 * fw], 1, 1).astype(BF)
            out[lax.rem(i, 2), :, feats] = part[:n]
            own[i, :, feats] = part[n:]
        to_sibling(i).start()
        return unused

    lax.fori_loop(0, 4, one_pair, 0)
    fx.wait_recv()

    def add(at, cols, slot):
        def body(j, carry):
            r = rows_of(j, 32)
            total = own[at, r, cols].astype(F32) + far[slot, r, :].astype(F32)
            own[at, r, cols] = total.astype(BF)
            return carry

        lax.fori_loop(0, n // 32, body, 0)

    add(2, left, 1)
    by.start()
    fy.wait_recv()
    add(1, right, 3)
    bx.start()

    line = LineSum(term, got, s2, r2, depth)
    deep = width // TERM_PIECES
    per = term.shape[0] // TERM_PIECES
    for i in range(TERM_PIECES):
        feats = pl.ds(i * deep, deep)
        tile = dot(nm[:, feats], grads[:, 0 : 2 * fw], 0, 0).astype(BF)
        term[i * per : (i + 1) * per] = tile.reshape((per,) + term.shape[1:])
        line.start_piece(i)
    for i in range(TERM_PIECES):
        feats = pl.ds(i * deep, deep)
        tile = dot(dy[:, feats], grads[:, 2 * fw :], 0, 0).astype(BF)
        tile = tile.reshape((per, depth, term.shape[2], fw))
        for g in range(depth):
            low_term_ref[g, i * per : (i + 1) * per] = tile[:, g]

    to_sibling(3).wait_recv()
    for made in (nx, ny, by, bx):
        made.wait_recv()

    def total_of(j, step):
        r = rows_of(j, step)
        total = own[3, r, :].astype(F32) + near[3, r, :].astype(F32)
        a = jnp.concatenate([far[0, r, :], far[2, r, :]], axis=1).astype(F32)
        b = jnp.concatenate([last[0, r, :], last[1, r, :]], axis=1).astype(F32)
        return total + a + b

    def body(j, carry):
        r = rows_of(j, STEP)
        grad = total_of(j, STEP)
        mid = mid_ref[r, :]
        inverse = mean_square_inverse(mid)
        weighted = grad * gain_ref[...]
        back = inverse * weighted - mid * inverse**3 * jnp.mean(
            weighted * mid, axis=1, keepdims=True
        )
        grad_mid = dy_ref[r, :].astype(F32) + back
        grad_mid_ref[r, :] = grad_mid
        mine[r, :] = grad_mid.astype(BF)
        return carry + jnp.sum(grad * mid * inverse, axis=0, keepdims=True)

    gain_term_ref[...] = lax.fori_loop(0, n // STEP, body, jnp.zeros((1, width), F32))
    gather = Gather(mine, branch_ref, s1, r1)
    gather.start()
    keep = pltpu.make_async_copy(mine, gather.block(0), l1.at[8])
    keep.start()
    line.pass_on(0)

    def down_part(i):
        chip = flip(s, (3, 1, 2, 0)[i]) if i < 3 else s
        made = []
        for half, core in enumerate((1 - c, c)):
            rows = pl.ds((2 * i + half) * n, n)
            for t in range(width // FFN_TILE):
                feats = pl.ds(t * FFN_TILE, FFN_TILE)
                part = dot(grads[rows, 2 * fw :], w[feats, 2 * fw :], 1, 1)
                stage[half, :, feats] = part.astype(BF)
            dst = pl.ds(pl.multiple_of((core * 4 + chip) * n, n), n)
            made.append(
                pltpu.make_async_copy(stage.at[half], down_part_ref.at[dst], l0.at[half])
            )
            made[-1].start()
        return made

    moved = []
    for i in range(4):
        for made in moved:
            made.wait()
        moved = down_part(i)
        if i == 1:
            line.pass_on(1)
    gather.relay()
    line.pass_on(2)
    gather.finish()
    for made in moved:
        made.wait()
    line.pass_on(3)
    line.collect(gu_rows_ref)
    keep.wait()
    for made in (fx, fy, nx, ny, by, bx):
        made.wait_send()
    for i in (2, 3):
        to_sibling(i).wait_send()
    line.finish()


def ffn(normed_all, cotangent_all, weights, cotangent, mid, gain, depth):
    n, width = mid.shape
    fw = weights.shape[1] // 3
    r = width // (8 * depth)
    dma = pltpu.SemaphoreType.DMA((16,))
    line = pltpu.SemaphoreType.DMA((2, depth, TERM_PIECES))
    vmem = pl.BlockSpec(memory_space=pltpu.VMEM)
    anywhere = pl.BlockSpec(memory_space=pl.ANY)
    return pl.pallas_call(
        functools.partial(ffn_kernel, depth=depth),
        name="ffn",
        out_shape=(
            jax.ShapeDtypeStruct((n, width), F32),
            jax.ShapeDtypeStruct((1, width), F32),
            jax.ShapeDtypeStruct((8 * n, width), BF),
            jax.ShapeDtypeStruct((8 * n, width), BF),
            jax.ShapeDtypeStruct((8, r, 2 * fw), BF),
            jax.ShapeDtypeStruct((depth, 8, r, fw), BF),
        ),
        in_specs=[anywhere] * 3 + [vmem] * 3,
        out_specs=[vmem, vmem, anywhere, anywhere, vmem, vmem],
        scratch_shapes=[
            pltpu.VMEM((8 * n, width), BF),
            pltpu.VMEM((8 * n, width), BF),
            pltpu.VMEM((width, 3 * fw), BF),
            pltpu.VMEM((8 * n, 3 * fw), BF),
            pltpu.VMEM((4, n, width), BF),
            pltpu.VMEM((4, n, width), BF),
            pltpu.VMEM((2, n, width), BF),
            pltpu.VMEM((4, n, width // 2), BF),
            pltpu.VMEM((2, n, width // 2), BF),
            pltpu.VMEM((8, depth, r, 2 * fw), BF),
            pltpu.VMEM((2, depth, 8, r, 2 * fw), BF),
            pltpu.VMEM((n, width), BF),
            pltpu.VMEM((2, n, width), BF),
            dma, dma, dma, dma, dma, dma, line, line,
        ],
        compiler_params=pltpu.CompilerParams(
            collective_id=3, has_side_effects=True, vmem_limit_bytes=63 * 1024 * 1024
        ),
        cost_estimate=pl.CostEstimate(
            flops=2 * 8 * n * width * fw * 9, bytes_accessed=4 * 8 * n * width * 2,
            transcendentals=0,
        ),
    )(normed_all, cotangent_all, weights, cotangent, mid, gain[None])


def leave_kernel(
    part_ref, down_ref, tok_ref, grad_mid_ref, mid_ref, gain_ref, small_ref, term_ref, mlp_ref, low_ref,
    grad_ref, small_sum_ref, out_ref, attn_rows_ref, mlp_rows_ref, low_rows_ref,
    near, sums, far, last, near2, sums2, far2, last2, small, plane_small, line_small, got, rows,
    s0, r0, s1, r1, s2, r2, s3, r3, s4, r4, s5, r5, s6, r6, *, depth,
):
    c, s, f = here()
    plane_peers = [
        (core, flip(s, k) if k else s, f, k + 4 * i)
        for i, core in enumerate((c, 1 - c))
        for k in range(4)
        if i or k
    ]
    line_peers = [(c, s, lax.rem(f + k, depth), k) for k in range(1, depth)]
    greet([p[:3] for p in plane_peers + line_peers])
    line = LineSum(term_ref, got, s3, r3, depth)
    line.start()
    reduce = Reduce(part_ref, (near, sums, far, last), s0, r0)
    other = Reduce(down_ref, (near2, sums2, far2, last2), s1, r1)
    mlp_rows = Exchange(mlp_ref, mlp_rows_ref, s4, r4, plane_peers)
    low_rows = Exchange(low_ref, low_rows_ref, s6, r6, plane_peers)
    reduce.start()
    other.start()
    reduce.first()
    mlp_rows.start()
    low_rows.start()
    reduce.second()
    line.pass_on(0)
    other.first()
    line.pass_on(1)
    reduce.arrive()

    def body(i, carry):
        r = rows_of(i, STEP)
        grad = reduce.total(i, STEP)
        tok = tok_ref[r, :].astype(F32)
        inverse = mean_square_inverse(tok)
        weighted = grad * gain_ref[...]
        back = inverse * weighted - tok * inverse**3 * jnp.mean(
            weighted * tok, axis=1, keepdims=True
        )
        grad_ref[r, :] = grad_mid_ref[r, :] + back
        return carry + jnp.sum(grad * tok * inverse, axis=0, keepdims=True)

    n, w = tok_ref.shape
    small[...] = small_ref[...]
    small[0:1, :] = lax.fori_loop(0, n // STEP, body, jnp.zeros((1, w), F32))
    place = c * 4 + s
    plane_small[pl.ds(place, 1)] = small[...][None]
    sent = []
    for core, other_s, other_f, k in plane_peers:
        made = REMOTE(
            small, plane_small.at[place], s2.at[k - 1], r2.at[k - 1], (core, other_s, other_f), MESH
        )
        made.start()
        sent.append(made)
    line.pass_on(2)
    other.second()
    line.pass_on(3)
    for made in sent:
        made.wait()
    total = plane_small[0]
    for i in range(1, 8):
        total = total + plane_small[i]
    small[...] = total
    line_small[pl.ds(f, 1)] = total[None]
    sent = []
    for core, other_s, other_f, k in line_peers:
        made = REMOTE(
            small, line_small.at[f], s2.at[6 + k], r2.at[6 + k], (core, other_s, other_f), MESH
        )
        made.start()
        sent.append(made)
    other.arrive()

    def body2(i, carry):
        r = rows_of(i, STEP)
        out_ref[r, :] = (mid_ref[r, :] + other.total(i, STEP)).astype(BF)
        return carry

    lax.fori_loop(0, n // STEP, body2, 0)
    line.collect(rows)
    attn_rows = Exchange(rows, attn_rows_ref, s5, r5, plane_peers)
    attn_rows.start()
    for made in sent:
        made.wait()
    total = line_small[0]
    for i in range(1, depth):
        total = total + line_small[i]
    small_sum_ref[...] = total
    reduce.finish()
    other.finish()
    line.finish()
    mlp_rows.finish()
    low_rows.finish()
    attn_rows.finish()


def leave(part, down_part, tokens, grad_mid, mid, gain, small, term, mlp_rows, low_rows, depth):
    n, w = mid.shape
    sems = pltpu.SemaphoreType.DMA((6 + depth,))
    plane, _, r, cols = term.shape
    dma = pltpu.SemaphoreType.DMA((16,))
    eight = pltpu.SemaphoreType.DMA((8,))
    line = pltpu.SemaphoreType.DMA((2, depth, TERM_PIECES))
    vmem = pl.BlockSpec(memory_space=pltpu.VMEM)
    return pl.pallas_call(
        functools.partial(leave_kernel, depth=depth),
        name="leave",
        out_shape=(
            jax.ShapeDtypeStruct((n, w), F32),
            jax.ShapeDtypeStruct((8, w), F32),
            jax.ShapeDtypeStruct((n, w), BF),
            jax.ShapeDtypeStruct((plane, r, cols), BF),
            jax.ShapeDtypeStruct(mlp_rows.shape, BF),
            jax.ShapeDtypeStruct(low_rows.shape, BF),
        ),
        in_specs=[vmem] * 10,
        out_specs=[vmem] * 6,
        scratch_shapes=Reduce.scratch(n, w)
        + Reduce.scratch(n, w)
        + [
            pltpu.VMEM((8, w), F32),
            pltpu.VMEM((8, 8, w), F32),
            pltpu.VMEM((depth, 8, w), F32),
            pltpu.VMEM((2, depth, plane, r, cols), BF),
            pltpu.VMEM((plane, r, cols), BF),
            dma, dma, dma, dma, sems, sems, line, line,
            eight, eight, eight, eight, eight, eight,
        ],
        compiler_params=pltpu.CompilerParams(
            collective_id=4, has_side_effects=True, vmem_limit_bytes=VMEM_BYTES
        ),
        cost_estimate=pl.CostEstimate(
            flops=50_000_000, bytes_accessed=4 * 8 * n * w * 2, transcendentals=0
        ),
    )(part, down_part, tokens, grad_mid, mid, gain[None], small, term, mlp_rows, low_rows)


def finish_kernel(
    attn_ref, mlp_ref, low_ref, small_ref, out_w_ref, block_ref, tok_grad_ref,
    q_ref, k_ref, v_ref, g_ref, f_ref, o_ref, gate_ref, up_ref, down_ref,
    gain1_ref, gain2_ref, bias_ref, out_ref, tokens_ref, *, hw, heads,
):
    plane = attn_ref.shape[0]
    fw = low_ref.shape[2]
    for i, ref in enumerate((q_ref, k_ref, v_ref, g_ref)):
        ref[...] = jnp.concatenate(
            [attn_ref[t, :, i * hw : (i + 1) * hw].astype(F32) for t in range(plane)], axis=1
        )
    a = lax.broadcasted_iota(jnp.int32, (128, 128), 0)
    b = lax.broadcasted_iota(jnp.int32, (128, 128), 1)
    total = jnp.zeros((attn_ref.shape[1], 128), F32)
    for t in range(plane):
        pick = jnp.where((a + t * heads == b) & (a < heads), 1.0, 0.0).astype(BF)
        total = total + dot(attn_ref[t, :, 4 * hw : 4 * hw + 128], pick, 1, 0)
    f_ref[...] = total[:, : f_ref.shape[1]]
    o_ref[...] = out_w_ref[...].astype(F32)
    for i, ref in enumerate((gate_ref, up_ref)):
        for t in range(plane):
            ref[:, t * fw : (t + 1) * fw] = mlp_ref[t, :, i * fw : (i + 1) * fw].astype(F32)
    for t in range(plane):
        down_ref[:, t * fw : (t + 1) * fw] = low_ref[t].astype(F32)
    gain1_ref[...] = small_ref[0:1, :]
    gain2_ref[...] = small_ref[1:2, :]
    bias_ref[...] = small_ref[2:3, 0 : bias_ref.shape[1]]
    out_ref[...] = block_ref[...]
    tokens_ref[...] = tok_grad_ref[...]


def finish(attn_rows, mlp_rows, low_rows, small, out_w, block_out, tokens_grad, hw, heads):
    plane, r, _ = attn_rows.shape
    n, w = tokens_grad.shape
    fw = low_rows.shape[2]
    vmem = pl.BlockSpec(memory_space=pltpu.VMEM)
    square = jax.ShapeDtypeStruct((r, plane * hw), F32)
    wide = jax.ShapeDtypeStruct((r, plane * fw), F32)
    row = jax.ShapeDtypeStruct((1, w), F32)
    return pl.pallas_call(
        functools.partial(finish_kernel, hw=hw, heads=heads),
        name="finish",
        out_shape=(
            square, square, square, square,
            jax.ShapeDtypeStruct((r, plane * heads), F32),
            jax.ShapeDtypeStruct(out_w.shape, F32),
            wide, wide, wide, row, row,
            jax.ShapeDtypeStruct((1, plane * heads), F32),
            jax.ShapeDtypeStruct((n, w), BF),
            jax.ShapeDtypeStruct((n, w), F32),
        ),
        in_specs=[vmem] * 7,
        out_specs=[vmem] * 14,
        compiler_params=pltpu.CompilerParams(vmem_limit_bytes=VMEM_BYTES),
    )(attn_rows, mlp_rows, low_rows, small, out_w, block_out, tokens_grad)


BQ = 256
BK = 256
AUG = 128


def dot(a, b, ca, cb):
    return lax.dot_general(a, b, (((ca,), (cb,)), ((), ())), preferred_element_type=F32)


def three_parts(v):
    hi = v.astype(BF).astype(F32)
    mid = (v - hi).astype(BF).astype(F32)
    low = (v - hi - mid).astype(BF).astype(F32)
    return hi, mid, low


def triangle(n, suffix):
    a = lax.broadcasted_iota(jnp.int32, (n, n), 0)
    b = lax.broadcasted_iota(jnp.int32, (n, n), 1)
    return jnp.where(a >= b if suffix else a <= b, 1.0, 0.0).astype(BF)


def log_sigmoid(v):
    return jnp.minimum(v, 0.0) - jnp.log1p(jnp.exp(-jnp.abs(v)))


def doc_starts(ends_ref, pos):
    start = jnp.zeros_like(pos)
    for n in range(ends_ref.shape[0]):
        end = ends_ref[n]
        start = jnp.where(pos >= end, jnp.maximum(start, end), start)
    return start


def first_block(ends_ref, pos):
    start = jnp.int32(0)
    for n in range(ends_ref.shape[0]):
        end = ends_ref[n]
        start = jnp.where(pos >= end, jnp.maximum(start, end), start)
    return start // BK


def extend(prefix_row, sign_first):
    hi, mid, low = three_parts(prefix_row)
    r = lax.broadcasted_iota(jnp.int32, (16, prefix_row.shape[1]), 0)
    base = 0 if sign_first else 3
    sign = 1.0 if sign_first else -1.0
    ones = (r >= 3) & (r < 6) if sign_first else r < 3
    out = jnp.where(ones, 1.0, 0.0)
    out = jnp.where(r == base, sign * hi, out)
    out = jnp.where(r == base + 1, sign * mid, out)
    return jnp.where(r == base + 2, sign * low, out)


def lay_out(place_ref, cat_ref, prefix_ref, heads, hd, slab, qa, ka, kta):
    hw = heads * hd
    slabs = cat_ref.shape[1] // slab
    for p in range(slabs):
        src = pl.ds(pl.multiple_of(place_ref[p] * slab, slab), slab)
        dst = pl.ds(p * slab, slab)
        for h in range(heads):
            q = cat_ref[h * hd : (h + 1) * hd, src].astype(BF).astype(F32)
            row = prefix_ref[h : h + 1, dst]
            rest = jnp.zeros((AUG - hd - 16, slab), F32)
            qe = jnp.concatenate([q * hd**-0.5, extend(row, True), rest], axis=0)
            qa[h, :, dst] = qe.astype(BF)
            k = cat_ref[hw + h * hd : hw + (h + 1) * hd, src].astype(BF).astype(F32)
            ke = jnp.concatenate([k, extend(row, False), rest], axis=0)
            if kta is not None:
                kta[h, :, dst] = ke.astype(BF)
            ka[h, dst, :] = ke.T.astype(BF)


def attention_kernel(
    place_ref, ends_ref, cat_ref, bias_ref,
    gated_ref, att_ref, exact_ref, lse_ref, prefix_ref,
    qa, ka, va, *, heads, hd, slab,
):
    hw = heads * hd
    tokens = cat_ref.shape[1]
    slabs = tokens // slab
    tri = triangle(slab, False)
    carry = jnp.zeros((16, 1), F32)
    for p in range(slabs):
        src = pl.ds(pl.multiple_of(place_ref[p] * slab, slab), slab)
        pre = cat_ref[4 * hw : 4 * hw + 16, src] + bias_ref[:, 0:1]
        steps = log_sigmoid(pre).astype(BF)
        part = dot(steps, tri, 1, 0) + carry
        prefix_ref[:, p * slab : (p + 1) * slab] = part
        carry = part[:, slab - 1 : slab]
        for h in range(heads):
            va[h, :, p * slab : (p + 1) * slab] = cat_ref[
                2 * hw + h * hd : 2 * hw + (h + 1) * hd, src
            ].astype(BF)
    lay_out(place_ref, cat_ref, prefix_ref, heads, hd, slab, qa, ka, None)
    per = slab // BQ

    def one_query_block(qb, unused):
        q0 = pl.multiple_of(qb * BQ, BQ)
        pos = q0 + lax.broadcasted_iota(jnp.int32, (1, BQ), 1)
        start = doc_starts(ends_ref, pos)
        low = first_block(ends_ref, q0)
        inside = lax.broadcasted_iota(jnp.int32, (BK, BQ), 0)

        def one_key_block(kb, held):
            k0 = pl.multiple_of(kb * BK, BK)
            allowed = (inside <= pos - k0) & (inside >= start - k0)
            out = []
            for h in range(heads):
                m, l, acc = held[h]
                st = dot(ka[h, pl.ds(k0, BK), :], qa[h, :, pl.ds(q0, BQ)], 1, 0)
                st = jnp.where(allowed, st, very_low)
                new = jnp.maximum(m, jnp.max(st, axis=0, keepdims=True))
                p = jnp.exp(st - new)
                scale = jnp.exp(m - new)
                l = l * scale + jnp.sum(p, axis=0, keepdims=True)
                acc = acc * scale + dot(va[h, :, pl.ds(k0, BK)], p.astype(BF), 1, 0)
                out.append((new, l, acc))
            return tuple(out)

        begin = tuple(
            (jnp.full((1, BQ), very_low, F32), jnp.zeros((1, BQ), F32), jnp.zeros((hd, BQ), F32))
            for _ in range(heads)
        )
        done = lax.fori_loop(low, qb + 1, one_key_block, begin)
        dst = pl.ds(pl.multiple_of(place_ref[qb // per] * slab + lax.rem(qb, per) * BQ, BQ), BQ)
        for h in range(heads):
            m, l, acc = done[h]
            lse_ref[h : h + 1, pl.ds(q0, BQ)] = m + jnp.log(l)
            exact = acc / l
            rounded = exact.astype(BF)
            exact_ref[h * hd : (h + 1) * hd, dst] = exact
            att_ref[h * hd : (h + 1) * hd, dst] = rounded
            gate = jax.nn.sigmoid(cat_ref[3 * hw + h * hd : 3 * hw + (h + 1) * hd, dst])
            gated_ref[h * hd : (h + 1) * hd, dst] = (rounded.astype(F32) * gate).astype(BF)
        return unused

    lse_ref[...] = jnp.zeros_like(lse_ref)
    lax.fori_loop(0, tokens // BQ, one_query_block, 0)


def attention(place, ends, cat, bias, heads, hd, slab):
    tokens = cat.shape[1]
    hw = heads * hd
    vmem = pl.BlockSpec(memory_space=pltpu.VMEM)
    smem = pl.BlockSpec(memory_space=pltpu.SMEM)
    return pl.pallas_call(
        functools.partial(attention_kernel, heads=heads, hd=hd, slab=slab),
        name="attention",
        out_shape=(
            jax.ShapeDtypeStruct((hw, tokens), BF),
            jax.ShapeDtypeStruct((hw, tokens), BF),
            jax.ShapeDtypeStruct((hw, tokens), F32),
            jax.ShapeDtypeStruct((8, tokens), F32),
            jax.ShapeDtypeStruct((16, tokens), F32),
        ),
        in_specs=[smem, smem, vmem, vmem],
        out_specs=[vmem] * 5,
        scratch_shapes=[
            pltpu.VMEM((heads, AUG, tokens), BF),
            pltpu.VMEM((heads, tokens, AUG), BF),
            pltpu.VMEM((heads, hd, tokens), BF),
        ],
        compiler_params=pltpu.CompilerParams(vmem_limit_bytes=VMEM_BYTES),
        cost_estimate=pl.CostEstimate(
            flops=8 * heads * tokens * tokens * hd, bytes_accessed=cat.size * 4,
            transcendentals=heads * tokens * tokens // 2,
        ),
    )(place, ends, cat, bias)


def attention_back_kernel(
    place_ref, ends_ref, cat_ref, bias_ref, gg_ref, att_ref, exact_ref, lse_ref, prefix_ref,
    out_ref, bias_grad_ref,
    qa, ka, kta, va, do, delta_ref, dk, dv, gp, *, heads, hd, slab,
):
    hw = heads * hd
    tokens = cat_ref.shape[1]
    slabs = tokens // slab
    per = slab // BQ
    lay_out(place_ref, cat_ref, prefix_ref, heads, hd, slab, qa, ka, kta)
    delta_ref[...] = jnp.zeros_like(delta_ref)
    gp[...] = jnp.zeros_like(gp)
    dk[...] = jnp.zeros_like(dk)
    dv[...] = jnp.zeros_like(dv)
    out_ref[4 * hw :, :] = jnp.zeros((out_ref.shape[0] - 4 * hw, tokens), BF)
    for p in range(slabs):
        src = pl.ds(pl.multiple_of(place_ref[p] * slab, slab), slab)
        dst = pl.ds(p * slab, slab)
        for h in range(heads):
            rows = slice(h * hd, (h + 1) * hd)
            gate = jax.nn.sigmoid(cat_ref[3 * hw + h * hd : 3 * hw + (h + 1) * hd, src])
            gg = gg_ref[rows, src]
            low = (gg * gate).astype(BF)
            do[h, :, dst] = low
            delta_ref[h : h + 1, dst] = jnp.sum(
                low.astype(F32) * exact_ref[rows, src], axis=0, keepdims=True
            )
            gate_grad = gg * att_ref[rows, src].astype(F32) * gate * (1.0 - gate)
            out_ref[3 * hw + h * hd : 3 * hw + (h + 1) * hd, src] = gate_grad.astype(BF)
            v = cat_ref[2 * hw + h * hd : 2 * hw + (h + 1) * hd, src]
            va[h, dst, :] = v.T.astype(BF)

    def one_query_block(qb, unused):
        q0 = pl.multiple_of(qb * BQ, BQ)
        pos = q0 + lax.broadcasted_iota(jnp.int32, (1, BQ), 1)
        start = doc_starts(ends_ref, pos)
        low = first_block(ends_ref, q0)
        inside = lax.broadcasted_iota(jnp.int32, (BK, BQ), 0)

        def one_key_block(kb, held):
            k0 = pl.multiple_of(kb * BK, BK)
            keys = pl.ds(k0, BK)
            allowed = (inside <= pos - k0) & (inside >= start - k0)
            out = []
            for h in range(heads):
                queries = qa[h, :, pl.ds(q0, BQ)]
                grads = do[h, :, pl.ds(q0, BQ)]
                st = dot(ka[h, keys, :], queries, 1, 0) - lse_ref[h : h + 1, pl.ds(q0, BQ)]
                p = jnp.exp(jnp.where(allowed, st, very_low))
                dp = dot(va[h, keys, :], grads, 1, 0) - delta_ref[h : h + 1, pl.ds(q0, BQ)]
                ds = (p * dp).astype(BF)
                out.append(held[h] + dot(kta[h, :, keys], ds, 1, 0))
                dk[h, :, keys] += dot(queries, ds, 1, 1)
                dv[h, :, keys] += dot(grads, p.astype(BF), 1, 1)
            return tuple(out)

        begin = tuple(jnp.zeros((AUG, BQ), F32) for _ in range(heads))
        done = lax.fori_loop(low, qb + 1, one_key_block, begin)
        dst = pl.ds(pl.multiple_of(place_ref[qb // per] * slab + lax.rem(qb, per) * BQ, BQ), BQ)
        for h in range(heads):
            out_ref[h * hd : (h + 1) * hd, dst] = (done[h][0:hd, :] * hd**-0.5).astype(BF)
            gp[h : h + 1, pl.ds(q0, BQ)] = done[h][hd : hd + 1, :]
        return unused

    lax.fori_loop(0, tokens // BQ, one_query_block, 0)
    tri = triangle(slab, True)
    carry = jnp.zeros((16, 1), F32)
    bias_grad = jnp.zeros((16, 1), F32)
    for p in reversed(range(slabs)):
        src = pl.ds(pl.multiple_of(place_ref[p] * slab, slab), slab)
        dst = pl.ds(p * slab, slab)
        for h in range(heads):
            out_ref[hw + h * hd : hw + (h + 1) * hd, src] = dk[h, 0:hd, dst].astype(BF)
            out_ref[2 * hw + h * hd : 2 * hw + (h + 1) * hd, src] = dv[h, :, dst].astype(BF)
            gp[h : h + 1, dst] = gp[h : h + 1, dst] - dk[h, hd + 3 : hd + 4, dst]
        grad = gp[:, dst]
        total = carry
        for piece in three_parts(grad):
            total = total + dot(piece.astype(BF), tri, 1, 0)
        carry = total[:, 0:1]
        pre = cat_ref[4 * hw : 4 * hw + 16, src] + bias_ref[:, 0:1]
        low = (total.astype(BF).astype(F32) * jax.nn.sigmoid(-pre)).astype(BF)
        out_ref[4 * hw : 4 * hw + 16, src] = low
        bias_grad = bias_grad + jnp.sum(low.astype(F32), axis=1, keepdims=True)
    bias_grad_ref[...] = jnp.broadcast_to(bias_grad, bias_grad_ref.shape)


def attention_back(place, ends, cat, bias, gg, att, exact, lse, prefix, heads, hd, slab):
    tokens = cat.shape[1]
    vmem = pl.BlockSpec(memory_space=pltpu.VMEM)
    smem = pl.BlockSpec(memory_space=pltpu.SMEM)
    return pl.pallas_call(
        functools.partial(attention_back_kernel, heads=heads, hd=hd, slab=slab),
        name="attention_back",
        out_shape=(
            jax.ShapeDtypeStruct(cat.shape, BF),
            jax.ShapeDtypeStruct((16, 128), F32),
        ),
        in_specs=[smem, smem] + [vmem] * 7,
        out_specs=[vmem] * 2,
        scratch_shapes=[
            pltpu.VMEM((heads, AUG, tokens), BF),
            pltpu.VMEM((heads, tokens, AUG), BF),
            pltpu.VMEM((heads, AUG, tokens), BF),
            pltpu.VMEM((heads, tokens, hd), BF),
            pltpu.VMEM((heads, hd, tokens), BF),
            pltpu.VMEM((8, tokens), F32),
            pltpu.VMEM((heads, AUG, tokens), F32),
            pltpu.VMEM((heads, hd, tokens), F32),
            pltpu.VMEM((16, tokens), F32),
        ],
        compiler_params=pltpu.CompilerParams(vmem_limit_bytes=VMEM_BYTES),
        cost_estimate=pl.CostEstimate(
            flops=20 * heads * tokens * tokens * hd, bytes_accessed=cat.size * 8,
            transcendentals=heads * tokens * tokens // 2,
        ),
    )(place, ends, cat, bias, gg, att, exact, lse, prefix)


def local_plane(
    tokens, out_cotangent, seq_lengths, slab_place, attn_gain, query_weight, key_weight,
    value_weight, outgate_weight, forget_weight, forget_bias, output_weight, mlp_gain,
    gate_weight, up_weight, down_weight,
):
    plane_axes = ("cp", "sp")
    plane = lax.axis_size("cp") * lax.axis_size("sp")
    depth = lax.axis_size("fsdp")
    place = lax.axis_index("cp") * lax.axis_size("sp") + lax.axis_index("sp")
    head_count = forget_weight.shape[1]
    width = tokens.shape[2]
    hd = width // head_count
    heads = head_count // plane
    hw = heads * hd
    fw = gate_weight.shape[1] // plane
    shard = query_weight.shape[0]
    group_rows = tokens.shape[1] * plane
    slab = group_rows // slab_place.shape[1]

    def columns(weight, count):
        return lax.dynamic_slice_in_dim(weight, place * count, count, 1)

    inputs, cotangent = tokens[0], out_cotangent[0]
    slabs = slab_place.shape[1]
    order = jnp.arange(slabs, dtype=jnp.int32)
    storage = jnp.sum(
        jnp.where(slab_place[0][None, :] == order[:, None], order[None, :], 0), axis=1
    )
    ends = jnp.cumsum(seq_lengths[0])

    own_attn = jnp.concatenate(
        [columns(w, hw) for w in (query_weight, key_weight, value_weight, outgate_weight)], axis=1
    )
    own_forget = jnp.pad(columns(forget_weight, heads).T, ((0, 16 - heads), (0, 0)))
    own_mlp = jnp.concatenate(
        [columns(gate_weight, fw), columns(up_weight, fw), columns(down_weight, fw)], axis=1
    )
    normed, cotangent_all, w_attn, w_out = enter(
        inputs, cotangent, attn_gain, own_attn, own_forget, output_weight, depth, hw
    )
    own_mlp, w_attn = lax.optimization_barrier((own_mlp, w_attn))
    w_mlp = lax.all_gather(own_mlp, "fsdp", axis=0, tiled=True)
    cat = dot(w_attn, normed, 0, 1)
    bias_own = lax.dynamic_slice_in_dim(forget_bias, place * heads, heads, 0)
    bias = jnp.broadcast_to(jnp.pad(bias_own, (0, 16 - heads))[:, None], (16, 128))
    gated, att, exact, lse, prefix = attention(storage, ends, cat, bias, heads, hd, slab)
    mid_part = dot(gated, w_out, 0, 0).astype(BF)
    mid, normed_mlp = middle(mid_part, inputs, mlp_gain)

    grad_mid, mlp_gain_term, branch, down_part, mlp_rows, low_term = ffn(
        normed_mlp, cotangent_all, w_mlp, cotangent, mid, mlp_gain, depth
    )
    low_grad = lax.psum_scatter(
        low_term.reshape(width, fw), "fsdp", scatter_dimension=0, tiled=True
    )

    grad_gated = dot(w_out, branch, 1, 1)
    grad_cat, bias_grad = attention_back(
        storage, ends, cat, bias, grad_gated, att, exact, lse, prefix, heads, hd, slab
    )
    out_term = dot(gated, branch, 1, 0).astype(BF)
    attn_term = dot(normed, grad_cat, 0, 1).astype(BF)
    out_term, low_grad = lax.optimization_barrier((out_term, low_grad))
    output_weight_grad = lax.psum_scatter(out_term, "fsdp", scatter_dimension=0, tiled=True)
    attn_part = dot(grad_cat, w_attn, 0, 1).astype(BF)
    bias_row = lax.dynamic_update_slice_in_dim(
        jnp.zeros((width,), F32), bias_grad[:heads, 0], place * heads, 0
    )
    small = jnp.concatenate(
        [jnp.zeros((1, width), F32), mlp_gain_term, bias_row[None], jnp.zeros((5, width), F32)]
    )
    part = width // (plane * depth)
    tokens_grad, small_sum, block_out, attn_rows, mlp_rows, low_rows = leave(
        attn_part, down_part, inputs, grad_mid, mid, attn_gain, small,
        attn_term.reshape(plane, depth, part, -1), mlp_rows, low_grad.reshape(plane, part, -1), depth,
    )
    (
        query_grad, key_grad, value_grad, outgate_grad, forget_grad, out_grad, gate_grad, up_grad,
        down_grad, attn_gain_grad, mlp_gain_grad, forget_bias_grad, block_out, tokens_grad,
    ) = finish(
        attn_rows, mlp_rows, low_rows, small_sum, output_weight_grad, block_out, tokens_grad,
        hw, heads,
    )
    return (
        block_out[None],
        tokens_grad[None],
        attn_gain_grad[0],
        query_grad,
        key_grad,
        value_grad,
        outgate_grad,
        forget_grad,
        forget_bias_grad[0],
        out_grad,
        mlp_gain_grad[0],
        gate_grad,
        up_grad,
        down_grad,
    )


def fits_plane(mesh, tokens, slab_place, forget_weight, gate_weight):
    sizes = dict(mesh.shape)
    if (sizes["cp"], sizes["sp"]) != (2, 4):
        return False
    plane = sizes["cp"] * sizes["sp"]
    width = tokens.shape[2]
    head_count = forget_weight.shape[1]
    group_rows = tokens.shape[1]
    slab = group_rows // slab_place.shape[1]
    heads = head_count // plane
    return (
        head_count % plane == 0
        and heads <= 8
        and width // head_count == 64
        and slab % 256 == 0
        and group_rows <= 2048
        and width % 256 == 0
        and gate_weight.shape[1] % (128 * plane) == 0
        and width % (16 * plane * sizes["fsdp"]) == 0
        and (group_rows // plane) % 64 == 0
    )


def shard(mesh, fn):
    return jax.shard_map(
        fn,
        mesh=mesh,
        in_specs=(
            P("fsdp", ("cp", "sp"), None),
            P("fsdp", ("cp", "sp"), None),
            P("fsdp", None),
            P("fsdp", None),
            P(),
            P("fsdp", None),
            P("fsdp", None),
            P("fsdp", None),
            P("fsdp", None),
            P("fsdp", None),
            P(),
            P("fsdp", None),
            P(),
            P("fsdp", None),
            P("fsdp", None),
            P("fsdp", None),
        ),
        out_specs=(
            P("fsdp", ("cp", "sp"), None),
            P("fsdp", ("cp", "sp"), None),
            P(),
            P(("cp", "sp", "fsdp"), None),
            P(("cp", "sp", "fsdp"), None),
            P(("cp", "sp", "fsdp"), None),
            P(("cp", "sp", "fsdp"), None),
            P(("cp", "sp", "fsdp"), None),
            P(),
            P(("cp", "sp", "fsdp"), None),
            P(),
            P(("cp", "sp", "fsdp"), None),
            P(("cp", "sp", "fsdp"), None),
            P(("cp", "sp", "fsdp"), None),
        ),
        check_vma=False,
    )


def solution(mesh):
    def run(*args):
        fast = fits_plane(mesh, args[0], args[3], args[9], args[13])
        return shard(mesh, local_plane if fast else local)(*args)

    return run
```

```python
import functools

import jax
import jax.numpy as jnp
from jax import lax
from jax.experimental import pallas as pl
from jax.experimental.pallas import tpu as pltpu
from jax.sharding import PartitionSpec as P

epsilon = 1e-06
very_low = -1e30
MESH = pl.DeviceIdType.MESH
BF = jnp.bfloat16
F32 = jnp.float32
REMOTE = pltpu.make_async_remote_copy
VMEM_BYTES = 60 * 1024 * 1024


def matmul(left, right):
    return jnp.dot(left, right, preferred_element_type=jnp.float32)


def matmul_right_t(left, right):
    return lax.dot_general(
        left, right, (((1,), (1,)), ((), ())), preferred_element_type=jnp.float32
    )


def matmul_left_t(left, right):
    return lax.dot_general(
        left, right, (((0,), (0,)), ((), ())), preferred_element_type=jnp.float32
    )


def rms_inverse(values):
    return lax.rsqrt(jnp.mean(values * values, axis=1, keepdims=True) + epsilon)


def norm_back(upstream, values, inverse, gain):
    weighted = upstream * gain
    return inverse * weighted - values * inverse**3 * jnp.mean(
        weighted * values, axis=1, keepdims=True
    )


def row_layout(place_row, lens_row, count, slab_rows):
    rows = jnp.arange(count, dtype=jnp.int32)
    slab_index = rows // slab_rows
    table = (
        slab_index[:, None] == jnp.arange(place_row.shape[0], dtype=jnp.int32)[None, :]
    ).astype(jnp.int32)
    position = jnp.sum(table * place_row[None, :], axis=1) * slab_rows + rows % slab_rows
    ends = jnp.cumsum(lens_row)
    segment = jnp.sum((position[:, None] >= ends[None, :]).astype(jnp.int32), axis=1)
    return (position, segment)


def forget_prefix(log_all, place_row, slab_rows):
    slabs = place_row.shape[0]
    steps = log_all.astype(jnp.float32).reshape(slabs, slab_rows, -1)
    inside = jnp.cumsum(steps, axis=1)
    totals = inside[:, -1, :]
    earlier = (place_row[None, :] < place_row[:, None]).astype(jnp.float32)
    offsets = jnp.dot(earlier, totals, precision=lax.Precision.HIGHEST)
    return (inside + offsets[:, None, :]).reshape(slabs * slab_rows, -1)


def prefix_back(grad_prefix, place_row, slab_rows):
    slabs = place_row.shape[0]
    steps = grad_prefix.reshape(slabs, slab_rows, -1)
    inside = jnp.flip(jnp.cumsum(jnp.flip(steps, 1), axis=1), 1)
    totals = inside[:, 0, :]
    later = (place_row[None, :] > place_row[:, None]).astype(jnp.float32)
    offsets = jnp.dot(later, totals, precision=lax.Precision.HIGHEST)
    return (inside + offsets[:, None, :]).reshape(slabs * slab_rows, -1)


def local(
    tokens,
    out_cotangent,
    seq_lengths,
    slab_place,
    attn_gain,
    query_weight,
    key_weight,
    value_weight,
    outgate_weight,
    forget_weight,
    forget_bias,
    output_weight,
    mlp_gain,
    gate_weight,
    up_weight,
    down_weight,
):
    seq_devices = lax.axis_size("sp")
    ctx_devices = lax.axis_size("cp")
    ctx_index = lax.axis_index("cp")
    tok_rows = tokens.shape[1]
    model_width = tokens.shape[2]
    head_count = forget_weight.shape[1]
    local_heads = head_count // seq_devices
    head_size = model_width // head_count
    ctx_rows = tok_rows * seq_devices
    group_rows = ctx_rows * ctx_devices
    slab_rows = ctx_rows // 2
    key_block = min(512, group_rows)
    key_blocks = group_rows // key_block
    score_scale = head_size ** (-0.5)
    place_row = slab_place[0]
    lens_row = seq_lengths[0]
    ctx_start = ctx_index * ctx_rows
    inputs = tokens[0]
    input_f = inputs.astype(jnp.float32)
    weights_attn = (
        lax.all_gather(query_weight, "fsdp", axis=0, tiled=True),
        lax.all_gather(key_weight, "fsdp", axis=0, tiled=True),
        lax.all_gather(value_weight, "fsdp", axis=0, tiled=True),
        lax.all_gather(outgate_weight, "fsdp", axis=0, tiled=True),
        lax.all_gather(forget_weight, "fsdp", axis=0, tiled=True),
        lax.all_gather(output_weight, "fsdp", axis=0, tiled=True),
    )
    full_query, full_key, full_value, full_outgate, full_forget, full_output = weights_attn
    inv_first = rms_inverse(input_f)
    normed = (input_f * inv_first * attn_gain).astype(jnp.bfloat16)
    queries = matmul(normed, full_query).astype(jnp.bfloat16)
    keys = matmul(normed, full_key).astype(jnp.bfloat16)
    values = matmul(normed, full_value).astype(jnp.bfloat16)
    out_gate = jax.nn.sigmoid(matmul(normed, full_outgate))
    forget_pre = matmul(normed, full_forget) + forget_bias
    log_forget = jax.nn.log_sigmoid(forget_pre).astype(jnp.bfloat16)
    head_query, head_key, head_value, head_forget = (
        lax.all_to_all(queries, "sp", split_axis=1, concat_axis=0, tiled=True),
        lax.all_to_all(keys, "sp", split_axis=1, concat_axis=0, tiled=True),
        lax.all_to_all(values, "sp", split_axis=1, concat_axis=0, tiled=True),
        lax.all_to_all(log_forget, "sp", split_axis=1, concat_axis=0, tiled=True),
    )
    keys_all, values_all, forget_all = (
        lax.all_gather(head_key, "cp", axis=0, tiled=True),
        lax.all_gather(head_value, "cp", axis=0, tiled=True),
        lax.all_gather(head_forget, "cp", axis=0, tiled=True),
    )
    prefix_all = forget_prefix(forget_all, place_row, slab_rows)
    pos_all, seg_all = row_layout(place_row, lens_row, group_rows, slab_rows)
    query_pos = lax.dynamic_slice_in_dim(pos_all, ctx_start, ctx_rows, 0)
    query_seg = lax.dynamic_slice_in_dim(seg_all, ctx_start, ctx_rows, 0)
    query_prefix = lax.dynamic_slice_in_dim(prefix_all, ctx_start, ctx_rows, 0)
    query_three = head_query.reshape(ctx_rows, local_heads, head_size)
    query_pos_top = jnp.max(query_pos)
    query_seg_low = jnp.min(query_seg)
    query_seg_top = jnp.max(query_seg)
    key_pieces = (
        keys_all.reshape(key_blocks, key_block, local_heads, head_size),
        values_all.reshape(key_blocks, key_block, local_heads, head_size),
        prefix_all.reshape(key_blocks, key_block, local_heads),
        pos_all.reshape(key_blocks, key_block),
        seg_all.reshape(key_blocks, key_block),
    )

    def block_live(key_pos, key_seg):
        return (
            (query_pos_top >= jnp.min(key_pos))
            & (query_seg_top >= jnp.min(key_seg))
            & (jnp.max(key_seg) >= query_seg_low)
        )

    def block_scores(key_piece, key_prefix, key_pos, key_seg):
        raw = (
            jnp.einsum("qhd,khd->hqk", query_three, key_piece, preferred_element_type=jnp.float32)
            * score_scale
        )
        raw = raw + query_prefix.T[:, :, None] - key_prefix.T[:, None, :]
        allowed = (query_pos[:, None] >= key_pos[None, :]) & (
            query_seg[:, None] == key_seg[None, :]
        )
        return (raw, allowed[None, :, :])

    def total_work(carry, piece):
        running_max, running_sum = carry
        key_piece, value_piece, key_prefix, key_pos, key_seg = piece
        raw, allowed = block_scores(key_piece, key_prefix, key_pos, key_seg)
        new_max = jnp.maximum(running_max, jnp.max(jnp.where(allowed, raw, very_low), axis=2))
        terms = jnp.where(allowed, jnp.exp(raw - new_max[:, :, None]), 0.0)
        new_sum = running_sum * jnp.exp(running_max - new_max) + jnp.sum(terms, axis=2)
        return (new_max, new_sum)

    def total_step(carry, piece):
        live = block_live(piece[3], piece[4])
        return (lax.cond(live, total_work, lambda held, unused: held, carry, piece), None)

    start_max = jnp.full((local_heads, ctx_rows), very_low, jnp.float32)
    start_sum = jnp.zeros((local_heads, ctx_rows), jnp.float32)
    (final_max, final_sum), _ = lax.scan(total_step, (start_max, start_sum), key_pieces)
    log_total = final_max + jnp.log(final_sum)

    def output_work(carry, piece):
        coarse, fine = carry
        key_piece, value_piece, key_prefix, key_pos, key_seg = piece
        raw, allowed = block_scores(key_piece, key_prefix, key_pos, key_seg)
        probs = jnp.where(allowed, jnp.exp(raw - log_total[:, :, None]), 0.0)
        rounded = probs.astype(jnp.bfloat16)
        rest = (probs - rounded.astype(jnp.float32)).astype(jnp.bfloat16)
        coarse = coarse + jnp.einsum(
            "hqk,khd->qhd", rounded, value_piece, preferred_element_type=jnp.float32
        )
        fine = fine + jnp.einsum(
            "hqk,khd->qhd", rest, value_piece, preferred_element_type=jnp.float32
        )
        return (coarse, fine)

    def output_step(carry, piece):
        live = block_live(piece[3], piece[4])
        return (lax.cond(live, output_work, lambda held, unused: held, carry, piece), None)

    zero_out = jnp.zeros((ctx_rows, local_heads, head_size), jnp.float32)
    (coarse_out, fine_out), _ = lax.scan(output_step, (zero_out, zero_out), key_pieces)
    exact_out = coarse_out + fine_out
    head_out = coarse_out.reshape(ctx_rows, local_heads * head_size).astype(jnp.bfloat16)
    token_out = lax.all_to_all(head_out, "sp", split_axis=0, concat_axis=1, tiled=True)
    token_out_f = token_out.astype(jnp.float32)
    gated = (token_out_f * out_gate).astype(jnp.bfloat16)
    mid = input_f + matmul(gated, full_output)
    weights_mlp = (
        lax.all_gather(gate_weight, "fsdp", axis=0, tiled=True),
        lax.all_gather(up_weight, "fsdp", axis=0, tiled=True),
        lax.all_gather(down_weight, "fsdp", axis=0, tiled=True),
    )
    full_gate, full_up, full_down = weights_mlp
    inv_second = rms_inverse(mid)
    normed_mlp = (mid * inv_second * mlp_gain).astype(jnp.bfloat16)
    gate_lin = matmul(normed_mlp, full_gate)
    up_lin = matmul(normed_mlp, full_up)
    gate_sig = jax.nn.sigmoid(gate_lin)
    activated = gate_lin * gate_sig
    hidden = (activated * up_lin).astype(jnp.bfloat16)
    block_out = (mid + matmul_right_t(hidden, full_down)).astype(jnp.bfloat16)
    cotangent = out_cotangent[0]
    grad_hidden = matmul(cotangent, full_down)
    grad_gate_lin = (grad_hidden * up_lin * gate_sig * (1.0 + gate_lin * (1.0 - gate_sig))).astype(
        jnp.bfloat16
    )
    grad_up_lin = (grad_hidden * activated).astype(jnp.bfloat16)
    grad_normed_mlp = matmul_right_t(grad_gate_lin, full_gate) + matmul_right_t(
        grad_up_lin, full_up
    )
    mlp_gain_term = jnp.sum(grad_normed_mlp * mid * inv_second, axis=0)
    grad_mid = cotangent.astype(jnp.float32) + norm_back(grad_normed_mlp, mid, inv_second, mlp_gain)
    gate_term = matmul_left_t(normed_mlp, grad_gate_lin)
    up_term = matmul_left_t(normed_mlp, grad_up_lin)
    down_term = matmul_left_t(cotangent, hidden)
    grad_branch = grad_mid.astype(jnp.bfloat16)
    grad_gated = matmul_right_t(grad_branch, full_output)
    grad_attended = (grad_gated * out_gate).astype(jnp.bfloat16)
    grad_gate_pre = (grad_gated * token_out_f * out_gate * (1.0 - out_gate)).astype(jnp.bfloat16)
    head_grad = lax.all_to_all(grad_attended, "sp", split_axis=1, concat_axis=0, tiled=True)
    grad_three = head_grad.reshape(ctx_rows, local_heads, head_size)
    delta = jnp.sum(grad_three.astype(jnp.float32) * exact_out, axis=2).T

    def back_work(carry, piece):
        grad_query_acc, grad_prefix_acc = carry
        key_piece, value_piece, key_prefix, key_pos, key_seg = piece
        raw, allowed = block_scores(key_piece, key_prefix, key_pos, key_seg)
        probs = jnp.where(allowed, jnp.exp(raw - log_total[:, :, None]), 0.0)
        rounded = probs.astype(jnp.bfloat16)
        grad_probs = jnp.einsum(
            "qhd,khd->hqk", grad_three, value_piece, preferred_element_type=jnp.float32
        )
        grad_scores = (probs * (grad_probs - delta[:, :, None])).astype(jnp.bfloat16)
        grad_query_acc = (
            grad_query_acc
            + jnp.einsum("hqk,khd->qhd", grad_scores, key_piece, preferred_element_type=jnp.float32)
            * score_scale
        )
        key_term = (
            jnp.einsum("hqk,qhd->khd", grad_scores, query_three, preferred_element_type=jnp.float32)
            * score_scale
        )
        value_term = jnp.einsum(
            "hqk,qhd->khd", rounded, grad_three, preferred_element_type=jnp.float32
        )
        score_f = grad_scores.astype(jnp.float32)
        grad_prefix_acc = grad_prefix_acc + jnp.sum(score_f, axis=2)
        prefix_term = -jnp.sum(score_f, axis=1)
        return ((grad_query_acc, grad_prefix_acc), (key_term, value_term, prefix_term))

    def back_skip(carry, piece):
        empty_kv = jnp.zeros((key_block, local_heads, head_size), jnp.float32)
        empty_prefix = jnp.zeros((local_heads, key_block), jnp.float32)
        return (carry, (empty_kv, empty_kv, empty_prefix))

    def back_step(carry, piece):
        live = block_live(piece[3], piece[4])
        return lax.cond(live, back_work, back_skip, carry, piece)

    start_prefix = jnp.zeros((local_heads, ctx_rows), jnp.float32)
    (grad_query_acc, grad_prefix_q), (key_terms, value_terms, prefix_terms) = lax.scan(
        back_step, (zero_out, start_prefix), key_pieces
    )
    keys_grad_all = key_terms.reshape(group_rows, local_heads * head_size)
    values_grad_all = value_terms.reshape(group_rows, local_heads * head_size)
    prefix_grad_all = jnp.transpose(prefix_terms, (0, 2, 1)).reshape(group_rows, local_heads)
    own_prefix = lax.dynamic_slice_in_dim(prefix_grad_all, ctx_start, ctx_rows, 0)
    prefix_grad_all = lax.dynamic_update_slice_in_dim(
        prefix_grad_all, own_prefix + grad_prefix_q.T, ctx_start, 0
    )
    forget_grad_term = prefix_back(prefix_grad_all, place_row, slab_rows)
    key_sum, value_sum, forget_sum = (
        lax.psum_scatter(keys_grad_all, "cp", scatter_dimension=0, tiled=True),
        lax.psum_scatter(values_grad_all, "cp", scatter_dimension=0, tiled=True),
        lax.psum_scatter(forget_grad_term, "cp", scatter_dimension=0, tiled=True),
    )
    grad_query_head = grad_query_acc.reshape(ctx_rows, local_heads * head_size).astype(jnp.bfloat16)
    grad_query_tok, grad_key_tok, grad_value_tok, grad_forget_tok = (
        lax.all_to_all(grad_query_head, "sp", split_axis=0, concat_axis=1, tiled=True),
        lax.all_to_all(key_sum.astype(jnp.bfloat16), "sp", split_axis=0, concat_axis=1, tiled=True),
        lax.all_to_all(
            value_sum.astype(jnp.bfloat16), "sp", split_axis=0, concat_axis=1, tiled=True
        ),
        lax.all_to_all(
            forget_sum.astype(jnp.bfloat16), "sp", split_axis=0, concat_axis=1, tiled=True
        ),
    )
    grad_forget_pre = (grad_forget_tok.astype(jnp.float32) * jax.nn.sigmoid(-forget_pre)).astype(
        jnp.bfloat16
    )
    grad_normed = (
        matmul_right_t(grad_query_tok, full_query)
        + matmul_right_t(grad_key_tok, full_key)
        + matmul_right_t(grad_value_tok, full_value)
        + matmul_right_t(grad_gate_pre, full_outgate)
        + matmul_right_t(grad_forget_pre, full_forget)
    )
    attn_gain_term = jnp.sum(grad_normed * input_f * inv_first, axis=0)
    bias_term = jnp.sum(grad_forget_pre.astype(jnp.float32), axis=0)
    tokens_grad = grad_mid + norm_back(grad_normed, input_f, inv_first, attn_gain)
    query_term = matmul_left_t(normed, grad_query_tok)
    key_term_w = matmul_left_t(normed, grad_key_tok)
    value_term_w = matmul_left_t(normed, grad_value_tok)
    outgate_term = matmul_left_t(normed, grad_gate_pre)
    forget_term = matmul_left_t(normed, grad_forget_pre)
    output_term = matmul_left_t(gated, grad_branch)
    (
        query_grad,
        key_grad,
        value_grad,
        outgate_grad,
        forget_grad,
        output_weight_grad,
        gate_grad,
        up_grad,
        down_grad,
    ) = (
        lax.psum_scatter(query_term, ("cp", "sp", "fsdp"), scatter_dimension=0, tiled=True),
        lax.psum_scatter(key_term_w, ("cp", "sp", "fsdp"), scatter_dimension=0, tiled=True),
        lax.psum_scatter(value_term_w, ("cp", "sp", "fsdp"), scatter_dimension=0, tiled=True),
        lax.psum_scatter(outgate_term, ("cp", "sp", "fsdp"), scatter_dimension=0, tiled=True),
        lax.psum_scatter(forget_term, ("cp", "sp", "fsdp"), scatter_dimension=0, tiled=True),
        lax.psum_scatter(output_term, ("cp", "sp", "fsdp"), scatter_dimension=0, tiled=True),
        lax.psum_scatter(gate_term, ("cp", "sp", "fsdp"), scatter_dimension=0, tiled=True),
        lax.psum_scatter(up_term, ("cp", "sp", "fsdp"), scatter_dimension=0, tiled=True),
        lax.psum_scatter(down_term, ("cp", "sp", "fsdp"), scatter_dimension=0, tiled=True),
    )
    attn_gain_grad, mlp_gain_grad, forget_bias_grad = lax.psum(
        (attn_gain_term, mlp_gain_term, bias_term), ("cp", "sp", "fsdp")
    )
    return (
        block_out[None],
        tokens_grad[None],
        attn_gain_grad,
        query_grad,
        key_grad,
        value_grad,
        outgate_grad,
        forget_grad,
        forget_bias_grad,
        output_weight_grad,
        mlp_gain_grad,
        gate_grad,
        up_grad,
        down_grad,
    )


def here():
    return (lax.axis_index("cp"), lax.axis_index("sp"), lax.axis_index("fsdp"))


def flip(s, k):
    if k == 1:
        return s + 1 - 2 * lax.rem(s, 2)
    if k == 2:
        return lax.rem(s + 2, 4)
    return 3 - s


def greet(devices):
    sem = pltpu.get_barrier_semaphore()
    for device in devices:
        pl.semaphore_signal(sem, inc=1, device_id=device, device_id_type=MESH)
    pl.semaphore_wait(sem, len(devices))


def rows_of(index, count):
    return pl.ds(pl.multiple_of(index * count, count), count)


def row_loop(total, step, body):
    def one(i, carry):
        return body(rows_of(i, step), carry)

    return one, total // step


class Gather:
    sems = 13

    def __init__(self, src, out, send, recv):
        c, s, f = here()
        self.src, self.out, self.send, self.recv = src, out, send, recv
        self.c, self.s, self.rows = c, s, src.shape[0]
        self.x, self.y, self.sib = (c, flip(s, 1), f), (c, flip(s, 2), f), (1 - c, s, f)
        self.made = []

    def block(self, k, half=None):
        index = self.c * 4 + (self.s if k == 0 else flip(self.s, k))
        n = self.rows
        if half is None:
            return self.out.at[pl.ds(pl.multiple_of(index * n, n), n)]
        return self.out.at[pl.ds(pl.multiple_of(index * n + half * (n // 2), n // 2), n // 2)]

    def copy(self, src, dst, k, device):
        made = REMOTE(src, dst, self.send.at[k], self.recv.at[k], device, MESH)
        made.start()
        self.made.append(made)
        return made

    def start(self):
        half = self.rows // 2
        low, high = self.src.at[pl.ds(0, half)], self.src.at[pl.ds(half, half)]
        self.a = [
            self.copy(low, self.block(0, 0), 0, self.x),
            self.copy(high, self.block(0, 1), 1, self.y),
            self.copy(high, self.block(0, 1), 2, self.x),
            self.copy(low, self.block(0, 0), 3, self.y),
        ]
        self.g = [self.copy(self.src, self.block(0), 4, self.sib)]

    def pass_on(self, ref, k):
        self.g.append(self.copy(ref, ref, k, self.sib))

    def relay(self):
        self.a[0].wait_recv()
        self.b0 = self.copy(self.block(1, 0), self.block(1, 0), 5, self.y)
        self.a[1].wait_recv()
        self.b1 = self.copy(self.block(2, 1), self.block(2, 1), 6, self.x)
        self.pass_on(self.block(1, 0), 7)
        self.pass_on(self.block(2, 1), 8)
        self.a[2].wait_recv()
        self.pass_on(self.block(1, 1), 9)
        self.a[3].wait_recv()
        self.pass_on(self.block(2, 0), 10)

    def finish(self):
        self.b0.wait_recv()
        self.pass_on(self.block(3, 0), 11)
        self.b1.wait_recv()
        self.pass_on(self.block(3, 1), 12)
        for made in self.g:
            made.wait_recv()
        for made in self.made:
            made.wait_send()


class PairSum:
    order = (3, 1, 2, 0)

    @staticmethod
    def scratch(n, w):
        return [
            pltpu.VMEM((4, n, w), BF),
            pltpu.VMEM((4, n, w), BF),
            pltpu.VMEM((2, n, w), BF),
            pltpu.VMEM((4, n, w // 2), BF),
            pltpu.VMEM((2, n, w // 2), BF),
            pltpu.SemaphoreType.DMA((10,)),
            pltpu.SemaphoreType.DMA((10,)),
        ]

    @staticmethod
    def tail_scratch(n, w):
        full = PairSum.scratch(n, w)
        return full[:1] + full[3:]

    def __init__(self, refs):
        if len(refs) == 5:
            refs = (refs[0], None, None) + tuple(refs[1:])
        self.own, self.near, self.out, self.far, self.last, self.send, self.recv = refs
        self.x, self.y, self.sib = partners()
        self.n, w = self.own.shape[1], self.own.shape[2]
        self.left, self.right = pl.ds(0, w // 2), pl.ds(w // 2, w // 2)
        self.fx = self.copy(self.own.at[0, :, self.left], self.far.at[1], 4, self.x)
        self.fy = self.copy(self.own.at[0, :, self.right], self.far.at[3], 5, self.y)
        self.nx = self.copy(self.own.at[1, :, self.left], self.far.at[0], 6, self.x)
        self.ny = self.copy(self.own.at[2, :, self.right], self.far.at[2], 7, self.y)
        self.by = self.copy(self.own.at[2, :, self.left], self.last.at[0], 8, self.y)
        self.bx = self.copy(self.own.at[1, :, self.right], self.last.at[1], 9, self.x)

    @staticmethod
    def blocks(c, s):
        return [
            core * 4 + (flip(s, k) if k else s) for k in PairSum.order for core in (1 - c, c)
        ]

    def copy(self, src, dst, k, device):
        return REMOTE(src, dst, self.send.at[k], self.recv.at[k], device, MESH)

    def to_sibling(self, i):
        return self.copy(self.out.at[lax.rem(i, 2)], self.near.at[i], i, self.sib)

    def combine(self, i):
        self.to_sibling(i).wait_recv()

        def body(j, carry):
            r = rows_of(j, 32)
            total = self.own[i, r, :].astype(F32) + self.near[i, r, :].astype(F32)
            self.own[i, r, :] = total.astype(BF)
            return carry

        lax.fori_loop(0, self.n // 32, body, 0)

    def between(self, i):
        @pl.when(i >= 1)
        def _():
            self.combine(i - 1)

        @pl.when(i == 1)
        def _():
            self.fx.start()
            self.fy.start()

        pl.when(i == 2)(self.nx.start)
        pl.when(i == 3)(self.ny.start)

        @pl.when(i >= 2)
        def _():
            self.to_sibling(i - 2).wait_send()

    def put(self, i, cols, part):
        self.out[lax.rem(i, 2), :, cols] = part[: self.n]
        self.own[i, :, cols] = part[self.n :]

    def add(self, at, cols, slot):
        def body(j, carry):
            r = rows_of(j, 32)
            total = self.own[at, r, cols].astype(F32) + self.far[slot, r, :].astype(F32)
            self.own[at, r, cols] = total.astype(BF)
            return carry

        lax.fori_loop(0, self.n // 32, body, 0)

    def relay(self):
        self.fx.wait_recv()
        self.add(2, self.left, 1)
        self.by.start()
        self.fy.wait_recv()
        self.add(1, self.right, 3)
        self.bx.start()

    def start(self):
        for made in (self.fx, self.fy, self.nx, self.ny):
            made.start()

    def arrive(self):
        if self.near is not None:
            self.to_sibling(3).wait_recv()
        for made in (self.nx, self.ny, self.by, self.bx):
            made.wait_recv()

    def total(self, j, step):
        r = rows_of(j, step)
        total = self.own[3, r, :].astype(F32)
        if self.near is not None:
            total = total + self.near[3, r, :].astype(F32)
        a = jnp.concatenate([self.far[0, r, :], self.far[2, r, :]], axis=1).astype(F32)
        b = jnp.concatenate([self.last[0, r, :], self.last[1, r, :]], axis=1).astype(F32)
        return total + a + b

    def finish(self):
        for made in (self.fx, self.fy, self.nx, self.ny, self.by, self.bx):
            made.wait_send()
        if self.near is not None:
            for i in (2, 3):
                self.to_sibling(i).wait_send()


def wait_for(i, loads):
    for at, pair in enumerate(loads):

        @pl.when(i == at)
        def _(pair=pair):
            for made in pair:
                made.wait()


def partners():
    c, s, f = here()
    return [(c, flip(s, 1), f), (c, flip(s, 2), f), (1 - c, s, f)]


STEP = 32


def mean_square_inverse(values):
    return lax.rsqrt(jnp.mean(values * values, axis=1, keepdims=True) + epsilon)


class Line:
    def __init__(self, own, slot, send, recv, depth):
        self.own, self.slot, self.send, self.recv, self.depth = own, slot, send, recv, depth
        self.c, self.s, self.f = here()

    def copy(self, i, distance, up):
        owner = self.f - (distance - 1) if up else self.f + (distance - 1)
        to = lax.rem(self.f + (1 if up else self.depth - 1), self.depth)
        src = self.own[i] if distance == 1 else self.slot(i, owner)
        k = 0 if up else 1
        return REMOTE(
            src,
            self.slot(i, owner),
            self.send.at[k, distance - 1, i],
            self.recv.at[k, distance - 1, i],
            (self.c, self.s, to),
            MESH,
        )

    def may_send(self, distance, up):
        if up:
            return (self.f < self.depth - 1) & (self.f >= distance - 1)
        return (self.f > 0) & (self.f + distance <= self.depth)

    def gets(self, distance, up):
        return self.f >= distance if up else self.f + distance < self.depth

    def start(self):
        for i in range(len(self.own)):
            for up in (True, False):
                pl.when(self.may_send(1, up))(self.copy(i, 1, up).start)

    def pass_on(self, distance):
        for i in range(len(self.own)):
            for up in (True, False):
                pl.when(self.gets(distance, up))(self.got(i, distance, up).wait_recv)
                if distance < self.depth - 1:
                    pl.when(self.may_send(distance + 1, up))(self.copy(i, distance + 1, up).start)

    def got(self, i, distance, up):
        owner = self.f - distance if up else self.f + distance
        k = 0 if up else 1
        place = self.slot(i, owner)
        return REMOTE(
            place,
            place,
            self.send.at[k, distance - 1, i],
            self.recv.at[k, distance - 1, i],
            (self.c, self.s, lax.rem(self.f + (self.depth - 1 if up else 1), self.depth)),
            MESH,
        )

    def finish(self):
        for distance in range(1, self.depth):
            for i in range(len(self.own)):
                for up in (True, False):
                    pl.when(self.may_send(distance, up))(self.copy(i, distance, up).wait_send)


class Spread:
    def __init__(self, src, dst, origin, send, recv, depth, pieces):
        self.c, self.s, self.f = here()
        self.src, self.dst, self.origin, self.depth = src, dst, origin, depth
        self.send, self.recv, self.pieces = send, recv, pieces
        self.n = dst.shape[0] // pieces

    def part(self, ref, i):
        return ref.at[pl.ds(i * self.n, self.n)]

    def copy(self, i, up, first):
        k = 0 if up else 1
        return REMOTE(
            self.part(self.src if first else self.dst, i),
            self.part(self.dst, i),
            self.send.at[k, i],
            self.recv.at[i],
            (self.c, self.s, lax.rem(self.f + (1 if up else self.depth - 1), self.depth)),
            MESH,
        )

    def above(self):
        return (self.f > self.origin) & (self.f < self.depth - 1)

    def below(self):
        return (self.f < self.origin) & (self.f > 0)

    def start(self, local):
        first = self.f == self.origin

        @pl.when(first)
        def _():
            pltpu.make_async_copy(self.src, self.dst, local).start()

        for i in range(self.pieces):
            pl.when(first & (self.f < self.depth - 1))(self.copy(i, True, True).start)
            pl.when(first & (self.f > 0))(self.copy(i, False, True).start)

    def pass_on(self):
        for i in range(self.pieces):
            pl.when(self.f != self.origin)(self.copy(i, True, False).wait_recv)
            pl.when(self.above())(self.copy(i, True, False).start)
            pl.when(self.below())(self.copy(i, False, False).start)

    def finish(self, local):
        first = self.f == self.origin

        @pl.when(first)
        def _():
            pltpu.make_async_copy(self.src, self.dst, local).wait()

        for i in range(self.pieces):
            pl.when((first & (self.f < self.depth - 1)) | self.above())(
                self.copy(i, True, False).wait_send
            )
            pl.when((first & (self.f > 0)) | self.below())(self.copy(i, False, False).wait_send)


WEIGHT_PIECES = 4
OUT_PIECES = 2


def enter_kernel(
    tok_ref, dy_ref, gain_ref, attn_ref, forget_ref, out_w_ref,
    normed_ref, dy_all_ref, w_attn_ref, w_out_ref, cat_ref,
    mine, forget_all, normed, turned, s0, r0, s1, r1, sz, rz, so, ro, l0, *, depth,
):
    c, s, f = here()
    lines = [(c, s, lax.rem(f + 1, depth)), (c, s, lax.rem(f + depth - 1, depth))]
    greet(partners() + lines)
    n = tok_ref.shape[0]
    shard, cols = attn_ref.shape
    step = shard // WEIGHT_PIECES
    own = [attn_ref.at[pl.ds(i * step, step)] for i in range(WEIGHT_PIECES)] + [forget_ref]

    def slot(i, owner):
        if i == WEIGHT_PIECES:
            return forget_all.at[owner]
        rows = pl.ds(pl.multiple_of(owner * shard + i * step, step), step)
        return w_attn_ref.at[rows, pl.ds(0, cols)]

    line = Line(own, slot, sz, rz, depth)
    line.start()
    heads_rows = w_out_ref.shape[0]
    t = c * 4 + s
    origin = (t * heads_rows) // shard
    spread = Spread(
        out_w_ref.at[pl.ds(pl.multiple_of(t * heads_rows - origin * shard, heads_rows), heads_rows)],
        w_out_ref, origin, so, ro, depth, OUT_PIECES,
    )
    keep = [
        pltpu.make_async_copy(
            attn_ref,
            w_attn_ref.at[pl.ds(pl.multiple_of(f * shard, shard), shard), pl.ds(0, cols)],
            l0.at[2],
        ),
        pltpu.make_async_copy(forget_ref, forget_all.at[f], l0.at[3]),
    ]

    def body(i, carry):
        r = rows_of(i, STEP)
        v = tok_ref[r, :].astype(F32)
        mine[r, :] = (v * mean_square_inverse(v) * gain_ref[...]).astype(BF)
        return carry

    lax.fori_loop(0, n // STEP, body, 0)
    first = Gather(mine, normed_ref, s0, r0)
    second = Gather(dy_ref, dy_all_ref, s1, r1)
    keep += [
        pltpu.make_async_copy(mine, first.block(0), l0.at[0]),
        pltpu.make_async_copy(dy_ref, second.block(0), l0.at[1]),
    ]
    first.start()
    for made in keep:
        made.start()
    line.pass_on(1)
    spread.start(l0.at[4])
    first.relay()
    second.start()
    line.pass_on(2)
    first.finish()
    for made in keep[2:3]:
        made.wait()
    load = pltpu.make_async_copy(normed_ref, normed, l0.at[5])
    load.start()
    keep[0].wait()
    keep[1].wait()

    def add_shard(owner, begin):
        small = forget_all[owner].astype(F32)
        tall = jnp.concatenate([small, jnp.zeros((128 - small.shape[0], shard), F32)], axis=0)
        rows = rows_of(owner, shard)
        w_attn_ref[rows, cols:] = tall.T.astype(BF)
        turned[...] = w_attn_ref[rows, :].T

        def tile(i, unused):
            tokens = rows_of(i, 512)
            part = dot(turned[...], normed[tokens, rows], 1, 1)
            if begin:
                cat_ref[:, tokens] = part
            else:
                cat_ref[:, tokens] += part
            return unused

        lax.fori_loop(0, normed.shape[0] // 512, tile, 0)

    half = depth // 2
    upper = lax.div(f, half)
    load.wait()
    for k in range(1, depth - 1):
        add_shard(jnp.int32(k), k == 1)
    add_shard(upper * (depth - 1), False)
    second.relay()
    spread.pass_on()
    line.pass_on(3)
    add_shard((1 - upper) * (depth - 1), False)
    second.finish()
    line.finish()
    keep[3].wait()
    spread.finish(l0.at[4])


def enter(tokens, cotangent, gain, own_attn, own_forget, output_weight, depth, heads_rows):
    n, w = tokens.shape
    shard, cols = own_attn.shape
    whole = jax.ShapeDtypeStruct((8 * n, w), BF)
    dma = pltpu.SemaphoreType.DMA((Gather.sems,))
    line = pltpu.SemaphoreType.DMA((2, depth - 1, WEIGHT_PIECES + 1))
    vmem = pl.BlockSpec(memory_space=pltpu.VMEM)
    anywhere = pl.BlockSpec(memory_space=pl.ANY)
    return pl.pallas_call(
        functools.partial(enter_kernel, depth=depth),
        name="enter",
        out_shape=(
            whole,
            whole,
            jax.ShapeDtypeStruct((depth * shard, cols + 128), BF),
            jax.ShapeDtypeStruct((heads_rows, w), BF),
            jax.ShapeDtypeStruct((cols + 128, 8 * n), F32),
        ),
        in_specs=[vmem] * 5 + [anywhere],
        out_specs=[anywhere, anywhere, vmem, anywhere, vmem],
        scratch_shapes=[
            pltpu.VMEM((n, w), BF),
            pltpu.VMEM((depth,) + own_forget.shape, BF),
            pltpu.VMEM((8 * n, w), BF),
            pltpu.VMEM((cols + 128, shard), BF),
            dma, dma, dma, dma, line, line,
            pltpu.SemaphoreType.DMA((2, OUT_PIECES)),
            pltpu.SemaphoreType.DMA((OUT_PIECES,)),
            pltpu.SemaphoreType.DMA((6,)),
        ],
        compiler_params=pltpu.CompilerParams(
            collective_id=1, has_side_effects=True, vmem_limit_bytes=VMEM_BYTES
        ),
        cost_estimate=pl.CostEstimate(
            flops=50_000_000, bytes_accessed=4 * 8 * n * w * 2, transcendentals=0
        ),
    )(tokens, cotangent, gain[None], own_attn, own_forget, output_weight)


TILE = 256


def middle_kernel(
    gated_ref, w_ref, tok_ref, gain_ref, mid_ref, normed_ref,
    gated, turned, mine, s1, r1, l0, *refs,
):
    c, s, f = here()
    pairs = PairSum(refs)
    n, width = mine.shape
    loads = [
        pltpu.make_async_copy(
            gated_ref.at[:, pl.ds(pl.multiple_of(block * n, n), n)],
            gated.at[:, pl.ds(i * n, n)],
            l0.at[i],
        )
        for i, block in enumerate(PairSum.blocks(c, s))
    ]
    for made in loads:
        made.start()
    greet(partners())
    for made in loads:
        made.wait()

    def one_pair(i, unused):
        pairs.between(i)
        turned[...] = gated[:, rows_of(i, 2 * n)].T
        for t in range(width // TILE):
            feats = pl.ds(t * TILE, TILE)
            pairs.put(i, feats, dot(turned[...], w_ref[:, feats], 1, 0).astype(BF))
        pairs.to_sibling(i).start()
        return unused

    lax.fori_loop(0, 4, one_pair, 0)
    pairs.relay()
    pairs.arrive()

    def body(i, carry):
        r = rows_of(i, STEP)
        mid = tok_ref[r, :].astype(F32) + pairs.total(i, STEP)
        mid_ref[r, :] = mid
        mine[r, :] = (mid * mean_square_inverse(mid) * gain_ref[...]).astype(BF)
        return carry

    lax.fori_loop(0, n // STEP, body, 0)
    gather = Gather(mine, normed_ref, s1, r1)
    gather.start()
    keep = pltpu.make_async_copy(mine, gather.block(0), l0.at[8])
    keep.start()
    gather.relay()
    gather.finish()
    pairs.finish()
    keep.wait()


def middle(gated, w_out, tokens, gain):
    n, w = tokens.shape
    dma = pltpu.SemaphoreType.DMA((16,))
    vmem = pl.BlockSpec(memory_space=pltpu.VMEM)
    anywhere = pl.BlockSpec(memory_space=pl.ANY)
    return pl.pallas_call(
        middle_kernel,
        name="middle",
        out_shape=(jax.ShapeDtypeStruct((n, w), F32), jax.ShapeDtypeStruct((8 * n, w), BF)),
        in_specs=[anywhere, vmem, vmem, vmem],
        out_specs=[vmem, anywhere],
        scratch_shapes=[
            pltpu.VMEM(gated.shape, BF),
            pltpu.VMEM((2 * n, gated.shape[0]), BF),
            pltpu.VMEM((n, w), BF),
            dma, dma, dma,
        ]
        + PairSum.scratch(n, w),
        compiler_params=pltpu.CompilerParams(
            collective_id=2, has_side_effects=True, vmem_limit_bytes=VMEM_BYTES
        ),
        cost_estimate=pl.CostEstimate(
            flops=2 * 8 * n * w * gated.shape[0], bytes_accessed=4 * 8 * n * w * 2,
            transcendentals=0,
        ),
    )(gated, w_out, tokens, gain[None])


TERM_PIECES = 4


class LineSum:
    def __init__(self, term, got, send, recv, depth):
        self.term, self.got, self.send, self.recv, self.depth = term, got, send, recv, depth
        self.c, self.s, self.f = here()
        self.n = term.shape[0] // TERM_PIECES

    def source(self, i, g):
        return self.term.at[pl.ds(i * self.n, self.n), g]

    def copy(self, k, g, i, src):
        to = lax.rem(self.f + (1 if k == 0 else self.depth - 1), self.depth)
        return REMOTE(
            src,
            self.got.at[k, g, pl.ds(i * self.n, self.n)],
            self.send.at[k, g, i],
            self.recv.at[k, g, i],
            (self.c, self.s, to),
            MESH,
        )

    def targets(self, k):
        return range(self.depth - 1, 0, -1) if k == 0 else range(self.depth - 1)

    def is_end(self, k):
        return self.f == (0 if k == 0 else self.depth - 1)

    def start_piece(self, i, n):
        for k in (0, 1):
            g = self.targets(k)[n]
            pl.when(self.is_end(k))(self.copy(k, g, i, self.source(i, g)).start)

    def add(self, k, g, i):
        rows = pl.ds(i * self.n, self.n)
        total = self.got[k, g, rows].astype(F32) + self.term[rows, g].astype(F32)
        self.got[k, g, rows] = total.astype(BF)

    def pass_on(self, i, n, hop):
        for k in (0, 1):
            g = self.targets(k)[n]
            at = hop if k == 0 else self.depth - 1 - hop

            @pl.when(self.f == at)
            def _(k=k, g=g):
                made = self.copy(k, g, i, self.got.at[k, g, pl.ds(i * self.n, self.n)])
                made.wait_recv()
                self.add(k, g, i)
                made.start()

    def steps(self):
        todo = [
            (n * TERM_PIECES + i + 2 * (hop - 1), -hop, i, n, hop)
            for n in range(self.depth - 2)
            for hop in range(1, self.depth - 1 - n)
            for i in range(TERM_PIECES)
        ]
        return [step[2:] for step in sorted(todo)]

    def collect(self, i, out):
        rows = pl.ds(i * self.n, self.n)
        for g in range(self.depth):

            @pl.when(self.f == g)
            def _(g=g):
                total = self.term[rows, g].astype(F32)
                for k in (0, 1):
                    if g != (0 if k == 0 else self.depth - 1):
                        self.copy(k, g, i, self.source(i, g)).wait_recv()
                        total = total + self.got[k, g, rows].astype(F32)
                out[rows] = total.astype(BF)

    def finish(self):
        for k in (0, 1):
            for g in self.targets(k):
                beyond = self.f < g if k == 0 else self.f > g
                for i in range(TERM_PIECES):
                    pl.when(beyond)(self.copy(k, g, i, self.source(i, g)).wait_send)


class Exchange:
    def __init__(self, rows, out, send, recv):
        self.c, self.s, self.f = here()
        self.place = self.c * 4 + self.s
        self.rows, self.out, self.send, self.recv = rows, out, send, recv

    def remote(self, j):
        return REMOTE(
            self.rows.at[j], self.out.at[self.place], self.send.at[j], self.recv.at[self.place],
            (j // 4, j % 4, self.f), MESH,
        )

    def local(self, j):
        return pltpu.make_async_copy(self.rows.at[j], self.out.at[j], self.send.at[j])

    def push(self, j):
        pl.when(self.place != j)(self.remote(j).start)
        pl.when(self.place == j)(self.local(j).start)

    def start(self):
        for j in range(8):
            self.push(j)

    def finish(self):
        for j in range(8):
            got = REMOTE(
                self.rows.at[j], self.out.at[j], self.send.at[j], self.recv.at[j],
                (j // 4, j % 4, self.f), MESH,
            )
            pl.when(self.place != j)(got.wait_recv)
            pl.when(self.place != j)(self.remote(j).wait_send)
            pl.when(self.place == j)(self.local(j).wait)


def plane_peers():
    c, s, f = here()
    return [
        (core, flip(s, k) if k else s, f, k + 4 * i)
        for i, core in enumerate((c, 1 - c))
        for k in range(4)
        if i or k
    ]


def ffn_kernel(
    nm_ref, dy_all_ref, w_ref, dy_ref, mid_ref, gain_ref,
    grad_mid_ref, gain_term_ref, branch_ref, down_ref, up_rows_ref, low_term_ref,
    nm, dy, w, grads, term, got, rows_sum, mine, down_own, down_near, down_out,
    l0, l1, l2, s1, r1, s2, r2, s3, r3, s4, r4, *refs, depth,
):
    c, s, f = here()
    n, width = dy_ref.shape
    fw = w.shape[1] // 3
    pairs = PairSum(refs)
    loads = []
    w_load = pltpu.make_async_copy(w_ref, w, l2.at[8])
    w_load.start()
    for i, block in enumerate(PairSum.blocks(c, s)):
        src, dst = pl.ds(pl.multiple_of(block * n, n), n), pl.ds(i * n, n)
        made = [
            pltpu.make_async_copy(nm_ref.at[src], nm.at[dst], l0.at[i]),
            pltpu.make_async_copy(dy_all_ref.at[src], dy.at[dst], l1.at[i]),
        ]
        for one in made:
            one.start()
        if i % 2:
            loads[-1] += made
        else:
            loads.append(made)
    greet([p[:3] for p in plane_peers()] + [
        (c, s, lax.rem(f + 1, depth)), (c, s, lax.rem(f + depth - 1, depth))
    ])
    w_load.wait()

    def one_pair(i, unused):
        rows = rows_of(i, 2 * n)
        wait_for(i, loads)
        for t in range(fw // TILE):
            cols = pl.ds(t * TILE, TILE)
            ups = pl.ds(fw + t * TILE, TILE)
            downs = pl.ds(2 * fw + t * TILE, TILE)
            gate_lin = dot(nm[rows, :], w[:, cols], 1, 0)
            up_lin = dot(nm[rows, :], w[:, ups], 1, 0)
            grad_hidden = dot(dy[rows, :], w[:, downs], 1, 0)
            sig = jax.nn.sigmoid(gate_lin)
            active = gate_lin * sig
            grads[rows, downs] = (active * up_lin).astype(BF)
            grads[rows, cols] = (
                grad_hidden * up_lin * sig * (1.0 + gate_lin * (1.0 - sig))
            ).astype(BF)
            grads[rows, ups] = (grad_hidden * active).astype(BF)
        pairs.between(i)
        for t in range(width // TILE):
            feats = pl.ds(t * TILE, TILE)
            part = dot(grads[rows, 0 : 2 * fw], w[feats, 0 : 2 * fw], 1, 1).astype(BF)
            pairs.put(i, feats, part)
        pairs.to_sibling(i).start()
        return unused

    lax.fori_loop(0, 4, one_pair, 0)
    pairs.relay()

    line = LineSum(term, got, s2, r2, depth)
    deep = width // TERM_PIECES
    per = term.shape[0] // TERM_PIECES
    for i in range(TERM_PIECES):
        feats = pl.ds(i * deep, deep)
        tile = dot(nm[:, feats], grads[:, 0 : 2 * fw], 0, 0).astype(BF)
        term[i * per : (i + 1) * per] = tile.reshape((per,) + term.shape[1:])
        line.start_piece(i, 0)
    for k in range(1, depth - 1):
        for i in range(TERM_PIECES):
            line.start_piece(i, k)
    todo = line.steps()
    pairs.arrive()

    def body(j, carry):
        r = rows_of(j, STEP)
        grad = pairs.total(j, STEP)
        mid = mid_ref[r, :]
        inverse = mean_square_inverse(mid)
        weighted = grad * gain_ref[...]
        back = inverse * weighted - mid * inverse**3 * jnp.mean(
            weighted * mid, axis=1, keepdims=True
        )
        grad_mid = dy_ref[r, :].astype(F32) + back
        grad_mid_ref[r, :] = grad_mid
        mine[r, :] = grad_mid.astype(BF)
        return carry + jnp.sum(grad * mid * inverse, axis=0, keepdims=True)

    gain_term_ref[...] = lax.fori_loop(0, n // STEP, body, jnp.zeros((1, width), F32))
    gather = Gather(mine, branch_ref, s1, r1)
    gather.start()
    keep = pltpu.make_async_copy(mine, gather.block(0), l0.at[8])
    keep.start()
    for i in range(TERM_PIECES):
        feats = pl.ds(i * deep, deep)
        tile = dot(dy[:, feats], grads[:, 2 * fw :], 0, 0).astype(BF)
        tile = tile.reshape((per, depth, term.shape[2], fw))
        for g in range(depth):
            low_term_ref[g, i * per : (i + 1) * per] = tile[:, g]
        for step in todo[i * 2 : i * 2 + 2]:
            line.pass_on(*step)

    def down_copy(i):
        return REMOTE(
            down_out.at[lax.rem(i, 2)], down_near.at[i], s3.at[i], r3.at[i], pairs.sib, MESH
        )

    def down_pair(i, unused):
        rows = rows_of(i, 2 * n)

        @pl.when(i >= 2)
        def _():
            down_copy(i - 2).wait_send()

        for t in range(width // TILE):
            feats = pl.ds(t * TILE, TILE)
            part = dot(grads[rows, 2 * fw :], w[feats, 2 * fw :], 1, 1).astype(BF)
            down_out[lax.rem(i, 2), :, feats] = part[:n]
            down_own[i, :, feats] = part[n:]
        down_copy(i).start()
        return unused

    lax.fori_loop(0, 4, down_pair, 0)
    gather.relay()
    for step in todo[2 * TERM_PIECES :]:
        line.pass_on(*step)

    def down_sum(i, unused):
        down_copy(i).wait_recv()

        def body(j, carry):
            r = rows_of(j, 32)
            total = down_own[i, r, :].astype(F32) + down_near[i, r, :].astype(F32)
            down_own[i, r, :] = total.astype(BF)
            return carry

        return lax.fori_loop(0, n // 32, body, unused)

    lax.fori_loop(0, 4, down_sum, 0)
    stores = [
        pltpu.make_async_copy(
            down_own.at[i], down_ref.at[flip(s, k) if k else s], l1.at[i]
        )
        for i, k in enumerate(PairSum.order)
    ]
    for made in stores:
        made.start()
    gather.finish()
    exchange = Exchange(rows_sum, up_rows_ref, s4, r4)
    for i in range(TERM_PIECES):
        line.collect(i, rows_sum)
        for j in range(i * per, (i + 1) * per):
            exchange.push(j)
    keep.wait()
    exchange.finish()
    for made in stores:
        made.wait()
    pairs.finish()
    for i in (2, 3):
        down_copy(i).wait_send()
    line.finish()


def ffn(normed_all, cotangent_all, weights, cotangent, mid, gain, depth):
    n, width = mid.shape
    fw = weights.shape[1] // 3
    r = width // (8 * depth)
    dma = pltpu.SemaphoreType.DMA((16,))
    four = pltpu.SemaphoreType.DMA((4,))
    eight = pltpu.SemaphoreType.DMA((8,))
    line = pltpu.SemaphoreType.DMA((2, depth, TERM_PIECES))
    vmem = pl.BlockSpec(memory_space=pltpu.VMEM)
    anywhere = pl.BlockSpec(memory_space=pl.ANY)
    return pl.pallas_call(
        functools.partial(ffn_kernel, depth=depth),
        name="ffn",
        out_shape=(
            jax.ShapeDtypeStruct((n, width), F32),
            jax.ShapeDtypeStruct((1, width), F32),
            jax.ShapeDtypeStruct((8 * n, width), BF),
            jax.ShapeDtypeStruct((4, n, width), BF),
            jax.ShapeDtypeStruct((8, r, 2 * fw), BF),
            jax.ShapeDtypeStruct((depth, 8, r, fw), BF),
        ),
        in_specs=[anywhere] * 3 + [vmem] * 3,
        out_specs=[vmem, vmem, anywhere, anywhere, vmem, vmem],
        scratch_shapes=[
            pltpu.VMEM((8 * n, width), BF),
            pltpu.VMEM((8 * n, width), BF),
            pltpu.VMEM((width, 3 * fw), BF),
            pltpu.VMEM((8 * n, 3 * fw), BF),
            pltpu.VMEM((8, depth, r, 2 * fw), BF),
            pltpu.VMEM((2, depth, 8, r, 2 * fw), BF),
            pltpu.VMEM((8, r, 2 * fw), BF),
            pltpu.VMEM((n, width), BF),
            pltpu.VMEM((4, n, width), BF),
            pltpu.VMEM((4, n, width), BF),
            pltpu.VMEM((2, n, width), BF),
            dma, dma, dma, dma, dma, line, line, four, four, eight, eight,
        ]
        + PairSum.scratch(n, width),
        compiler_params=pltpu.CompilerParams(
            collective_id=3, has_side_effects=True, vmem_limit_bytes=63 * 1024 * 1024
        ),
        cost_estimate=pl.CostEstimate(
            flops=2 * 8 * n * width * fw * 9, bytes_accessed=4 * 8 * n * width * 2,
            transcendentals=0,
        ),
    )(normed_all, cotangent_all, weights, cotangent, mid, gain[None])


def leave_kernel(
    normed_ref, cat_ref, w_ref, down_ref, tok_ref, grad_mid_ref, mid_ref, gain_ref, small_ref,
    low_ref,
    grad_ref, small_sum_ref, out_ref, attn_rows_ref, low_rows_ref,
    normed, cat, turned, w, small, plane_small, line_small, term, got, rows,
    l0, l1, s2, r2, s3, r3, s5, r5, s6, r6, *refs, depth,
):
    c, s, f = here()
    n, width = tok_ref.shape
    pairs = PairSum(refs[:7])
    down = PairSum(refs[7:])
    down_loads = [
        pltpu.make_async_copy(down_ref.at[flip(s, k) if k else s], down.own.at[i], l0.at[9 + i])
        for i, k in enumerate(PairSum.order)
    ]
    loads = []
    for i, block in enumerate(PairSum.blocks(c, s)):
        src, dst = pl.ds(pl.multiple_of(block * n, n), n), pl.ds(i * n, n)
        loads.append(pltpu.make_async_copy(cat_ref.at[:, src], cat.at[:, dst], l0.at[i]))
        loads.append(pltpu.make_async_copy(normed_ref.at[src], normed.at[dst], l1.at[i]))
    w_load = pltpu.make_async_copy(w_ref, w, l0.at[8])
    for made in down_loads + loads:
        made.start()
    w_load.start()
    peers = plane_peers()
    line_peers = [(c, s, lax.rem(f + k, depth), k) for k in range(1, depth)]
    greet([p[:3] for p in peers + line_peers])
    line = LineSum(term, got, s3, r3, depth)
    low_rows = Exchange(low_ref, low_rows_ref, s6, r6)
    deep = width // TERM_PIECES
    per = term.shape[0] // TERM_PIECES
    for made in down_loads:
        made.wait()
    down.start()
    low_rows.start()
    for made in loads:
        made.wait()
    for i in range(TERM_PIECES):
        tile = dot(cat[...], normed[:, pl.ds(i * deep, deep)], 1, 0).T.astype(BF)
        term[i * per : (i + 1) * per] = tile.reshape((per,) + term.shape[1:])
        line.start_piece(i, 0)
    for k in range(1, depth - 1):
        for i in range(TERM_PIECES):
            line.start_piece(i, k)
    w_load.wait()

    def one_pair(i, unused):
        pairs.between(i)
        turned[...] = cat[:, rows_of(i, 2 * n)].T
        for t in range(width // TILE):
            feats = pl.ds(t * TILE, TILE)
            pairs.put(i, feats, dot(turned[...], w[feats, :], 1, 1).astype(BF))
        pairs.to_sibling(i).start()
        for at in range(4):

            @pl.when(i == at)
            def _(at=at):
                for step in todo[at : at + 1]:
                    line.pass_on(*step)

        return unused

    todo = line.steps()
    lax.fori_loop(0, 4, one_pair, 0)
    for step in todo[4:6]:
        line.pass_on(*step)
    pairs.relay()
    down.relay()
    for step in todo[6:]:
        line.pass_on(*step)
    attn_rows = Exchange(rows, attn_rows_ref, s5, r5)

    def collect(i):
        line.collect(i, rows)
        for j in range(i * per, (i + 1) * per):
            attn_rows.push(j)

    pairs.arrive()

    def body(i, carry):
        r = rows_of(i, STEP)
        grad = pairs.total(i, STEP)
        tok = tok_ref[r, :].astype(F32)
        inverse = mean_square_inverse(tok)
        weighted = grad * gain_ref[...]
        back = inverse * weighted - tok * inverse**3 * jnp.mean(
            weighted * tok, axis=1, keepdims=True
        )
        grad_ref[r, :] = grad_mid_ref[r, :] + back
        return carry + jnp.sum(grad * tok * inverse, axis=0, keepdims=True)

    gain_term = lax.fori_loop(0, n // STEP, body, jnp.zeros((1, width), F32))
    lane = small.shape[1]
    small[...] = small_ref[...]
    for k in range(width // lane):
        small[k : k + 1, :] = gain_term[:, k * lane : (k + 1) * lane]
    place = c * 4 + s
    plane_small[pl.ds(place, 1)] = small[...][None]
    sent = []
    for core, other_s, other_f, k in peers:
        made = REMOTE(
            small, plane_small.at[place], s2.at[k - 1], r2.at[k - 1], (core, other_s, other_f), MESH
        )
        made.start()
        sent.append(made)
    collect(0)
    collect(1)
    for made in sent:
        made.wait()
    total = plane_small[0]
    for i in range(1, 8):
        total = total + plane_small[i]
    small[...] = total
    line_small[pl.ds(f, 1)] = total[None]
    sent = []
    for core, other_s, other_f, k in line_peers:
        made = REMOTE(
            small, line_small.at[f], s2.at[6 + k], r2.at[6 + k], (core, other_s, other_f), MESH
        )
        made.start()
        sent.append(made)
    collect(2)
    collect(3)
    down.arrive()

    def body2(i, carry):
        r = rows_of(i, STEP)
        out_ref[r, :] = (mid_ref[r, :] + down.total(i, STEP)).astype(BF)
        return carry

    lax.fori_loop(0, n // STEP, body2, 0)
    for made in sent:
        made.wait()
    total = line_small[0]
    for i in range(1, depth):
        total = total + line_small[i]
    small_sum_ref[...] = total
    pairs.finish()
    down.finish()
    line.finish()
    low_rows.finish()
    attn_rows.finish()


def leave(normed, cat, w_attn, down_sum, tokens, grad_mid, mid, gain, small, low_rows, depth):
    n, w = grad_mid.shape
    plane = 8
    cols = w_attn.shape[1]
    r = w // (plane * depth)
    sems = pltpu.SemaphoreType.DMA((6 + depth,))
    dma = pltpu.SemaphoreType.DMA((16,))
    eight = pltpu.SemaphoreType.DMA((8,))
    line = pltpu.SemaphoreType.DMA((2, depth, TERM_PIECES))
    vmem = pl.BlockSpec(memory_space=pltpu.VMEM)
    anywhere = pl.BlockSpec(memory_space=pl.ANY)
    return pl.pallas_call(
        functools.partial(leave_kernel, depth=depth),
        name="leave",
        out_shape=(
            jax.ShapeDtypeStruct((n, w), F32),
            jax.ShapeDtypeStruct(small.shape, F32),
            jax.ShapeDtypeStruct((n, w), BF),
            jax.ShapeDtypeStruct((plane, r, cols), BF),
            jax.ShapeDtypeStruct(low_rows.shape, BF),
        ),
        in_specs=[anywhere] * 4 + [vmem] * 6,
        out_specs=[vmem] * 5,
        scratch_shapes=[
            pltpu.VMEM(normed.shape, BF),
            pltpu.VMEM(cat.shape, BF),
            pltpu.VMEM((2 * n, cols), BF),
            pltpu.VMEM(w_attn.shape, BF),
            pltpu.VMEM(small.shape, F32),
            pltpu.VMEM((8,) + small.shape, F32),
            pltpu.VMEM((depth,) + small.shape, F32),
            pltpu.VMEM((plane, depth, r, cols), BF),
            pltpu.VMEM((2, depth, plane, r, cols), BF),
            pltpu.VMEM((plane, r, cols), BF),
            dma, dma, sems, sems, line, line, eight, eight, eight, eight,
        ]
        + PairSum.scratch(n, w)
        + PairSum.tail_scratch(n, w),
        compiler_params=pltpu.CompilerParams(
            collective_id=4, has_side_effects=True, vmem_limit_bytes=VMEM_BYTES
        ),
        cost_estimate=pl.CostEstimate(
            flops=4 * 8 * n * w * cols, bytes_accessed=4 * 8 * n * w * 2, transcendentals=0
        ),
    )(normed, cat, w_attn, down_sum, tokens, grad_mid, mid, gain[None], small, low_rows)


def finish_kernel(
    attn_ref, up_rows_ref, low_ref, small_ref, out_w_ref, block_ref, tok_grad_ref,
    q_ref, k_ref, v_ref, g_ref, f_ref, o_ref, gate_ref, up_ref, down_ref,
    gain1_ref, gain2_ref, bias_ref, out_ref, tokens_ref, *, hw, heads,
):
    plane = attn_ref.shape[0]
    fw = low_ref.shape[2]
    for i, ref in enumerate((q_ref, k_ref, v_ref, g_ref)):
        ref[...] = jnp.concatenate(
            [attn_ref[t, :, i * hw : (i + 1) * hw].astype(F32) for t in range(plane)], axis=1
        )
    a = lax.broadcasted_iota(jnp.int32, (128, 128), 0)
    b = lax.broadcasted_iota(jnp.int32, (128, 128), 1)
    total = jnp.zeros((attn_ref.shape[1], 128), F32)
    for t in range(plane):
        pick = jnp.where((a + t * heads == b) & (a < heads), 1.0, 0.0).astype(BF)
        total = total + dot(attn_ref[t, :, 4 * hw : 4 * hw + 128], pick, 1, 0)
    f_ref[...] = total[:, : f_ref.shape[1]]
    o_ref[...] = out_w_ref[...].astype(F32)
    for t in range(plane):
        cols = slice(t * fw, (t + 1) * fw)
        gate_ref[:, cols] = up_rows_ref[t, :, 0:fw].astype(F32)
        up_ref[:, cols] = up_rows_ref[t, :, fw:].astype(F32)
        down_ref[:, cols] = low_ref[t].astype(F32)
    lane = small_ref.shape[1]
    count = gain1_ref.shape[1] // lane
    for k in range(count):
        gain1_ref[:, k * lane : (k + 1) * lane] = small_ref[k : k + 1, :]
        gain2_ref[:, k * lane : (k + 1) * lane] = small_ref[count + k : count + k + 1, :]
    bias_ref[...] = small_ref[2 * count : 2 * count + 1, 0 : bias_ref.shape[1]]
    out_ref[...] = block_ref[...]
    tokens_ref[...] = tok_grad_ref[...]


def finish(attn_rows, up_rows, low_rows, small, out_w, block_out, tokens_grad, hw, heads):
    plane, r, _ = attn_rows.shape
    n, w = tokens_grad.shape
    fw = low_rows.shape[2]
    vmem = pl.BlockSpec(memory_space=pltpu.VMEM)
    square = jax.ShapeDtypeStruct((r, plane * hw), F32)
    wide = jax.ShapeDtypeStruct((r, plane * fw), F32)
    row = jax.ShapeDtypeStruct((1, w), F32)
    return pl.pallas_call(
        functools.partial(finish_kernel, hw=hw, heads=heads),
        name="finish",
        out_shape=(
            square, square, square, square,
            jax.ShapeDtypeStruct((r, plane * heads), F32),
            jax.ShapeDtypeStruct(out_w.shape, F32),
            wide, wide, wide, row, row,
            jax.ShapeDtypeStruct((1, plane * heads), F32),
            jax.ShapeDtypeStruct((n, w), BF),
            jax.ShapeDtypeStruct((n, w), F32),
        ),
        in_specs=[vmem] * 7,
        out_specs=[vmem] * 14,
        compiler_params=pltpu.CompilerParams(vmem_limit_bytes=VMEM_BYTES),
    )(attn_rows, up_rows, low_rows, small, out_w, block_out, tokens_grad)


BQ = 256
BK = 256
AUG = 128


def dot(a, b, ca, cb):
    return lax.dot_general(a, b, (((ca,), (cb,)), ((), ())), preferred_element_type=F32)


def three_parts(v):
    hi = v.astype(BF).astype(F32)
    mid = (v - hi).astype(BF).astype(F32)
    low = (v - hi - mid).astype(BF).astype(F32)
    return hi, mid, low


def triangle(n, suffix):
    a = lax.broadcasted_iota(jnp.int32, (n, n), 0)
    b = lax.broadcasted_iota(jnp.int32, (n, n), 1)
    return jnp.where(a >= b if suffix else a <= b, 1.0, 0.0).astype(BF)


def log_sigmoid(v):
    return jnp.minimum(v, 0.0) - jnp.log1p(jnp.exp(-jnp.abs(v)))


def doc_starts(ends_ref, pos):
    start = jnp.zeros_like(pos)
    for n in range(ends_ref.shape[0]):
        end = ends_ref[n]
        start = jnp.where(pos >= end, jnp.maximum(start, end), start)
    return start


def first_block(ends_ref, pos):
    start = jnp.int32(0)
    for n in range(ends_ref.shape[0]):
        end = ends_ref[n]
        start = jnp.where(pos >= end, jnp.maximum(start, end), start)
    return start // BK


def extend(prefix_row, sign_first):
    hi, mid, low = three_parts(prefix_row)
    r = lax.broadcasted_iota(jnp.int32, (16, prefix_row.shape[1]), 0)
    base = 0 if sign_first else 3
    sign = 1.0 if sign_first else -1.0
    ones = (r >= 3) & (r < 6) if sign_first else r < 3
    out = jnp.where(ones, 1.0, 0.0)
    out = jnp.where(r == base, sign * hi, out)
    out = jnp.where(r == base + 1, sign * mid, out)
    return jnp.where(r == base + 2, sign * low, out)


def lay_out(place_ref, cat_ref, prefix_ref, heads, hd, slab, qa, ka, kta):
    hw = heads * hd
    slabs = cat_ref.shape[1] // slab
    for p in range(slabs):
        src = pl.ds(pl.multiple_of(place_ref[p] * slab, slab), slab)
        dst = pl.ds(p * slab, slab)
        for h in range(heads):
            q = cat_ref[h * hd : (h + 1) * hd, src].astype(BF).astype(F32)
            row = prefix_ref[h : h + 1, dst]
            rest = jnp.zeros((AUG - hd - 16, slab), F32)
            qe = jnp.concatenate([q * hd**-0.5, extend(row, True), rest], axis=0)
            qa[h, :, dst] = qe.astype(BF)
            k = cat_ref[hw + h * hd : hw + (h + 1) * hd, src].astype(BF).astype(F32)
            ke = jnp.concatenate([k, extend(row, False), rest], axis=0)
            if kta is not None:
                kta[h, :, dst] = ke.astype(BF)
            ka[h, dst, :] = ke.T.astype(BF)


def attention_kernel(
    place_ref, ends_ref, cat_ref, bias_ref,
    gated_ref, att_ref, exact_ref, lse_ref, prefix_ref,
    qa, ka, va, *, heads, hd, slab,
):
    hw = heads * hd
    tokens = cat_ref.shape[1]
    slabs = tokens // slab
    tri = triangle(slab, False)
    carry = jnp.zeros((16, 1), F32)
    for p in range(slabs):
        src = pl.ds(pl.multiple_of(place_ref[p] * slab, slab), slab)
        pre = cat_ref[4 * hw : 4 * hw + 16, src] + bias_ref[:, 0:1]
        steps = log_sigmoid(pre).astype(BF)
        part = dot(steps, tri, 1, 0) + carry
        prefix_ref[:, p * slab : (p + 1) * slab] = part
        carry = part[:, slab - 1 : slab]
        for h in range(heads):
            va[h, :, p * slab : (p + 1) * slab] = cat_ref[
                2 * hw + h * hd : 2 * hw + (h + 1) * hd, src
            ].astype(BF)
    lay_out(place_ref, cat_ref, prefix_ref, heads, hd, slab, qa, ka, None)
    per = slab // BQ

    def one_query_block(qb, unused):
        q0 = pl.multiple_of(qb * BQ, BQ)
        pos = q0 + lax.broadcasted_iota(jnp.int32, (1, BQ), 1)
        start = doc_starts(ends_ref, pos)
        low = first_block(ends_ref, q0)
        inside = lax.broadcasted_iota(jnp.int32, (BK, BQ), 0)

        def one_key_block(kb, held):
            k0 = pl.multiple_of(kb * BK, BK)
            allowed = (inside <= pos - k0) & (inside >= start - k0)
            out = []
            for h in range(heads):
                m, l, acc = held[h]
                st = dot(ka[h, pl.ds(k0, BK), :], qa[h, :, pl.ds(q0, BQ)], 1, 0)
                st = jnp.where(allowed, st, very_low)
                new = jnp.maximum(m, jnp.max(st, axis=0, keepdims=True))
                p = jnp.exp(st - new)
                scale = jnp.exp(m - new)
                l = l * scale + jnp.sum(p, axis=0, keepdims=True)
                acc = acc * scale + dot(va[h, :, pl.ds(k0, BK)], p.astype(BF), 1, 0)
                out.append((new, l, acc))
            return tuple(out)

        begin = tuple(
            (jnp.full((1, BQ), very_low, F32), jnp.zeros((1, BQ), F32), jnp.zeros((hd, BQ), F32))
            for _ in range(heads)
        )
        done = lax.fori_loop(low, qb + 1, one_key_block, begin)
        dst = pl.ds(pl.multiple_of(place_ref[qb // per] * slab + lax.rem(qb, per) * BQ, BQ), BQ)
        for h in range(heads):
            m, l, acc = done[h]
            lse_ref[h : h + 1, pl.ds(q0, BQ)] = m + jnp.log(l)
            exact = acc / l
            rounded = exact.astype(BF)
            exact_ref[h * hd : (h + 1) * hd, dst] = exact
            att_ref[h * hd : (h + 1) * hd, dst] = rounded
            gate = jax.nn.sigmoid(cat_ref[3 * hw + h * hd : 3 * hw + (h + 1) * hd, dst])
            gated_ref[h * hd : (h + 1) * hd, dst] = (rounded.astype(F32) * gate).astype(BF)
        return unused

    lse_ref[...] = jnp.zeros_like(lse_ref)
    lax.fori_loop(0, tokens // BQ, one_query_block, 0)


def attention(place, ends, cat, bias, heads, hd, slab):
    tokens = cat.shape[1]
    hw = heads * hd
    vmem = pl.BlockSpec(memory_space=pltpu.VMEM)
    smem = pl.BlockSpec(memory_space=pltpu.SMEM)
    return pl.pallas_call(
        functools.partial(attention_kernel, heads=heads, hd=hd, slab=slab),
        name="attention",
        out_shape=(
            jax.ShapeDtypeStruct((hw, tokens), BF),
            jax.ShapeDtypeStruct((hw, tokens), BF),
            jax.ShapeDtypeStruct((hw, tokens), F32),
            jax.ShapeDtypeStruct((8, tokens), F32),
            jax.ShapeDtypeStruct((16, tokens), F32),
        ),
        in_specs=[smem, smem, vmem, vmem],
        out_specs=[vmem] * 5,
        scratch_shapes=[
            pltpu.VMEM((heads, AUG, tokens), BF),
            pltpu.VMEM((heads, tokens, AUG), BF),
            pltpu.VMEM((heads, hd, tokens), BF),
        ],
        compiler_params=pltpu.CompilerParams(vmem_limit_bytes=VMEM_BYTES),
        cost_estimate=pl.CostEstimate(
            flops=8 * heads * tokens * tokens * hd, bytes_accessed=cat.size * 4,
            transcendentals=heads * tokens * tokens // 2,
        ),
    )(place, ends, cat, bias)


def attention_back_kernel(
    place_ref, ends_ref, cat_ref, bias_ref, gg_ref, att_ref, exact_ref, lse_ref, prefix_ref,
    out_ref, bias_grad_ref,
    qa, ka, kta, va, do, delta_ref, dk, dv, gp, *, heads, hd, slab,
):
    hw = heads * hd
    tokens = cat_ref.shape[1]
    slabs = tokens // slab
    per = slab // BQ
    lay_out(place_ref, cat_ref, prefix_ref, heads, hd, slab, qa, ka, kta)
    delta_ref[...] = jnp.zeros_like(delta_ref)
    gp[...] = jnp.zeros_like(gp)
    dk[...] = jnp.zeros_like(dk)
    dv[...] = jnp.zeros_like(dv)
    out_ref[4 * hw :, :] = jnp.zeros((out_ref.shape[0] - 4 * hw, tokens), BF)
    for p in range(slabs):
        src = pl.ds(pl.multiple_of(place_ref[p] * slab, slab), slab)
        dst = pl.ds(p * slab, slab)
        for h in range(heads):
            rows = slice(h * hd, (h + 1) * hd)
            gate = jax.nn.sigmoid(cat_ref[3 * hw + h * hd : 3 * hw + (h + 1) * hd, src])
            gg = gg_ref[rows, src]
            low = (gg * gate).astype(BF)
            do[h, :, dst] = low
            delta_ref[h : h + 1, dst] = jnp.sum(
                low.astype(F32) * exact_ref[rows, src], axis=0, keepdims=True
            )
            gate_grad = gg * att_ref[rows, src].astype(F32) * gate * (1.0 - gate)
            out_ref[3 * hw + h * hd : 3 * hw + (h + 1) * hd, src] = gate_grad.astype(BF)
            v = cat_ref[2 * hw + h * hd : 2 * hw + (h + 1) * hd, src]
            va[h, dst, :] = v.T.astype(BF)

    def one_query_block(qb, unused):
        q0 = pl.multiple_of(qb * BQ, BQ)
        pos = q0 + lax.broadcasted_iota(jnp.int32, (1, BQ), 1)
        start = doc_starts(ends_ref, pos)
        low = first_block(ends_ref, q0)
        inside = lax.broadcasted_iota(jnp.int32, (BK, BQ), 0)

        def one_key_block(kb, held):
            k0 = pl.multiple_of(kb * BK, BK)
            keys = pl.ds(k0, BK)
            allowed = (inside <= pos - k0) & (inside >= start - k0)
            out = []
            for h in range(heads):
                queries = qa[h, :, pl.ds(q0, BQ)]
                grads = do[h, :, pl.ds(q0, BQ)]
                st = dot(ka[h, keys, :], queries, 1, 0) - lse_ref[h : h + 1, pl.ds(q0, BQ)]
                p = jnp.exp(jnp.where(allowed, st, very_low))
                dp = dot(va[h, keys, :], grads, 1, 0) - delta_ref[h : h + 1, pl.ds(q0, BQ)]
                ds = (p * dp).astype(BF)
                out.append(held[h] + dot(kta[h, :, keys], ds, 1, 0))
                dk[h, :, keys] += dot(queries, ds, 1, 1)
                dv[h, :, keys] += dot(grads, p.astype(BF), 1, 1)
            return tuple(out)

        begin = tuple(jnp.zeros((AUG, BQ), F32) for _ in range(heads))
        done = lax.fori_loop(low, qb + 1, one_key_block, begin)
        dst = pl.ds(pl.multiple_of(place_ref[qb // per] * slab + lax.rem(qb, per) * BQ, BQ), BQ)
        for h in range(heads):
            out_ref[h * hd : (h + 1) * hd, dst] = (done[h][0:hd, :] * hd**-0.5).astype(BF)
            gp[h : h + 1, pl.ds(q0, BQ)] = done[h][hd : hd + 1, :]
        return unused

    lax.fori_loop(0, tokens // BQ, one_query_block, 0)
    tri = triangle(slab, True)
    carry = jnp.zeros((16, 1), F32)
    bias_grad = jnp.zeros((16, 1), F32)
    for p in reversed(range(slabs)):
        src = pl.ds(pl.multiple_of(place_ref[p] * slab, slab), slab)
        dst = pl.ds(p * slab, slab)
        for h in range(heads):
            out_ref[hw + h * hd : hw + (h + 1) * hd, src] = dk[h, 0:hd, dst].astype(BF)
            out_ref[2 * hw + h * hd : 2 * hw + (h + 1) * hd, src] = dv[h, :, dst].astype(BF)
            gp[h : h + 1, dst] = gp[h : h + 1, dst] - dk[h, hd + 3 : hd + 4, dst]
        grad = gp[:, dst]
        total = carry
        for piece in three_parts(grad):
            total = total + dot(piece.astype(BF), tri, 1, 0)
        carry = total[:, 0:1]
        pre = cat_ref[4 * hw : 4 * hw + 16, src] + bias_ref[:, 0:1]
        low = (total.astype(BF).astype(F32) * jax.nn.sigmoid(-pre)).astype(BF)
        out_ref[4 * hw : 4 * hw + 16, src] = low
        bias_grad = bias_grad + jnp.sum(low.astype(F32), axis=1, keepdims=True)
    bias_grad_ref[...] = jnp.broadcast_to(bias_grad, bias_grad_ref.shape)


def attention_back(place, ends, cat, bias, gg, att, exact, lse, prefix, heads, hd, slab):
    tokens = cat.shape[1]
    vmem = pl.BlockSpec(memory_space=pltpu.VMEM)
    smem = pl.BlockSpec(memory_space=pltpu.SMEM)
    return pl.pallas_call(
        functools.partial(attention_back_kernel, heads=heads, hd=hd, slab=slab),
        name="attention_back",
        out_shape=(
            jax.ShapeDtypeStruct(cat.shape, BF),
            jax.ShapeDtypeStruct((16, 128), F32),
        ),
        in_specs=[smem, smem] + [vmem] * 7,
        out_specs=[vmem] * 2,
        scratch_shapes=[
            pltpu.VMEM((heads, AUG, tokens), BF),
            pltpu.VMEM((heads, tokens, AUG), BF),
            pltpu.VMEM((heads, AUG, tokens), BF),
            pltpu.VMEM((heads, tokens, hd), BF),
            pltpu.VMEM((heads, hd, tokens), BF),
            pltpu.VMEM((8, tokens), F32),
            pltpu.VMEM((heads, AUG, tokens), F32),
            pltpu.VMEM((heads, hd, tokens), F32),
            pltpu.VMEM((16, tokens), F32),
        ],
        compiler_params=pltpu.CompilerParams(vmem_limit_bytes=VMEM_BYTES),
        cost_estimate=pl.CostEstimate(
            flops=20 * heads * tokens * tokens * hd, bytes_accessed=cat.size * 8,
            transcendentals=heads * tokens * tokens // 2,
        ),
    )(place, ends, cat, bias, gg, att, exact, lse, prefix)


def local_plane(
    tokens, out_cotangent, seq_lengths, slab_place, attn_gain, query_weight, key_weight,
    value_weight, outgate_weight, forget_weight, forget_bias, output_weight, mlp_gain,
    gate_weight, up_weight, down_weight,
):
    plane_axes = ("cp", "sp")
    plane = lax.axis_size("cp") * lax.axis_size("sp")
    depth = lax.axis_size("fsdp")
    place = lax.axis_index("cp") * lax.axis_size("sp") + lax.axis_index("sp")
    head_count = forget_weight.shape[1]
    width = tokens.shape[2]
    hd = width // head_count
    heads = head_count // plane
    hw = heads * hd
    fw = gate_weight.shape[1] // plane
    shard = query_weight.shape[0]
    group_rows = tokens.shape[1] * plane
    slab = group_rows // slab_place.shape[1]

    def columns(weight, count):
        return lax.dynamic_slice_in_dim(weight, place * count, count, 1)

    inputs, cotangent = tokens[0], out_cotangent[0]
    slabs = slab_place.shape[1]
    order = jnp.arange(slabs, dtype=jnp.int32)
    storage = jnp.sum(
        jnp.where(slab_place[0][None, :] == order[:, None], order[None, :], 0), axis=1
    )
    ends = jnp.cumsum(seq_lengths[0])

    own_attn = jnp.concatenate(
        [columns(w, hw) for w in (query_weight, key_weight, value_weight, outgate_weight)], axis=1
    )
    own_forget = jnp.pad(columns(forget_weight, heads).T, ((0, 16 - heads), (0, 0)))
    own_mlp = jnp.concatenate(
        [columns(gate_weight, fw), columns(up_weight, fw), columns(down_weight, fw)], axis=1
    )
    normed, cotangent_all, w_attn, w_out, cat = enter(
        inputs, cotangent, attn_gain, own_attn, own_forget, output_weight, depth, hw
    )
    own_mlp, w_attn = lax.optimization_barrier((own_mlp, w_attn))
    w_mlp = lax.all_gather(own_mlp, "fsdp", axis=0, tiled=True)
    bias_own = lax.dynamic_slice_in_dim(forget_bias, place * heads, heads, 0)
    bias = jnp.broadcast_to(jnp.pad(bias_own, (0, 16 - heads))[:, None], (16, 128))
    gated, att, exact, lse, prefix = attention(storage, ends, cat, bias, heads, hd, slab)
    mid, normed_mlp = middle(gated, w_out, inputs, mlp_gain)

    grad_mid, mlp_gain_term, branch, down_sum, up_rows, low_term = ffn(
        normed_mlp, cotangent_all, w_mlp, cotangent, mid, mlp_gain, depth
    )
    low_grad = lax.psum_scatter(
        low_term.reshape(width, fw), "fsdp", scatter_dimension=0, tiled=True
    )

    grad_gated, out_term = lax.optimization_barrier(
        (dot(w_out, branch, 1, 1), dot(gated, branch, 1, 0).astype(BF))
    )
    grad_cat, bias_grad = attention_back(
        storage, ends, cat, bias, grad_gated, att, exact, lse, prefix, heads, hd, slab
    )
    output_weight_grad = lax.psum_scatter(out_term, "fsdp", scatter_dimension=0, tiled=True)
    lane = width // 3
    bias_row = lax.dynamic_update_slice_in_dim(
        jnp.zeros((lane,), F32), bias_grad[:heads, 0], place * heads, 0
    )
    small = jnp.concatenate(
        [jnp.zeros((3, lane), F32), mlp_gain_term.reshape(3, lane), bias_row[None]]
        + [jnp.zeros((1, lane), F32)]
    )
    part = width // (plane * depth)
    tokens_grad, small_sum, block_out, attn_rows, low_rows = leave(
        normed, grad_cat, w_attn, down_sum, inputs, grad_mid, mid, attn_gain, small,
        low_grad.reshape(plane, part, fw), depth,
    )
    (
        query_grad, key_grad, value_grad, outgate_grad, forget_grad, out_grad, gate_grad, up_grad,
        down_grad, attn_gain_grad, mlp_gain_grad, forget_bias_grad, block_out, tokens_grad,
    ) = finish(
        attn_rows, up_rows, low_rows, small_sum, output_weight_grad, block_out, tokens_grad,
        hw, heads,
    )
    return (
        block_out[None],
        tokens_grad[None],
        attn_gain_grad[0],
        query_grad,
        key_grad,
        value_grad,
        outgate_grad,
        forget_grad,
        forget_bias_grad[0],
        out_grad,
        mlp_gain_grad[0],
        gate_grad,
        up_grad,
        down_grad,
    )


def fits_plane(mesh, tokens, slab_place, forget_weight, gate_weight):
    sizes = dict(mesh.shape)
    if (sizes["cp"], sizes["sp"]) != (2, 4):
        return False
    plane = sizes["cp"] * sizes["sp"]
    width = tokens.shape[2]
    head_count = forget_weight.shape[1]
    group_rows = tokens.shape[1]
    slab = group_rows // slab_place.shape[1]
    heads = head_count // plane
    return (
        head_count % plane == 0
        and heads <= 8
        and width // head_count == 64
        and slab % 256 == 0
        and group_rows <= 2048
        and width % 768 == 0
        and gate_weight.shape[1] % (128 * plane) == 0
        and width % (16 * plane * sizes["fsdp"]) == 0
        and (group_rows // plane) % 64 == 0
    )


def shard(mesh, fn):
    return jax.shard_map(
        fn,
        mesh=mesh,
        in_specs=(
            P("fsdp", ("cp", "sp"), None),
            P("fsdp", ("cp", "sp"), None),
            P("fsdp", None),
            P("fsdp", None),
            P(),
            P("fsdp", None),
            P("fsdp", None),
            P("fsdp", None),
            P("fsdp", None),
            P("fsdp", None),
            P(),
            P("fsdp", None),
            P(),
            P("fsdp", None),
            P("fsdp", None),
            P("fsdp", None),
        ),
        out_specs=(
            P("fsdp", ("cp", "sp"), None),
            P("fsdp", ("cp", "sp"), None),
            P(),
            P(("cp", "sp", "fsdp"), None),
            P(("cp", "sp", "fsdp"), None),
            P(("cp", "sp", "fsdp"), None),
            P(("cp", "sp", "fsdp"), None),
            P(("cp", "sp", "fsdp"), None),
            P(),
            P(("cp", "sp", "fsdp"), None),
            P(),
            P(("cp", "sp", "fsdp"), None),
            P(("cp", "sp", "fsdp"), None),
            P(("cp", "sp", "fsdp"), None),
        ),
        check_vma=False,
    )


def solution(mesh):
    def run(*args):
        fast = fits_plane(mesh, args[0], args[3], args[9], args[13])
        return shard(mesh, local_plane if fast else local)(*args)

    return run
```

```python
import functools

import jax
import jax.numpy as jnp
from jax import lax
from jax.experimental import pallas as pl
from jax.experimental.pallas import tpu as pltpu
from jax.sharding import PartitionSpec as P

epsilon = 1e-06
very_low = -1e30
MESH = pl.DeviceIdType.MESH
BF = jnp.bfloat16
F32 = jnp.float32
REMOTE = pltpu.make_async_remote_copy
VMEM_BYTES = 60 * 1024 * 1024


def matmul(left, right):
    return jnp.dot(left, right, preferred_element_type=jnp.float32)


def matmul_right_t(left, right):
    return lax.dot_general(
        left, right, (((1,), (1,)), ((), ())), preferred_element_type=jnp.float32
    )


def matmul_left_t(left, right):
    return lax.dot_general(
        left, right, (((0,), (0,)), ((), ())), preferred_element_type=jnp.float32
    )


def rms_inverse(values):
    return lax.rsqrt(jnp.mean(values * values, axis=1, keepdims=True) + epsilon)


def norm_back(upstream, values, inverse, gain):
    weighted = upstream * gain
    return inverse * weighted - values * inverse**3 * jnp.mean(
        weighted * values, axis=1, keepdims=True
    )


def row_layout(place_row, lens_row, count, slab_rows):
    rows = jnp.arange(count, dtype=jnp.int32)
    slab_index = rows // slab_rows
    table = (
        slab_index[:, None] == jnp.arange(place_row.shape[0], dtype=jnp.int32)[None, :]
    ).astype(jnp.int32)
    position = jnp.sum(table * place_row[None, :], axis=1) * slab_rows + rows % slab_rows
    ends = jnp.cumsum(lens_row)
    segment = jnp.sum((position[:, None] >= ends[None, :]).astype(jnp.int32), axis=1)
    return (position, segment)


def forget_prefix(log_all, place_row, slab_rows):
    slabs = place_row.shape[0]
    steps = log_all.astype(jnp.float32).reshape(slabs, slab_rows, -1)
    inside = jnp.cumsum(steps, axis=1)
    totals = inside[:, -1, :]
    earlier = (place_row[None, :] < place_row[:, None]).astype(jnp.float32)
    offsets = jnp.dot(earlier, totals, precision=lax.Precision.HIGHEST)
    return (inside + offsets[:, None, :]).reshape(slabs * slab_rows, -1)


def prefix_back(grad_prefix, place_row, slab_rows):
    slabs = place_row.shape[0]
    steps = grad_prefix.reshape(slabs, slab_rows, -1)
    inside = jnp.flip(jnp.cumsum(jnp.flip(steps, 1), axis=1), 1)
    totals = inside[:, 0, :]
    later = (place_row[None, :] > place_row[:, None]).astype(jnp.float32)
    offsets = jnp.dot(later, totals, precision=lax.Precision.HIGHEST)
    return (inside + offsets[:, None, :]).reshape(slabs * slab_rows, -1)


def local(
    tokens,
    out_cotangent,
    seq_lengths,
    slab_place,
    attn_gain,
    query_weight,
    key_weight,
    value_weight,
    outgate_weight,
    forget_weight,
    forget_bias,
    output_weight,
    mlp_gain,
    gate_weight,
    up_weight,
    down_weight,
):
    seq_devices = lax.axis_size("sp")
    ctx_devices = lax.axis_size("cp")
    ctx_index = lax.axis_index("cp")
    tok_rows = tokens.shape[1]
    model_width = tokens.shape[2]
    head_count = forget_weight.shape[1]
    local_heads = head_count // seq_devices
    head_size = model_width // head_count
    ctx_rows = tok_rows * seq_devices
    group_rows = ctx_rows * ctx_devices
    slab_rows = ctx_rows // 2
    key_block = min(512, group_rows)
    key_blocks = group_rows // key_block
    score_scale = head_size ** (-0.5)
    place_row = slab_place[0]
    lens_row = seq_lengths[0]
    ctx_start = ctx_index * ctx_rows
    inputs = tokens[0]
    input_f = inputs.astype(jnp.float32)
    weights_attn = (
        lax.all_gather(query_weight, "fsdp", axis=0, tiled=True),
        lax.all_gather(key_weight, "fsdp", axis=0, tiled=True),
        lax.all_gather(value_weight, "fsdp", axis=0, tiled=True),
        lax.all_gather(outgate_weight, "fsdp", axis=0, tiled=True),
        lax.all_gather(forget_weight, "fsdp", axis=0, tiled=True),
        lax.all_gather(output_weight, "fsdp", axis=0, tiled=True),
    )
    full_query, full_key, full_value, full_outgate, full_forget, full_output = weights_attn
    inv_first = rms_inverse(input_f)
    normed = (input_f * inv_first * attn_gain).astype(jnp.bfloat16)
    queries = matmul(normed, full_query).astype(jnp.bfloat16)
    keys = matmul(normed, full_key).astype(jnp.bfloat16)
    values = matmul(normed, full_value).astype(jnp.bfloat16)
    out_gate = jax.nn.sigmoid(matmul(normed, full_outgate))
    forget_pre = matmul(normed, full_forget) + forget_bias
    log_forget = jax.nn.log_sigmoid(forget_pre).astype(jnp.bfloat16)
    head_query, head_key, head_value, head_forget = (
        lax.all_to_all(queries, "sp", split_axis=1, concat_axis=0, tiled=True),
        lax.all_to_all(keys, "sp", split_axis=1, concat_axis=0, tiled=True),
        lax.all_to_all(values, "sp", split_axis=1, concat_axis=0, tiled=True),
        lax.all_to_all(log_forget, "sp", split_axis=1, concat_axis=0, tiled=True),
    )
    keys_all, values_all, forget_all = (
        lax.all_gather(head_key, "cp", axis=0, tiled=True),
        lax.all_gather(head_value, "cp", axis=0, tiled=True),
        lax.all_gather(head_forget, "cp", axis=0, tiled=True),
    )
    prefix_all = forget_prefix(forget_all, place_row, slab_rows)
    pos_all, seg_all = row_layout(place_row, lens_row, group_rows, slab_rows)
    query_pos = lax.dynamic_slice_in_dim(pos_all, ctx_start, ctx_rows, 0)
    query_seg = lax.dynamic_slice_in_dim(seg_all, ctx_start, ctx_rows, 0)
    query_prefix = lax.dynamic_slice_in_dim(prefix_all, ctx_start, ctx_rows, 0)
    query_three = head_query.reshape(ctx_rows, local_heads, head_size)
    query_pos_top = jnp.max(query_pos)
    query_seg_low = jnp.min(query_seg)
    query_seg_top = jnp.max(query_seg)
    key_pieces = (
        keys_all.reshape(key_blocks, key_block, local_heads, head_size),
        values_all.reshape(key_blocks, key_block, local_heads, head_size),
        prefix_all.reshape(key_blocks, key_block, local_heads),
        pos_all.reshape(key_blocks, key_block),
        seg_all.reshape(key_blocks, key_block),
    )

    def block_live(key_pos, key_seg):
        return (
            (query_pos_top >= jnp.min(key_pos))
            & (query_seg_top >= jnp.min(key_seg))
            & (jnp.max(key_seg) >= query_seg_low)
        )

    def block_scores(key_piece, key_prefix, key_pos, key_seg):
        raw = (
            jnp.einsum("qhd,khd->hqk", query_three, key_piece, preferred_element_type=jnp.float32)
            * score_scale
        )
        raw = raw + query_prefix.T[:, :, None] - key_prefix.T[:, None, :]
        allowed = (query_pos[:, None] >= key_pos[None, :]) & (
            query_seg[:, None] == key_seg[None, :]
        )
        return (raw, allowed[None, :, :])

    def total_work(carry, piece):
        running_max, running_sum = carry
        key_piece, value_piece, key_prefix, key_pos, key_seg = piece
        raw, allowed = block_scores(key_piece, key_prefix, key_pos, key_seg)
        new_max = jnp.maximum(running_max, jnp.max(jnp.where(allowed, raw, very_low), axis=2))
        terms = jnp.where(allowed, jnp.exp(raw - new_max[:, :, None]), 0.0)
        new_sum = running_sum * jnp.exp(running_max - new_max) + jnp.sum(terms, axis=2)
        return (new_max, new_sum)

    def total_step(carry, piece):
        live = block_live(piece[3], piece[4])
        return (lax.cond(live, total_work, lambda held, unused: held, carry, piece), None)

    start_max = jnp.full((local_heads, ctx_rows), very_low, jnp.float32)
    start_sum = jnp.zeros((local_heads, ctx_rows), jnp.float32)
    (final_max, final_sum), _ = lax.scan(total_step, (start_max, start_sum), key_pieces)
    log_total = final_max + jnp.log(final_sum)

    def output_work(carry, piece):
        coarse, fine = carry
        key_piece, value_piece, key_prefix, key_pos, key_seg = piece
        raw, allowed = block_scores(key_piece, key_prefix, key_pos, key_seg)
        probs = jnp.where(allowed, jnp.exp(raw - log_total[:, :, None]), 0.0)
        rounded = probs.astype(jnp.bfloat16)
        rest = (probs - rounded.astype(jnp.float32)).astype(jnp.bfloat16)
        coarse = coarse + jnp.einsum(
            "hqk,khd->qhd", rounded, value_piece, preferred_element_type=jnp.float32
        )
        fine = fine + jnp.einsum(
            "hqk,khd->qhd", rest, value_piece, preferred_element_type=jnp.float32
        )
        return (coarse, fine)

    def output_step(carry, piece):
        live = block_live(piece[3], piece[4])
        return (lax.cond(live, output_work, lambda held, unused: held, carry, piece), None)

    zero_out = jnp.zeros((ctx_rows, local_heads, head_size), jnp.float32)
    (coarse_out, fine_out), _ = lax.scan(output_step, (zero_out, zero_out), key_pieces)
    exact_out = coarse_out + fine_out
    head_out = coarse_out.reshape(ctx_rows, local_heads * head_size).astype(jnp.bfloat16)
    token_out = lax.all_to_all(head_out, "sp", split_axis=0, concat_axis=1, tiled=True)
    token_out_f = token_out.astype(jnp.float32)
    gated = (token_out_f * out_gate).astype(jnp.bfloat16)
    mid = input_f + matmul(gated, full_output)
    weights_mlp = (
        lax.all_gather(gate_weight, "fsdp", axis=0, tiled=True),
        lax.all_gather(up_weight, "fsdp", axis=0, tiled=True),
        lax.all_gather(down_weight, "fsdp", axis=0, tiled=True),
    )
    full_gate, full_up, full_down = weights_mlp
    inv_second = rms_inverse(mid)
    normed_mlp = (mid * inv_second * mlp_gain).astype(jnp.bfloat16)
    gate_lin = matmul(normed_mlp, full_gate)
    up_lin = matmul(normed_mlp, full_up)
    gate_sig = jax.nn.sigmoid(gate_lin)
    activated = gate_lin * gate_sig
    hidden = (activated * up_lin).astype(jnp.bfloat16)
    block_out = (mid + matmul_right_t(hidden, full_down)).astype(jnp.bfloat16)
    cotangent = out_cotangent[0]
    grad_hidden = matmul(cotangent, full_down)
    grad_gate_lin = (grad_hidden * up_lin * gate_sig * (1.0 + gate_lin * (1.0 - gate_sig))).astype(
        jnp.bfloat16
    )
    grad_up_lin = (grad_hidden * activated).astype(jnp.bfloat16)
    grad_normed_mlp = matmul_right_t(grad_gate_lin, full_gate) + matmul_right_t(
        grad_up_lin, full_up
    )
    mlp_gain_term = jnp.sum(grad_normed_mlp * mid * inv_second, axis=0)
    grad_mid = cotangent.astype(jnp.float32) + norm_back(grad_normed_mlp, mid, inv_second, mlp_gain)
    gate_term = matmul_left_t(normed_mlp, grad_gate_lin)
    up_term = matmul_left_t(normed_mlp, grad_up_lin)
    down_term = matmul_left_t(cotangent, hidden)
    grad_branch = grad_mid.astype(jnp.bfloat16)
    grad_gated = matmul_right_t(grad_branch, full_output)
    grad_attended = (grad_gated * out_gate).astype(jnp.bfloat16)
    grad_gate_pre = (grad_gated * token_out_f * out_gate * (1.0 - out_gate)).astype(jnp.bfloat16)
    head_grad = lax.all_to_all(grad_attended, "sp", split_axis=1, concat_axis=0, tiled=True)
    grad_three = head_grad.reshape(ctx_rows, local_heads, head_size)
    delta = jnp.sum(grad_three.astype(jnp.float32) * exact_out, axis=2).T

    def back_work(carry, piece):
        grad_query_acc, grad_prefix_acc = carry
        key_piece, value_piece, key_prefix, key_pos, key_seg = piece
        raw, allowed = block_scores(key_piece, key_prefix, key_pos, key_seg)
        probs = jnp.where(allowed, jnp.exp(raw - log_total[:, :, None]), 0.0)
        rounded = probs.astype(jnp.bfloat16)
        grad_probs = jnp.einsum(
            "qhd,khd->hqk", grad_three, value_piece, preferred_element_type=jnp.float32
        )
        grad_scores = (probs * (grad_probs - delta[:, :, None])).astype(jnp.bfloat16)
        grad_query_acc = (
            grad_query_acc
            + jnp.einsum("hqk,khd->qhd", grad_scores, key_piece, preferred_element_type=jnp.float32)
            * score_scale
        )
        key_term = (
            jnp.einsum("hqk,qhd->khd", grad_scores, query_three, preferred_element_type=jnp.float32)
            * score_scale
        )
        value_term = jnp.einsum(
            "hqk,qhd->khd", rounded, grad_three, preferred_element_type=jnp.float32
        )
        score_f = grad_scores.astype(jnp.float32)
        grad_prefix_acc = grad_prefix_acc + jnp.sum(score_f, axis=2)
        prefix_term = -jnp.sum(score_f, axis=1)
        return ((grad_query_acc, grad_prefix_acc), (key_term, value_term, prefix_term))

    def back_skip(carry, piece):
        empty_kv = jnp.zeros((key_block, local_heads, head_size), jnp.float32)
        empty_prefix = jnp.zeros((local_heads, key_block), jnp.float32)
        return (carry, (empty_kv, empty_kv, empty_prefix))

    def back_step(carry, piece):
        live = block_live(piece[3], piece[4])
        return lax.cond(live, back_work, back_skip, carry, piece)

    start_prefix = jnp.zeros((local_heads, ctx_rows), jnp.float32)
    (grad_query_acc, grad_prefix_q), (key_terms, value_terms, prefix_terms) = lax.scan(
        back_step, (zero_out, start_prefix), key_pieces
    )
    keys_grad_all = key_terms.reshape(group_rows, local_heads * head_size)
    values_grad_all = value_terms.reshape(group_rows, local_heads * head_size)
    prefix_grad_all = jnp.transpose(prefix_terms, (0, 2, 1)).reshape(group_rows, local_heads)
    own_prefix = lax.dynamic_slice_in_dim(prefix_grad_all, ctx_start, ctx_rows, 0)
    prefix_grad_all = lax.dynamic_update_slice_in_dim(
        prefix_grad_all, own_prefix + grad_prefix_q.T, ctx_start, 0
    )
    forget_grad_term = prefix_back(prefix_grad_all, place_row, slab_rows)
    key_sum, value_sum, forget_sum = (
        lax.psum_scatter(keys_grad_all, "cp", scatter_dimension=0, tiled=True),
        lax.psum_scatter(values_grad_all, "cp", scatter_dimension=0, tiled=True),
        lax.psum_scatter(forget_grad_term, "cp", scatter_dimension=0, tiled=True),
    )
    grad_query_head = grad_query_acc.reshape(ctx_rows, local_heads * head_size).astype(jnp.bfloat16)
    grad_query_tok, grad_key_tok, grad_value_tok, grad_forget_tok = (
        lax.all_to_all(grad_query_head, "sp", split_axis=0, concat_axis=1, tiled=True),
        lax.all_to_all(key_sum.astype(jnp.bfloat16), "sp", split_axis=0, concat_axis=1, tiled=True),
        lax.all_to_all(
            value_sum.astype(jnp.bfloat16), "sp", split_axis=0, concat_axis=1, tiled=True
        ),
        lax.all_to_all(
            forget_sum.astype(jnp.bfloat16), "sp", split_axis=0, concat_axis=1, tiled=True
        ),
    )
    grad_forget_pre = (grad_forget_tok.astype(jnp.float32) * jax.nn.sigmoid(-forget_pre)).astype(
        jnp.bfloat16
    )
    grad_normed = (
        matmul_right_t(grad_query_tok, full_query)
        + matmul_right_t(grad_key_tok, full_key)
        + matmul_right_t(grad_value_tok, full_value)
        + matmul_right_t(grad_gate_pre, full_outgate)
        + matmul_right_t(grad_forget_pre, full_forget)
    )
    attn_gain_term = jnp.sum(grad_normed * input_f * inv_first, axis=0)
    bias_term = jnp.sum(grad_forget_pre.astype(jnp.float32), axis=0)
    tokens_grad = grad_mid + norm_back(grad_normed, input_f, inv_first, attn_gain)
    query_term = matmul_left_t(normed, grad_query_tok)
    key_term_w = matmul_left_t(normed, grad_key_tok)
    value_term_w = matmul_left_t(normed, grad_value_tok)
    outgate_term = matmul_left_t(normed, grad_gate_pre)
    forget_term = matmul_left_t(normed, grad_forget_pre)
    output_term = matmul_left_t(gated, grad_branch)
    (
        query_grad,
        key_grad,
        value_grad,
        outgate_grad,
        forget_grad,
        output_weight_grad,
        gate_grad,
        up_grad,
        down_grad,
    ) = (
        lax.psum_scatter(query_term, ("cp", "sp", "fsdp"), scatter_dimension=0, tiled=True),
        lax.psum_scatter(key_term_w, ("cp", "sp", "fsdp"), scatter_dimension=0, tiled=True),
        lax.psum_scatter(value_term_w, ("cp", "sp", "fsdp"), scatter_dimension=0, tiled=True),
        lax.psum_scatter(outgate_term, ("cp", "sp", "fsdp"), scatter_dimension=0, tiled=True),
        lax.psum_scatter(forget_term, ("cp", "sp", "fsdp"), scatter_dimension=0, tiled=True),
        lax.psum_scatter(output_term, ("cp", "sp", "fsdp"), scatter_dimension=0, tiled=True),
        lax.psum_scatter(gate_term, ("cp", "sp", "fsdp"), scatter_dimension=0, tiled=True),
        lax.psum_scatter(up_term, ("cp", "sp", "fsdp"), scatter_dimension=0, tiled=True),
        lax.psum_scatter(down_term, ("cp", "sp", "fsdp"), scatter_dimension=0, tiled=True),
    )
    attn_gain_grad, mlp_gain_grad, forget_bias_grad = lax.psum(
        (attn_gain_term, mlp_gain_term, bias_term), ("cp", "sp", "fsdp")
    )
    return (
        block_out[None],
        tokens_grad[None],
        attn_gain_grad,
        query_grad,
        key_grad,
        value_grad,
        outgate_grad,
        forget_grad,
        forget_bias_grad,
        output_weight_grad,
        mlp_gain_grad,
        gate_grad,
        up_grad,
        down_grad,
    )


def here():
    return (lax.axis_index("cp"), lax.axis_index("sp"), lax.axis_index("fsdp"))


def flip(s, k):
    if k == 1:
        return s + 1 - 2 * lax.rem(s, 2)
    if k == 2:
        return lax.rem(s + 2, 4)
    return 3 - s


def greet(devices):
    sem = pltpu.get_barrier_semaphore()
    for device in devices:
        pl.semaphore_signal(sem, inc=1, device_id=device, device_id_type=MESH)
    pl.semaphore_wait(sem, len(devices))


def signal_line(devices, depth):
    c, s, f = here()
    sem = pltpu.get_barrier_semaphore()
    for device in devices:
        pl.semaphore_signal(sem, inc=1, device_id=device, device_id_type=MESH)

    @pl.when(f < depth - 1)
    def _():
        up = (c, s, lax.rem(f + 1, depth))
        pl.semaphore_signal(sem, inc=1, device_id=up, device_id_type=MESH)

    @pl.when(f > 0)
    def _():
        down = (c, s, lax.rem(f + depth - 1, depth))
        pl.semaphore_signal(sem, inc=1, device_id=down, device_id_type=MESH)

    neighbours = lax.div(f + depth - 1, depth) + lax.div(2 * depth - 2 - f, depth)
    return len(devices) + neighbours


def rows_of(index, count):
    return pl.ds(pl.multiple_of(index * count, count), count)


def row_loop(total, step, body):
    def one(i, carry):
        return body(rows_of(i, step), carry)

    return one, total // step


class Gather:
    sems = 13

    def __init__(self, src, out, send, recv):
        c, s, f = here()
        self.src, self.out, self.send, self.recv = src, out, send, recv
        self.c, self.s, self.rows = c, s, src.shape[0]
        self.x, self.y, self.sib = (c, flip(s, 1), f), (c, flip(s, 2), f), (1 - c, s, f)
        self.made = []

    def block(self, k, half=None):
        index = self.c * 4 + (self.s if k == 0 else flip(self.s, k))
        n = self.rows
        if half is None:
            return self.out.at[pl.ds(pl.multiple_of(index * n, n), n)]
        return self.out.at[pl.ds(pl.multiple_of(index * n + half * (n // 2), n // 2), n // 2)]

    def copy(self, src, dst, k, device):
        made = REMOTE(src, dst, self.send.at[k], self.recv.at[k], device, MESH)
        made.start()
        self.made.append(made)
        return made

    def start(self):
        half = self.rows // 2
        low, high = self.src.at[pl.ds(0, half)], self.src.at[pl.ds(half, half)]
        self.a = [
            self.copy(low, self.block(0, 0), 0, self.x),
            self.copy(high, self.block(0, 1), 1, self.y),
            self.copy(high, self.block(0, 1), 2, self.x),
            self.copy(low, self.block(0, 0), 3, self.y),
        ]
        self.g = [self.copy(self.src, self.block(0), 4, self.sib)]

    def pass_on(self, ref, k):
        self.g.append(self.copy(ref, ref, k, self.sib))

    def relay(self):
        self.a[0].wait_recv()
        self.b0 = self.copy(self.block(1, 0), self.block(1, 0), 5, self.y)
        self.a[1].wait_recv()
        self.b1 = self.copy(self.block(2, 1), self.block(2, 1), 6, self.x)
        self.pass_on(self.block(1, 0), 7)
        self.pass_on(self.block(2, 1), 8)
        self.a[2].wait_recv()
        self.pass_on(self.block(1, 1), 9)
        self.a[3].wait_recv()
        self.pass_on(self.block(2, 0), 10)

    def finish(self):
        self.b0.wait_recv()
        self.pass_on(self.block(3, 0), 11)
        self.b1.wait_recv()
        self.pass_on(self.block(3, 1), 12)
        for made in self.g:
            made.wait_recv()
        for made in self.made:
            made.wait_send()


class PairSum:
    order = (3, 1, 2, 0)

    @staticmethod
    def scratch(n, w):
        return [
            pltpu.VMEM((4, n, w), BF),
            pltpu.VMEM((4, n, w), BF),
            pltpu.VMEM((2, n, w), BF),
            pltpu.VMEM((4, n, w // 2), BF),
            pltpu.VMEM((2, n, w // 2), BF),
            pltpu.SemaphoreType.DMA((10,)),
            pltpu.SemaphoreType.DMA((10,)),
        ]

    def __init__(self, refs):
        self.own, self.near, self.out, self.far, self.last, self.send, self.recv = refs
        self.x, self.y, self.sib = partners()
        self.n, w = self.own.shape[1], self.own.shape[2]
        self.left, self.right = pl.ds(0, w // 2), pl.ds(w // 2, w // 2)
        self.fx = self.copy(self.own.at[0, :, self.left], self.far.at[1], 4, self.x)
        self.fy = self.copy(self.own.at[0, :, self.right], self.far.at[3], 5, self.y)
        self.nx = self.copy(self.own.at[1, :, self.left], self.far.at[0], 6, self.x)
        self.ny = self.copy(self.own.at[2, :, self.right], self.far.at[2], 7, self.y)
        self.by = self.copy(self.own.at[2, :, self.left], self.last.at[0], 8, self.y)
        self.bx = self.copy(self.own.at[1, :, self.right], self.last.at[1], 9, self.x)

    @staticmethod
    def blocks(c, s):
        return [
            core * 4 + (flip(s, k) if k else s) for k in PairSum.order for core in (1 - c, c)
        ]

    def copy(self, src, dst, k, device):
        return REMOTE(src, dst, self.send.at[k], self.recv.at[k], device, MESH)

    def to_sibling(self, i):
        return self.copy(self.out.at[lax.rem(i, 2)], self.near.at[i], i, self.sib)

    def combine(self, i):
        self.to_sibling(i).wait_recv()

        def body(j, carry):
            r = rows_of(j, 32)
            total = self.own[i, r, :].astype(F32) + self.near[i, r, :].astype(F32)
            self.own[i, r, :] = total.astype(BF)
            return carry

        lax.fori_loop(0, self.n // 32, body, 0)

    def between(self, i):
        @pl.when(i >= 1)
        def _():
            self.combine(i - 1)

        @pl.when(i == 1)
        def _():
            self.fx.start()
            self.fy.start()

        pl.when(i == 2)(self.nx.start)
        pl.when(i == 3)(self.ny.start)

        @pl.when(i >= 2)
        def _():
            self.to_sibling(i - 2).wait_send()

    def put(self, i, cols, part):
        self.out[lax.rem(i, 2), :, cols] = part[: self.n]
        self.own[i, :, cols] = part[self.n :]

    def add(self, at, cols, slot):
        def body(j, carry):
            r = rows_of(j, 32)
            total = self.own[at, r, cols].astype(F32) + self.far[slot, r, :].astype(F32)
            self.own[at, r, cols] = total.astype(BF)
            return carry

        lax.fori_loop(0, self.n // 32, body, 0)

    def relay(self):
        self.fx.wait_recv()
        self.add(2, self.left, 1)
        self.by.start()
        self.fy.wait_recv()
        self.add(1, self.right, 3)
        self.bx.start()

    def arrive(self):
        self.to_sibling(3).wait_recv()
        for made in (self.nx, self.ny, self.by, self.bx):
            made.wait_recv()

    def total(self, j, step):
        r = rows_of(j, step)
        total = self.own[3, r, :].astype(F32) + self.near[3, r, :].astype(F32)
        a = jnp.concatenate([self.far[0, r, :], self.far[2, r, :]], axis=1).astype(F32)
        b = jnp.concatenate([self.last[0, r, :], self.last[1, r, :]], axis=1).astype(F32)
        return total + a + b

    def finish_plane(self):
        for made in (self.fx, self.fy, self.nx, self.ny, self.by, self.bx):
            made.wait_send()

    def finish(self):
        self.finish_plane()
        for i in (2, 3):
            self.to_sibling(i).wait_send()


class PairTail:
    @staticmethod
    def scratch(n, w):
        return [
            pltpu.VMEM((3, n, w), BF),
            pltpu.VMEM((4, n, w // 2), BF),
            pltpu.SemaphoreType.DMA((4,)),
            pltpu.SemaphoreType.DMA((4,)),
        ]

    def __init__(self, refs):
        self.own, self.far, send, recv = refs
        x, y, sib = partners()
        w = self.own.shape[2]
        left, right = pl.ds(0, w // 2), pl.ds(w // 2, w // 2)
        self.made = [
            REMOTE(src, self.far.at[i], send.at[i], recv.at[i], device, MESH)
            for i, (src, device) in enumerate((
                (self.own.at[0, :, left], x),
                (self.own.at[0, :, right], x),
                (self.own.at[1, :, left], y),
                (self.own.at[1, :, right], y),
            ))
        ]

    def start(self):
        for made in self.made:
            made.start()

    def arrive(self):
        for made in self.made:
            made.wait_recv()

    def total(self, j, step):
        r = rows_of(j, step)
        total = self.own[2, r, :].astype(F32)
        a = jnp.concatenate([self.far[0, r, :], self.far[1, r, :]], axis=1).astype(F32)
        b = jnp.concatenate([self.far[2, r, :], self.far[3, r, :]], axis=1).astype(F32)
        return total + a + b

    def finish(self):
        for made in self.made:
            made.wait_send()


def wait_for(i, loads):
    for at, pair in enumerate(loads):

        @pl.when(i == at)
        def _(pair=pair):
            for made in pair:
                made.wait()


def partners():
    c, s, f = here()
    return [(c, flip(s, 1), f), (c, flip(s, 2), f), (1 - c, s, f)]


STEP = 32


def gain_row(ref):
    return ref[...].reshape(1, ref.shape[0])


def mean_square_inverse(values):
    return lax.rsqrt(jnp.mean(values * values, axis=1, keepdims=True) + epsilon)


class Line:
    def __init__(self, own, slot, send, recv, depth):
        self.own, self.slot, self.send, self.recv, self.depth = own, slot, send, recv, depth
        self.c, self.s, self.f = here()

    def copy(self, i, distance, up):
        owner = self.f - (distance - 1) if up else self.f + (distance - 1)
        to = lax.rem(self.f + (1 if up else self.depth - 1), self.depth)
        src = self.own[i] if distance == 1 else self.slot(i, owner)
        k = 0 if up else 1
        return REMOTE(
            src,
            self.slot(i, owner),
            self.send.at[k, distance - 1, i],
            self.recv.at[k, distance - 1, i],
            (self.c, self.s, to),
            MESH,
        )

    def may_send(self, distance, up):
        if up:
            return (self.f < self.depth - 1) & (self.f >= distance - 1)
        return (self.f > 0) & (self.f + distance <= self.depth)

    def gets(self, distance, up):
        return self.f >= distance if up else self.f + distance < self.depth

    def start(self, i):
        for up in (True, False):
            pl.when(self.may_send(1, up))(self.copy(i, 1, up).start)

    def pass_on(self, distance):
        for i in range(len(self.own)):
            for up in (True, False):
                pl.when(self.gets(distance, up))(self.got(i, distance, up).wait_recv)
                if distance < self.depth - 1:
                    pl.when(self.may_send(distance + 1, up))(self.copy(i, distance + 1, up).start)

    def got(self, i, distance, up):
        owner = self.f - distance if up else self.f + distance
        k = 0 if up else 1
        place = self.slot(i, owner)
        return REMOTE(
            place,
            place,
            self.send.at[k, distance - 1, i],
            self.recv.at[k, distance - 1, i],
            (self.c, self.s, lax.rem(self.f + (self.depth - 1 if up else 1), self.depth)),
            MESH,
        )

    def finish(self):
        for distance in range(1, self.depth):
            for i in range(len(self.own)):
                for up in (True, False):
                    pl.when(self.may_send(distance, up))(self.copy(i, distance, up).wait_send)


class Spread:
    def __init__(self, src, dst, origin, send, recv, depth, pieces):
        self.c, self.s, self.f = here()
        self.src, self.dst, self.origin, self.depth = src, dst, origin, depth
        self.send, self.recv, self.pieces = send, recv, pieces
        self.n = dst.shape[0] // pieces

    def part(self, ref, i):
        return ref.at[pl.ds(i * self.n, self.n)]

    def copy(self, i, up, first):
        k = 0 if up else 1
        return REMOTE(
            self.part(self.src if first else self.dst, i),
            self.part(self.dst, i),
            self.send.at[k, i],
            self.recv.at[i],
            (self.c, self.s, lax.rem(self.f + (1 if up else self.depth - 1), self.depth)),
            MESH,
        )

    def above(self):
        return (self.f > self.origin) & (self.f < self.depth - 1)

    def below(self):
        return (self.f < self.origin) & (self.f > 0)

    def start(self, local):
        first = self.f == self.origin

        @pl.when(first)
        def _():
            pltpu.make_async_copy(self.src, self.dst, local).start()

        for i in range(self.pieces):
            pl.when(first & (self.f < self.depth - 1))(self.copy(i, True, True).start)
            pl.when(first & (self.f > 0))(self.copy(i, False, True).start)

    def pass_on(self):
        for i in range(self.pieces):
            pl.when(self.f != self.origin)(self.copy(i, True, False).wait_recv)
            pl.when(self.above())(self.copy(i, True, False).start)
            pl.when(self.below())(self.copy(i, False, False).start)

    def finish(self, local):
        first = self.f == self.origin

        @pl.when(first)
        def _():
            pltpu.make_async_copy(self.src, self.dst, local).wait()

        for i in range(self.pieces):
            pl.when((first & (self.f < self.depth - 1)) | self.above())(
                self.copy(i, True, False).wait_send
            )
            pl.when((first & (self.f > 0)) | self.below())(self.copy(i, False, False).wait_send)


WEIGHT_PIECES = 4
OUT_PIECES = 2


def enter_kernel(
    tok_ref, dy_ref, gain_ref, bias_ref, forget_ref,
    query_ref, key_ref, value_ref, outgate_ref, gate_ref, up_ref, down_ref, out_w_ref,
    normed_ref, dy_all_ref, w_attn_ref, w_out_ref, cat_ref, mlp_ref,
    mine, windows, attn, own_forget, forget_all, mlp, normed, turned, cat,
    s0, r0, s1, r1, sz, rz, so, ro, l0, l1, l2, *, depth, heads,
):
    c, s, f = here()
    t = c * 4 + s
    n = tok_ref.shape[0]
    shard, cols = attn.shape
    hw = cols // 4
    fw = mlp.shape[1] // 3
    base = ((t * hw) // 128) * 128
    window = pl.ds(pl.multiple_of(base, 128), windows.shape[2])
    slices = [
        pltpu.make_async_copy(ref.at[:, window], windows.at[i], l2.at[i])
        for i, ref in enumerate((query_ref, key_ref, value_ref, outgate_ref))
    ]
    hidden = pl.ds(pl.multiple_of(t * fw, fw), fw)
    mlp_loads = [
        pltpu.make_async_copy(ref.at[:, hidden], mlp.at[:, pl.ds(i * fw, fw)], l2.at[4 + i])
        for i, ref in enumerate((gate_ref, up_ref, down_ref))
    ]
    for made in slices + mlp_loads:
        made.start()
    greeted = signal_line(partners(), depth)
    gain = gain_ref[...].reshape(1, gain_ref.shape[0])

    def body(i, carry):
        r = rows_of(i, STEP)
        v = tok_ref[r, :].astype(F32)
        mine[r, :] = (v * mean_square_inverse(v) * gain).astype(BF)
        return carry

    lax.fori_loop(0, n // STEP, body, 0)
    a = lax.broadcasted_iota(jnp.int32, (own_forget.shape[0], forget_ref.shape[1]), 0)
    b = lax.broadcasted_iota(jnp.int32, (own_forget.shape[0], forget_ref.shape[1]), 1)
    pick = jnp.where((b == a + t * heads) & (a < heads), 1.0, 0.0).astype(BF)
    own_forget[...] = dot(pick, forget_ref[...], 1, 1).astype(BF)
    for made in slices:
        made.wait()

    step = shard // WEIGHT_PIECES
    own = [attn.at[pl.ds(i * step, step)] for i in range(WEIGHT_PIECES)] + [own_forget]

    def slot(i, owner):
        if i == WEIGHT_PIECES:
            return forget_all.at[owner]
        rows = pl.ds(pl.multiple_of(owner * shard + i * step, step), step)
        return w_attn_ref.at[rows, pl.ds(0, cols)]

    line = Line(own, slot, sz, rz, depth)
    pl.semaphore_wait(pltpu.get_barrier_semaphore(), greeted)
    first = Gather(mine, normed_ref, s0, r0)
    second = Gather(dy_ref, dy_all_ref, s1, r1)
    first.start()
    for i in range(WEIGHT_PIECES):
        rows = slice(i * step, (i + 1) * step)
        for begin in (0, 64):

            @pl.when(t * hw - base == begin)
            def _(rows=rows, begin=begin):
                attn[rows, :] = jnp.concatenate(
                    [windows[k, rows, begin : begin + hw].astype(F32) for k in range(4)], axis=1
                ).astype(BF)

        line.start(i)
    line.start(WEIGHT_PIECES)
    heads_rows = w_out_ref.shape[0]
    origin = (t * heads_rows) // shard
    spread = Spread(
        out_w_ref.at[pl.ds(pl.multiple_of(t * heads_rows - origin * shard, heads_rows), heads_rows)],
        w_out_ref, origin, so, ro, depth, OUT_PIECES,
    )
    keep = [
        pltpu.make_async_copy(
            attn,
            w_attn_ref.at[pl.ds(pl.multiple_of(f * shard, shard), shard), pl.ds(0, cols)],
            l0.at[2],
        ),
        pltpu.make_async_copy(own_forget, forget_all.at[f], l0.at[3]),
        pltpu.make_async_copy(mine, first.block(0), l0.at[0]),
        pltpu.make_async_copy(dy_ref, second.block(0), l0.at[1]),
    ]
    for made in keep:
        made.start()
    for made in mlp_loads:
        made.wait()
    mlp_store = pltpu.make_async_copy(mlp, mlp_ref, l2.at[7])
    mlp_store.start()
    line.pass_on(1)
    spread.start(l0.at[4])
    first.relay()
    second.start()
    line.pass_on(2)
    first.finish()
    for made in keep[2:3]:
        made.wait()
    load = pltpu.make_async_copy(normed_ref, normed, l0.at[5])
    load.start()
    keep[0].wait()
    keep[1].wait()
    r = lax.broadcasted_iota(jnp.int32, (16, 1), 0)
    bias = jnp.zeros((16, 1), F32)
    for h in range(heads):
        bias = jnp.where(r == h, bias_ref[t * heads + h], bias)

    def store(i):
        tokens = rows_of(i, 512)
        return pltpu.make_async_copy(cat.at[:, tokens], cat_ref.at[:, tokens], l1.at[i])

    def add_shard(owner, begin, end):
        small = forget_all[owner].astype(F32)
        tall = jnp.concatenate([small, jnp.zeros((128 - small.shape[0], shard), F32)], axis=0)
        rows = rows_of(owner, shard)
        w_attn_ref[rows, cols:] = tall.T.astype(BF)
        turned[...] = w_attn_ref[rows, :].T

        def tile(i, unused):
            tokens = rows_of(i, 512)
            part = dot(turned[...], normed[tokens, rows], 1, 1)
            if begin:
                cat[:, tokens] = part
            else:
                cat[:, tokens] += part
            if end:
                cat[4 * hw : 4 * hw + 16, tokens] += bias
                store(i).start()
            return unused

        lax.fori_loop(0, normed.shape[0] // 512, tile, 0)

    half = depth // 2
    upper = lax.div(f, half)
    load.wait()
    for k in range(1, depth - 1):
        add_shard(jnp.int32(k), k == 1, False)
    add_shard(upper * (depth - 1), False, False)
    second.relay()
    spread.pass_on()
    line.pass_on(3)
    add_shard((1 - upper) * (depth - 1), False, True)
    second.finish()
    line.finish()
    keep[3].wait()
    spread.finish(l0.at[4])
    mlp_store.wait()
    for i in range(normed.shape[0] // 512):
        store(i).wait()


def enter(tokens, cotangent, gain, bias, forget_weight, attn_weights, mlp_weights, out_weight, depth):
    n, w = tokens.shape
    shard, head_count = forget_weight.shape
    heads = head_count // 8
    hw = w // 8
    cols, fw = 4 * hw, mlp_weights[0].shape[1] // 8
    whole = jax.ShapeDtypeStruct((8 * n, w), BF)
    dma = pltpu.SemaphoreType.DMA((Gather.sems,))
    line = pltpu.SemaphoreType.DMA((2, depth - 1, WEIGHT_PIECES + 1))
    vmem = pl.BlockSpec(memory_space=pltpu.VMEM)
    smem = pl.BlockSpec(memory_space=pltpu.SMEM)
    anywhere = pl.BlockSpec(memory_space=pl.ANY)
    return pl.pallas_call(
        functools.partial(enter_kernel, depth=depth, heads=heads),
        name="enter",
        out_shape=(
            whole,
            whole,
            jax.ShapeDtypeStruct((depth * shard, cols + 128), BF),
            jax.ShapeDtypeStruct((hw, w), BF),
            jax.ShapeDtypeStruct((cols + 128, 8 * n), F32),
            jax.ShapeDtypeStruct((shard, 3 * fw), BF),
        ),
        in_specs=[vmem, vmem, vmem, smem, vmem] + [anywhere] * 8,
        out_specs=[anywhere, anywhere, vmem, anywhere, anywhere, anywhere],
        scratch_shapes=[
            pltpu.VMEM((n, w), BF),
            pltpu.VMEM((4, shard, hw + 64), BF),
            pltpu.VMEM((shard, cols), BF),
            pltpu.VMEM((16, shard), BF),
            pltpu.VMEM((depth, 16, shard), BF),
            pltpu.VMEM((shard, 3 * fw), BF),
            pltpu.VMEM((8 * n, w), BF),
            pltpu.VMEM((cols + 128, shard), BF),
            pltpu.VMEM((cols + 128, 8 * n), F32),
            dma, dma, dma, dma, line, line,
            pltpu.SemaphoreType.DMA((2, OUT_PIECES)),
            pltpu.SemaphoreType.DMA((OUT_PIECES,)),
            pltpu.SemaphoreType.DMA((6,)),
            pltpu.SemaphoreType.DMA((8 * n // 512,)),
            pltpu.SemaphoreType.DMA((8,)),
        ],
        compiler_params=pltpu.CompilerParams(
            collective_id=1, has_side_effects=True, vmem_limit_bytes=VMEM_BYTES
        ),
        cost_estimate=pl.CostEstimate(
            flops=2 * 8 * n * w * cols, bytes_accessed=4 * 8 * n * w * 2, transcendentals=0
        ),
    )(tokens, cotangent, gain, bias, forget_weight, *attn_weights, *mlp_weights, out_weight)


TILE = 256


def middle_kernel(
    gated_ref, w_ref, tok_ref, gain_ref, mid_ref, normed_ref,
    gated, turned, mine, s1, r1, l0, *refs,
):
    c, s, f = here()
    pairs = PairSum(refs)
    n, width = mine.shape
    loads = [
        pltpu.make_async_copy(
            gated_ref.at[:, pl.ds(pl.multiple_of(block * n, n), n)],
            gated.at[:, pl.ds(i * n, n)],
            l0.at[i],
        )
        for i, block in enumerate(PairSum.blocks(c, s))
    ]
    for made in loads:
        made.start()
    greet(partners())
    for made in loads:
        made.wait()

    def one_pair(i, unused):
        pairs.between(i)
        turned[...] = gated[:, rows_of(i, 2 * n)].T
        for t in range(width // TILE):
            feats = pl.ds(t * TILE, TILE)
            pairs.put(i, feats, dot(turned[...], w_ref[:, feats], 1, 0).astype(BF))
        pairs.to_sibling(i).start()
        return unused

    lax.fori_loop(0, 4, one_pair, 0)
    pairs.relay()
    pairs.arrive()

    def body(i, carry):
        r = rows_of(i, STEP)
        mid = tok_ref[r, :].astype(F32) + pairs.total(i, STEP)
        mid_ref[r, :] = mid
        mine[r, :] = (mid * mean_square_inverse(mid) * gain_row(gain_ref)).astype(BF)
        return carry

    lax.fori_loop(0, n // STEP, body, 0)
    gather = Gather(mine, normed_ref, s1, r1)
    gather.start()
    keep = pltpu.make_async_copy(mine, gather.block(0), l0.at[8])
    keep.start()
    gather.relay()
    gather.finish()
    pairs.finish()
    keep.wait()


def middle(gated, w_out, tokens, gain):
    n, w = tokens.shape
    dma = pltpu.SemaphoreType.DMA((16,))
    vmem = pl.BlockSpec(memory_space=pltpu.VMEM)
    anywhere = pl.BlockSpec(memory_space=pl.ANY)
    return pl.pallas_call(
        middle_kernel,
        name="middle",
        out_shape=(jax.ShapeDtypeStruct((n, w), F32), jax.ShapeDtypeStruct((8 * n, w), BF)),
        in_specs=[anywhere, vmem, vmem, vmem],
        out_specs=[vmem, anywhere],
        scratch_shapes=[
            pltpu.VMEM(gated.shape, BF),
            pltpu.VMEM((2 * n, gated.shape[0]), BF),
            pltpu.VMEM((n, w), BF),
            dma, dma, dma,
        ]
        + PairSum.scratch(n, w),
        compiler_params=pltpu.CompilerParams(
            collective_id=2, has_side_effects=True, vmem_limit_bytes=VMEM_BYTES
        ),
        cost_estimate=pl.CostEstimate(
            flops=2 * 8 * n * w * gated.shape[0], bytes_accessed=4 * 8 * n * w * 2,
            transcendentals=0,
        ),
    )(gated, w_out, tokens, gain)


TERM_PIECES = 4


class LineSum:
    def __init__(self, term, got, send, recv, depth, pieces=TERM_PIECES):
        self.term, self.got, self.send, self.recv, self.depth = term, got, send, recv, depth
        self.c, self.s, self.f = here()
        self.pieces = pieces
        self.n = term.shape[0] // pieces

    def source(self, i, g):
        return self.term.at[pl.ds(i * self.n, self.n), g]

    def copy(self, k, g, i, src):
        to = lax.rem(self.f + (1 if k == 0 else self.depth - 1), self.depth)
        return REMOTE(
            src,
            self.got.at[k, g + k - 1, pl.ds(i * self.n, self.n)],
            self.send.at[k, g, i],
            self.recv.at[k, g, i],
            (self.c, self.s, to),
            MESH,
        )

    def targets(self, k):
        return range(self.depth - 1, 0, -1) if k == 0 else range(self.depth - 1)

    def is_end(self, k):
        return self.f == (0 if k == 0 else self.depth - 1)

    def start_piece(self, i, n):
        for k in (0, 1):
            g = self.targets(k)[n]
            pl.when(self.is_end(k))(self.copy(k, g, i, self.source(i, g)).start)

    def add(self, k, g, i):
        rows = pl.ds(i * self.n, self.n)
        total = self.got[k, g + k - 1, rows].astype(F32) + self.term[rows, g].astype(F32)
        self.got[k, g + k - 1, rows] = total.astype(BF)

    def pass_on(self, i, n, hop):
        for k in (0, 1):
            g = self.targets(k)[n]
            at = hop if k == 0 else self.depth - 1 - hop

            @pl.when(self.f == at)
            def _(k=k, g=g):
                made = self.copy(k, g, i, self.got.at[k, g + k - 1, pl.ds(i * self.n, self.n)])
                made.wait_recv()
                self.add(k, g, i)
                made.start()

    def steps(self):
        todo = [
            (n * self.pieces + i + 2 * (hop - 1), -hop, i, n, hop)
            for n in range(self.depth - 2)
            for hop in range(1, self.depth - 1 - n)
            for i in range(self.pieces)
        ]
        return [step[2:] for step in sorted(todo)]

    def collect(self, i, out):
        rows = pl.ds(i * self.n, self.n)
        for g in range(self.depth):

            @pl.when(self.f == g)
            def _(g=g):
                total = self.term[rows, g].astype(F32)
                for k in (0, 1):
                    if g != (0 if k == 0 else self.depth - 1):
                        self.copy(k, g, i, self.source(i, g)).wait_recv()
                        total = total + self.got[k, g + k - 1, rows].astype(F32)
                out[rows] = total.astype(BF)

    def finish(self):
        for k in (0, 1):
            for g in self.targets(k):
                beyond = self.f < g if k == 0 else self.f > g
                for i in range(self.pieces):
                    pl.when(beyond)(self.copy(k, g, i, self.source(i, g)).wait_send)


class Exchange:
    def __init__(self, rows, out, send, recv):
        self.c, self.s, self.f = here()
        self.place = self.c * 4 + self.s
        self.rows, self.out, self.send, self.recv = rows, out, send, recv

    def remote(self, j):
        return REMOTE(
            self.rows.at[j], self.out.at[self.place], self.send.at[j], self.recv.at[self.place],
            (j // 4, j % 4, self.f), MESH,
        )

    def local(self, j):
        return pltpu.make_async_copy(self.rows.at[j], self.out.at[j], self.send.at[j])

    def push(self, j):
        pl.when(self.place != j)(self.remote(j).start)
        pl.when(self.place == j)(self.local(j).start)

    def start(self):
        for j in range(8):
            self.push(j)

    def finish(self):
        for j in range(8):
            got = REMOTE(
                self.rows.at[j], self.out.at[j], self.send.at[j], self.recv.at[j],
                (j // 4, j % 4, self.f), MESH,
            )
            pl.when(self.place != j)(got.wait_recv)
            pl.when(self.place != j)(self.remote(j).wait_send)
            pl.when(self.place == j)(self.local(j).wait)


def plane_peers():
    c, s, f = here()
    return [
        (core, flip(s, k) if k else s, f, k + 4 * i)
        for i, core in enumerate((c, 1 - c))
        for k in range(4)
        if i or k
    ]


def ffn_kernel(
    nm_ref, dy_all_ref, w_ref, mid_ref, gain_ref, gated_ref, w_out_ref,
    grad_mid_ref, gain_term_ref, gg_ref, out_term_ref, down_ref, up_rows_ref, low_term_ref,
    nm, dy, w, grads, term, got, rows_sum, mine, branch, stage, down_own, down_near, down_far,
    l0, l1, l2, s1, r1, s2, r2, s3, r3, s4, r4, *refs, depth,
):
    c, s, f = here()
    n, width = mid_ref.shape
    fw = w.shape[1] // 3
    pairs = PairSum(refs)
    loads = []
    w_load = pltpu.make_async_copy(w_ref, w, l2.at[8])
    w_load.start()
    for i, block in enumerate(PairSum.blocks(c, s)):
        src, dst = pl.ds(pl.multiple_of(block * n, n), n), pl.ds(i * n, n)
        made = [
            pltpu.make_async_copy(nm_ref.at[src], nm.at[dst], l0.at[i]),
            pltpu.make_async_copy(dy_all_ref.at[src], dy.at[dst], l1.at[i]),
        ]
        for one in made:
            one.start()
        if i % 2:
            loads[-1] += made
        else:
            loads.append(made)
    greeted = signal_line([p[:3] for p in plane_peers()], depth)
    pl.semaphore_wait(pltpu.get_barrier_semaphore(), greeted)
    w_load.wait()

    def one_pair(i, unused):
        rows = rows_of(i, 2 * n)
        wait_for(i, loads)
        for t in range(fw // TILE):
            cols = pl.ds(t * TILE, TILE)
            ups = pl.ds(fw + t * TILE, TILE)
            downs = pl.ds(2 * fw + t * TILE, TILE)
            gate_lin = dot(nm[rows, :], w[:, cols], 1, 0)
            up_lin = dot(nm[rows, :], w[:, ups], 1, 0)
            grad_hidden = dot(dy[rows, :], w[:, downs], 1, 0)
            sig = jax.nn.sigmoid(gate_lin)
            active = gate_lin * sig
            grads[rows, downs] = (active * up_lin).astype(BF)
            grads[rows, cols] = (
                grad_hidden * up_lin * sig * (1.0 + gate_lin * (1.0 - sig))
            ).astype(BF)
            grads[rows, ups] = (grad_hidden * active).astype(BF)
        pairs.between(i)
        for t in range(width // TILE):
            feats = pl.ds(t * TILE, TILE)
            part = dot(grads[rows, 0 : 2 * fw], w[feats, 0 : 2 * fw], 1, 1).astype(BF)
            pairs.put(i, feats, part)
        pairs.to_sibling(i).start()
        return unused

    lax.fori_loop(0, 4, one_pair, 0)
    pairs.relay()

    line = LineSum(term, got, s2, r2, depth)
    deep = width // TERM_PIECES
    per = term.shape[0] // TERM_PIECES
    for i in range(TERM_PIECES):
        feats = pl.ds(i * deep, deep)
        tile = dot(nm[:, feats], grads[:, 0 : 2 * fw], 0, 0).astype(BF)
        term[i * per : (i + 1) * per] = tile.reshape((per,) + term.shape[1:])
        line.start_piece(i, 0)
    for k in range(1, depth - 1):
        for i in range(TERM_PIECES):
            line.start_piece(i, k)
    hw = gated_ref.shape[0]
    w_out, out_term = nm.at[pl.ds(0, hw)], nm.at[pl.ds(hw, hw)]
    w_out_load = pltpu.make_async_copy(w_out_ref, w_out, l2.at[9])
    w_out_load.start()
    todo = line.steps()
    pairs.arrive()

    def body(j, carry):
        r = rows_of(j, STEP)
        grad = pairs.total(j, STEP)
        mid = mid_ref[r, :]
        inverse = mean_square_inverse(mid)
        weighted = grad * gain_row(gain_ref)
        back = inverse * weighted - mid * inverse**3 * jnp.mean(
            weighted * mid, axis=1, keepdims=True
        )
        own_dy = dy[pl.ds(pl.multiple_of(7 * n + j * STEP, STEP), STEP), :]
        grad_mid = own_dy.astype(F32) + back
        grad_mid_ref[r, :] = grad_mid
        mine[r, :] = grad_mid.astype(BF)
        return carry + jnp.sum(grad * mid * inverse, axis=0, keepdims=True)

    gain_term_ref[...] = lax.fori_loop(0, n // STEP, body, jnp.zeros((1, width), F32))
    gather = Gather(mine, branch, s1, r1)
    gather.start()
    keep = pltpu.make_async_copy(mine, gather.block(0), l0.at[8])
    keep.start()
    for i in range(TERM_PIECES):
        feats = pl.ds(i * deep, deep)
        tile = dot(dy[:, feats], grads[:, 2 * fw :], 0, 0).astype(BF)
        tile = tile.reshape((per, depth, term.shape[2], fw))
        for g in range(depth):
            low_term_ref[g, i * per : (i + 1) * per] = tile[:, g]
        for step in todo[i * 2 : i * 2 + 2]:
            line.pass_on(*step)

    def down_copy(i):
        return REMOTE(
            pairs.out.at[lax.rem(i, 2)], down_near.at[i], s3.at[i], r3.at[i], pairs.sib, MESH
        )

    for i in (2, 3):
        pairs.to_sibling(i).wait_send()

    def down_pair(i, unused):
        rows = rows_of(i, 2 * n)

        @pl.when(i >= 2)
        def _():
            down_copy(i - 2).wait_send()

        for t in range(width // TILE):
            feats = pl.ds(t * TILE, TILE)
            part = dot(grads[rows, 2 * fw :], w[feats, 2 * fw :], 1, 1).astype(BF)
            pairs.out[lax.rem(i, 2), :, feats] = part[:n]
            down_own[i, :, feats] = part[n:]
        down_copy(i).start()
        return unused

    lax.fori_loop(0, 4, down_pair, 0)
    gather.relay()
    for step in todo[2 * TERM_PIECES :]:
        line.pass_on(*step)

    def down_sum(i, unused):
        down_copy(i).wait_recv()

        def body(j, carry):
            r = rows_of(j, 32)
            total = down_own[i, r, :].astype(F32) + down_near[i, r, :].astype(F32)
            down_own[i, r, :] = total.astype(BF)
            return carry

        return lax.fori_loop(0, n // 32, body, unused)

    lax.fori_loop(0, 4, down_sum, 0)
    down_fx = REMOTE(
        down_own.at[0, :, pairs.left], down_far.at[0], s3.at[4], r3.at[4], pairs.x, MESH
    )
    down_fy = REMOTE(
        down_own.at[0, :, pairs.right], down_far.at[1], s3.at[5], r3.at[5], pairs.y, MESH
    )
    down_fx.start()
    down_fy.start()
    gather.finish()
    keep.wait()

    def gg_copy(i):
        return pltpu.make_async_copy(
            stage.at[lax.rem(i, 2)], gg_ref.at[:, rows_of(i, stage.shape[2])], l2.at[lax.rem(i, 2)]
        )

    def gg_tile(i, unused):
        @pl.when(i >= 2)
        def _():
            gg_copy(i - 2).wait()

        stage[lax.rem(i, 2)] = dot(w_out[...], branch[rows_of(i, stage.shape[2]), :], 1, 1)
        gg_copy(i).start()
        return unused

    tiles = branch.shape[0] // stage.shape[2]
    w_out_load.wait()
    lax.fori_loop(0, tiles, gg_tile, 0)
    out_term[...] = dot(gated_ref[...], branch[...], 1, 0).astype(BF)
    out_store = pltpu.make_async_copy(out_term, out_term_ref, l2.at[10])
    out_store.start()
    exchange = Exchange(rows_sum, up_rows_ref, s4, r4)
    down_fx.wait_recv()
    down_fy.wait_recv()

    def down_add(at, cols, slot):
        def body(j, carry):
            r = rows_of(j, 32)
            total = down_own[at, r, cols].astype(F32) + down_far[slot, r, :].astype(F32)
            down_own[at, r, cols] = total.astype(BF)
            return carry

        lax.fori_loop(0, n // 32, body, 0)

    down_add(2, pairs.left, 0)
    down_add(1, pairs.right, 1)
    stores = [
        pltpu.make_async_copy(down_own.at[i], down_ref.at[i - 1], l1.at[i]) for i in (1, 2, 3)
    ]
    for made in stores:
        made.start()
    for i in range(TERM_PIECES):
        line.collect(i, rows_sum)
        for j in range(i * per, (i + 1) * per):
            exchange.push(j)
    exchange.finish()
    for made in stores:
        made.wait()
    for i in (2, 3):
        gg_copy(jnp.int32(tiles - 4 + i)).wait()
    out_store.wait()
    down_fx.wait_send()
    down_fy.wait_send()
    pairs.finish_plane()
    for i in (2, 3):
        down_copy(i).wait_send()
    line.finish()


def ffn(normed_all, cotangent_all, weights, mid, gain, gated, w_out, depth):
    n, width = mid.shape
    fw = weights.shape[1] // 3
    r = width // (8 * depth)
    hw = gated.shape[0]
    dma = pltpu.SemaphoreType.DMA((16,))
    six = pltpu.SemaphoreType.DMA((6,))
    eight = pltpu.SemaphoreType.DMA((8,))
    line = pltpu.SemaphoreType.DMA((2, depth, TERM_PIECES))
    vmem = pl.BlockSpec(memory_space=pltpu.VMEM)
    anywhere = pl.BlockSpec(memory_space=pl.ANY)
    return pl.pallas_call(
        functools.partial(ffn_kernel, depth=depth),
        name="ffn",
        out_shape=(
            jax.ShapeDtypeStruct((n, width), F32),
            jax.ShapeDtypeStruct((1, width), F32),
            jax.ShapeDtypeStruct((hw, 8 * n), F32),
            jax.ShapeDtypeStruct((hw, width), BF),
            jax.ShapeDtypeStruct((3, n, width), BF),
            jax.ShapeDtypeStruct((8, r, 2 * fw), BF),
            jax.ShapeDtypeStruct((depth, 8, r, fw), BF),
        ),
        in_specs=[anywhere] * 3 + [vmem] * 3 + [anywhere],
        out_specs=[vmem, vmem, anywhere, anywhere, anywhere, vmem, vmem],
        scratch_shapes=[
            pltpu.VMEM((8 * n, width), BF),
            pltpu.VMEM((8 * n, width), BF),
            pltpu.VMEM((width, 3 * fw), BF),
            pltpu.VMEM((8 * n, 3 * fw), BF),
            pltpu.VMEM((8, depth, r, 2 * fw), BF),
            pltpu.VMEM((2, depth - 1, 8, r, 2 * fw), BF),
            pltpu.VMEM((8, r, 2 * fw), BF),
            pltpu.VMEM((n, width), BF),
            pltpu.VMEM((8 * n, width), BF),
            pltpu.VMEM((2, hw, 256), F32),
            pltpu.VMEM((4, n, width), BF),
            pltpu.VMEM((4, n, width), BF),
            pltpu.VMEM((2, n, width // 2), BF),
            dma, dma, dma, dma, dma, line, line, six, six, eight, eight,
        ]
        + PairSum.scratch(n, width),
        compiler_params=pltpu.CompilerParams(
            collective_id=3, has_side_effects=True, vmem_limit_bytes=67_043_328
        ),
        cost_estimate=pl.CostEstimate(
            flops=2 * 8 * n * width * fw * 9, bytes_accessed=4 * 8 * n * width * 2,
            transcendentals=0,
        ),
    )(normed_all, cotangent_all, weights, mid, gain, gated, w_out)


def leave_kernel(
    normed_ref, cat_ref, w_ref, down_ref, tok_ref, grad_mid_ref, mid_ref, gain_ref,
    mlp_term_ref, bias_grad_ref, low_ref, wide_ref,
    grad_ref, small_sum_ref, out_ref, attn_rows_ref, low_rows_ref, wide_rows_ref,
    normed, cat, turned, w, small, plane_small, line_small, term, got, rows, wide_got,
    l0, l1, s2, r2, s3, r3, s5, r5, s6, r6, s7, r7, *refs, depth, heads,
):
    c, s, f = here()
    n, width = tok_ref.shape
    pairs = PairSum(refs[:7])
    down = PairTail(refs[7:])
    down_loads = [pltpu.make_async_copy(down_ref, down.own, l0.at[9])]
    loads = []
    for i, block in enumerate(PairSum.blocks(c, s)):
        src, dst = pl.ds(pl.multiple_of(block * n, n), n), pl.ds(i * n, n)
        loads.append(pltpu.make_async_copy(cat_ref.at[:, src], cat.at[:, dst], l0.at[i]))
        loads.append(pltpu.make_async_copy(normed_ref.at[src], normed.at[dst], l1.at[i]))
    w_load = pltpu.make_async_copy(w_ref, w, l0.at[8])
    for made in down_loads + loads:
        made.start()
    w_load.start()
    peers = plane_peers()
    line_peers = [(c, s, lax.rem(f + k, depth), k) for k in range(1, depth)]
    greet([p[:3] for p in peers + line_peers])
    wide = LineSum(wide_ref, wide_got, s7, r7, depth, 1)
    for k in range(depth - 1):
        wide.start_piece(0, k)
    line = LineSum(term, got, s3, r3, depth)
    low_rows = Exchange(low_ref, low_rows_ref, s6, r6)
    deep = width // TERM_PIECES
    per = term.shape[0] // TERM_PIECES
    for made in down_loads:
        made.wait()
    down.start()
    low_rows.start()
    for made in loads:
        made.wait()
    for i in range(TERM_PIECES):
        tile = dot(cat[...], normed[:, pl.ds(i * deep, deep)], 1, 0).T.astype(BF)
        term[i * per : (i + 1) * per] = tile.reshape((per,) + term.shape[1:])
        line.start_piece(i, 0)
    for k in range(1, depth - 1):
        for i in range(TERM_PIECES):
            line.start_piece(i, k)
    w_load.wait()

    def one_pair(i, unused):
        pairs.between(i)
        turned[...] = cat[:, rows_of(i, 2 * n)].T
        for t in range(width // TILE):
            feats = pl.ds(t * TILE, TILE)
            pairs.put(i, feats, dot(turned[...], w[feats, :], 1, 1).astype(BF))
        pairs.to_sibling(i).start()
        for at in range(4):

            @pl.when(i == at)
            def _(at=at):
                for step in todo[at : at + 1]:
                    line.pass_on(*step)

        return unused

    todo = line.steps()
    for step in wide.steps():
        wide.pass_on(*step)
    lax.fori_loop(0, 4, one_pair, 0)
    for step in todo[4:6]:
        line.pass_on(*step)
    pairs.relay()
    for step in todo[6:]:
        line.pass_on(*step)
    attn_rows = Exchange(rows, attn_rows_ref, s5, r5)

    def collect(i):
        line.collect(i, rows)
        for j in range(i * per, (i + 1) * per):
            attn_rows.push(j)

    pairs.arrive()

    def body(i, carry):
        r = rows_of(i, STEP)
        grad = pairs.total(i, STEP)
        tok = tok_ref[r, :].astype(F32)
        inverse = mean_square_inverse(tok)
        weighted = grad * gain_row(gain_ref)
        back = inverse * weighted - tok * inverse**3 * jnp.mean(
            weighted * tok, axis=1, keepdims=True
        )
        grad_ref[r, :] = grad_mid_ref[r, :] + back
        return carry + jnp.sum(grad * tok * inverse, axis=0, keepdims=True)

    gain_term = lax.fori_loop(0, n // STEP, body, jnp.zeros((1, width), F32))
    lane = small.shape[1]
    place = c * 4 + s
    for k in range(3):
        small[k : k + 1, :] = gain_term[:, k * lane : (k + 1) * lane]
        small[3 + k : 4 + k, :] = mlp_term_ref[:, k * lane : (k + 1) * lane]
    at = lax.broadcasted_iota(jnp.int32, (1, lane), 1)
    bias_row = jnp.zeros((1, lane), F32)
    for h in range(heads):
        bias_row = jnp.where(at == place * heads + h, bias_grad_ref[h : h + 1, 0:1], bias_row)
    small[6:7, :] = bias_row
    small[7:8, :] = jnp.zeros((1, lane), F32)
    plane_small[pl.ds(place, 1)] = small[...][None]
    sent = []
    for core, other_s, other_f, k in peers:
        made = REMOTE(
            small, plane_small.at[place], s2.at[k - 1], r2.at[k - 1], (core, other_s, other_f), MESH
        )
        made.start()
        sent.append(made)
    wide.collect(0, wide_rows_ref)
    collect(0)
    collect(1)
    for made in sent:
        made.wait()
    total = plane_small[0]
    for i in range(1, 8):
        total = total + plane_small[i]
    small[...] = total
    line_small[pl.ds(f, 1)] = total[None]
    sent = []
    for core, other_s, other_f, k in line_peers:
        made = REMOTE(
            small, line_small.at[f], s2.at[6 + k], r2.at[6 + k], (core, other_s, other_f), MESH
        )
        made.start()
        sent.append(made)
    collect(2)
    collect(3)
    down.arrive()

    def body2(i, carry):
        r = rows_of(i, STEP)
        out_ref[r, :] = (mid_ref[r, :] + down.total(i, STEP)).astype(BF)
        return carry

    lax.fori_loop(0, n // STEP, body2, 0)
    for made in sent:
        made.wait()
    total = line_small[0]
    for i in range(1, depth):
        total = total + line_small[i]
    small_sum_ref[...] = total
    pairs.finish()
    down.finish()
    line.finish()
    wide.finish()
    low_rows.finish()
    attn_rows.finish()


def leave(
    normed, cat, w_attn, down_sum, tokens, grad_mid, mid, gain, mlp_term, bias_grad, low_rows, wide,
    depth, heads,
):
    n, w = grad_mid.shape
    plane = 8
    cols = w_attn.shape[1]
    r = w // (plane * depth)
    sems = pltpu.SemaphoreType.DMA((6 + depth,))
    dma = pltpu.SemaphoreType.DMA((16,))
    eight = pltpu.SemaphoreType.DMA((8,))
    line = pltpu.SemaphoreType.DMA((2, depth, TERM_PIECES))
    one = pltpu.SemaphoreType.DMA((2, depth, 1))
    vmem = pl.BlockSpec(memory_space=pltpu.VMEM)
    anywhere = pl.BlockSpec(memory_space=pl.ANY)
    return pl.pallas_call(
        functools.partial(leave_kernel, depth=depth, heads=heads),
        name="leave",
        out_shape=(
            jax.ShapeDtypeStruct((n, w), F32),
            jax.ShapeDtypeStruct((8, w // 3), F32),
            jax.ShapeDtypeStruct((n, w), BF),
            jax.ShapeDtypeStruct((plane, r, cols), BF),
            jax.ShapeDtypeStruct(low_rows.shape, BF),
            jax.ShapeDtypeStruct((1,) + wide.shape[2:], BF),
        ),
        in_specs=[anywhere] * 4 + [vmem] * 8,
        out_specs=[vmem] * 6,
        scratch_shapes=[
            pltpu.VMEM(normed.shape, BF),
            pltpu.VMEM(cat.shape, BF),
            pltpu.VMEM((2 * n, cols), BF),
            pltpu.VMEM(w_attn.shape, BF),
            pltpu.VMEM((8, w // 3), F32),
            pltpu.VMEM((8, 8, w // 3), F32),
            pltpu.VMEM((depth, 8, w // 3), F32),
            pltpu.VMEM((plane, depth, r, cols), BF),
            pltpu.VMEM((2, depth - 1, plane, r, cols), BF),
            pltpu.VMEM((plane, r, cols), BF),
            pltpu.VMEM((2, depth - 1, 1) + wide.shape[2:], BF),
            dma, dma, sems, sems, line, line, eight, eight, eight, eight, one, one,
        ]
        + PairSum.scratch(n, w)
        + PairTail.scratch(n, w),
        compiler_params=pltpu.CompilerParams(
            collective_id=4, has_side_effects=True, vmem_limit_bytes=VMEM_BYTES
        ),
        cost_estimate=pl.CostEstimate(
            flops=4 * 8 * n * w * cols, bytes_accessed=4 * 8 * n * w * 2, transcendentals=0
        ),
    )(
        normed, cat, w_attn, down_sum, tokens, grad_mid, mid, gain, mlp_term, bias_grad, low_rows,
        wide,
    )


def finish_kernel(
    attn_ref, up_rows_ref, low_ref, small_ref, out_w_ref, block_ref, tok_grad_ref,
    q_ref, k_ref, v_ref, g_ref, f_ref, o_ref, gate_ref, up_ref, down_ref,
    gain1_ref, gain2_ref, bias_ref, out_ref, tokens_ref, *, hw, heads,
):
    plane = attn_ref.shape[0]
    fw = low_ref.shape[2]
    for i, ref in enumerate((q_ref, k_ref, v_ref, g_ref)):
        ref[...] = jnp.concatenate(
            [attn_ref[t, :, i * hw : (i + 1) * hw].astype(F32) for t in range(plane)], axis=1
        )
    a = lax.broadcasted_iota(jnp.int32, (128, 128), 0)
    b = lax.broadcasted_iota(jnp.int32, (128, 128), 1)
    total = jnp.zeros((attn_ref.shape[1], 128), F32)
    for t in range(plane):
        pick = jnp.where((a + t * heads == b) & (a < heads), 1.0, 0.0).astype(BF)
        total = total + dot(attn_ref[t, :, 4 * hw : 4 * hw + 128], pick, 1, 0)
    f_ref[...] = total.T[: f_ref.shape[0]]
    o_ref[...] = out_w_ref[0].astype(F32)
    for t in range(plane):
        cols = slice(t * fw, (t + 1) * fw)
        gate_ref[:, cols] = up_rows_ref[t, :, 0:fw].astype(F32)
        up_ref[:, cols] = up_rows_ref[t, :, fw:].astype(F32)
        down_ref[:, cols] = low_ref[t].astype(F32)
    lane = small_ref.shape[1]
    count = gain1_ref.shape[0] // lane
    for k in range(count):
        gain1_ref[k * lane : (k + 1) * lane] = small_ref[k, :]
        gain2_ref[k * lane : (k + 1) * lane] = small_ref[count + k, :]
    bias_ref[...] = small_ref[2 * count : 2 * count + 1, 0 : bias_ref.shape[1]]
    out_ref[...] = block_ref[...]
    tokens_ref[...] = tok_grad_ref[...]


def finish(attn_rows, up_rows, low_rows, small, out_w, block_out, tokens_grad, hw, heads):
    plane, r, _ = attn_rows.shape
    n, w = tokens_grad.shape
    fw = low_rows.shape[2]
    vmem = pl.BlockSpec(memory_space=pltpu.VMEM)
    square = jax.ShapeDtypeStruct((r, plane * hw), F32)
    wide = jax.ShapeDtypeStruct((r, plane * fw), F32)
    row = jax.ShapeDtypeStruct((w,), F32)
    return pl.pallas_call(
        functools.partial(finish_kernel, hw=hw, heads=heads),
        name="finish",
        out_shape=(
            square, square, square, square,
            jax.ShapeDtypeStruct((plane * heads, r), F32),
            jax.ShapeDtypeStruct(out_w.shape[1:], F32),
            wide, wide, wide, row, row,
            jax.ShapeDtypeStruct((1, plane * heads), F32),
            jax.ShapeDtypeStruct((n, w), BF),
            jax.ShapeDtypeStruct((n, w), F32),
        ),
        in_specs=[vmem] * 7,
        out_specs=[vmem] * 14,
        compiler_params=pltpu.CompilerParams(vmem_limit_bytes=VMEM_BYTES),
    )(attn_rows, up_rows, low_rows, small, out_w, block_out, tokens_grad)


BQ = 512
BK = 512
AUG = 128


def dot(a, b, ca, cb):
    return lax.dot_general(a, b, (((ca,), (cb,)), ((), ())), preferred_element_type=F32)


def three_parts(v):
    hi = v.astype(BF).astype(F32)
    mid = (v - hi).astype(BF).astype(F32)
    low = (v - hi - mid).astype(BF).astype(F32)
    return hi, mid, low


def triangle(n, suffix):
    a = lax.broadcasted_iota(jnp.int32, (n, n), 0)
    b = lax.broadcasted_iota(jnp.int32, (n, n), 1)
    return jnp.where(a >= b if suffix else a <= b, 1.0, 0.0).astype(BF)


def log_sigmoid(v):
    return jnp.minimum(v, 0.0) - jnp.log1p(jnp.exp(-jnp.abs(v)))


def doc_starts(lens_ref, pos):
    start, end = jnp.zeros_like(pos), jnp.int32(0)
    for n in range(lens_ref.shape[1]):
        end = end + lens_ref[0, n]
        start = jnp.where(pos >= end, end, start)
    return start


def storage_of(place_ref, p):
    found = jnp.int32(0)
    for n in range(place_ref.shape[1]):
        found = jnp.where(place_ref[0, n] == p, n, found)
    return found


def extend(prefix_row, sign_first):
    hi, mid, low = three_parts(prefix_row)
    r = lax.broadcasted_iota(jnp.int32, (16, prefix_row.shape[1]), 0)
    base = 0 if sign_first else 3
    sign = 1.0 if sign_first else -1.0
    ones = (r >= 3) & (r < 6) if sign_first else r < 3
    out = jnp.where(ones, 1.0, 0.0)
    out = jnp.where(r == base, sign * hi, out)
    out = jnp.where(r == base + 1, sign * mid, out)
    return jnp.where(r == base + 2, sign * low, out)


def lay_out(place_ref, cat_ref, prefix_ref, heads, hd, slab, qa, ka, kta):
    hw = heads * hd
    slabs = cat_ref.shape[1] // slab
    for p in range(slabs):
        src = pl.ds(pl.multiple_of(storage_of(place_ref, p) * slab, slab), slab)
        dst = pl.ds(p * slab, slab)
        for h in range(heads):
            q = cat_ref[h * hd : (h + 1) * hd, src].astype(BF).astype(F32)
            row = prefix_ref[h : h + 1, dst]
            rest = jnp.zeros((AUG - hd - 16, slab), F32)
            qe = jnp.concatenate([q * hd**-0.5, extend(row, True), rest], axis=0)
            qa[h, :, dst] = qe.astype(BF)
            k = cat_ref[hw + h * hd : hw + (h + 1) * hd, src].astype(BF).astype(F32)
            ke = jnp.concatenate([k, extend(row, False), rest], axis=0)
            if kta is not None:
                kta[h, :, dst] = ke.astype(BF)
            ka[h, dst, :] = ke.T.astype(BF)


def attention_kernel(
    place_ref, lens_ref, cat_ref,
    gated_ref, att_ref, exact_ref, lse_ref, prefix_ref,
    qa, ka, va, *, heads, hd, slab,
):
    hw = heads * hd
    tokens = cat_ref.shape[1]
    slabs = tokens // slab
    tri = triangle(slab, False)
    carry = jnp.zeros((16, 1), F32)
    for p in range(slabs):
        src = pl.ds(pl.multiple_of(storage_of(place_ref, p) * slab, slab), slab)
        pre = cat_ref[4 * hw : 4 * hw + 16, src]
        steps = log_sigmoid(pre).astype(BF)
        part = dot(steps, tri, 1, 0) + carry
        prefix_ref[:, p * slab : (p + 1) * slab] = part
        carry = part[:, slab - 1 : slab]
        for h in range(heads):
            va[h, :, p * slab : (p + 1) * slab] = cat_ref[
                2 * hw + h * hd : 2 * hw + (h + 1) * hd, src
            ].astype(BF)
    lay_out(place_ref, cat_ref, prefix_ref, heads, hd, slab, qa, ka, None)
    per = slab // BQ

    def one_query_block(qb, unused):
        q0 = pl.multiple_of(qb * BQ, BQ)
        pos = q0 + lax.broadcasted_iota(jnp.int32, (1, BQ), 1)
        start = doc_starts(lens_ref, pos)
        low = doc_starts(lens_ref, q0) // BK
        inside = lax.broadcasted_iota(jnp.int32, (BK, BQ), 0)

        def one_key_block(kb, held):
            k0 = pl.multiple_of(kb * BK, BK)
            allowed = (inside <= pos - k0) & (inside >= start - k0)
            out = []
            for h in range(heads):
                m, l, acc = held[h]
                st = dot(ka[h, pl.ds(k0, BK), :], qa[h, :, pl.ds(q0, BQ)], 1, 0)
                st = jnp.where(allowed, st, very_low)
                new = jnp.maximum(m, jnp.max(st, axis=0, keepdims=True))
                p = jnp.exp(st - new)
                scale = jnp.exp(m - new)
                l = l * scale + jnp.sum(p, axis=0, keepdims=True)
                acc = acc * scale + dot(va[h, :, pl.ds(k0, BK)], p.astype(BF), 1, 0)
                out.append((new, l, acc))
            return tuple(out)

        begin = tuple(
            (jnp.full((1, BQ), very_low, F32), jnp.zeros((1, BQ), F32), jnp.zeros((hd, BQ), F32))
            for _ in range(heads)
        )
        done = lax.fori_loop(low, (q0 + BQ + BK - 1) // BK, one_key_block, begin)
        dst = pl.ds(pl.multiple_of(storage_of(place_ref, qb // per) * slab + lax.rem(qb, per) * BQ, BQ), BQ)
        for h in range(heads):
            m, l, acc = done[h]
            lse_ref[h : h + 1, pl.ds(q0, BQ)] = m + jnp.log(l)
            exact = acc / l
            rounded = exact.astype(BF)
            exact_ref[h * hd : (h + 1) * hd, dst] = exact
            att_ref[h * hd : (h + 1) * hd, dst] = rounded
            gate = jax.nn.sigmoid(cat_ref[3 * hw + h * hd : 3 * hw + (h + 1) * hd, dst])
            gated_ref[h * hd : (h + 1) * hd, dst] = (rounded.astype(F32) * gate).astype(BF)
        return unused

    lse_ref[...] = jnp.zeros_like(lse_ref)
    lax.fori_loop(0, tokens // BQ, one_query_block, 0)


def attention(place, lens, cat, heads, hd, slab):
    tokens = cat.shape[1]
    hw = heads * hd
    vmem = pl.BlockSpec(memory_space=pltpu.VMEM)
    smem = pl.BlockSpec(memory_space=pltpu.SMEM)
    return pl.pallas_call(
        functools.partial(attention_kernel, heads=heads, hd=hd, slab=slab),
        name="attention",
        out_shape=(
            jax.ShapeDtypeStruct((hw, tokens), BF),
            jax.ShapeDtypeStruct((hw, tokens), BF),
            jax.ShapeDtypeStruct((hw, tokens), F32),
            jax.ShapeDtypeStruct((8, tokens), F32),
            jax.ShapeDtypeStruct((16, tokens), F32),
        ),
        in_specs=[smem, smem, vmem],
        out_specs=[vmem] * 5,
        scratch_shapes=[
            pltpu.VMEM((heads, AUG, tokens), BF),
            pltpu.VMEM((heads, tokens, AUG), BF),
            pltpu.VMEM((heads, hd, tokens), BF),
        ],
        compiler_params=pltpu.CompilerParams(vmem_limit_bytes=VMEM_BYTES),
        cost_estimate=pl.CostEstimate(
            flops=8 * heads * tokens * tokens * hd, bytes_accessed=cat.size * 4,
            transcendentals=heads * tokens * tokens // 2,
        ),
    )(place, lens, cat)


def attention_back_kernel(
    place_ref, lens_ref, cat_ref, gg_ref, att_ref, exact_ref, lse_ref, prefix_ref,
    out_ref, bias_grad_ref,
    qa, ka, kta, va, do, delta_ref, dk, dv, gp, *, heads, hd, slab,
):
    hw = heads * hd
    tokens = cat_ref.shape[1]
    slabs = tokens // slab
    per = slab // BQ
    lay_out(place_ref, cat_ref, prefix_ref, heads, hd, slab, qa, ka, kta)
    delta_ref[...] = jnp.zeros_like(delta_ref)
    gp[...] = jnp.zeros_like(gp)
    dk[...] = jnp.zeros_like(dk)
    dv[...] = jnp.zeros_like(dv)
    out_ref[4 * hw :, :] = jnp.zeros((out_ref.shape[0] - 4 * hw, tokens), BF)
    for p in range(slabs):
        src = pl.ds(pl.multiple_of(storage_of(place_ref, p) * slab, slab), slab)
        dst = pl.ds(p * slab, slab)
        for h in range(heads):
            rows = slice(h * hd, (h + 1) * hd)
            gate = jax.nn.sigmoid(cat_ref[3 * hw + h * hd : 3 * hw + (h + 1) * hd, src])
            gg = gg_ref[rows, src]
            low = (gg * gate).astype(BF)
            do[h, :, dst] = low
            delta_ref[h : h + 1, dst] = jnp.sum(
                low.astype(F32) * exact_ref[rows, src], axis=0, keepdims=True
            )
            gate_grad = gg * att_ref[rows, src].astype(F32) * gate * (1.0 - gate)
            out_ref[3 * hw + h * hd : 3 * hw + (h + 1) * hd, src] = gate_grad.astype(BF)
            v = cat_ref[2 * hw + h * hd : 2 * hw + (h + 1) * hd, src]
            va[h, dst, :] = v.T.astype(BF)

    def one_query_block(qb, unused):
        q0 = pl.multiple_of(qb * BQ, BQ)
        pos = q0 + lax.broadcasted_iota(jnp.int32, (1, BQ), 1)
        start = doc_starts(lens_ref, pos)
        low = doc_starts(lens_ref, q0) // BK
        inside = lax.broadcasted_iota(jnp.int32, (BK, BQ), 0)

        def one_key_block(kb, held):
            k0 = pl.multiple_of(kb * BK, BK)
            keys = pl.ds(k0, BK)
            allowed = (inside <= pos - k0) & (inside >= start - k0)
            out = []
            for h in range(heads):
                queries = qa[h, :, pl.ds(q0, BQ)]
                grads = do[h, :, pl.ds(q0, BQ)]
                st = dot(ka[h, keys, :], queries, 1, 0) - lse_ref[h : h + 1, pl.ds(q0, BQ)]
                p = jnp.exp(jnp.where(allowed, st, very_low))
                dp = dot(va[h, keys, :], grads, 1, 0) - delta_ref[h : h + 1, pl.ds(q0, BQ)]
                ds = (p * dp).astype(BF)
                out.append(held[h] + dot(kta[h, :, keys], ds, 1, 0))
                dk[h, :, keys] += dot(queries, ds, 1, 1)
                dv[h, :, keys] += dot(grads, p.astype(BF), 1, 1)
            return tuple(out)

        begin = tuple(jnp.zeros((AUG, BQ), F32) for _ in range(heads))
        done = lax.fori_loop(low, (q0 + BQ + BK - 1) // BK, one_key_block, begin)
        dst = pl.ds(pl.multiple_of(storage_of(place_ref, qb // per) * slab + lax.rem(qb, per) * BQ, BQ), BQ)
        for h in range(heads):
            out_ref[h * hd : (h + 1) * hd, dst] = (done[h][0:hd, :] * hd**-0.5).astype(BF)
            gp[h : h + 1, pl.ds(q0, BQ)] = done[h][hd : hd + 1, :]
        return unused

    lax.fori_loop(0, tokens // BQ, one_query_block, 0)
    tri = triangle(slab, True)
    carry = jnp.zeros((16, 1), F32)
    bias_grad = jnp.zeros((16, 1), F32)
    for p in reversed(range(slabs)):
        src = pl.ds(pl.multiple_of(storage_of(place_ref, p) * slab, slab), slab)
        dst = pl.ds(p * slab, slab)
        for h in range(heads):
            out_ref[hw + h * hd : hw + (h + 1) * hd, src] = dk[h, 0:hd, dst].astype(BF)
            out_ref[2 * hw + h * hd : 2 * hw + (h + 1) * hd, src] = dv[h, :, dst].astype(BF)
            gp[h : h + 1, dst] = gp[h : h + 1, dst] - dk[h, hd + 3 : hd + 4, dst]
        grad = gp[:, dst]
        total = carry
        for piece in three_parts(grad):
            total = total + dot(piece.astype(BF), tri, 1, 0)
        carry = total[:, 0:1]
        pre = cat_ref[4 * hw : 4 * hw + 16, src]
        low = (total.astype(BF).astype(F32) * jax.nn.sigmoid(-pre)).astype(BF)
        out_ref[4 * hw : 4 * hw + 16, src] = low
        bias_grad = bias_grad + jnp.sum(low.astype(F32), axis=1, keepdims=True)
    bias_grad_ref[...] = jnp.broadcast_to(bias_grad, bias_grad_ref.shape)


def attention_back(place, lens, cat, gg, att, exact, lse, prefix, heads, hd, slab):
    tokens = cat.shape[1]
    vmem = pl.BlockSpec(memory_space=pltpu.VMEM)
    smem = pl.BlockSpec(memory_space=pltpu.SMEM)
    return pl.pallas_call(
        functools.partial(attention_back_kernel, heads=heads, hd=hd, slab=slab),
        name="attention_back",
        out_shape=(
            jax.ShapeDtypeStruct(cat.shape, BF),
            jax.ShapeDtypeStruct((16, 128), F32),
        ),
        in_specs=[smem, smem] + [vmem] * 6,
        out_specs=[vmem] * 2,
        scratch_shapes=[
            pltpu.VMEM((heads, AUG, tokens), BF),
            pltpu.VMEM((heads, tokens, AUG), BF),
            pltpu.VMEM((heads, AUG, tokens), BF),
            pltpu.VMEM((heads, tokens, hd), BF),
            pltpu.VMEM((heads, hd, tokens), BF),
            pltpu.VMEM((8, tokens), F32),
            pltpu.VMEM((heads, AUG, tokens), F32),
            pltpu.VMEM((heads, hd, tokens), F32),
            pltpu.VMEM((16, tokens), F32),
        ],
        compiler_params=pltpu.CompilerParams(vmem_limit_bytes=VMEM_BYTES),
        cost_estimate=pl.CostEstimate(
            flops=20 * heads * tokens * tokens * hd, bytes_accessed=cat.size * 8,
            transcendentals=heads * tokens * tokens // 2,
        ),
    )(place, lens, cat, gg, att, exact, lse, prefix)


def local_plane(
    tokens, out_cotangent, seq_lengths, slab_place, attn_gain, query_weight, key_weight,
    value_weight, outgate_weight, forget_weight, forget_bias, output_weight, mlp_gain,
    gate_weight, up_weight, down_weight,
):
    plane_axes = ("cp", "sp")
    plane = lax.axis_size("cp") * lax.axis_size("sp")
    depth = lax.axis_size("fsdp")
    place = lax.axis_index("cp") * lax.axis_size("sp") + lax.axis_index("sp")
    head_count = forget_weight.shape[1]
    width = tokens.shape[2]
    hd = width // head_count
    heads = head_count // plane
    hw = heads * hd
    fw = gate_weight.shape[1] // plane
    shard = query_weight.shape[0]
    group_rows = tokens.shape[1] * plane
    slab = group_rows // slab_place.shape[1]

    inputs, cotangent = tokens[0], out_cotangent[0]
    normed, cotangent_all, w_attn, w_out, cat, own_mlp = enter(
        inputs, cotangent, attn_gain, forget_bias, forget_weight,
        (query_weight, key_weight, value_weight, outgate_weight),
        (gate_weight, up_weight, down_weight), output_weight, depth,
    )
    w_mlp = lax.all_gather(own_mlp, "fsdp", axis=0, tiled=True)
    gated, att, exact, lse, prefix = attention(slab_place, seq_lengths, cat, heads, hd, slab)
    mid, normed_mlp = middle(gated, w_out, inputs, mlp_gain)

    grad_mid, mlp_gain_term, grad_gated, out_term, down_sum, up_rows, low_term = ffn(
        normed_mlp, cotangent_all, w_mlp, mid, mlp_gain, gated, w_out, depth
    )
    low_grad = lax.psum_scatter(
        low_term.reshape(width, fw), "fsdp", scatter_dimension=0, tiled=True
    )

    grad_cat, bias_grad = attention_back(
        slab_place, seq_lengths, cat, grad_gated, att, exact, lse, prefix, heads, hd, slab
    )
    part = width // (plane * depth)
    tokens_grad, small_sum, block_out, attn_rows, low_rows, wide_rows = leave(
        normed, grad_cat, w_attn, down_sum, inputs, grad_mid, mid, attn_gain, mlp_gain_term,
        bias_grad, low_grad.reshape(plane, part, fw), out_term.reshape(1, depth, part, width),
        depth, heads,
    )
    (
        query_grad, key_grad, value_grad, outgate_grad, forget_grad, out_grad, gate_grad, up_grad,
        down_grad, attn_gain_grad, mlp_gain_grad, forget_bias_grad, block_out, tokens_grad,
    ) = finish(
        attn_rows, up_rows, low_rows, small_sum, wide_rows, block_out, tokens_grad,
        hw, heads,
    )
    return (
        block_out[None],
        tokens_grad[None],
        attn_gain_grad,
        query_grad,
        key_grad,
        value_grad,
        outgate_grad,
        forget_grad.T,
        forget_bias_grad[0],
        out_grad,
        mlp_gain_grad,
        gate_grad,
        up_grad,
        down_grad,
    )


def fits_plane(mesh, tokens, slab_place, forget_weight, gate_weight):
    sizes = dict(mesh.shape)
    if (sizes["cp"], sizes["sp"]) != (2, 4):
        return False
    plane = sizes["cp"] * sizes["sp"]
    width = tokens.shape[2]
    head_count = forget_weight.shape[1]
    group_rows = tokens.shape[1]
    slab = group_rows // slab_place.shape[1]
    heads = head_count // plane
    return (
        head_count % plane == 0
        and heads <= 8
        and width // head_count == 64
        and heads % 2 == 1
        and width == 8 * heads * 64
        and slab % 512 == 0
        and group_rows <= 2048
        and width % 768 == 0
        and gate_weight.shape[1] % (128 * plane) == 0
        and width % (16 * plane * sizes["fsdp"]) == 0
        and (group_rows // plane) % 64 == 0
    )


def shard(mesh, fn):
    return jax.shard_map(
        fn,
        mesh=mesh,
        in_specs=(
            P("fsdp", ("cp", "sp"), None),
            P("fsdp", ("cp", "sp"), None),
            P("fsdp", None),
            P("fsdp", None),
            P(),
            P("fsdp", None),
            P("fsdp", None),
            P("fsdp", None),
            P("fsdp", None),
            P("fsdp", None),
            P(),
            P("fsdp", None),
            P(),
            P("fsdp", None),
            P("fsdp", None),
            P("fsdp", None),
        ),
        out_specs=(
            P("fsdp", ("cp", "sp"), None),
            P("fsdp", ("cp", "sp"), None),
            P(),
            P(("cp", "sp", "fsdp"), None),
            P(("cp", "sp", "fsdp"), None),
            P(("cp", "sp", "fsdp"), None),
            P(("cp", "sp", "fsdp"), None),
            P(("cp", "sp", "fsdp"), None),
            P(),
            P(("cp", "sp", "fsdp"), None),
            P(),
            P(("cp", "sp", "fsdp"), None),
            P(("cp", "sp", "fsdp"), None),
            P(("cp", "sp", "fsdp"), None),
        ),
        check_vma=False,
    )


def solution(mesh):
    def run(*args):
        fast = fits_plane(mesh, args[0], args[3], args[9], args[13])
        return shard(mesh, local_plane if fast else local)(*args)

    return run
```

```python
import functools

import jax
import jax.numpy as jnp
from jax import lax
from jax.experimental import pallas as pl
from jax.experimental.pallas import tpu as pltpu
from jax.sharding import PartitionSpec as P

epsilon = 1e-06
very_low = -1e30
MESH = pl.DeviceIdType.MESH
BF = jnp.bfloat16
F32 = jnp.float32
REMOTE = pltpu.make_async_remote_copy
VMEM_BYTES = 60 * 1024 * 1024


def matmul(left, right):
    return jnp.dot(left, right, preferred_element_type=jnp.float32)


def matmul_right_t(left, right):
    return lax.dot_general(
        left, right, (((1,), (1,)), ((), ())), preferred_element_type=jnp.float32
    )


def matmul_left_t(left, right):
    return lax.dot_general(
        left, right, (((0,), (0,)), ((), ())), preferred_element_type=jnp.float32
    )


def rms_inverse(values):
    return lax.rsqrt(jnp.mean(values * values, axis=1, keepdims=True) + epsilon)


def norm_back(upstream, values, inverse, gain):
    weighted = upstream * gain
    return inverse * weighted - values * inverse**3 * jnp.mean(
        weighted * values, axis=1, keepdims=True
    )


def row_layout(place_row, lens_row, count, slab_rows):
    rows = jnp.arange(count, dtype=jnp.int32)
    slab_index = rows // slab_rows
    table = (
        slab_index[:, None] == jnp.arange(place_row.shape[0], dtype=jnp.int32)[None, :]
    ).astype(jnp.int32)
    position = jnp.sum(table * place_row[None, :], axis=1) * slab_rows + rows % slab_rows
    ends = jnp.cumsum(lens_row)
    segment = jnp.sum((position[:, None] >= ends[None, :]).astype(jnp.int32), axis=1)
    return (position, segment)


def forget_prefix(log_all, place_row, slab_rows):
    slabs = place_row.shape[0]
    steps = log_all.astype(jnp.float32).reshape(slabs, slab_rows, -1)
    inside = jnp.cumsum(steps, axis=1)
    totals = inside[:, -1, :]
    earlier = (place_row[None, :] < place_row[:, None]).astype(jnp.float32)
    offsets = jnp.dot(earlier, totals, precision=lax.Precision.HIGHEST)
    return (inside + offsets[:, None, :]).reshape(slabs * slab_rows, -1)


def prefix_back(grad_prefix, place_row, slab_rows):
    slabs = place_row.shape[0]
    steps = grad_prefix.reshape(slabs, slab_rows, -1)
    inside = jnp.flip(jnp.cumsum(jnp.flip(steps, 1), axis=1), 1)
    totals = inside[:, 0, :]
    later = (place_row[None, :] > place_row[:, None]).astype(jnp.float32)
    offsets = jnp.dot(later, totals, precision=lax.Precision.HIGHEST)
    return (inside + offsets[:, None, :]).reshape(slabs * slab_rows, -1)


def local(
    tokens,
    out_cotangent,
    seq_lengths,
    slab_place,
    attn_gain,
    query_weight,
    key_weight,
    value_weight,
    outgate_weight,
    forget_weight,
    forget_bias,
    output_weight,
    mlp_gain,
    gate_weight,
    up_weight,
    down_weight,
):
    seq_devices = lax.axis_size("sp")
    ctx_devices = lax.axis_size("cp")
    ctx_index = lax.axis_index("cp")
    tok_rows = tokens.shape[1]
    model_width = tokens.shape[2]
    head_count = forget_weight.shape[1]
    local_heads = head_count // seq_devices
    head_size = model_width // head_count
    ctx_rows = tok_rows * seq_devices
    group_rows = ctx_rows * ctx_devices
    slab_rows = ctx_rows // 2
    key_block = min(512, group_rows)
    key_blocks = group_rows // key_block
    score_scale = head_size ** (-0.5)
    place_row = slab_place[0]
    lens_row = seq_lengths[0]
    ctx_start = ctx_index * ctx_rows
    inputs = tokens[0]
    input_f = inputs.astype(jnp.float32)
    weights_attn = (
        lax.all_gather(query_weight, "fsdp", axis=0, tiled=True),
        lax.all_gather(key_weight, "fsdp", axis=0, tiled=True),
        lax.all_gather(value_weight, "fsdp", axis=0, tiled=True),
        lax.all_gather(outgate_weight, "fsdp", axis=0, tiled=True),
        lax.all_gather(forget_weight, "fsdp", axis=0, tiled=True),
        lax.all_gather(output_weight, "fsdp", axis=0, tiled=True),
    )
    full_query, full_key, full_value, full_outgate, full_forget, full_output = weights_attn
    inv_first = rms_inverse(input_f)
    normed = (input_f * inv_first * attn_gain).astype(jnp.bfloat16)
    queries = matmul(normed, full_query).astype(jnp.bfloat16)
    keys = matmul(normed, full_key).astype(jnp.bfloat16)
    values = matmul(normed, full_value).astype(jnp.bfloat16)
    out_gate = jax.nn.sigmoid(matmul(normed, full_outgate))
    forget_pre = matmul(normed, full_forget) + forget_bias
    log_forget = jax.nn.log_sigmoid(forget_pre).astype(jnp.bfloat16)
    head_query, head_key, head_value, head_forget = (
        lax.all_to_all(queries, "sp", split_axis=1, concat_axis=0, tiled=True),
        lax.all_to_all(keys, "sp", split_axis=1, concat_axis=0, tiled=True),
        lax.all_to_all(values, "sp", split_axis=1, concat_axis=0, tiled=True),
        lax.all_to_all(log_forget, "sp", split_axis=1, concat_axis=0, tiled=True),
    )
    keys_all, values_all, forget_all = (
        lax.all_gather(head_key, "cp", axis=0, tiled=True),
        lax.all_gather(head_value, "cp", axis=0, tiled=True),
        lax.all_gather(head_forget, "cp", axis=0, tiled=True),
    )
    prefix_all = forget_prefix(forget_all, place_row, slab_rows)
    pos_all, seg_all = row_layout(place_row, lens_row, group_rows, slab_rows)
    query_pos = lax.dynamic_slice_in_dim(pos_all, ctx_start, ctx_rows, 0)
    query_seg = lax.dynamic_slice_in_dim(seg_all, ctx_start, ctx_rows, 0)
    query_prefix = lax.dynamic_slice_in_dim(prefix_all, ctx_start, ctx_rows, 0)
    query_three = head_query.reshape(ctx_rows, local_heads, head_size)
    query_pos_top = jnp.max(query_pos)
    query_seg_low = jnp.min(query_seg)
    query_seg_top = jnp.max(query_seg)
    key_pieces = (
        keys_all.reshape(key_blocks, key_block, local_heads, head_size),
        values_all.reshape(key_blocks, key_block, local_heads, head_size),
        prefix_all.reshape(key_blocks, key_block, local_heads),
        pos_all.reshape(key_blocks, key_block),
        seg_all.reshape(key_blocks, key_block),
    )

    def block_live(key_pos, key_seg):
        return (
            (query_pos_top >= jnp.min(key_pos))
            & (query_seg_top >= jnp.min(key_seg))
            & (jnp.max(key_seg) >= query_seg_low)
        )

    def block_scores(key_piece, key_prefix, key_pos, key_seg):
        raw = (
            jnp.einsum("qhd,khd->hqk", query_three, key_piece, preferred_element_type=jnp.float32)
            * score_scale
        )
        raw = raw + query_prefix.T[:, :, None] - key_prefix.T[:, None, :]
        allowed = (query_pos[:, None] >= key_pos[None, :]) & (
            query_seg[:, None] == key_seg[None, :]
        )
        return (raw, allowed[None, :, :])

    def total_work(carry, piece):
        running_max, running_sum = carry
        key_piece, value_piece, key_prefix, key_pos, key_seg = piece
        raw, allowed = block_scores(key_piece, key_prefix, key_pos, key_seg)
        new_max = jnp.maximum(running_max, jnp.max(jnp.where(allowed, raw, very_low), axis=2))
        terms = jnp.where(allowed, jnp.exp(raw - new_max[:, :, None]), 0.0)
        new_sum = running_sum * jnp.exp(running_max - new_max) + jnp.sum(terms, axis=2)
        return (new_max, new_sum)

    def total_step(carry, piece):
        live = block_live(piece[3], piece[4])
        return (lax.cond(live, total_work, lambda held, unused: held, carry, piece), None)

    start_max = jnp.full((local_heads, ctx_rows), very_low, jnp.float32)
    start_sum = jnp.zeros((local_heads, ctx_rows), jnp.float32)
    (final_max, final_sum), _ = lax.scan(total_step, (start_max, start_sum), key_pieces)
    log_total = final_max + jnp.log(final_sum)

    def output_work(carry, piece):
        coarse, fine = carry
        key_piece, value_piece, key_prefix, key_pos, key_seg = piece
        raw, allowed = block_scores(key_piece, key_prefix, key_pos, key_seg)
        probs = jnp.where(allowed, jnp.exp(raw - log_total[:, :, None]), 0.0)
        rounded = probs.astype(jnp.bfloat16)
        rest = (probs - rounded.astype(jnp.float32)).astype(jnp.bfloat16)
        coarse = coarse + jnp.einsum(
            "hqk,khd->qhd", rounded, value_piece, preferred_element_type=jnp.float32
        )
        fine = fine + jnp.einsum(
            "hqk,khd->qhd", rest, value_piece, preferred_element_type=jnp.float32
        )
        return (coarse, fine)

    def output_step(carry, piece):
        live = block_live(piece[3], piece[4])
        return (lax.cond(live, output_work, lambda held, unused: held, carry, piece), None)

    zero_out = jnp.zeros((ctx_rows, local_heads, head_size), jnp.float32)
    (coarse_out, fine_out), _ = lax.scan(output_step, (zero_out, zero_out), key_pieces)
    exact_out = coarse_out + fine_out
    head_out = coarse_out.reshape(ctx_rows, local_heads * head_size).astype(jnp.bfloat16)
    token_out = lax.all_to_all(head_out, "sp", split_axis=0, concat_axis=1, tiled=True)
    token_out_f = token_out.astype(jnp.float32)
    gated = (token_out_f * out_gate).astype(jnp.bfloat16)
    mid = input_f + matmul(gated, full_output)
    weights_mlp = (
        lax.all_gather(gate_weight, "fsdp", axis=0, tiled=True),
        lax.all_gather(up_weight, "fsdp", axis=0, tiled=True),
        lax.all_gather(down_weight, "fsdp", axis=0, tiled=True),
    )
    full_gate, full_up, full_down = weights_mlp
    inv_second = rms_inverse(mid)
    normed_mlp = (mid * inv_second * mlp_gain).astype(jnp.bfloat16)
    gate_lin = matmul(normed_mlp, full_gate)
    up_lin = matmul(normed_mlp, full_up)
    gate_sig = jax.nn.sigmoid(gate_lin)
    activated = gate_lin * gate_sig
    hidden = (activated * up_lin).astype(jnp.bfloat16)
    block_out = (mid + matmul_right_t(hidden, full_down)).astype(jnp.bfloat16)
    cotangent = out_cotangent[0]
    grad_hidden = matmul(cotangent, full_down)
    grad_gate_lin = (grad_hidden * up_lin * gate_sig * (1.0 + gate_lin * (1.0 - gate_sig))).astype(
        jnp.bfloat16
    )
    grad_up_lin = (grad_hidden * activated).astype(jnp.bfloat16)
    grad_normed_mlp = matmul_right_t(grad_gate_lin, full_gate) + matmul_right_t(
        grad_up_lin, full_up
    )
    mlp_gain_term = jnp.sum(grad_normed_mlp * mid * inv_second, axis=0)
    grad_mid = cotangent.astype(jnp.float32) + norm_back(grad_normed_mlp, mid, inv_second, mlp_gain)
    gate_term = matmul_left_t(normed_mlp, grad_gate_lin)
    up_term = matmul_left_t(normed_mlp, grad_up_lin)
    down_term = matmul_left_t(cotangent, hidden)
    grad_branch = grad_mid.astype(jnp.bfloat16)
    grad_gated = matmul_right_t(grad_branch, full_output)
    grad_attended = (grad_gated * out_gate).astype(jnp.bfloat16)
    grad_gate_pre = (grad_gated * token_out_f * out_gate * (1.0 - out_gate)).astype(jnp.bfloat16)
    head_grad = lax.all_to_all(grad_attended, "sp", split_axis=1, concat_axis=0, tiled=True)
    grad_three = head_grad.reshape(ctx_rows, local_heads, head_size)
    delta = jnp.sum(grad_three.astype(jnp.float32) * exact_out, axis=2).T

    def back_work(carry, piece):
        grad_query_acc, grad_prefix_acc = carry
        key_piece, value_piece, key_prefix, key_pos, key_seg = piece
        raw, allowed = block_scores(key_piece, key_prefix, key_pos, key_seg)
        probs = jnp.where(allowed, jnp.exp(raw - log_total[:, :, None]), 0.0)
        rounded = probs.astype(jnp.bfloat16)
        grad_probs = jnp.einsum(
            "qhd,khd->hqk", grad_three, value_piece, preferred_element_type=jnp.float32
        )
        grad_scores = (probs * (grad_probs - delta[:, :, None])).astype(jnp.bfloat16)
        grad_query_acc = (
            grad_query_acc
            + jnp.einsum("hqk,khd->qhd", grad_scores, key_piece, preferred_element_type=jnp.float32)
            * score_scale
        )
        key_term = (
            jnp.einsum("hqk,qhd->khd", grad_scores, query_three, preferred_element_type=jnp.float32)
            * score_scale
        )
        value_term = jnp.einsum(
            "hqk,qhd->khd", rounded, grad_three, preferred_element_type=jnp.float32
        )
        score_f = grad_scores.astype(jnp.float32)
        grad_prefix_acc = grad_prefix_acc + jnp.sum(score_f, axis=2)
        prefix_term = -jnp.sum(score_f, axis=1)
        return ((grad_query_acc, grad_prefix_acc), (key_term, value_term, prefix_term))

    def back_skip(carry, piece):
        empty_kv = jnp.zeros((key_block, local_heads, head_size), jnp.float32)
        empty_prefix = jnp.zeros((local_heads, key_block), jnp.float32)
        return (carry, (empty_kv, empty_kv, empty_prefix))

    def back_step(carry, piece):
        live = block_live(piece[3], piece[4])
        return lax.cond(live, back_work, back_skip, carry, piece)

    start_prefix = jnp.zeros((local_heads, ctx_rows), jnp.float32)
    (grad_query_acc, grad_prefix_q), (key_terms, value_terms, prefix_terms) = lax.scan(
        back_step, (zero_out, start_prefix), key_pieces
    )
    keys_grad_all = key_terms.reshape(group_rows, local_heads * head_size)
    values_grad_all = value_terms.reshape(group_rows, local_heads * head_size)
    prefix_grad_all = jnp.transpose(prefix_terms, (0, 2, 1)).reshape(group_rows, local_heads)
    own_prefix = lax.dynamic_slice_in_dim(prefix_grad_all, ctx_start, ctx_rows, 0)
    prefix_grad_all = lax.dynamic_update_slice_in_dim(
        prefix_grad_all, own_prefix + grad_prefix_q.T, ctx_start, 0
    )
    forget_grad_term = prefix_back(prefix_grad_all, place_row, slab_rows)
    key_sum, value_sum, forget_sum = (
        lax.psum_scatter(keys_grad_all, "cp", scatter_dimension=0, tiled=True),
        lax.psum_scatter(values_grad_all, "cp", scatter_dimension=0, tiled=True),
        lax.psum_scatter(forget_grad_term, "cp", scatter_dimension=0, tiled=True),
    )
    grad_query_head = grad_query_acc.reshape(ctx_rows, local_heads * head_size).astype(jnp.bfloat16)
    grad_query_tok, grad_key_tok, grad_value_tok, grad_forget_tok = (
        lax.all_to_all(grad_query_head, "sp", split_axis=0, concat_axis=1, tiled=True),
        lax.all_to_all(key_sum.astype(jnp.bfloat16), "sp", split_axis=0, concat_axis=1, tiled=True),
        lax.all_to_all(
            value_sum.astype(jnp.bfloat16), "sp", split_axis=0, concat_axis=1, tiled=True
        ),
        lax.all_to_all(
            forget_sum.astype(jnp.bfloat16), "sp", split_axis=0, concat_axis=1, tiled=True
        ),
    )
    grad_forget_pre = (grad_forget_tok.astype(jnp.float32) * jax.nn.sigmoid(-forget_pre)).astype(
        jnp.bfloat16
    )
    grad_normed = (
        matmul_right_t(grad_query_tok, full_query)
        + matmul_right_t(grad_key_tok, full_key)
        + matmul_right_t(grad_value_tok, full_value)
        + matmul_right_t(grad_gate_pre, full_outgate)
        + matmul_right_t(grad_forget_pre, full_forget)
    )
    attn_gain_term = jnp.sum(grad_normed * input_f * inv_first, axis=0)
    bias_term = jnp.sum(grad_forget_pre.astype(jnp.float32), axis=0)
    tokens_grad = grad_mid + norm_back(grad_normed, input_f, inv_first, attn_gain)
    query_term = matmul_left_t(normed, grad_query_tok)
    key_term_w = matmul_left_t(normed, grad_key_tok)
    value_term_w = matmul_left_t(normed, grad_value_tok)
    outgate_term = matmul_left_t(normed, grad_gate_pre)
    forget_term = matmul_left_t(normed, grad_forget_pre)
    output_term = matmul_left_t(gated, grad_branch)
    (
        query_grad,
        key_grad,
        value_grad,
        outgate_grad,
        forget_grad,
        output_weight_grad,
        gate_grad,
        up_grad,
        down_grad,
    ) = (
        lax.psum_scatter(query_term, ("cp", "sp", "fsdp"), scatter_dimension=0, tiled=True),
        lax.psum_scatter(key_term_w, ("cp", "sp", "fsdp"), scatter_dimension=0, tiled=True),
        lax.psum_scatter(value_term_w, ("cp", "sp", "fsdp"), scatter_dimension=0, tiled=True),
        lax.psum_scatter(outgate_term, ("cp", "sp", "fsdp"), scatter_dimension=0, tiled=True),
        lax.psum_scatter(forget_term, ("cp", "sp", "fsdp"), scatter_dimension=0, tiled=True),
        lax.psum_scatter(output_term, ("cp", "sp", "fsdp"), scatter_dimension=0, tiled=True),
        lax.psum_scatter(gate_term, ("cp", "sp", "fsdp"), scatter_dimension=0, tiled=True),
        lax.psum_scatter(up_term, ("cp", "sp", "fsdp"), scatter_dimension=0, tiled=True),
        lax.psum_scatter(down_term, ("cp", "sp", "fsdp"), scatter_dimension=0, tiled=True),
    )
    attn_gain_grad, mlp_gain_grad, forget_bias_grad = lax.psum(
        (attn_gain_term, mlp_gain_term, bias_term), ("cp", "sp", "fsdp")
    )
    return (
        block_out[None],
        tokens_grad[None],
        attn_gain_grad,
        query_grad,
        key_grad,
        value_grad,
        outgate_grad,
        forget_grad,
        forget_bias_grad,
        output_weight_grad,
        mlp_gain_grad,
        gate_grad,
        up_grad,
        down_grad,
    )


def here():
    return (lax.axis_index("cp"), lax.axis_index("sp"), lax.axis_index("fsdp"))


def flip(s, k):
    if k == 1:
        return s + 1 - 2 * lax.rem(s, 2)
    if k == 2:
        return lax.rem(s + 2, 4)
    return 3 - s


def greet(devices):
    sem = pltpu.get_barrier_semaphore()
    for device in devices:
        pl.semaphore_signal(sem, inc=1, device_id=device, device_id_type=MESH)
    pl.semaphore_wait(sem, len(devices))


def signal_line(devices, depth):
    c, s, f = here()
    sem = pltpu.get_barrier_semaphore()
    for device in devices:
        pl.semaphore_signal(sem, inc=1, device_id=device, device_id_type=MESH)

    @pl.when(f < depth - 1)
    def _():
        up = (c, s, lax.rem(f + 1, depth))
        pl.semaphore_signal(sem, inc=1, device_id=up, device_id_type=MESH)

    @pl.when(f > 0)
    def _():
        down = (c, s, lax.rem(f + depth - 1, depth))
        pl.semaphore_signal(sem, inc=1, device_id=down, device_id_type=MESH)

    neighbours = lax.div(f + depth - 1, depth) + lax.div(2 * depth - 2 - f, depth)
    return len(devices) + neighbours


def rows_of(index, count):
    return pl.ds(pl.multiple_of(index * count, count), count)


def row_loop(total, step, body):
    def one(i, carry):
        return body(rows_of(i, step), carry)

    return one, total // step


class Gather:
    sems = 13

    def __init__(self, src, out, send, recv, stride=None, offset=0):
        c, s, f = here()
        self.src, self.out, self.send, self.recv = src, out, send, recv
        self.c, self.s, self.rows = c, s, src.shape[0]
        self.stride, self.offset = stride or self.rows, offset
        self.x, self.y, self.sib = (c, flip(s, 1), f), (c, flip(s, 2), f), (1 - c, s, f)
        self.made = []

    def block(self, k, half=None):
        index = self.c * 4 + (self.s if k == 0 else flip(self.s, k))
        n = self.rows
        begin = index * self.stride + self.offset
        if half is None:
            return self.out.at[pl.ds(pl.multiple_of(begin, n), n)]
        return self.out.at[pl.ds(pl.multiple_of(begin + half * (n // 2), n // 2), n // 2)]

    def copy(self, src, dst, k, device):
        made = REMOTE(src, dst, self.send.at[k], self.recv.at[k], device, MESH)
        made.start()
        self.made.append(made)
        return made

    def start(self):
        half = self.rows // 2
        low, high = self.src.at[pl.ds(0, half)], self.src.at[pl.ds(half, half)]
        self.a = [
            self.copy(low, self.block(0, 0), 0, self.x),
            self.copy(high, self.block(0, 1), 1, self.y),
            self.copy(high, self.block(0, 1), 2, self.x),
            self.copy(low, self.block(0, 0), 3, self.y),
        ]
        self.g = [self.copy(self.src, self.block(0), 4, self.sib)]

    def pass_on(self, ref, k):
        self.g.append(self.copy(ref, ref, k, self.sib))

    def relay(self):
        self.a[0].wait_recv()
        self.b0 = self.copy(self.block(1, 0), self.block(1, 0), 5, self.y)
        self.a[1].wait_recv()
        self.b1 = self.copy(self.block(2, 1), self.block(2, 1), 6, self.x)
        self.pass_on(self.block(1, 0), 7)
        self.pass_on(self.block(2, 1), 8)
        self.a[2].wait_recv()
        self.pass_on(self.block(1, 1), 9)
        self.a[3].wait_recv()
        self.pass_on(self.block(2, 0), 10)

    def finish(self):
        self.b0.wait_recv()
        self.pass_on(self.block(3, 0), 11)
        self.b1.wait_recv()
        self.pass_on(self.block(3, 1), 12)
        for made in self.g:
            made.wait_recv()
        for made in self.made:
            made.wait_send()


class PairSum:
    order = (3, 1, 2, 0)

    @staticmethod
    def scratch(n, w):
        return [
            pltpu.VMEM((4, n, w), BF),
            pltpu.VMEM((4, n, w), BF),
            pltpu.VMEM((2, n, w), BF),
            pltpu.VMEM((4, n, w // 2), BF),
            pltpu.VMEM((2, n, w // 2), BF),
            pltpu.SemaphoreType.DMA((10,)),
            pltpu.SemaphoreType.DMA((10,)),
        ]

    def __init__(self, refs):
        self.own, self.near, self.out, self.far, self.last, self.send, self.recv = refs
        self.x, self.y, self.sib = partners()
        self.n, w = self.own.shape[1], self.own.shape[2]
        self.left, self.right = pl.ds(0, w // 2), pl.ds(w // 2, w // 2)
        self.fx = self.copy(self.own.at[0, :, self.left], self.far.at[1], 4, self.x)
        self.fy = self.copy(self.own.at[0, :, self.right], self.far.at[3], 5, self.y)
        self.nx = self.copy(self.own.at[1, :, self.left], self.far.at[0], 6, self.x)
        self.ny = self.copy(self.own.at[2, :, self.right], self.far.at[2], 7, self.y)
        self.by = self.copy(self.own.at[2, :, self.left], self.last.at[0], 8, self.y)
        self.bx = self.copy(self.own.at[1, :, self.right], self.last.at[1], 9, self.x)

    @staticmethod
    def blocks(c, s):
        return [
            core * 4 + (flip(s, k) if k else s) for k in PairSum.order for core in (1 - c, c)
        ]

    def copy(self, src, dst, k, device):
        return REMOTE(src, dst, self.send.at[k], self.recv.at[k], device, MESH)

    def to_sibling(self, i):
        return self.copy(self.out.at[lax.rem(i, 2)], self.near.at[i], i, self.sib)

    def combine(self, i):
        self.to_sibling(i).wait_recv()

        def body(j, carry):
            r = rows_of(j, 32)
            total = self.own[i, r, :].astype(F32) + self.near[i, r, :].astype(F32)
            self.own[i, r, :] = total.astype(BF)
            return carry

        lax.fori_loop(0, self.n // 32, body, 0)

    def between(self, i):
        @pl.when(i >= 1)
        def _():
            self.combine(i - 1)

        @pl.when(i == 1)
        def _():
            self.fx.start()
            self.fy.start()

        pl.when(i == 2)(self.nx.start)
        pl.when(i == 3)(self.ny.start)

        @pl.when(i >= 2)
        def _():
            self.to_sibling(i - 2).wait_send()

    def put(self, i, cols, part):
        self.out[lax.rem(i, 2), :, cols] = part[: self.n]
        self.own[i, :, cols] = part[self.n :]

    def add(self, at, cols, slot):
        def body(j, carry):
            r = rows_of(j, 32)
            total = self.own[at, r, cols].astype(F32) + self.far[slot, r, :].astype(F32)
            self.own[at, r, cols] = total.astype(BF)
            return carry

        lax.fori_loop(0, self.n // 32, body, 0)

    def relay(self):
        self.fx.wait_recv()
        self.add(2, self.left, 1)
        self.by.start()
        self.fy.wait_recv()
        self.add(1, self.right, 3)
        self.bx.start()

    def arrive(self):
        self.to_sibling(3).wait_recv()
        for made in (self.nx, self.ny, self.by, self.bx):
            made.wait_recv()

    def total(self, j, step):
        r = rows_of(j, step)
        total = self.own[3, r, :].astype(F32) + self.near[3, r, :].astype(F32)
        a = jnp.concatenate([self.far[0, r, :], self.far[2, r, :]], axis=1).astype(F32)
        b = jnp.concatenate([self.last[0, r, :], self.last[1, r, :]], axis=1).astype(F32)
        return total + a + b

    def finish_plane(self):
        for made in (self.fx, self.fy, self.nx, self.ny, self.by, self.bx):
            made.wait_send()

    def finish(self):
        self.finish_plane()
        for i in (2, 3):
            self.to_sibling(i).wait_send()


class PairTail:
    @staticmethod
    def scratch(n, w):
        return [
            pltpu.VMEM((3, n, w), BF),
            pltpu.VMEM((4, n, w // 2), BF),
            pltpu.SemaphoreType.DMA((4,)),
            pltpu.SemaphoreType.DMA((4,)),
        ]

    def __init__(self, refs):
        self.own, self.far, send, recv = refs
        x, y, sib = partners()
        w = self.own.shape[2]
        left, right = pl.ds(0, w // 2), pl.ds(w // 2, w // 2)
        self.made = [
            REMOTE(src, self.far.at[i], send.at[i], recv.at[i], device, MESH)
            for i, (src, device) in enumerate((
                (self.own.at[0, :, left], x),
                (self.own.at[0, :, right], x),
                (self.own.at[1, :, left], y),
                (self.own.at[1, :, right], y),
            ))
        ]

    def start(self, part):
        for made in self.made[part::2]:
            made.start()

    def arrive(self):
        for made in self.made:
            made.wait_recv()

    def total(self, j, step):
        r = rows_of(j, step)
        total = self.own[2, r, :].astype(F32)
        a = jnp.concatenate([self.far[0, r, :], self.far[1, r, :]], axis=1).astype(F32)
        b = jnp.concatenate([self.far[2, r, :], self.far[3, r, :]], axis=1).astype(F32)
        return total + a + b

    def finish(self):
        for made in self.made:
            made.wait_send()


def wait_for(i, loads):
    for at, pair in enumerate(loads):

        @pl.when(i == at)
        def _(pair=pair):
            for made in pair:
                made.wait()


def partners():
    c, s, f = here()
    return [(c, flip(s, 1), f), (c, flip(s, 2), f), (1 - c, s, f)]


STEP = 32


def gain_row(ref):
    return ref[...].reshape(1, ref.shape[0])


def mean_square_inverse(values):
    return lax.rsqrt(jnp.mean(values * values, axis=1, keepdims=True) + epsilon)


class Line:
    def __init__(self, own, slot, send, recv, depth):
        self.own, self.slot, self.send, self.recv, self.depth = own, slot, send, recv, depth
        self.c, self.s, self.f = here()

    def copy(self, i, distance, up):
        owner = self.f - (distance - 1) if up else self.f + (distance - 1)
        to = lax.rem(self.f + (1 if up else self.depth - 1), self.depth)
        src = self.own[i] if distance == 1 else self.slot(i, owner)
        k = 0 if up else 1
        return REMOTE(
            src,
            self.slot(i, owner),
            self.send.at[k, distance - 1, i],
            self.recv.at[k, distance - 1, i],
            (self.c, self.s, to),
            MESH,
        )

    def may_send(self, distance, up):
        if up:
            return (self.f < self.depth - 1) & (self.f >= distance - 1)
        return (self.f > 0) & (self.f + distance <= self.depth)

    def gets(self, distance, up):
        return self.f >= distance if up else self.f + distance < self.depth

    def start(self, i):
        for up in (True, False):
            pl.when(self.may_send(1, up))(self.copy(i, 1, up).start)

    def pass_on(self, distance):
        for i in range(len(self.own)):
            for up in (True, False):
                pl.when(self.gets(distance, up))(self.got(i, distance, up).wait_recv)
                if distance < self.depth - 1:
                    pl.when(self.may_send(distance + 1, up))(self.copy(i, distance + 1, up).start)

    def got(self, i, distance, up):
        owner = self.f - distance if up else self.f + distance
        k = 0 if up else 1
        place = self.slot(i, owner)
        return REMOTE(
            place,
            place,
            self.send.at[k, distance - 1, i],
            self.recv.at[k, distance - 1, i],
            (self.c, self.s, lax.rem(self.f + (self.depth - 1 if up else 1), self.depth)),
            MESH,
        )

    def finish(self):
        for distance in range(1, self.depth):
            for i in range(len(self.own)):
                for up in (True, False):
                    pl.when(self.may_send(distance, up))(self.copy(i, distance, up).wait_send)


class Spread:
    def __init__(self, src, dst, origin, send, recv, depth, pieces):
        self.c, self.s, self.f = here()
        self.src, self.dst, self.origin, self.depth = src, dst, origin, depth
        self.send, self.recv, self.pieces = send, recv, pieces
        self.n = dst.shape[0] // pieces

    def part(self, ref, i):
        return ref.at[pl.ds(i * self.n, self.n)]

    def copy(self, i, up, first):
        k = 0 if up else 1
        return REMOTE(
            self.part(self.src if first else self.dst, i),
            self.part(self.dst, i),
            self.send.at[k, i],
            self.recv.at[i],
            (self.c, self.s, lax.rem(self.f + (1 if up else self.depth - 1), self.depth)),
            MESH,
        )

    def above(self):
        return (self.f > self.origin) & (self.f < self.depth - 1)

    def below(self):
        return (self.f < self.origin) & (self.f > 0)

    def start(self, local):
        first = self.f == self.origin

        @pl.when(first)
        def _():
            pltpu.make_async_copy(self.src, self.dst, local).start()

        for i in range(self.pieces):
            pl.when(first & (self.f < self.depth - 1))(self.copy(i, True, True).start)
            pl.when(first & (self.f > 0))(self.copy(i, False, True).start)

    def pass_on(self):
        for i in range(self.pieces):
            pl.when(self.f != self.origin)(self.copy(i, True, False).wait_recv)
            pl.when(self.above())(self.copy(i, True, False).start)
            pl.when(self.below())(self.copy(i, False, False).start)

    def finish(self, local):
        first = self.f == self.origin

        @pl.when(first)
        def _():
            pltpu.make_async_copy(self.src, self.dst, local).wait()

        for i in range(self.pieces):
            pl.when((first & (self.f < self.depth - 1)) | self.above())(
                self.copy(i, True, False).wait_send
            )
            pl.when((first & (self.f > 0)) | self.below())(self.copy(i, False, False).wait_send)


WEIGHT_PIECES = 4
OUT_PIECES = 2
EARLY = 128


def enter_kernel(
    tok_ref, dy_ref, gain_ref, bias_ref, forget_ref,
    query_ref, key_ref, value_ref, outgate_ref, gate_ref, up_ref, down_ref, out_w_ref,
    normed_ref, dy_all_ref, w_attn_ref, w_out_ref, cat_ref, mlp_ref, early_ref,
    mine, windows, attn, own_forget, forget_all, mlp, normed, turned, cat,
    s0, r0, s1, r1, sz, rz, se, re, so, ro, l0, l1, l2, *, depth, heads,
):
    c, s, f = here()
    t = c * 4 + s
    n = tok_ref.shape[0]
    shard, cols = attn.shape
    hw = cols // 4
    fw = mlp.shape[1] // 3
    base = ((t * hw) // 128) * 128
    window = pl.ds(pl.multiple_of(base, 128), windows.shape[2])
    slices = [
        pltpu.make_async_copy(ref.at[:, window], windows.at[i], l2.at[i])
        for i, ref in enumerate((query_ref, key_ref, value_ref, outgate_ref))
    ]
    hidden = pl.ds(pl.multiple_of(t * fw, fw), fw)
    mlp_loads = [
        pltpu.make_async_copy(ref.at[:, hidden], mlp.at[:, pl.ds(i * fw, fw)], l2.at[4 + i])
        for i, ref in enumerate((gate_ref, up_ref, down_ref))
    ]
    for made in slices + mlp_loads:
        made.start()
    greeted = signal_line(partners(), depth)
    gain = gain_ref[...].reshape(1, gain_ref.shape[0])

    def body(i, carry):
        r = rows_of(i, STEP)
        v = tok_ref[r, :].astype(F32)
        mine[r, :] = (v * mean_square_inverse(v) * gain).astype(BF)
        return carry

    lax.fori_loop(0, n // STEP, body, 0)
    a = lax.broadcasted_iota(jnp.int32, (own_forget.shape[0], forget_ref.shape[0]), 0)
    b = lax.broadcasted_iota(jnp.int32, (own_forget.shape[0], forget_ref.shape[0]), 1)
    pick = jnp.where((b == a + t * heads) & (a < heads), 1.0, 0.0).astype(BF)
    own_forget[...] = dot(pick, forget_ref[...], 1, 0).astype(BF)
    for made in slices:
        made.wait()

    step = shard // WEIGHT_PIECES
    own = [attn.at[pl.ds(i * step, step)] for i in range(WEIGHT_PIECES)] + [own_forget]

    def slot(i, owner):
        if i == WEIGHT_PIECES:
            return forget_all.at[owner]
        rows = pl.ds(pl.multiple_of(owner * shard + i * step, step), step)
        return w_attn_ref.at[rows, pl.ds(0, cols)]

    line = Line(own, slot, sz, rz, depth)
    pl.semaphore_wait(pltpu.get_barrier_semaphore(), greeted)
    first = Gather(mine, normed_ref, s0, r0)
    second = Gather(dy_ref, dy_all_ref, s1, r1)
    first.start()
    for i in range(WEIGHT_PIECES):
        rows = slice(i * step, (i + 1) * step)
        for begin in (0, 64):

            @pl.when(t * hw - base == begin)
            def _(rows=rows, begin=begin):
                attn[rows, :] = jnp.concatenate(
                    [windows[k, rows, begin : begin + hw].astype(F32) for k in range(4)], axis=1
                ).astype(BF)

        line.start(i)
    line.start(WEIGHT_PIECES)
    heads_rows = w_out_ref.shape[0]
    origin = (t * heads_rows) // shard
    spread = Spread(
        out_w_ref.at[pl.ds(pl.multiple_of(t * heads_rows - origin * shard, heads_rows), heads_rows)],
        w_out_ref, origin, so, ro, depth, OUT_PIECES,
    )
    keep = [
        pltpu.make_async_copy(
            attn,
            w_attn_ref.at[pl.ds(pl.multiple_of(f * shard, shard), shard), pl.ds(0, cols)],
            l0.at[2],
        ),
        pltpu.make_async_copy(own_forget, forget_all.at[f], l0.at[3]),
        pltpu.make_async_copy(mine, first.block(0), l0.at[0]),
        pltpu.make_async_copy(dy_ref, second.block(0), l0.at[1]),
    ]
    for made in keep:
        made.start()
    for made in mlp_loads:
        made.wait()
    mlp_store = pltpu.make_async_copy(mlp.at[:, pl.ds(EARLY, 3 * fw - EARLY)], mlp_ref, l2.at[7])
    mlp_store.start()
    first_columns = mlp.at[:, pl.ds(0, EARLY)]

    def early_slot(i, owner):
        return early_ref.at[pl.ds(pl.multiple_of(owner * shard, shard), shard)]

    early = Line([first_columns], early_slot, se, re, depth)
    early_keep = pltpu.make_async_copy(first_columns, early_slot(0, f), l2.at[8])
    early_keep.start()
    line.pass_on(1)
    spread.start(l0.at[4])
    early.start(0)
    first.relay()
    second.start()
    line.pass_on(2)
    first.finish()
    for made in keep[2:3]:
        made.wait()
    load = pltpu.make_async_copy(normed_ref, normed, l0.at[5])
    load.start()
    keep[0].wait()
    keep[1].wait()
    r = lax.broadcasted_iota(jnp.int32, (16, 1), 0)
    bias = jnp.zeros((16, 1), F32)
    for h in range(heads):
        bias = jnp.where(r == h, bias_ref[t * heads + h], bias)

    def store(i):
        tokens = rows_of(i, 512)
        return pltpu.make_async_copy(cat.at[:, tokens], cat_ref.at[:, tokens], l1.at[i])

    def add_shard(owner, begin, end):
        small = forget_all[owner].astype(F32)
        tall = jnp.concatenate([small, jnp.zeros((128 - small.shape[0], shard), F32)], axis=0)
        rows = rows_of(owner, shard)
        w_attn_ref[rows, cols:] = tall.T.astype(BF)
        turned[...] = w_attn_ref[rows, :].T

        def tile(i, unused):
            tokens = rows_of(i, 512)
            part = dot(turned[...], normed[tokens, rows], 1, 1)
            if begin:
                cat[:, tokens] = part
            else:
                cat[:, tokens] += part
            if end:
                cat[4 * hw : 4 * hw + 16, tokens] += bias
                store(i).start()
            return unused

        lax.fori_loop(0, normed.shape[0] // 512, tile, 0)

    half = depth // 2
    upper = lax.div(f, half)
    load.wait()
    for k in range(1, depth - 1):
        add_shard(jnp.int32(k), k == 1, False)
    add_shard(upper * (depth - 1), False, False)
    early.pass_on(1)
    second.relay()
    spread.pass_on()
    early.pass_on(2)
    line.pass_on(3)
    add_shard((1 - upper) * (depth - 1), False, True)
    early.pass_on(3)
    second.finish()
    line.finish()
    early.finish()
    early_keep.wait()
    keep[3].wait()
    spread.finish(l0.at[4])
    mlp_store.wait()
    for i in range(normed.shape[0] // 512):
        store(i).wait()


def enter(tokens, cotangent, gain, bias, forget_weight, attn_weights, mlp_weights, out_weight, depth):
    n, w = tokens.shape
    shard, head_count = forget_weight.shape
    heads = head_count // 8
    hw = w // 8
    cols, fw = 4 * hw, mlp_weights[0].shape[1] // 8
    whole = jax.ShapeDtypeStruct((8 * n, w), BF)
    dma = pltpu.SemaphoreType.DMA((Gather.sems,))
    line = pltpu.SemaphoreType.DMA((2, depth - 1, WEIGHT_PIECES + 1))
    early = pltpu.SemaphoreType.DMA((2, depth - 1, 1))
    vmem = pl.BlockSpec(memory_space=pltpu.VMEM)
    smem = pl.BlockSpec(memory_space=pltpu.SMEM)
    anywhere = pl.BlockSpec(memory_space=pl.ANY)
    return pl.pallas_call(
        functools.partial(enter_kernel, depth=depth, heads=heads),
        name="enter",
        out_shape=(
            whole,
            whole,
            jax.ShapeDtypeStruct((depth * shard, cols + 128), BF),
            jax.ShapeDtypeStruct((hw, w), BF),
            jax.ShapeDtypeStruct((cols + 128, 8 * n), F32),
            jax.ShapeDtypeStruct((shard, 3 * fw - EARLY), BF),
            jax.ShapeDtypeStruct((depth * shard, EARLY), BF),
        ),
        in_specs=[vmem, vmem, vmem, smem, vmem] + [anywhere] * 8,
        out_specs=[anywhere, anywhere, vmem, anywhere, anywhere, anywhere, anywhere],
        scratch_shapes=[
            pltpu.VMEM((n, w), BF),
            pltpu.VMEM((4, shard, hw + 64), BF),
            pltpu.VMEM((shard, cols), BF),
            pltpu.VMEM((16, shard), BF),
            pltpu.VMEM((depth, 16, shard), BF),
            pltpu.VMEM((shard, 3 * fw), BF),
            pltpu.VMEM((8 * n, w), BF),
            pltpu.VMEM((cols + 128, shard), BF),
            pltpu.VMEM((cols + 128, 8 * n), F32),
            dma, dma, dma, dma, line, line, early, early,
            pltpu.SemaphoreType.DMA((2, OUT_PIECES)),
            pltpu.SemaphoreType.DMA((OUT_PIECES,)),
            pltpu.SemaphoreType.DMA((6,)),
            pltpu.SemaphoreType.DMA((8 * n // 512,)),
            pltpu.SemaphoreType.DMA((9,)),
        ],
        compiler_params=pltpu.CompilerParams(
            collective_id=1, has_side_effects=True, vmem_limit_bytes=VMEM_BYTES
        ),
        cost_estimate=pl.CostEstimate(
            flops=2 * 8 * n * w * cols, bytes_accessed=4 * 8 * n * w * 2, transcendentals=0
        ),
    )(tokens, cotangent, gain, bias, forget_weight.T, *attn_weights, *mlp_weights, out_weight)


TILE = 256


def middle_kernel(
    gated_ref, w_ref, tok_ref, gain_ref, mid_ref, normed_ref,
    gated, turned, mine, s0, r0, s1, r1, l0, *refs,
):
    c, s, f = here()
    n, width = mine.shape
    h = n // 2
    count = len(refs) // 2
    halves = [PairSum(refs[:count]), PairSum(refs[count:])]
    loads = [
        pltpu.make_async_copy(
            gated_ref.at[:, pl.ds(pl.multiple_of(block * n, n), n)],
            gated.at[:, pl.ds(i * n, n)],
            l0.at[i],
        )
        for i, block in enumerate(PairSum.blocks(c, s))
    ]
    for made in loads:
        made.start()
    greet(partners())
    for made in loads:
        made.wait()
    for q, pairs in enumerate(halves):

        def one_pair(i, unused, q=q, pairs=pairs):
            pairs.between(i)
            for core in (0, 1):
                tokens = pl.ds(pl.multiple_of((2 * i + core) * n + q * h, h), h)
                turned[core * h : (core + 1) * h, :] = gated[:, tokens].T
            for t in range(width // TILE):
                feats = pl.ds(t * TILE, TILE)
                pairs.put(i, feats, dot(turned[...], w_ref[:, feats], 1, 0).astype(BF))
            pairs.to_sibling(i).start()
            return unused

        lax.fori_loop(0, 4, one_pair, 0)
    for pairs in halves:
        pairs.relay()
    gathers = [
        Gather(mine.at[pl.ds(q * h, h)], normed_ref, send, recv, n, q * h)
        for q, (send, recv) in enumerate(((s0, r0), (s1, r1)))
    ]
    keep = []
    for q, pairs in enumerate(halves):
        pairs.arrive()

        def body(i, carry, q=q, pairs=pairs):
            r = pl.ds(pl.multiple_of(q * h + i * STEP, STEP), STEP)
            mid = tok_ref[r, :].astype(F32) + pairs.total(i, STEP)
            mid_ref[r, :] = mid
            mine[r, :] = (mid * mean_square_inverse(mid) * gain_row(gain_ref)).astype(BF)
            return carry

        lax.fori_loop(0, h // STEP, body, 0)
        gathers[q].start()
        keep.append(pltpu.make_async_copy(gathers[q].src, gathers[q].block(0), l0.at[8 + q]))
        keep[q].start()
    for gather in gathers:
        gather.relay()
        gather.finish()
    for pairs in halves:
        pairs.finish()
    for made in keep:
        made.wait()


def middle(gated, w_out, tokens, gain):
    n, w = tokens.shape
    dma = pltpu.SemaphoreType.DMA((16,))
    vmem = pl.BlockSpec(memory_space=pltpu.VMEM)
    anywhere = pl.BlockSpec(memory_space=pl.ANY)
    return pl.pallas_call(
        middle_kernel,
        name="middle",
        out_shape=(jax.ShapeDtypeStruct((n, w), F32), jax.ShapeDtypeStruct((8 * n, w), BF)),
        in_specs=[anywhere, vmem, vmem, vmem],
        out_specs=[vmem, anywhere],
        scratch_shapes=[
            pltpu.VMEM(gated.shape, BF),
            pltpu.VMEM((n, gated.shape[0]), BF),
            pltpu.VMEM((n, w), BF),
            dma, dma, dma, dma, dma,
        ]
        + PairSum.scratch(n // 2, w)
        + PairSum.scratch(n // 2, w),
        compiler_params=pltpu.CompilerParams(
            collective_id=2, has_side_effects=True, vmem_limit_bytes=VMEM_BYTES
        ),
        cost_estimate=pl.CostEstimate(
            flops=2 * 8 * n * w * gated.shape[0], bytes_accessed=4 * 8 * n * w * 2,
            transcendentals=0,
        ),
    )(gated, w_out, tokens, gain)


TERM_PIECES = 4


class LineSum:
    def __init__(self, term, got, send, recv, depth, pieces=TERM_PIECES):
        self.term, self.got, self.send, self.recv, self.depth = term, got, send, recv, depth
        self.c, self.s, self.f = here()
        self.pieces = pieces
        self.n = term.shape[0] // pieces

    def source(self, i, g):
        return self.term.at[pl.ds(i * self.n, self.n), g]

    def copy(self, k, g, i, src):
        to = lax.rem(self.f + (1 if k == 0 else self.depth - 1), self.depth)
        return REMOTE(
            src,
            self.got.at[k, g + k - 1, pl.ds(i * self.n, self.n)],
            self.send.at[k, g, i],
            self.recv.at[k, g, i],
            (self.c, self.s, to),
            MESH,
        )

    def targets(self, k):
        return range(self.depth - 1, 0, -1) if k == 0 else range(self.depth - 1)

    def is_end(self, k):
        return self.f == (0 if k == 0 else self.depth - 1)

    def start_piece(self, i, n):
        for k in (0, 1):
            g = self.targets(k)[n]
            pl.when(self.is_end(k))(self.copy(k, g, i, self.source(i, g)).start)

    def add(self, k, g, i):
        rows = pl.ds(i * self.n, self.n)
        total = self.got[k, g + k - 1, rows].astype(F32) + self.term[rows, g].astype(F32)
        self.got[k, g + k - 1, rows] = total.astype(BF)

    def pass_on(self, i, n, hop):
        for k in (0, 1):
            g = self.targets(k)[n]
            at = hop if k == 0 else self.depth - 1 - hop

            @pl.when(self.f == at)
            def _(k=k, g=g):
                made = self.copy(k, g, i, self.got.at[k, g + k - 1, pl.ds(i * self.n, self.n)])
                made.wait_recv()
                self.add(k, g, i)
                made.start()

    def steps(self):
        todo = [
            (n * self.pieces + i + 2 * (hop - 1), -hop, i, n, hop)
            for n in range(self.depth - 2)
            for hop in range(1, self.depth - 1 - n)
            for i in range(self.pieces)
        ]
        return [step[2:] for step in sorted(todo)]

    def collect(self, i, out):
        rows = pl.ds(i * self.n, self.n)
        for g in range(self.depth):

            @pl.when(self.f == g)
            def _(g=g):
                total = self.term[rows, g].astype(F32)
                for k in (0, 1):
                    if g != (0 if k == 0 else self.depth - 1):
                        self.copy(k, g, i, self.source(i, g)).wait_recv()
                        total = total + self.got[k, g + k - 1, rows].astype(F32)
                out[rows] = total.astype(BF)

    def finish(self):
        for k in (0, 1):
            for g in self.targets(k):
                beyond = self.f < g if k == 0 else self.f > g
                for i in range(self.pieces):
                    pl.when(beyond)(self.copy(k, g, i, self.source(i, g)).wait_send)


class Exchange:
    def __init__(self, rows, out, send, recv, cols=None):
        self.c, self.s, self.f = here()
        self.place = self.c * 4 + self.s
        self.rows, self.out, self.send, self.recv, self.cols = rows, out, send, recv, cols

    def mine(self, j):
        return self.rows.at[j] if self.cols is None else self.rows.at[j, :, self.cols]

    def remote(self, j):
        return REMOTE(
            self.mine(j), self.out.at[self.place], self.send.at[j], self.recv.at[self.place],
            (j // 4, j % 4, self.f), MESH,
        )

    def local(self, j):
        return pltpu.make_async_copy(self.mine(j), self.out.at[j], self.send.at[j])

    def push(self, j):
        pl.when(self.place != j)(self.remote(j).start)
        pl.when(self.place == j)(self.local(j).start)

    def start(self):
        for j in range(8):
            self.push(j)

    def finish(self):
        for j in range(8):
            got = REMOTE(
                self.mine(j), self.out.at[j], self.send.at[j], self.recv.at[j],
                (j // 4, j % 4, self.f), MESH,
            )
            pl.when(self.place != j)(got.wait_recv)
            pl.when(self.place != j)(self.remote(j).wait_send)
            pl.when(self.place == j)(self.local(j).wait)


def plane_peers():
    c, s, f = here()
    return [
        (core, flip(s, k) if k else s, f, k + 4 * i)
        for i, core in enumerate((c, 1 - c))
        for k in range(4)
        if i or k
    ]


def ffn_kernel(
    nm_ref, dy_all_ref, early_ref, mid_ref, gain_ref, gated_ref, w_out_ref, *more, depth,
):
    w_refs, more = more[:depth], more[depth:]
    (
        grad_mid_ref, gain_term_ref, gg_ref, out_term_ref, down_ref, gate_rows_ref, up_own_ref,
    ) = more[:7]
    low_refs, more = more[7 : 7 + depth], more[7 + depth :]
    (
        nm, dy, w, grads, term, got, rows_sum, mine, branch, stage, down_own, down_near, down_far,
        l0, l1, l2, s1, r1, s2, r2, s3, r3, s4, r4, *refs,
    ) = more
    c, s, f = here()
    n, width = mid_ref.shape
    fw = w.shape[1] // 3
    pairs = PairSum(refs)
    loads = []
    w_loads = [
        pltpu.make_async_copy(early_ref, w.at[:, pl.ds(0, EARLY)], l2.at[11]),
    ]
    shard = w_refs[0].shape[0]
    for k, ref in enumerate(w_refs):
        rows = pl.ds(pl.multiple_of(lax.rem(f + depth - k, depth) * shard, shard), shard)
        w_loads.append(
            pltpu.make_async_copy(ref, w.at[rows, pl.ds(EARLY, 3 * fw - EARLY)], l2.at[12 + k])
        )
    for made in w_loads:
        made.start()
    for i, block in enumerate(PairSum.blocks(c, s)):
        src, dst = pl.ds(pl.multiple_of(block * n, n), n), pl.ds(i * n, n)
        made = [
            pltpu.make_async_copy(nm_ref.at[src], nm.at[dst], l0.at[i]),
            pltpu.make_async_copy(dy_all_ref.at[src], dy.at[dst], l1.at[i]),
        ]
        for one in made:
            one.start()
        if i % 2:
            loads[-1] += made
        else:
            loads.append(made)
    greeted = signal_line([p[:3] for p in plane_peers()], depth)
    pl.semaphore_wait(pltpu.get_barrier_semaphore(), greeted)
    for made in w_loads:
        made.wait()

    def one_pair(i, unused):
        rows = rows_of(i, 2 * n)
        wait_for(i, loads)
        for t in range(fw // TILE):
            cols = pl.ds(t * TILE, TILE)
            ups = pl.ds(fw + t * TILE, TILE)
            downs = pl.ds(2 * fw + t * TILE, TILE)
            gate_lin = dot(nm[rows, :], w[:, cols], 1, 0)
            up_lin = dot(nm[rows, :], w[:, ups], 1, 0)
            grad_hidden = dot(dy[rows, :], w[:, downs], 1, 0)
            sig = jax.nn.sigmoid(gate_lin)
            active = gate_lin * sig
            grads[rows, downs] = (active * up_lin).astype(BF)
            grads[rows, cols] = (
                grad_hidden * up_lin * sig * (1.0 + gate_lin * (1.0 - sig))
            ).astype(BF)
            grads[rows, ups] = (grad_hidden * active).astype(BF)
        pairs.between(i)
        for t in range(width // TILE):
            feats = pl.ds(t * TILE, TILE)
            part = dot(grads[rows, 0 : 2 * fw], w[feats, 0 : 2 * fw], 1, 1).astype(BF)
            pairs.put(i, feats, part)
        pairs.to_sibling(i).start()
        return unused

    lax.fori_loop(0, 4, one_pair, 0)
    pairs.relay()

    line = LineSum(term, got, s2, r2, depth)
    deep = width // TERM_PIECES
    per = term.shape[0] // TERM_PIECES
    for i in range(TERM_PIECES):
        feats = pl.ds(i * deep, deep)
        tile = dot(nm[:, feats], grads[:, 0 : 2 * fw], 0, 0).astype(BF)
        term[i * per : (i + 1) * per] = tile.reshape((per,) + term.shape[1:])
        line.start_piece(i, 0)
    for k in range(1, depth - 1):
        for i in range(TERM_PIECES):
            line.start_piece(i, k)
    hw = gated_ref.shape[0]
    w_out, out_term = nm.at[pl.ds(0, hw)], nm.at[pl.ds(hw, hw)]
    w_out_load = pltpu.make_async_copy(w_out_ref, w_out, l2.at[9])
    w_out_load.start()
    todo = line.steps()
    pairs.arrive()

    def body(j, carry):
        r = rows_of(j, STEP)
        grad = pairs.total(j, STEP)
        mid = mid_ref[r, :]
        inverse = mean_square_inverse(mid)
        weighted = grad * gain_row(gain_ref)
        back = inverse * weighted - mid * inverse**3 * jnp.mean(
            weighted * mid, axis=1, keepdims=True
        )
        own_dy = dy[pl.ds(pl.multiple_of(7 * n + j * STEP, STEP), STEP), :]
        grad_mid = own_dy.astype(F32) + back
        grad_mid_ref[r, :] = grad_mid
        mine[r, :] = grad_mid.astype(BF)
        return carry + jnp.sum(grad * mid * inverse, axis=0, keepdims=True)

    gain_term_ref[...] = lax.fori_loop(0, n // STEP, body, jnp.zeros((1, width), F32))
    gather = Gather(mine, branch, s1, r1)
    gather.start()
    keep = pltpu.make_async_copy(mine, gather.block(0), l0.at[8])
    keep.start()
    for i in range(TERM_PIECES):
        feats = pl.ds(i * deep, deep)
        tile = dot(dy[:, feats], grads[:, 2 * fw :], 0, 0).astype(BF)
        tile = tile.reshape((per, depth, term.shape[2], fw))
        for g in range(depth):
            for k in range(depth):

                @pl.when(lax.rem(g + depth - f, depth) == k)
                def _(g=g, k=k, tile=tile):
                    low_refs[k][i * per : (i + 1) * per] = tile[:, g]

        for step in todo[i * 2 : i * 2 + 2]:
            line.pass_on(*step)

    def down_copy(i):
        return REMOTE(
            pairs.out.at[lax.rem(i, 2)], down_near.at[i], s3.at[i], r3.at[i], pairs.sib, MESH
        )

    for i in (2, 3):
        pairs.to_sibling(i).wait_send()

    def down_pair(i, unused):
        rows = rows_of(i, 2 * n)

        @pl.when(i >= 2)
        def _():
            down_copy(i - 2).wait_send()

        for t in range(width // TILE):
            feats = pl.ds(t * TILE, TILE)
            part = dot(grads[rows, 2 * fw :], w[feats, 2 * fw :], 1, 1).astype(BF)
            pairs.out[lax.rem(i, 2), :, feats] = part[:n]
            down_own[i, :, feats] = part[n:]
        down_copy(i).start()
        return unused

    lax.fori_loop(0, 4, down_pair, 0)
    gather.relay()
    for step in todo[2 * TERM_PIECES :]:
        line.pass_on(*step)

    def down_sum(i, unused):
        down_copy(i).wait_recv()

        def body(j, carry):
            r = rows_of(j, 32)
            total = down_own[i, r, :].astype(F32) + down_near[i, r, :].astype(F32)
            down_own[i, r, :] = total.astype(BF)
            return carry

        return lax.fori_loop(0, n // 32, body, unused)

    lax.fori_loop(0, 4, down_sum, 0)
    down_fx = REMOTE(
        down_own.at[0, :, pairs.left], down_far.at[0], s3.at[4], r3.at[4], pairs.x, MESH
    )
    down_fy = REMOTE(
        down_own.at[0, :, pairs.right], down_far.at[1], s3.at[5], r3.at[5], pairs.y, MESH
    )
    down_fx.start()
    down_fy.start()
    gather.finish()
    keep.wait()

    def gg_copy(i):
        return pltpu.make_async_copy(
            stage.at[lax.rem(i, 2)], gg_ref.at[:, rows_of(i, stage.shape[2])], l2.at[lax.rem(i, 2)]
        )

    def gg_tile(i, unused):
        @pl.when(i >= 2)
        def _():
            gg_copy(i - 2).wait()

        stage[lax.rem(i, 2)] = dot(w_out[...], branch[rows_of(i, stage.shape[2]), :], 1, 1)
        gg_copy(i).start()
        return unused

    exchange = Exchange(rows_sum, gate_rows_ref, s4, r4, pl.ds(0, fw))

    def collect(i):
        line.collect(i, rows_sum)
        for j in range(i * per, (i + 1) * per):
            exchange.push(j)

    collect(0)
    collect(1)
    tiles = branch.shape[0] // stage.shape[2]
    w_out_load.wait()
    lax.fori_loop(0, tiles, gg_tile, 0)
    collect(2)
    out_term[...] = dot(gated_ref[...], branch[...], 1, 0).astype(BF)
    out_store = pltpu.make_async_copy(out_term, out_term_ref, l2.at[10])
    out_store.start()

    def down_add(at, cols, slot):
        def body(j, carry):
            r = rows_of(j, 32)
            total = down_own[at, r, cols].astype(F32) + down_far[slot, r, :].astype(F32)
            down_own[at, r, cols] = total.astype(BF)
            return carry

        lax.fori_loop(0, n // 32, body, 0)

    collect(3)
    down_fx.wait_recv()
    down_fy.wait_recv()
    down_add(2, pairs.left, 0)
    down_add(1, pairs.right, 1)
    stores = [
        pltpu.make_async_copy(down_own.at[i], down_ref.at[i - 1], l1.at[i]) for i in (1, 2, 3)
    ]
    for made in stores:
        made.start()
    up_own_ref[...] = rows_sum[:, :, fw:]
    exchange.finish()
    for made in stores:
        made.wait()
    for i in (2, 3):
        gg_copy(jnp.int32(tiles - 4 + i)).wait()
    out_store.wait()
    down_fx.wait_send()
    down_fy.wait_send()
    pairs.finish_plane()
    for i in (2, 3):
        down_copy(i).wait_send()
    line.finish()


def ffn(normed_all, cotangent_all, weights, early, mid, gain, gated, w_out, depth):
    n, width = mid.shape
    fw = (weights[0].shape[1] + EARLY) // 3
    r = width // (8 * depth)
    hw = gated.shape[0]
    dma = pltpu.SemaphoreType.DMA((16,))
    six = pltpu.SemaphoreType.DMA((6,))
    eight = pltpu.SemaphoreType.DMA((8,))
    line = pltpu.SemaphoreType.DMA((2, depth, TERM_PIECES))
    vmem = pl.BlockSpec(memory_space=pltpu.VMEM)
    anywhere = pl.BlockSpec(memory_space=pl.ANY)
    return pl.pallas_call(
        functools.partial(ffn_kernel, depth=depth),
        name="ffn",
        out_shape=(
            jax.ShapeDtypeStruct((n, width), F32),
            jax.ShapeDtypeStruct((1, width), F32),
            jax.ShapeDtypeStruct((hw, 8 * n), F32),
            jax.ShapeDtypeStruct((hw, width), BF),
            jax.ShapeDtypeStruct((3, n, width), BF),
            jax.ShapeDtypeStruct((8, r, fw), BF),
            jax.ShapeDtypeStruct((8, r, fw), BF),
        )
        + (jax.ShapeDtypeStruct((8, r, fw), BF),) * depth,
        in_specs=[anywhere] * 3 + [vmem] * 3 + [anywhere] * (1 + depth),
        out_specs=[vmem, vmem, anywhere, anywhere, anywhere, vmem, vmem] + [vmem] * depth,
        scratch_shapes=[
            pltpu.VMEM((8 * n, width), BF),
            pltpu.VMEM((8 * n, width), BF),
            pltpu.VMEM((width, 3 * fw), BF),
            pltpu.VMEM((8 * n, 3 * fw), BF),
            pltpu.VMEM((8, depth, r, 2 * fw), BF),
            pltpu.VMEM((2, depth - 1, 8, r, 2 * fw), BF),
            pltpu.VMEM((8, r, 2 * fw), BF),
            pltpu.VMEM((n, width), BF),
            pltpu.VMEM((8 * n, width), BF),
            pltpu.VMEM((2, hw, 256), F32),
            pltpu.VMEM((4, n, width), BF),
            pltpu.VMEM((4, n, width), BF),
            pltpu.VMEM((2, n, width // 2), BF),
            dma, dma, dma, dma, dma, line, line, six, six, eight, eight,
        ]
        + PairSum.scratch(n, width),
        compiler_params=pltpu.CompilerParams(
            collective_id=3, has_side_effects=True, vmem_limit_bytes=67_043_328
        ),
        cost_estimate=pl.CostEstimate(
            flops=2 * 8 * n * width * fw * 9, bytes_accessed=4 * 8 * n * width * 2,
            transcendentals=0,
        ),
    )(normed_all, cotangent_all, early, mid, gain, gated, w_out, *weights)


def leave_kernel(
    normed_ref, cat_ref, w_ref, down_ref, tok_ref, grad_mid_ref, mid_ref, gain_ref,
    mlp_term_ref, bias_grad_ref, up_ref, wide_ref, *more, depth, heads,
):
    low_refs, more = more[:depth], more[depth:]
    (
        grad_ref, small_sum_ref, out_ref, attn_rows_ref, low_rows_ref, up_rows_ref, wide_rows_ref,
        normed, cat, turned, w, small, plane_small, line_small, term, got, rows, wide_got, low_sum,
        l0, l1, s2, r2, s3, r3, s5, r5, s6, r6, s7, r7, s8, r8, *refs,
    ) = more
    c, s, f = here()
    n, width = tok_ref.shape
    pairs = PairSum(refs[:7])
    down = PairTail(refs[7:])
    down_loads = [pltpu.make_async_copy(down_ref, down.own, l0.at[9])]
    loads = []
    for i, block in enumerate(PairSum.blocks(c, s)):
        src, dst = pl.ds(pl.multiple_of(block * n, n), n), pl.ds(i * n, n)
        loads.append(pltpu.make_async_copy(cat_ref.at[:, src], cat.at[:, dst], l0.at[i]))
        loads.append(pltpu.make_async_copy(normed_ref.at[src], normed.at[dst], l1.at[i]))
    w_load = pltpu.make_async_copy(w_ref, w, l0.at[8])
    for made in down_loads + loads:
        made.start()
    w_load.start()
    peers = plane_peers()
    line_peers = [(c, s, lax.rem(f + k, depth), k) for k in range(1, depth)]
    greet([p[:3] for p in peers + line_peers])
    wide = LineSum(wide_ref, wide_got, s7, r7, depth, 1)
    for k in range(depth - 1):
        wide.start_piece(0, k)
    line = LineSum(term, got, s3, r3, depth)
    low_total = low_refs[0][...].astype(F32)
    for ref in low_refs[1:]:
        low_total = low_total + ref[...].astype(F32)
    low_sum[...] = low_total.astype(BF)
    low_rows = Exchange(low_sum, low_rows_ref, s6, r6)
    deep = width // TERM_PIECES
    per = term.shape[0] // TERM_PIECES
    low_rows.start()
    up_rows = Exchange(up_ref, up_rows_ref, s8, r8)
    up_rows.start()
    for made in down_loads:
        made.wait()
    down.start(0)
    for made in loads:
        made.wait()
    for i in range(TERM_PIECES):
        tile = dot(cat[...], normed[:, pl.ds(i * deep, deep)], 1, 0).T.astype(BF)
        term[i * per : (i + 1) * per] = tile.reshape((per,) + term.shape[1:])
        line.start_piece(i, 0)
    for k in range(1, depth - 1):
        for i in range(TERM_PIECES):
            line.start_piece(i, k)
    w_load.wait()

    def one_pair(i, unused):
        pairs.between(i)
        turned[...] = cat[:, rows_of(i, 2 * n)].T
        for t in range(width // TILE):
            feats = pl.ds(t * TILE, TILE)
            pairs.put(i, feats, dot(turned[...], w[feats, :], 1, 1).astype(BF))
        pairs.to_sibling(i).start()
        for at in range(4):

            @pl.when(i == at)
            def _(at=at):
                for step in todo[at : at + 1]:
                    line.pass_on(*step)

        return unused

    todo = line.steps()
    for step in wide.steps():
        wide.pass_on(*step)
    lax.fori_loop(0, 4, one_pair, 0)
    for step in todo[4:6]:
        line.pass_on(*step)
    pairs.relay()
    down.start(1)
    for step in todo[6:]:
        line.pass_on(*step)
    attn_rows = Exchange(rows, attn_rows_ref, s5, r5)

    def collect(i):
        line.collect(i, rows)
        for j in range(i * per, (i + 1) * per):
            attn_rows.push(j)

    pairs.arrive()

    def body(i, carry):
        r = rows_of(i, STEP)
        grad = pairs.total(i, STEP)
        tok = tok_ref[r, :].astype(F32)
        inverse = mean_square_inverse(tok)
        weighted = grad * gain_row(gain_ref)
        back = inverse * weighted - tok * inverse**3 * jnp.mean(
            weighted * tok, axis=1, keepdims=True
        )
        grad_ref[r, :] = grad_mid_ref[r, :] + back
        return carry + jnp.sum(grad * tok * inverse, axis=0, keepdims=True)

    gain_term = lax.fori_loop(0, n // STEP, body, jnp.zeros((1, width), F32))
    lane = small.shape[1]
    place = c * 4 + s
    for k in range(3):
        small[k : k + 1, :] = gain_term[:, k * lane : (k + 1) * lane]
        small[3 + k : 4 + k, :] = mlp_term_ref[:, k * lane : (k + 1) * lane]
    at = lax.broadcasted_iota(jnp.int32, (1, lane), 1)
    bias_row = jnp.zeros((1, lane), F32)
    for h in range(heads):
        bias_row = jnp.where(at == place * heads + h, bias_grad_ref[h : h + 1, 0:1], bias_row)
    small[6:7, :] = bias_row
    small[7:8, :] = jnp.zeros((1, lane), F32)
    plane_small[pl.ds(place, 1)] = small[...][None]
    sent = []
    for core, other_s, other_f, k in peers:
        made = REMOTE(
            small, plane_small.at[place], s2.at[k - 1], r2.at[k - 1], (core, other_s, other_f), MESH
        )
        made.start()
        sent.append(made)
    wide.collect(0, wide_rows_ref)
    collect(0)
    collect(1)
    for made in sent:
        made.wait()
    total = plane_small[0]
    for i in range(1, 8):
        total = total + plane_small[i]
    small[...] = total
    line_small[pl.ds(f, 1)] = total[None]
    sent = []
    for core, other_s, other_f, k in line_peers:
        made = REMOTE(
            small, line_small.at[f], s2.at[6 + k], r2.at[6 + k], (core, other_s, other_f), MESH
        )
        made.start()
        sent.append(made)
    collect(2)
    collect(3)
    down.arrive()

    def body2(i, carry):
        r = rows_of(i, STEP)
        out_ref[r, :] = (mid_ref[r, :] + down.total(i, STEP)).astype(BF)
        return carry

    lax.fori_loop(0, n // STEP, body2, 0)
    for made in sent:
        made.wait()
    total = line_small[0]
    for i in range(1, depth):
        total = total + line_small[i]
    small_sum_ref[...] = total
    pairs.finish()
    down.finish()
    line.finish()
    wide.finish()
    low_rows.finish()
    up_rows.finish()
    attn_rows.finish()


def leave(
    normed, cat, w_attn, down_sum, tokens, grad_mid, mid, gain, mlp_term, bias_grad, low, up_own,
    wide, depth, heads,
):
    n, w = grad_mid.shape
    plane = 8
    cols = w_attn.shape[1]
    r = w // (plane * depth)
    sems = pltpu.SemaphoreType.DMA((6 + depth,))
    dma = pltpu.SemaphoreType.DMA((16,))
    eight = pltpu.SemaphoreType.DMA((8,))
    line = pltpu.SemaphoreType.DMA((2, depth, TERM_PIECES))
    one = pltpu.SemaphoreType.DMA((2, depth, 1))
    vmem = pl.BlockSpec(memory_space=pltpu.VMEM)
    anywhere = pl.BlockSpec(memory_space=pl.ANY)
    return pl.pallas_call(
        functools.partial(leave_kernel, depth=depth, heads=heads),
        name="leave",
        out_shape=(
            jax.ShapeDtypeStruct((n, w), F32),
            jax.ShapeDtypeStruct((8, w // 3), F32),
            jax.ShapeDtypeStruct((n, w), BF),
            jax.ShapeDtypeStruct((plane, r, cols), BF),
            jax.ShapeDtypeStruct(low[0].shape, BF),
            jax.ShapeDtypeStruct(up_own.shape, BF),
            jax.ShapeDtypeStruct((1,) + wide.shape[2:], BF),
        ),
        in_specs=[anywhere] * 4 + [vmem] * (8 + depth),
        out_specs=[vmem] * 7,
        scratch_shapes=[
            pltpu.VMEM(normed.shape, BF),
            pltpu.VMEM(cat.shape, BF),
            pltpu.VMEM((2 * n, cols), BF),
            pltpu.VMEM(w_attn.shape, BF),
            pltpu.VMEM((8, w // 3), F32),
            pltpu.VMEM((8, 8, w // 3), F32),
            pltpu.VMEM((depth, 8, w // 3), F32),
            pltpu.VMEM((plane, depth, r, cols), BF),
            pltpu.VMEM((2, depth - 1, plane, r, cols), BF),
            pltpu.VMEM((plane, r, cols), BF),
            pltpu.VMEM((2, depth - 1, 1) + wide.shape[2:], BF),
            pltpu.VMEM(low[0].shape, BF),
            dma, dma, sems, sems, line, line, eight, eight, eight, eight, one, one, eight, eight,
        ]
        + PairSum.scratch(n, w)
        + PairTail.scratch(n, w),
        compiler_params=pltpu.CompilerParams(
            collective_id=4, has_side_effects=True, vmem_limit_bytes=VMEM_BYTES
        ),
        cost_estimate=pl.CostEstimate(
            flops=4 * 8 * n * w * cols, bytes_accessed=4 * 8 * n * w * 2, transcendentals=0
        ),
    )(
        normed, cat, w_attn, down_sum, tokens, grad_mid, mid, gain, mlp_term, bias_grad, up_own,
        wide, *low,
    )


def finish_kernel(
    attn_ref, gate_rows_ref, up_rows_ref, low_ref, small_ref, out_w_ref, block_ref, tok_grad_ref,
    q_ref, k_ref, v_ref, g_ref, f_ref, o_ref, gate_ref, up_ref, down_ref,
    gain1_ref, gain2_ref, bias_ref, out_ref, tokens_ref, *, hw, heads,
):
    plane = attn_ref.shape[0]
    fw = low_ref.shape[2]
    for i, ref in enumerate((q_ref, k_ref, v_ref, g_ref)):
        ref[...] = jnp.concatenate(
            [attn_ref[t, :, i * hw : (i + 1) * hw].astype(F32) for t in range(plane)], axis=1
        )
    a = lax.broadcasted_iota(jnp.int32, (128, 128), 0)
    b = lax.broadcasted_iota(jnp.int32, (128, 128), 1)
    total = jnp.zeros((attn_ref.shape[1], 128), F32)
    for t in range(plane):
        pick = jnp.where((a + t * heads == b) & (a < heads), 1.0, 0.0).astype(BF)
        total = total + dot(attn_ref[t, :, 4 * hw : 4 * hw + 128], pick, 1, 0)
    f_ref[...] = total.T[: f_ref.shape[0]]
    o_ref[...] = out_w_ref[0].astype(F32)
    for t in range(plane):
        cols = slice(t * fw, (t + 1) * fw)
        gate_ref[:, cols] = gate_rows_ref[t].astype(F32)
        up_ref[:, cols] = up_rows_ref[t].astype(F32)
        down_ref[:, cols] = low_ref[t].astype(F32)
    lane = small_ref.shape[1]
    count = gain1_ref.shape[0] // lane
    for k in range(count):
        gain1_ref[k * lane : (k + 1) * lane] = small_ref[k, :]
        gain2_ref[k * lane : (k + 1) * lane] = small_ref[count + k, :]
    bias_ref[...] = small_ref[2 * count : 2 * count + 1, 0 : bias_ref.shape[1]]
    out_ref[...] = block_ref[...]
    tokens_ref[...] = tok_grad_ref[...]


def finish(
    attn_rows, gate_rows, up_rows, low_rows, small, out_w, block_out, tokens_grad, hw, heads
):
    plane, r, _ = attn_rows.shape
    n, w = tokens_grad.shape
    fw = low_rows.shape[2]
    vmem = pl.BlockSpec(memory_space=pltpu.VMEM)
    square = jax.ShapeDtypeStruct((r, plane * hw), F32)
    wide = jax.ShapeDtypeStruct((r, plane * fw), F32)
    row = jax.ShapeDtypeStruct((w,), F32)
    return pl.pallas_call(
        functools.partial(finish_kernel, hw=hw, heads=heads),
        name="finish",
        out_shape=(
            square, square, square, square,
            jax.ShapeDtypeStruct((plane * heads, r), F32),
            jax.ShapeDtypeStruct(out_w.shape[1:], F32),
            wide, wide, wide, row, row,
            jax.ShapeDtypeStruct((1, plane * heads), F32),
            jax.ShapeDtypeStruct((n, w), BF),
            jax.ShapeDtypeStruct((n, w), F32),
        ),
        in_specs=[vmem] * 8,
        out_specs=[vmem] * 14,
        compiler_params=pltpu.CompilerParams(vmem_limit_bytes=VMEM_BYTES),
    )(attn_rows, gate_rows, up_rows, low_rows, small, out_w, block_out, tokens_grad)


BQ = 512
BK = 512
AUG = 128


def dot(a, b, ca, cb):
    return lax.dot_general(a, b, (((ca,), (cb,)), ((), ())), preferred_element_type=F32)


def three_parts(v):
    hi = v.astype(BF).astype(F32)
    mid = (v - hi).astype(BF).astype(F32)
    low = (v - hi - mid).astype(BF).astype(F32)
    return hi, mid, low


def triangle(n, suffix):
    a = lax.broadcasted_iota(jnp.int32, (n, n), 0)
    b = lax.broadcasted_iota(jnp.int32, (n, n), 1)
    return jnp.where(a >= b if suffix else a <= b, 1.0, 0.0).astype(BF)


def log_sigmoid(v):
    return jnp.minimum(v, 0.0) - jnp.log1p(jnp.exp(-jnp.abs(v)))


def doc_starts(lens_ref, pos):
    start, end = jnp.zeros_like(pos), jnp.int32(0)
    for n in range(lens_ref.shape[1]):
        end = end + lens_ref[0, n]
        start = jnp.where(pos >= end, end, start)
    return start


def storage_of(place_ref, p):
    found = jnp.int32(0)
    for n in range(place_ref.shape[1]):
        found = jnp.where(place_ref[0, n] == p, n, found)
    return found


def extend(prefix_row, sign_first):
    hi, mid, low = three_parts(prefix_row)
    r = lax.broadcasted_iota(jnp.int32, (16, prefix_row.shape[1]), 0)
    base = 0 if sign_first else 3
    sign = 1.0 if sign_first else -1.0
    ones = (r >= 3) & (r < 6) if sign_first else r < 3
    out = jnp.where(ones, 1.0, 0.0)
    out = jnp.where(r == base, sign * hi, out)
    out = jnp.where(r == base + 1, sign * mid, out)
    return jnp.where(r == base + 2, sign * low, out)


def lay_out(place_ref, cat_ref, prefix_ref, heads, hd, slab, qa, ka, kta):
    hw = heads * hd
    slabs = cat_ref.shape[1] // slab
    for p in range(slabs):
        src = pl.ds(pl.multiple_of(storage_of(place_ref, p) * slab, slab), slab)
        dst = pl.ds(p * slab, slab)
        for h in range(heads):
            q = cat_ref[h * hd : (h + 1) * hd, src].astype(BF).astype(F32)
            row = prefix_ref[h : h + 1, dst]
            rest = jnp.zeros((AUG - hd - 16, slab), F32)
            qe = jnp.concatenate([q * hd**-0.5, extend(row, True), rest], axis=0)
            qa[h, :, dst] = qe.astype(BF)
            k = cat_ref[hw + h * hd : hw + (h + 1) * hd, src].astype(BF).astype(F32)
            ke = jnp.concatenate([k, extend(row, False), rest], axis=0)
            if kta is not None:
                kta[h, :, dst] = ke.astype(BF)
            ka[h, dst, :] = ke.T.astype(BF)


def attention_kernel(
    place_ref, lens_ref, cat_ref,
    gated_ref, att_ref, exact_ref, lse_ref, prefix_ref,
    qa, ka, va, *, heads, hd, slab,
):
    hw = heads * hd
    tokens = cat_ref.shape[1]
    slabs = tokens // slab
    tri = triangle(slab, False)
    carry = jnp.zeros((16, 1), F32)
    for p in range(slabs):
        src = pl.ds(pl.multiple_of(storage_of(place_ref, p) * slab, slab), slab)
        pre = cat_ref[4 * hw : 4 * hw + 16, src]
        steps = log_sigmoid(pre).astype(BF)
        part = dot(steps, tri, 1, 0) + carry
        prefix_ref[:, p * slab : (p + 1) * slab] = part
        carry = part[:, slab - 1 : slab]
        for h in range(heads):
            va[h, :, p * slab : (p + 1) * slab] = cat_ref[
                2 * hw + h * hd : 2 * hw + (h + 1) * hd, src
            ].astype(BF)
    lay_out(place_ref, cat_ref, prefix_ref, heads, hd, slab, qa, ka, None)
    per = slab // BQ

    def one_query_block(qb, unused):
        q0 = pl.multiple_of(qb * BQ, BQ)
        pos = q0 + lax.broadcasted_iota(jnp.int32, (1, BQ), 1)
        start = doc_starts(lens_ref, pos)
        low = doc_starts(lens_ref, q0) // BK
        inside = lax.broadcasted_iota(jnp.int32, (BK, BQ), 0)

        def one_key_block(kb, held):
            k0 = pl.multiple_of(kb * BK, BK)
            allowed = (inside <= pos - k0) & (inside >= start - k0)
            out = []
            for h in range(heads):
                m, l, acc = held[h]
                st = dot(ka[h, pl.ds(k0, BK), :], qa[h, :, pl.ds(q0, BQ)], 1, 0)
                st = jnp.where(allowed, st, very_low)
                new = jnp.maximum(m, jnp.max(st, axis=0, keepdims=True))
                p = jnp.exp(st - new)
                scale = jnp.exp(m - new)
                l = l * scale + jnp.sum(p, axis=0, keepdims=True)
                acc = acc * scale + dot(va[h, :, pl.ds(k0, BK)], p.astype(BF), 1, 0)
                out.append((new, l, acc))
            return tuple(out)

        begin = tuple(
            (jnp.full((1, BQ), very_low, F32), jnp.zeros((1, BQ), F32), jnp.zeros((hd, BQ), F32))
            for _ in range(heads)
        )
        done = lax.fori_loop(low, (q0 + BQ + BK - 1) // BK, one_key_block, begin)
        dst = pl.ds(pl.multiple_of(storage_of(place_ref, qb // per) * slab + lax.rem(qb, per) * BQ, BQ), BQ)
        for h in range(heads):
            m, l, acc = done[h]
            lse_ref[h : h + 1, pl.ds(q0, BQ)] = m + jnp.log(l)
            exact = acc / l
            rounded = exact.astype(BF)
            exact_ref[h * hd : (h + 1) * hd, dst] = exact
            att_ref[h * hd : (h + 1) * hd, dst] = rounded
            gate = jax.nn.sigmoid(cat_ref[3 * hw + h * hd : 3 * hw + (h + 1) * hd, dst])
            gated_ref[h * hd : (h + 1) * hd, dst] = (rounded.astype(F32) * gate).astype(BF)
        return unused

    lse_ref[...] = jnp.zeros_like(lse_ref)
    lax.fori_loop(0, tokens // BQ, one_query_block, 0)


def attention(place, lens, cat, heads, hd, slab):
    tokens = cat.shape[1]
    hw = heads * hd
    vmem = pl.BlockSpec(memory_space=pltpu.VMEM)
    smem = pl.BlockSpec(memory_space=pltpu.SMEM)
    return pl.pallas_call(
        functools.partial(attention_kernel, heads=heads, hd=hd, slab=slab),
        name="attention",
        out_shape=(
            jax.ShapeDtypeStruct((hw, tokens), BF),
            jax.ShapeDtypeStruct((hw, tokens), BF),
            jax.ShapeDtypeStruct((hw, tokens), F32),
            jax.ShapeDtypeStruct((8, tokens), F32),
            jax.ShapeDtypeStruct((16, tokens), F32),
        ),
        in_specs=[smem, smem, vmem],
        out_specs=[vmem] * 5,
        scratch_shapes=[
            pltpu.VMEM((heads, AUG, tokens), BF),
            pltpu.VMEM((heads, tokens, AUG), BF),
            pltpu.VMEM((heads, hd, tokens), BF),
        ],
        compiler_params=pltpu.CompilerParams(vmem_limit_bytes=VMEM_BYTES),
        cost_estimate=pl.CostEstimate(
            flops=8 * heads * tokens * tokens * hd, bytes_accessed=cat.size * 4,
            transcendentals=heads * tokens * tokens // 2,
        ),
    )(place, lens, cat)


def attention_back_kernel(
    place_ref, lens_ref, cat_ref, gg_ref, att_ref, exact_ref, lse_ref, prefix_ref,
    out_ref, bias_grad_ref,
    qa, ka, kta, va, do, delta_ref, dk, dv, gp, *, heads, hd, slab,
):
    hw = heads * hd
    tokens = cat_ref.shape[1]
    slabs = tokens // slab
    per = slab // BQ
    lay_out(place_ref, cat_ref, prefix_ref, heads, hd, slab, qa, ka, kta)
    delta_ref[...] = jnp.zeros_like(delta_ref)
    gp[...] = jnp.zeros_like(gp)
    dk[...] = jnp.zeros_like(dk)
    dv[...] = jnp.zeros_like(dv)
    out_ref[4 * hw :, :] = jnp.zeros((out_ref.shape[0] - 4 * hw, tokens), BF)
    for p in range(slabs):
        src = pl.ds(pl.multiple_of(storage_of(place_ref, p) * slab, slab), slab)
        dst = pl.ds(p * slab, slab)
        for h in range(heads):
            rows = slice(h * hd, (h + 1) * hd)
            gate = jax.nn.sigmoid(cat_ref[3 * hw + h * hd : 3 * hw + (h + 1) * hd, src])
            gg = gg_ref[rows, src]
            low = (gg * gate).astype(BF)
            do[h, :, dst] = low
            delta_ref[h : h + 1, dst] = jnp.sum(
                low.astype(F32) * exact_ref[rows, src], axis=0, keepdims=True
            )
            gate_grad = gg * att_ref[rows, src].astype(F32) * gate * (1.0 - gate)
            out_ref[3 * hw + h * hd : 3 * hw + (h + 1) * hd, src] = gate_grad.astype(BF)
            v = cat_ref[2 * hw + h * hd : 2 * hw + (h + 1) * hd, src]
            va[h, dst, :] = v.T.astype(BF)

    def one_query_block(qb, unused):
        q0 = pl.multiple_of(qb * BQ, BQ)
        pos = q0 + lax.broadcasted_iota(jnp.int32, (1, BQ), 1)
        start = doc_starts(lens_ref, pos)
        low = doc_starts(lens_ref, q0) // BK
        inside = lax.broadcasted_iota(jnp.int32, (BK, BQ), 0)

        def one_key_block(kb, held):
            k0 = pl.multiple_of(kb * BK, BK)
            keys = pl.ds(k0, BK)
            allowed = (inside <= pos - k0) & (inside >= start - k0)
            out = []
            for h in range(heads):
                queries = qa[h, :, pl.ds(q0, BQ)]
                grads = do[h, :, pl.ds(q0, BQ)]
                st = dot(ka[h, keys, :], queries, 1, 0) - lse_ref[h : h + 1, pl.ds(q0, BQ)]
                p = jnp.exp(jnp.where(allowed, st, very_low))
                dp = dot(va[h, keys, :], grads, 1, 0) - delta_ref[h : h + 1, pl.ds(q0, BQ)]
                ds = (p * dp).astype(BF)
                out.append(held[h] + dot(kta[h, :, keys], ds, 1, 0))
                dk[h, :, keys] += dot(queries, ds, 1, 1)
                dv[h, :, keys] += dot(grads, p.astype(BF), 1, 1)
            return tuple(out)

        begin = tuple(jnp.zeros((AUG, BQ), F32) for _ in range(heads))
        done = lax.fori_loop(low, (q0 + BQ + BK - 1) // BK, one_key_block, begin)
        dst = pl.ds(pl.multiple_of(storage_of(place_ref, qb // per) * slab + lax.rem(qb, per) * BQ, BQ), BQ)
        for h in range(heads):
            out_ref[h * hd : (h + 1) * hd, dst] = (done[h][0:hd, :] * hd**-0.5).astype(BF)
            gp[h : h + 1, pl.ds(q0, BQ)] = done[h][hd : hd + 1, :]
        return unused

    lax.fori_loop(0, tokens // BQ, one_query_block, 0)
    tri = triangle(slab, True)
    carry = jnp.zeros((16, 1), F32)
    bias_grad = jnp.zeros((16, 1), F32)
    for p in reversed(range(slabs)):
        src = pl.ds(pl.multiple_of(storage_of(place_ref, p) * slab, slab), slab)
        dst = pl.ds(p * slab, slab)
        for h in range(heads):
            out_ref[hw + h * hd : hw + (h + 1) * hd, src] = dk[h, 0:hd, dst].astype(BF)
            out_ref[2 * hw + h * hd : 2 * hw + (h + 1) * hd, src] = dv[h, :, dst].astype(BF)
            gp[h : h + 1, dst] = gp[h : h + 1, dst] - dk[h, hd + 3 : hd + 4, dst]
        grad = gp[:, dst]
        total = carry
        for piece in three_parts(grad):
            total = total + dot(piece.astype(BF), tri, 1, 0)
        carry = total[:, 0:1]
        pre = cat_ref[4 * hw : 4 * hw + 16, src]
        low = (total.astype(BF).astype(F32) * jax.nn.sigmoid(-pre)).astype(BF)
        out_ref[4 * hw : 4 * hw + 16, src] = low
        bias_grad = bias_grad + jnp.sum(low.astype(F32), axis=1, keepdims=True)
    bias_grad_ref[...] = jnp.broadcast_to(bias_grad, bias_grad_ref.shape)


def attention_back(place, lens, cat, gg, att, exact, lse, prefix, heads, hd, slab):
    tokens = cat.shape[1]
    vmem = pl.BlockSpec(memory_space=pltpu.VMEM)
    smem = pl.BlockSpec(memory_space=pltpu.SMEM)
    return pl.pallas_call(
        functools.partial(attention_back_kernel, heads=heads, hd=hd, slab=slab),
        name="attention_back",
        out_shape=(
            jax.ShapeDtypeStruct(cat.shape, BF),
            jax.ShapeDtypeStruct((16, 128), F32),
        ),
        in_specs=[smem, smem] + [vmem] * 6,
        out_specs=[vmem] * 2,
        scratch_shapes=[
            pltpu.VMEM((heads, AUG, tokens), BF),
            pltpu.VMEM((heads, tokens, AUG), BF),
            pltpu.VMEM((heads, AUG, tokens), BF),
            pltpu.VMEM((heads, tokens, hd), BF),
            pltpu.VMEM((heads, hd, tokens), BF),
            pltpu.VMEM((8, tokens), F32),
            pltpu.VMEM((heads, AUG, tokens), F32),
            pltpu.VMEM((heads, hd, tokens), F32),
            pltpu.VMEM((16, tokens), F32),
        ],
        compiler_params=pltpu.CompilerParams(vmem_limit_bytes=VMEM_BYTES),
        cost_estimate=pl.CostEstimate(
            flops=20 * heads * tokens * tokens * hd, bytes_accessed=cat.size * 8,
            transcendentals=heads * tokens * tokens // 2,
        ),
    )(place, lens, cat, gg, att, exact, lse, prefix)


def local_plane(
    tokens, out_cotangent, seq_lengths, slab_place, attn_gain, query_weight, key_weight,
    value_weight, outgate_weight, forget_weight, forget_bias, output_weight, mlp_gain,
    gate_weight, up_weight, down_weight,
):
    plane_axes = ("cp", "sp")
    plane = lax.axis_size("cp") * lax.axis_size("sp")
    depth = lax.axis_size("fsdp")
    place = lax.axis_index("cp") * lax.axis_size("sp") + lax.axis_index("sp")
    head_count = forget_weight.shape[1]
    width = tokens.shape[2]
    hd = width // head_count
    heads = head_count // plane
    hw = heads * hd
    fw = gate_weight.shape[1] // plane
    shard = query_weight.shape[0]
    group_rows = tokens.shape[1] * plane
    slab = group_rows // slab_place.shape[1]

    def shift(value, k):
        return lax.ppermute(value, "fsdp", [(j, (j + k) % depth) for j in range(depth)])

    inputs, cotangent = tokens[0], out_cotangent[0]
    normed, cotangent_all, w_attn, w_out, cat, own_mlp, early = enter(
        inputs, cotangent, attn_gain, forget_bias, forget_weight,
        (query_weight, key_weight, value_weight, outgate_weight),
        (gate_weight, up_weight, down_weight), output_weight, depth,
    )
    w_mlp = [own_mlp] + [shift(own_mlp, k) for k in range(1, depth)]
    gated, att, exact, lse, prefix = attention(slab_place, seq_lengths, cat, heads, hd, slab)
    mid, normed_mlp = middle(gated, w_out, inputs, mlp_gain)

    grad_mid, mlp_gain_term, grad_gated, out_term, down_sum, gate_rows, up_own, *low_terms = ffn(
        normed_mlp, cotangent_all, w_mlp, early, mid, mlp_gain, gated, w_out, depth
    )
    low = [low_terms[0]] + [shift(low_terms[k], k) for k in range(1, depth)]

    grad_cat, bias_grad = attention_back(
        slab_place, seq_lengths, cat, grad_gated, att, exact, lse, prefix, heads, hd, slab
    )
    part = width // (plane * depth)
    tokens_grad, small_sum, block_out, attn_rows, low_rows, up_rows, wide_rows = leave(
        normed, grad_cat, w_attn, down_sum, inputs, grad_mid, mid, attn_gain, mlp_gain_term,
        bias_grad, low, up_own,
        out_term.reshape(1, depth, part, width), depth, heads,
    )
    (
        query_grad, key_grad, value_grad, outgate_grad, forget_grad, out_grad, gate_grad, up_grad,
        down_grad, attn_gain_grad, mlp_gain_grad, forget_bias_grad, block_out, tokens_grad,
    ) = finish(
        attn_rows, gate_rows, up_rows, low_rows, small_sum, wide_rows, block_out, tokens_grad,
        hw, heads,
    )
    return (
        block_out[None],
        tokens_grad[None],
        attn_gain_grad,
        query_grad,
        key_grad,
        value_grad,
        outgate_grad,
        forget_grad.T,
        forget_bias_grad[0],
        out_grad,
        mlp_gain_grad,
        gate_grad,
        up_grad,
        down_grad,
    )


def fits_plane(mesh, tokens, slab_place, forget_weight, gate_weight):
    sizes = dict(mesh.shape)
    if (sizes["cp"], sizes["sp"]) != (2, 4):
        return False
    plane = sizes["cp"] * sizes["sp"]
    width = tokens.shape[2]
    head_count = forget_weight.shape[1]
    group_rows = tokens.shape[1]
    slab = group_rows // slab_place.shape[1]
    heads = head_count // plane
    return (
        head_count % plane == 0
        and heads <= 8
        and width // head_count == 64
        and heads % 2 == 1
        and width == 8 * heads * 64
        and slab % 512 == 0
        and group_rows <= 2048
        and width % 768 == 0
        and gate_weight.shape[1] % (128 * plane) == 0
        and width % (16 * plane * sizes["fsdp"]) == 0
        and (group_rows // plane) % 64 == 0
    )


def shard(mesh, fn):
    return jax.shard_map(
        fn,
        mesh=mesh,
        in_specs=(
            P("fsdp", ("cp", "sp"), None),
            P("fsdp", ("cp", "sp"), None),
            P("fsdp", None),
            P("fsdp", None),
            P(),
            P("fsdp", None),
            P("fsdp", None),
            P("fsdp", None),
            P("fsdp", None),
            P("fsdp", None),
            P(),
            P("fsdp", None),
            P(),
            P("fsdp", None),
            P("fsdp", None),
            P("fsdp", None),
        ),
        out_specs=(
            P("fsdp", ("cp", "sp"), None),
            P("fsdp", ("cp", "sp"), None),
            P(),
            P(("cp", "sp", "fsdp"), None),
            P(("cp", "sp", "fsdp"), None),
            P(("cp", "sp", "fsdp"), None),
            P(("cp", "sp", "fsdp"), None),
            P(("cp", "sp", "fsdp"), None),
            P(),
            P(("cp", "sp", "fsdp"), None),
            P(),
            P(("cp", "sp", "fsdp"), None),
            P(("cp", "sp", "fsdp"), None),
            P(("cp", "sp", "fsdp"), None),
        ),
        check_vma=False,
    )


def solution(mesh):
    def run(*args):
        fast = fits_plane(mesh, args[0], args[3], args[9], args[13])
        return shard(mesh, local_plane if fast else local)(*args)

    return run
```

```python
import functools

import jax
import jax.numpy as jnp
from jax import lax
from jax.experimental import pallas as pl
from jax.experimental.pallas import tpu as pltpu
from jax.sharding import PartitionSpec as P

epsilon = 1e-06
very_low = -1e30
MESH = pl.DeviceIdType.MESH
BF = jnp.bfloat16
F32 = jnp.float32
REMOTE = pltpu.make_async_remote_copy
VMEM_BYTES = 60 * 1024 * 1024


def matmul(left, right):
    return jnp.dot(left, right, preferred_element_type=jnp.float32)


def matmul_right_t(left, right):
    return lax.dot_general(
        left, right, (((1,), (1,)), ((), ())), preferred_element_type=jnp.float32
    )


def matmul_left_t(left, right):
    return lax.dot_general(
        left, right, (((0,), (0,)), ((), ())), preferred_element_type=jnp.float32
    )


def rms_inverse(values):
    return lax.rsqrt(jnp.mean(values * values, axis=1, keepdims=True) + epsilon)


def norm_back(upstream, values, inverse, gain):
    weighted = upstream * gain
    return inverse * weighted - values * inverse**3 * jnp.mean(
        weighted * values, axis=1, keepdims=True
    )


def row_layout(place_row, lens_row, count, slab_rows):
    rows = jnp.arange(count, dtype=jnp.int32)
    slab_index = rows // slab_rows
    table = (
        slab_index[:, None] == jnp.arange(place_row.shape[0], dtype=jnp.int32)[None, :]
    ).astype(jnp.int32)
    position = jnp.sum(table * place_row[None, :], axis=1) * slab_rows + rows % slab_rows
    ends = jnp.cumsum(lens_row)
    segment = jnp.sum((position[:, None] >= ends[None, :]).astype(jnp.int32), axis=1)
    return (position, segment)


def forget_prefix(log_all, place_row, slab_rows):
    slabs = place_row.shape[0]
    steps = log_all.astype(jnp.float32).reshape(slabs, slab_rows, -1)
    inside = jnp.cumsum(steps, axis=1)
    totals = inside[:, -1, :]
    earlier = (place_row[None, :] < place_row[:, None]).astype(jnp.float32)
    offsets = jnp.dot(earlier, totals, precision=lax.Precision.HIGHEST)
    return (inside + offsets[:, None, :]).reshape(slabs * slab_rows, -1)


def prefix_back(grad_prefix, place_row, slab_rows):
    slabs = place_row.shape[0]
    steps = grad_prefix.reshape(slabs, slab_rows, -1)
    inside = jnp.flip(jnp.cumsum(jnp.flip(steps, 1), axis=1), 1)
    totals = inside[:, 0, :]
    later = (place_row[None, :] > place_row[:, None]).astype(jnp.float32)
    offsets = jnp.dot(later, totals, precision=lax.Precision.HIGHEST)
    return (inside + offsets[:, None, :]).reshape(slabs * slab_rows, -1)


def local(
    tokens,
    out_cotangent,
    seq_lengths,
    slab_place,
    attn_gain,
    query_weight,
    key_weight,
    value_weight,
    outgate_weight,
    forget_weight,
    forget_bias,
    output_weight,
    mlp_gain,
    gate_weight,
    up_weight,
    down_weight,
):
    seq_devices = lax.axis_size("sp")
    ctx_devices = lax.axis_size("cp")
    ctx_index = lax.axis_index("cp")
    tok_rows = tokens.shape[1]
    model_width = tokens.shape[2]
    head_count = forget_weight.shape[1]
    local_heads = head_count // seq_devices
    head_size = model_width // head_count
    ctx_rows = tok_rows * seq_devices
    group_rows = ctx_rows * ctx_devices
    slab_rows = ctx_rows // 2
    key_block = min(512, group_rows)
    key_blocks = group_rows // key_block
    score_scale = head_size ** (-0.5)
    place_row = slab_place[0]
    lens_row = seq_lengths[0]
    ctx_start = ctx_index * ctx_rows
    inputs = tokens[0]
    input_f = inputs.astype(jnp.float32)
    weights_attn = (
        lax.all_gather(query_weight, "fsdp", axis=0, tiled=True),
        lax.all_gather(key_weight, "fsdp", axis=0, tiled=True),
        lax.all_gather(value_weight, "fsdp", axis=0, tiled=True),
        lax.all_gather(outgate_weight, "fsdp", axis=0, tiled=True),
        lax.all_gather(forget_weight, "fsdp", axis=0, tiled=True),
        lax.all_gather(output_weight, "fsdp", axis=0, tiled=True),
    )
    full_query, full_key, full_value, full_outgate, full_forget, full_output = weights_attn
    inv_first = rms_inverse(input_f)
    normed = (input_f * inv_first * attn_gain).astype(jnp.bfloat16)
    queries = matmul(normed, full_query).astype(jnp.bfloat16)
    keys = matmul(normed, full_key).astype(jnp.bfloat16)
    values = matmul(normed, full_value).astype(jnp.bfloat16)
    out_gate = jax.nn.sigmoid(matmul(normed, full_outgate))
    forget_pre = matmul(normed, full_forget) + forget_bias
    log_forget = jax.nn.log_sigmoid(forget_pre).astype(jnp.bfloat16)
    head_query, head_key, head_value, head_forget = (
        lax.all_to_all(queries, "sp", split_axis=1, concat_axis=0, tiled=True),
        lax.all_to_all(keys, "sp", split_axis=1, concat_axis=0, tiled=True),
        lax.all_to_all(values, "sp", split_axis=1, concat_axis=0, tiled=True),
        lax.all_to_all(log_forget, "sp", split_axis=1, concat_axis=0, tiled=True),
    )
    keys_all, values_all, forget_all = (
        lax.all_gather(head_key, "cp", axis=0, tiled=True),
        lax.all_gather(head_value, "cp", axis=0, tiled=True),
        lax.all_gather(head_forget, "cp", axis=0, tiled=True),
    )
    prefix_all = forget_prefix(forget_all, place_row, slab_rows)
    pos_all, seg_all = row_layout(place_row, lens_row, group_rows, slab_rows)
    query_pos = lax.dynamic_slice_in_dim(pos_all, ctx_start, ctx_rows, 0)
    query_seg = lax.dynamic_slice_in_dim(seg_all, ctx_start, ctx_rows, 0)
    query_prefix = lax.dynamic_slice_in_dim(prefix_all, ctx_start, ctx_rows, 0)
    query_three = head_query.reshape(ctx_rows, local_heads, head_size)
    query_pos_top = jnp.max(query_pos)
    query_seg_low = jnp.min(query_seg)
    query_seg_top = jnp.max(query_seg)
    key_pieces = (
        keys_all.reshape(key_blocks, key_block, local_heads, head_size),
        values_all.reshape(key_blocks, key_block, local_heads, head_size),
        prefix_all.reshape(key_blocks, key_block, local_heads),
        pos_all.reshape(key_blocks, key_block),
        seg_all.reshape(key_blocks, key_block),
    )

    def block_live(key_pos, key_seg):
        return (
            (query_pos_top >= jnp.min(key_pos))
            & (query_seg_top >= jnp.min(key_seg))
            & (jnp.max(key_seg) >= query_seg_low)
        )

    def block_scores(key_piece, key_prefix, key_pos, key_seg):
        raw = (
            jnp.einsum("qhd,khd->hqk", query_three, key_piece, preferred_element_type=jnp.float32)
            * score_scale
        )
        raw = raw + query_prefix.T[:, :, None] - key_prefix.T[:, None, :]
        allowed = (query_pos[:, None] >= key_pos[None, :]) & (
            query_seg[:, None] == key_seg[None, :]
        )
        return (raw, allowed[None, :, :])

    def total_work(carry, piece):
        running_max, running_sum = carry
        key_piece, value_piece, key_prefix, key_pos, key_seg = piece
        raw, allowed = block_scores(key_piece, key_prefix, key_pos, key_seg)
        new_max = jnp.maximum(running_max, jnp.max(jnp.where(allowed, raw, very_low), axis=2))
        terms = jnp.where(allowed, jnp.exp(raw - new_max[:, :, None]), 0.0)
        new_sum = running_sum * jnp.exp(running_max - new_max) + jnp.sum(terms, axis=2)
        return (new_max, new_sum)

    def total_step(carry, piece):
        live = block_live(piece[3], piece[4])
        return (lax.cond(live, total_work, lambda held, unused: held, carry, piece), None)

    start_max = jnp.full((local_heads, ctx_rows), very_low, jnp.float32)
    start_sum = jnp.zeros((local_heads, ctx_rows), jnp.float32)
    (final_max, final_sum), _ = lax.scan(total_step, (start_max, start_sum), key_pieces)
    log_total = final_max + jnp.log(final_sum)

    def output_work(carry, piece):
        coarse, fine = carry
        key_piece, value_piece, key_prefix, key_pos, key_seg = piece
        raw, allowed = block_scores(key_piece, key_prefix, key_pos, key_seg)
        probs = jnp.where(allowed, jnp.exp(raw - log_total[:, :, None]), 0.0)
        rounded = probs.astype(jnp.bfloat16)
        rest = (probs - rounded.astype(jnp.float32)).astype(jnp.bfloat16)
        coarse = coarse + jnp.einsum(
            "hqk,khd->qhd", rounded, value_piece, preferred_element_type=jnp.float32
        )
        fine = fine + jnp.einsum(
            "hqk,khd->qhd", rest, value_piece, preferred_element_type=jnp.float32
        )
        return (coarse, fine)

    def output_step(carry, piece):
        live = block_live(piece[3], piece[4])
        return (lax.cond(live, output_work, lambda held, unused: held, carry, piece), None)

    zero_out = jnp.zeros((ctx_rows, local_heads, head_size), jnp.float32)
    (coarse_out, fine_out), _ = lax.scan(output_step, (zero_out, zero_out), key_pieces)
    exact_out = coarse_out + fine_out
    head_out = coarse_out.reshape(ctx_rows, local_heads * head_size).astype(jnp.bfloat16)
    token_out = lax.all_to_all(head_out, "sp", split_axis=0, concat_axis=1, tiled=True)
    token_out_f = token_out.astype(jnp.float32)
    gated = (token_out_f * out_gate).astype(jnp.bfloat16)
    mid = input_f + matmul(gated, full_output)
    weights_mlp = (
        lax.all_gather(gate_weight, "fsdp", axis=0, tiled=True),
        lax.all_gather(up_weight, "fsdp", axis=0, tiled=True),
        lax.all_gather(down_weight, "fsdp", axis=0, tiled=True),
    )
    full_gate, full_up, full_down = weights_mlp
    inv_second = rms_inverse(mid)
    normed_mlp = (mid * inv_second * mlp_gain).astype(jnp.bfloat16)
    gate_lin = matmul(normed_mlp, full_gate)
    up_lin = matmul(normed_mlp, full_up)
    gate_sig = jax.nn.sigmoid(gate_lin)
    activated = gate_lin * gate_sig
    hidden = (activated * up_lin).astype(jnp.bfloat16)
    block_out = (mid + matmul_right_t(hidden, full_down)).astype(jnp.bfloat16)
    cotangent = out_cotangent[0]
    grad_hidden = matmul(cotangent, full_down)
    grad_gate_lin = (grad_hidden * up_lin * gate_sig * (1.0 + gate_lin * (1.0 - gate_sig))).astype(
        jnp.bfloat16
    )
    grad_up_lin = (grad_hidden * activated).astype(jnp.bfloat16)
    grad_normed_mlp = matmul_right_t(grad_gate_lin, full_gate) + matmul_right_t(
        grad_up_lin, full_up
    )
    mlp_gain_term = jnp.sum(grad_normed_mlp * mid * inv_second, axis=0)
    grad_mid = cotangent.astype(jnp.float32) + norm_back(grad_normed_mlp, mid, inv_second, mlp_gain)
    gate_term = matmul_left_t(normed_mlp, grad_gate_lin)
    up_term = matmul_left_t(normed_mlp, grad_up_lin)
    down_term = matmul_left_t(cotangent, hidden)
    grad_branch = grad_mid.astype(jnp.bfloat16)
    grad_gated = matmul_right_t(grad_branch, full_output)
    grad_attended = (grad_gated * out_gate).astype(jnp.bfloat16)
    grad_gate_pre = (grad_gated * token_out_f * out_gate * (1.0 - out_gate)).astype(jnp.bfloat16)
    head_grad = lax.all_to_all(grad_attended, "sp", split_axis=1, concat_axis=0, tiled=True)
    grad_three = head_grad.reshape(ctx_rows, local_heads, head_size)
    delta = jnp.sum(grad_three.astype(jnp.float32) * exact_out, axis=2).T

    def back_work(carry, piece):
        grad_query_acc, grad_prefix_acc = carry
        key_piece, value_piece, key_prefix, key_pos, key_seg = piece
        raw, allowed = block_scores(key_piece, key_prefix, key_pos, key_seg)
        probs = jnp.where(allowed, jnp.exp(raw - log_total[:, :, None]), 0.0)
        rounded = probs.astype(jnp.bfloat16)
        grad_probs = jnp.einsum(
            "qhd,khd->hqk", grad_three, value_piece, preferred_element_type=jnp.float32
        )
        grad_scores = (probs * (grad_probs - delta[:, :, None])).astype(jnp.bfloat16)
        grad_query_acc = (
            grad_query_acc
            + jnp.einsum("hqk,khd->qhd", grad_scores, key_piece, preferred_element_type=jnp.float32)
            * score_scale
        )
        key_term = (
            jnp.einsum("hqk,qhd->khd", grad_scores, query_three, preferred_element_type=jnp.float32)
            * score_scale
        )
        value_term = jnp.einsum(
            "hqk,qhd->khd", rounded, grad_three, preferred_element_type=jnp.float32
        )
        score_f = grad_scores.astype(jnp.float32)
        grad_prefix_acc = grad_prefix_acc + jnp.sum(score_f, axis=2)
        prefix_term = -jnp.sum(score_f, axis=1)
        return ((grad_query_acc, grad_prefix_acc), (key_term, value_term, prefix_term))

    def back_skip(carry, piece):
        empty_kv = jnp.zeros((key_block, local_heads, head_size), jnp.float32)
        empty_prefix = jnp.zeros((local_heads, key_block), jnp.float32)
        return (carry, (empty_kv, empty_kv, empty_prefix))

    def back_step(carry, piece):
        live = block_live(piece[3], piece[4])
        return lax.cond(live, back_work, back_skip, carry, piece)

    start_prefix = jnp.zeros((local_heads, ctx_rows), jnp.float32)
    (grad_query_acc, grad_prefix_q), (key_terms, value_terms, prefix_terms) = lax.scan(
        back_step, (zero_out, start_prefix), key_pieces
    )
    keys_grad_all = key_terms.reshape(group_rows, local_heads * head_size)
    values_grad_all = value_terms.reshape(group_rows, local_heads * head_size)
    prefix_grad_all = jnp.transpose(prefix_terms, (0, 2, 1)).reshape(group_rows, local_heads)
    own_prefix = lax.dynamic_slice_in_dim(prefix_grad_all, ctx_start, ctx_rows, 0)
    prefix_grad_all = lax.dynamic_update_slice_in_dim(
        prefix_grad_all, own_prefix + grad_prefix_q.T, ctx_start, 0
    )
    forget_grad_term = prefix_back(prefix_grad_all, place_row, slab_rows)
    key_sum, value_sum, forget_sum = (
        lax.psum_scatter(keys_grad_all, "cp", scatter_dimension=0, tiled=True),
        lax.psum_scatter(values_grad_all, "cp", scatter_dimension=0, tiled=True),
        lax.psum_scatter(forget_grad_term, "cp", scatter_dimension=0, tiled=True),
    )
    grad_query_head = grad_query_acc.reshape(ctx_rows, local_heads * head_size).astype(jnp.bfloat16)
    grad_query_tok, grad_key_tok, grad_value_tok, grad_forget_tok = (
        lax.all_to_all(grad_query_head, "sp", split_axis=0, concat_axis=1, tiled=True),
        lax.all_to_all(key_sum.astype(jnp.bfloat16), "sp", split_axis=0, concat_axis=1, tiled=True),
        lax.all_to_all(
            value_sum.astype(jnp.bfloat16), "sp", split_axis=0, concat_axis=1, tiled=True
        ),
        lax.all_to_all(
            forget_sum.astype(jnp.bfloat16), "sp", split_axis=0, concat_axis=1, tiled=True
        ),
    )
    grad_forget_pre = (grad_forget_tok.astype(jnp.float32) * jax.nn.sigmoid(-forget_pre)).astype(
        jnp.bfloat16
    )
    grad_normed = (
        matmul_right_t(grad_query_tok, full_query)
        + matmul_right_t(grad_key_tok, full_key)
        + matmul_right_t(grad_value_tok, full_value)
        + matmul_right_t(grad_gate_pre, full_outgate)
        + matmul_right_t(grad_forget_pre, full_forget)
    )
    attn_gain_term = jnp.sum(grad_normed * input_f * inv_first, axis=0)
    bias_term = jnp.sum(grad_forget_pre.astype(jnp.float32), axis=0)
    tokens_grad = grad_mid + norm_back(grad_normed, input_f, inv_first, attn_gain)
    query_term = matmul_left_t(normed, grad_query_tok)
    key_term_w = matmul_left_t(normed, grad_key_tok)
    value_term_w = matmul_left_t(normed, grad_value_tok)
    outgate_term = matmul_left_t(normed, grad_gate_pre)
    forget_term = matmul_left_t(normed, grad_forget_pre)
    output_term = matmul_left_t(gated, grad_branch)
    (
        query_grad,
        key_grad,
        value_grad,
        outgate_grad,
        forget_grad,
        output_weight_grad,
        gate_grad,
        up_grad,
        down_grad,
    ) = (
        lax.psum_scatter(query_term, ("cp", "sp", "fsdp"), scatter_dimension=0, tiled=True),
        lax.psum_scatter(key_term_w, ("cp", "sp", "fsdp"), scatter_dimension=0, tiled=True),
        lax.psum_scatter(value_term_w, ("cp", "sp", "fsdp"), scatter_dimension=0, tiled=True),
        lax.psum_scatter(outgate_term, ("cp", "sp", "fsdp"), scatter_dimension=0, tiled=True),
        lax.psum_scatter(forget_term, ("cp", "sp", "fsdp"), scatter_dimension=0, tiled=True),
        lax.psum_scatter(output_term, ("cp", "sp", "fsdp"), scatter_dimension=0, tiled=True),
        lax.psum_scatter(gate_term, ("cp", "sp", "fsdp"), scatter_dimension=0, tiled=True),
        lax.psum_scatter(up_term, ("cp", "sp", "fsdp"), scatter_dimension=0, tiled=True),
        lax.psum_scatter(down_term, ("cp", "sp", "fsdp"), scatter_dimension=0, tiled=True),
    )
    attn_gain_grad, mlp_gain_grad, forget_bias_grad = lax.psum(
        (attn_gain_term, mlp_gain_term, bias_term), ("cp", "sp", "fsdp")
    )
    return (
        block_out[None],
        tokens_grad[None],
        attn_gain_grad,
        query_grad,
        key_grad,
        value_grad,
        outgate_grad,
        forget_grad,
        forget_bias_grad,
        output_weight_grad,
        mlp_gain_grad,
        gate_grad,
        up_grad,
        down_grad,
    )


def here():
    return (lax.axis_index("cp"), lax.axis_index("sp"), lax.axis_index("fsdp"))


def flip(s, k):
    if k == 1:
        return s + 1 - 2 * lax.rem(s, 2)
    if k == 2:
        return lax.rem(s + 2, 4)
    return 3 - s


def greet(devices):
    sem = pltpu.get_barrier_semaphore()
    for device in devices:
        pl.semaphore_signal(sem, inc=1, device_id=device, device_id_type=MESH)
    pl.semaphore_wait(sem, len(devices))


def signal_line(devices, depth):
    c, s, f = here()
    sem = pltpu.get_barrier_semaphore()
    for device in devices:
        pl.semaphore_signal(sem, inc=1, device_id=device, device_id_type=MESH)

    @pl.when(f < depth - 1)
    def _():
        up = (c, s, lax.rem(f + 1, depth))
        pl.semaphore_signal(sem, inc=1, device_id=up, device_id_type=MESH)

    @pl.when(f > 0)
    def _():
        down = (c, s, lax.rem(f + depth - 1, depth))
        pl.semaphore_signal(sem, inc=1, device_id=down, device_id_type=MESH)

    neighbours = lax.div(f + depth - 1, depth) + lax.div(2 * depth - 2 - f, depth)
    return len(devices) + neighbours


def rows_of(index, count):
    return pl.ds(pl.multiple_of(index * count, count), count)


def row_loop(total, step, body):
    def one(i, carry):
        return body(rows_of(i, step), carry)

    return one, total // step


class Gather:
    sems = 13

    def __init__(self, src, out, send, recv, stride=None, offset=0):
        c, s, f = here()
        self.src, self.out, self.send, self.recv = src, out, send, recv
        self.c, self.s, self.rows = c, s, src.shape[0]
        self.stride, self.offset = stride or self.rows, offset
        self.x, self.y, self.sib = (c, flip(s, 1), f), (c, flip(s, 2), f), (1 - c, s, f)
        self.made = []

    def block(self, k, half=None):
        index = self.c * 4 + (self.s if k == 0 else flip(self.s, k))
        n = self.rows
        begin = index * self.stride + self.offset
        if half is None:
            return self.out.at[pl.ds(pl.multiple_of(begin, n), n)]
        return self.out.at[pl.ds(pl.multiple_of(begin + half * (n // 2), n // 2), n // 2)]

    def copy(self, src, dst, k, device):
        made = REMOTE(src, dst, self.send.at[k], self.recv.at[k], device, MESH)
        made.start()
        self.made.append(made)
        return made

    def start(self):
        half = self.rows // 2
        low, high = self.src.at[pl.ds(0, half)], self.src.at[pl.ds(half, half)]
        self.a = [
            self.copy(low, self.block(0, 0), 0, self.x),
            self.copy(high, self.block(0, 1), 1, self.y),
            self.copy(high, self.block(0, 1), 2, self.x),
            self.copy(low, self.block(0, 0), 3, self.y),
        ]
        self.g = [self.copy(self.src, self.block(0), 4, self.sib)]

    def pass_on(self, ref, k):
        self.g.append(self.copy(ref, ref, k, self.sib))

    def relay(self):
        self.a[0].wait_recv()
        self.b0 = self.copy(self.block(1, 0), self.block(1, 0), 5, self.y)
        self.a[1].wait_recv()
        self.b1 = self.copy(self.block(2, 1), self.block(2, 1), 6, self.x)
        self.pass_on(self.block(1, 0), 7)
        self.pass_on(self.block(2, 1), 8)
        self.a[2].wait_recv()
        self.pass_on(self.block(1, 1), 9)
        self.a[3].wait_recv()
        self.pass_on(self.block(2, 0), 10)

    def finish(self):
        self.b0.wait_recv()
        self.pass_on(self.block(3, 0), 11)
        self.b1.wait_recv()
        self.pass_on(self.block(3, 1), 12)
        for made in self.g:
            made.wait_recv()
        for made in self.made:
            made.wait_send()


class PairSum:
    order = (3, 1, 2, 0)

    @staticmethod
    def scratch(n, w):
        return [
            pltpu.VMEM((4, n, w), BF),
            pltpu.VMEM((4, n, w), BF),
            pltpu.VMEM((2, n, w), BF),
            pltpu.VMEM((4, n, w // 2), BF),
            pltpu.VMEM((2, n, w // 2), BF),
            pltpu.SemaphoreType.DMA((10,)),
            pltpu.SemaphoreType.DMA((10,)),
        ]

    def __init__(self, refs):
        self.own, self.near, self.out, self.far, self.last, self.send, self.recv = refs
        self.x, self.y, self.sib = partners()
        self.n, w = self.own.shape[1], self.own.shape[2]
        self.left, self.right = pl.ds(0, w // 2), pl.ds(w // 2, w // 2)
        self.fx = self.copy(self.own.at[0, :, self.left], self.far.at[1], 4, self.x)
        self.fy = self.copy(self.own.at[0, :, self.right], self.far.at[3], 5, self.y)
        self.nx = self.copy(self.own.at[1, :, self.left], self.far.at[0], 6, self.x)
        self.ny = self.copy(self.own.at[2, :, self.right], self.far.at[2], 7, self.y)
        self.by = self.copy(self.own.at[2, :, self.left], self.last.at[0], 8, self.y)
        self.bx = self.copy(self.own.at[1, :, self.right], self.last.at[1], 9, self.x)

    @staticmethod
    def blocks(c, s):
        return [
            core * 4 + (flip(s, k) if k else s) for k in PairSum.order for core in (1 - c, c)
        ]

    def copy(self, src, dst, k, device):
        return REMOTE(src, dst, self.send.at[k], self.recv.at[k], device, MESH)

    def to_sibling(self, i):
        return self.copy(self.out.at[lax.rem(i, 2)], self.near.at[i], i, self.sib)

    def combine(self, i):
        self.to_sibling(i).wait_recv()

        def body(j, carry):
            r = rows_of(j, 32)
            total = self.own[i, r, :].astype(F32) + self.near[i, r, :].astype(F32)
            self.own[i, r, :] = total.astype(BF)
            return carry

        lax.fori_loop(0, self.n // 32, body, 0)

    def between(self, i):
        @pl.when(i >= 1)
        def _():
            self.combine(i - 1)

        @pl.when(i == 1)
        def _():
            self.fx.start()
            self.fy.start()

        pl.when(i == 2)(self.nx.start)
        pl.when(i == 3)(self.ny.start)

        @pl.when(i >= 2)
        def _():
            self.to_sibling(i - 2).wait_send()

    def put(self, i, cols, part):
        self.out[lax.rem(i, 2), :, cols] = part[: self.n]
        self.own[i, :, cols] = part[self.n :]

    def add(self, at, cols, slot):
        def body(j, carry):
            r = rows_of(j, 32)
            total = self.own[at, r, cols].astype(F32) + self.far[slot, r, :].astype(F32)
            self.own[at, r, cols] = total.astype(BF)
            return carry

        lax.fori_loop(0, self.n // 32, body, 0)

    def relay(self):
        self.fx.wait_recv()
        self.add(2, self.left, 1)
        self.by.start()
        self.fy.wait_recv()
        self.add(1, self.right, 3)
        self.bx.start()

    def arrive(self):
        self.to_sibling(3).wait_recv()
        for made in (self.nx, self.ny, self.by, self.bx):
            made.wait_recv()

    def total(self, j, step):
        r = rows_of(j, step)
        total = self.own[3, r, :].astype(F32) + self.near[3, r, :].astype(F32)
        a = jnp.concatenate([self.far[0, r, :], self.far[2, r, :]], axis=1).astype(F32)
        b = jnp.concatenate([self.last[0, r, :], self.last[1, r, :]], axis=1).astype(F32)
        return total + a + b

    def finish_plane(self):
        for made in (self.fx, self.fy, self.nx, self.ny, self.by, self.bx):
            made.wait_send()

    def finish(self):
        self.finish_plane()
        for i in (2, 3):
            self.to_sibling(i).wait_send()


class PairTail:
    @staticmethod
    def scratch(n, w):
        return [
            pltpu.VMEM((3, n, w), BF),
            pltpu.VMEM((4, n, w // 2), BF),
            pltpu.SemaphoreType.DMA((4,)),
            pltpu.SemaphoreType.DMA((4,)),
        ]

    def __init__(self, refs):
        self.own, self.far, send, recv = refs
        x, y, sib = partners()
        w = self.own.shape[2]
        left, right = pl.ds(0, w // 2), pl.ds(w // 2, w // 2)
        self.made = [
            REMOTE(src, self.far.at[i], send.at[i], recv.at[i], device, MESH)
            for i, (src, device) in enumerate((
                (self.own.at[0, :, left], x),
                (self.own.at[0, :, right], x),
                (self.own.at[1, :, left], y),
                (self.own.at[1, :, right], y),
            ))
        ]

    def start(self, part):
        for made in self.made[part::2]:
            made.start()

    def arrive(self):
        for made in self.made:
            made.wait_recv()

    def total(self, j, step):
        r = rows_of(j, step)
        total = self.own[2, r, :].astype(F32)
        a = jnp.concatenate([self.far[0, r, :], self.far[1, r, :]], axis=1).astype(F32)
        b = jnp.concatenate([self.far[2, r, :], self.far[3, r, :]], axis=1).astype(F32)
        return total + a + b

    def finish(self):
        for made in self.made:
            made.wait_send()


def wait_for(i, loads):
    for at, pair in enumerate(loads):

        @pl.when(i == at)
        def _(pair=pair):
            for made in pair:
                made.wait()


def partners():
    c, s, f = here()
    return [(c, flip(s, 1), f), (c, flip(s, 2), f), (1 - c, s, f)]


STEP = 32


def gain_row(ref):
    return ref[...].reshape(1, ref.shape[0])


def mean_square_inverse(values):
    return lax.rsqrt(jnp.mean(values * values, axis=1, keepdims=True) + epsilon)


class Line:
    def __init__(self, own, slot, send, recv, depth):
        self.own, self.slot, self.send, self.recv, self.depth = own, slot, send, recv, depth
        self.c, self.s, self.f = here()

    def copy(self, i, distance, up):
        owner = self.f - (distance - 1) if up else self.f + (distance - 1)
        to = lax.rem(self.f + (1 if up else self.depth - 1), self.depth)
        src = self.own[i] if distance == 1 else self.slot(i, owner)
        k = 0 if up else 1
        return REMOTE(
            src,
            self.slot(i, owner),
            self.send.at[k, distance - 1, i],
            self.recv.at[k, distance - 1, i],
            (self.c, self.s, to),
            MESH,
        )

    def may_send(self, distance, up):
        if up:
            return (self.f < self.depth - 1) & (self.f >= distance - 1)
        return (self.f > 0) & (self.f + distance <= self.depth)

    def gets(self, distance, up):
        return self.f >= distance if up else self.f + distance < self.depth

    def start(self, i):
        for up in (True, False):
            pl.when(self.may_send(1, up))(self.copy(i, 1, up).start)

    def pass_on(self, distance):
        for i in range(len(self.own)):
            for up in (True, False):
                pl.when(self.gets(distance, up))(self.got(i, distance, up).wait_recv)
                if distance < self.depth - 1:
                    pl.when(self.may_send(distance + 1, up))(self.copy(i, distance + 1, up).start)

    def got(self, i, distance, up):
        owner = self.f - distance if up else self.f + distance
        k = 0 if up else 1
        place = self.slot(i, owner)
        return REMOTE(
            place,
            place,
            self.send.at[k, distance - 1, i],
            self.recv.at[k, distance - 1, i],
            (self.c, self.s, lax.rem(self.f + (self.depth - 1 if up else 1), self.depth)),
            MESH,
        )

    def finish(self):
        for distance in range(1, self.depth):
            for i in range(len(self.own)):
                for up in (True, False):
                    pl.when(self.may_send(distance, up))(self.copy(i, distance, up).wait_send)


class Spread:
    def __init__(self, src, dst, origin, send, recv, depth, pieces):
        self.c, self.s, self.f = here()
        self.src, self.dst, self.origin, self.depth = src, dst, origin, depth
        self.send, self.recv, self.pieces = send, recv, pieces
        self.n = dst.shape[0] // pieces

    def part(self, ref, i):
        return ref.at[pl.ds(i * self.n, self.n)]

    def copy(self, i, up, first):
        k = 0 if up else 1
        return REMOTE(
            self.part(self.src if first else self.dst, i),
            self.part(self.dst, i),
            self.send.at[k, i],
            self.recv.at[i],
            (self.c, self.s, lax.rem(self.f + (1 if up else self.depth - 1), self.depth)),
            MESH,
        )

    def above(self):
        return (self.f > self.origin) & (self.f < self.depth - 1)

    def below(self):
        return (self.f < self.origin) & (self.f > 0)

    def start(self, local):
        first = self.f == self.origin

        @pl.when(first)
        def _():
            pltpu.make_async_copy(self.src, self.dst, local).start()

        for i in range(self.pieces):
            pl.when(first & (self.f < self.depth - 1))(self.copy(i, True, True).start)
            pl.when(first & (self.f > 0))(self.copy(i, False, True).start)

    def pass_on(self):
        for i in range(self.pieces):
            pl.when(self.f != self.origin)(self.copy(i, True, False).wait_recv)
            pl.when(self.above())(self.copy(i, True, False).start)
            pl.when(self.below())(self.copy(i, False, False).start)

    def finish(self, local):
        first = self.f == self.origin

        @pl.when(first)
        def _():
            pltpu.make_async_copy(self.src, self.dst, local).wait()

        for i in range(self.pieces):
            pl.when((first & (self.f < self.depth - 1)) | self.above())(
                self.copy(i, True, False).wait_send
            )
            pl.when((first & (self.f > 0)) | self.below())(self.copy(i, False, False).wait_send)


WEIGHT_PIECES = 4
OUT_PIECES = 2
EARLY = 128


def enter_kernel(
    tok_ref, dy_ref, gain_ref, bias_ref, forget_ref,
    query_ref, key_ref, value_ref, outgate_ref, gate_ref, up_ref, down_ref, out_w_ref,
    normed_ref, dy_all_ref, w_attn_ref, w_out_ref, cat_ref, mlp_ref, early_ref,
    mine, windows, attn, own_forget, forget_all, mlp, normed, turned, cat,
    s0, r0, s1, r1, sz, rz, se, re, so, ro, l0, l1, l2, *, depth, heads,
):
    c, s, f = here()
    t = c * 4 + s
    n = tok_ref.shape[0]
    shard, cols = attn.shape
    hw = cols // 4
    fw = mlp.shape[1] // 3
    base = ((t * hw) // 128) * 128
    window = pl.ds(pl.multiple_of(base, 128), windows.shape[2])
    slices = [
        pltpu.make_async_copy(ref.at[:, window], windows.at[i], l2.at[i])
        for i, ref in enumerate((query_ref, key_ref, value_ref, outgate_ref))
    ]
    hidden = pl.ds(pl.multiple_of(t * fw, fw), fw)
    mlp_loads = [
        pltpu.make_async_copy(ref.at[:, hidden], mlp.at[:, pl.ds(i * fw, fw)], l2.at[4 + i])
        for i, ref in enumerate((gate_ref, up_ref, down_ref))
    ]
    for made in slices + mlp_loads:
        made.start()
    greeted = signal_line(partners(), depth)
    gain = gain_ref[...].reshape(1, gain_ref.shape[0])

    def body(i, carry):
        r = rows_of(i, STEP)
        v = tok_ref[r, :].astype(F32)
        mine[r, :] = (v * mean_square_inverse(v) * gain).astype(BF)
        return carry

    lax.fori_loop(0, n // STEP, body, 0)
    a = lax.broadcasted_iota(jnp.int32, (own_forget.shape[0], forget_ref.shape[0]), 0)
    b = lax.broadcasted_iota(jnp.int32, (own_forget.shape[0], forget_ref.shape[0]), 1)
    pick = jnp.where((b == a + t * heads) & (a < heads), 1.0, 0.0).astype(BF)
    own_forget[...] = dot(pick, forget_ref[...], 1, 0).astype(BF)
    for made in slices:
        made.wait()

    step = shard // WEIGHT_PIECES
    own = [attn.at[pl.ds(i * step, step)] for i in range(WEIGHT_PIECES)] + [own_forget]

    def slot(i, owner):
        if i == WEIGHT_PIECES:
            return forget_all.at[owner]
        rows = pl.ds(pl.multiple_of(owner * shard + i * step, step), step)
        return w_attn_ref.at[rows, pl.ds(0, cols)]

    line = Line(own, slot, sz, rz, depth)
    pl.semaphore_wait(pltpu.get_barrier_semaphore(), greeted)
    first = Gather(mine, normed_ref, s0, r0)
    second = Gather(dy_ref, dy_all_ref, s1, r1)
    first.start()
    for i in range(WEIGHT_PIECES):
        rows = slice(i * step, (i + 1) * step)
        for begin in (0, 64):

            @pl.when(t * hw - base == begin)
            def _(rows=rows, begin=begin):
                attn[rows, :] = jnp.concatenate(
                    [windows[k, rows, begin : begin + hw].astype(F32) for k in range(4)], axis=1
                ).astype(BF)

        line.start(i)
    line.start(WEIGHT_PIECES)
    heads_rows = w_out_ref.shape[0]
    origin = (t * heads_rows) // shard
    spread = Spread(
        out_w_ref.at[pl.ds(pl.multiple_of(t * heads_rows - origin * shard, heads_rows), heads_rows)],
        w_out_ref, origin, so, ro, depth, OUT_PIECES,
    )
    keep = [
        pltpu.make_async_copy(
            attn,
            w_attn_ref.at[pl.ds(pl.multiple_of(f * shard, shard), shard), pl.ds(0, cols)],
            l0.at[2],
        ),
        pltpu.make_async_copy(own_forget, forget_all.at[f], l0.at[3]),
        pltpu.make_async_copy(mine, first.block(0), l0.at[0]),
        pltpu.make_async_copy(dy_ref, second.block(0), l0.at[1]),
    ]
    for made in keep:
        made.start()
    for made in mlp_loads:
        made.wait()
    mlp_store = pltpu.make_async_copy(mlp.at[:, pl.ds(EARLY, 3 * fw - EARLY)], mlp_ref, l2.at[7])
    mlp_store.start()
    first_columns = mlp.at[:, pl.ds(0, EARLY)]

    def early_slot(i, owner):
        return early_ref.at[pl.ds(pl.multiple_of(owner * shard, shard), shard)]

    early = Line([first_columns], early_slot, se, re, depth)
    early_keep = pltpu.make_async_copy(first_columns, early_slot(0, f), l2.at[8])
    early_keep.start()
    line.pass_on(1)
    spread.start(l0.at[4])
    early.start(0)
    first.relay()
    second.start()
    line.pass_on(2)
    first.finish()
    for made in keep[2:3]:
        made.wait()
    load = pltpu.make_async_copy(normed_ref, normed, l0.at[5])
    load.start()
    keep[0].wait()
    keep[1].wait()
    r = lax.broadcasted_iota(jnp.int32, (16, 1), 0)
    bias = jnp.zeros((16, 1), F32)
    for h in range(heads):
        bias = jnp.where(r == h, bias_ref[t * heads + h], bias)

    def store(i):
        tokens = rows_of(i, 512)
        return pltpu.make_async_copy(cat.at[:, tokens], cat_ref.at[:, tokens], l1.at[i])

    def add_shard(owner, begin, end):
        small = forget_all[owner].astype(F32)
        tall = jnp.concatenate([small, jnp.zeros((128 - small.shape[0], shard), F32)], axis=0)
        rows = rows_of(owner, shard)
        w_attn_ref[rows, cols:] = tall.T.astype(BF)
        turned[...] = w_attn_ref[rows, :].T

        def tile(i, unused):
            tokens = rows_of(i, 512)
            part = dot(turned[...], normed[tokens, rows], 1, 1)
            if begin:
                cat[:, tokens] = part
            else:
                cat[:, tokens] += part
            if end:
                cat[4 * hw : 4 * hw + 16, tokens] += bias
                store(i).start()
            return unused

        lax.fori_loop(0, normed.shape[0] // 512, tile, 0)

    half = depth // 2
    upper = lax.div(f, half)
    load.wait()
    for k in range(1, depth - 1):
        add_shard(jnp.int32(k), k == 1, False)
    add_shard(upper * (depth - 1), False, False)
    early.pass_on(1)
    second.relay()
    spread.pass_on()
    early.pass_on(2)
    line.pass_on(3)
    add_shard((1 - upper) * (depth - 1), False, True)
    early.pass_on(3)
    second.finish()
    line.finish()
    early.finish()
    early_keep.wait()
    keep[3].wait()
    spread.finish(l0.at[4])
    mlp_store.wait()
    for i in range(normed.shape[0] // 512):
        store(i).wait()


def enter(tokens, cotangent, gain, bias, forget_weight, attn_weights, mlp_weights, out_weight, depth):
    n, w = tokens.shape
    shard, head_count = forget_weight.shape
    heads = head_count // 8
    hw = w // 8
    cols, fw = 4 * hw, mlp_weights[0].shape[1] // 8
    whole = jax.ShapeDtypeStruct((8 * n, w), BF)
    dma = pltpu.SemaphoreType.DMA((Gather.sems,))
    line = pltpu.SemaphoreType.DMA((2, depth - 1, WEIGHT_PIECES + 1))
    early = pltpu.SemaphoreType.DMA((2, depth - 1, 1))
    vmem = pl.BlockSpec(memory_space=pltpu.VMEM)
    smem = pl.BlockSpec(memory_space=pltpu.SMEM)
    anywhere = pl.BlockSpec(memory_space=pl.ANY)
    return pl.pallas_call(
        functools.partial(enter_kernel, depth=depth, heads=heads),
        name="enter",
        out_shape=(
            whole,
            whole,
            jax.ShapeDtypeStruct((depth * shard, cols + 128), BF),
            jax.ShapeDtypeStruct((hw, w), BF),
            jax.ShapeDtypeStruct((cols + 128, 8 * n), F32),
            jax.ShapeDtypeStruct((shard, 3 * fw - EARLY), BF),
            jax.ShapeDtypeStruct((depth * shard, EARLY), BF),
        ),
        in_specs=[vmem, vmem, vmem, smem, vmem] + [anywhere] * 8,
        out_specs=[anywhere, anywhere, vmem, anywhere, anywhere, anywhere, anywhere],
        scratch_shapes=[
            pltpu.VMEM((n, w), BF),
            pltpu.VMEM((4, shard, hw + 64), BF),
            pltpu.VMEM((shard, cols), BF),
            pltpu.VMEM((16, shard), BF),
            pltpu.VMEM((depth, 16, shard), BF),
            pltpu.VMEM((shard, 3 * fw), BF),
            pltpu.VMEM((8 * n, w), BF),
            pltpu.VMEM((cols + 128, shard), BF),
            pltpu.VMEM((cols + 128, 8 * n), F32),
            dma, dma, dma, dma, line, line, early, early,
            pltpu.SemaphoreType.DMA((2, OUT_PIECES)),
            pltpu.SemaphoreType.DMA((OUT_PIECES,)),
            pltpu.SemaphoreType.DMA((6,)),
            pltpu.SemaphoreType.DMA((8 * n // 512,)),
            pltpu.SemaphoreType.DMA((9,)),
        ],
        compiler_params=pltpu.CompilerParams(
            collective_id=1, has_side_effects=True, vmem_limit_bytes=VMEM_BYTES
        ),
        cost_estimate=pl.CostEstimate(
            flops=2 * 8 * n * w * cols, bytes_accessed=4 * 8 * n * w * 2, transcendentals=0
        ),
    )(tokens, cotangent, gain, bias, forget_weight.T, *attn_weights, *mlp_weights, out_weight)


TILE = 256


def middle_kernel(
    gated_ref, w_ref, tok_ref, gain_ref, mid_ref, normed_ref,
    gated, turned, mine, s0, r0, s1, r1, l0, *refs,
):
    c, s, f = here()
    n, width = mine.shape
    h = n // 2
    count = len(refs) // 2
    halves = [PairSum(refs[:count]), PairSum(refs[count:])]
    loads = [
        pltpu.make_async_copy(
            gated_ref.at[:, pl.ds(pl.multiple_of(block * n, n), n)],
            gated.at[:, pl.ds(i * n, n)],
            l0.at[i],
        )
        for i, block in enumerate(PairSum.blocks(c, s))
    ]
    for made in loads:
        made.start()
    greet(partners())
    for made in loads:
        made.wait()
    for q, pairs in enumerate(halves):

        def one_pair(i, unused, q=q, pairs=pairs):
            pairs.between(i)
            for core in (0, 1):
                tokens = pl.ds(pl.multiple_of((2 * i + core) * n + q * h, h), h)
                turned[core * h : (core + 1) * h, :] = gated[:, tokens].T
            for t in range(width // TILE):
                feats = pl.ds(t * TILE, TILE)
                pairs.put(i, feats, dot(turned[...], w_ref[:, feats], 1, 0).astype(BF))
            pairs.to_sibling(i).start()
            return unused

        lax.fori_loop(0, 4, one_pair, 0)
    for pairs in halves:
        pairs.relay()
    gathers = [
        Gather(mine.at[pl.ds(q * h, h)], normed_ref, send, recv, n, q * h)
        for q, (send, recv) in enumerate(((s0, r0), (s1, r1)))
    ]
    keep = []
    for q, pairs in enumerate(halves):
        pairs.arrive()

        def body(i, carry, q=q, pairs=pairs):
            r = pl.ds(pl.multiple_of(q * h + i * STEP, STEP), STEP)
            mid = tok_ref[r, :].astype(F32) + pairs.total(i, STEP)
            mid_ref[r, :] = mid
            mine[r, :] = (mid * mean_square_inverse(mid) * gain_row(gain_ref)).astype(BF)
            return carry

        lax.fori_loop(0, h // STEP, body, 0)
        gathers[q].start()
        keep.append(pltpu.make_async_copy(gathers[q].src, gathers[q].block(0), l0.at[8 + q]))
        keep[q].start()
    for gather in gathers:
        gather.relay()
        gather.finish()
    for pairs in halves:
        pairs.finish()
    for made in keep:
        made.wait()


def middle(gated, w_out, tokens, gain):
    n, w = tokens.shape
    dma = pltpu.SemaphoreType.DMA((16,))
    vmem = pl.BlockSpec(memory_space=pltpu.VMEM)
    anywhere = pl.BlockSpec(memory_space=pl.ANY)
    return pl.pallas_call(
        middle_kernel,
        name="middle",
        out_shape=(jax.ShapeDtypeStruct((n, w), F32), jax.ShapeDtypeStruct((8 * n, w), BF)),
        in_specs=[anywhere, vmem, vmem, vmem],
        out_specs=[vmem, anywhere],
        scratch_shapes=[
            pltpu.VMEM(gated.shape, BF),
            pltpu.VMEM((n, gated.shape[0]), BF),
            pltpu.VMEM((n, w), BF),
            dma, dma, dma, dma, dma,
        ]
        + PairSum.scratch(n // 2, w)
        + PairSum.scratch(n // 2, w),
        compiler_params=pltpu.CompilerParams(
            collective_id=2, has_side_effects=True, vmem_limit_bytes=VMEM_BYTES
        ),
        cost_estimate=pl.CostEstimate(
            flops=2 * 8 * n * w * gated.shape[0], bytes_accessed=4 * 8 * n * w * 2,
            transcendentals=0,
        ),
    )(gated, w_out, tokens, gain)


TERM_PIECES = 4


class LineSum:
    def __init__(self, term, got, send, recv, depth, pieces=TERM_PIECES):
        self.term, self.got, self.send, self.recv, self.depth = term, got, send, recv, depth
        self.c, self.s, self.f = here()
        self.pieces = pieces
        self.n = term.shape[0] // pieces

    def source(self, i, g):
        return self.term.at[pl.ds(i * self.n, self.n), g]

    def copy(self, k, g, i, src):
        to = lax.rem(self.f + (1 if k == 0 else self.depth - 1), self.depth)
        return REMOTE(
            src,
            self.got.at[k, g + k - 1, pl.ds(i * self.n, self.n)],
            self.send.at[k, g, i],
            self.recv.at[k, g, i],
            (self.c, self.s, to),
            MESH,
        )

    def targets(self, k):
        return range(self.depth - 1, 0, -1) if k == 0 else range(self.depth - 1)

    def is_end(self, k):
        return self.f == (0 if k == 0 else self.depth - 1)

    def start_piece(self, i, n):
        for k in (0, 1):
            g = self.targets(k)[n]
            pl.when(self.is_end(k))(self.copy(k, g, i, self.source(i, g)).start)

    def add(self, k, g, i):
        rows = pl.ds(i * self.n, self.n)
        total = self.got[k, g + k - 1, rows].astype(F32) + self.term[rows, g].astype(F32)
        self.got[k, g + k - 1, rows] = total.astype(BF)

    def pass_on(self, i, n, hop):
        for k in (0, 1):
            g = self.targets(k)[n]
            at = hop if k == 0 else self.depth - 1 - hop

            @pl.when(self.f == at)
            def _(k=k, g=g):
                made = self.copy(k, g, i, self.got.at[k, g + k - 1, pl.ds(i * self.n, self.n)])
                made.wait_recv()
                self.add(k, g, i)
                made.start()

    def steps(self):
        todo = [
            (n * self.pieces + i + 2 * (hop - 1), -hop, i, n, hop)
            for n in range(self.depth - 2)
            for hop in range(1, self.depth - 1 - n)
            for i in range(self.pieces)
        ]
        return [step[2:] for step in sorted(todo)]

    def collect(self, i, out):
        rows = pl.ds(i * self.n, self.n)
        for g in range(self.depth):

            @pl.when(self.f == g)
            def _(g=g):
                total = self.term[rows, g].astype(F32)
                for k in (0, 1):
                    if g != (0 if k == 0 else self.depth - 1):
                        self.copy(k, g, i, self.source(i, g)).wait_recv()
                        total = total + self.got[k, g + k - 1, rows].astype(F32)
                out[rows] = total.astype(BF)

    def finish(self):
        for k in (0, 1):
            for g in self.targets(k):
                beyond = self.f < g if k == 0 else self.f > g
                for i in range(self.pieces):
                    pl.when(beyond)(self.copy(k, g, i, self.source(i, g)).wait_send)


class Exchange:
    def __init__(self, rows, out, send, recv, cols=None):
        self.c, self.s, self.f = here()
        self.place = self.c * 4 + self.s
        self.rows, self.out, self.send, self.recv, self.cols = rows, out, send, recv, cols

    def mine(self, j):
        return self.rows.at[j] if self.cols is None else self.rows.at[j, :, self.cols]

    def remote(self, j):
        return REMOTE(
            self.mine(j), self.out.at[self.place], self.send.at[j], self.recv.at[self.place],
            (j // 4, j % 4, self.f), MESH,
        )

    def local(self, j):
        return pltpu.make_async_copy(self.mine(j), self.out.at[j], self.send.at[j])

    def push(self, j):
        pl.when(self.place != j)(self.remote(j).start)
        pl.when(self.place == j)(self.local(j).start)

    def start(self):
        for j in range(8):
            self.push(j)

    def finish(self):
        for j in range(8):
            got = REMOTE(
                self.mine(j), self.out.at[j], self.send.at[j], self.recv.at[j],
                (j // 4, j % 4, self.f), MESH,
            )
            pl.when(self.place != j)(got.wait_recv)
            pl.when(self.place != j)(self.remote(j).wait_send)
            pl.when(self.place == j)(self.local(j).wait)


def plane_peers():
    c, s, f = here()
    return [
        (core, flip(s, k) if k else s, f, k + 4 * i)
        for i, core in enumerate((c, 1 - c))
        for k in range(4)
        if i or k
    ]


def ffn_kernel(
    nm_ref, dy_all_ref, early_ref, mid_ref, gain_ref, gated_ref, w_out_ref, *more, depth,
):
    w_refs, more = more[:depth], more[depth:]
    (
        grad_mid_ref, gain_term_ref, gg_ref, out_term_ref, down_ref, gate_rows_ref, up_own_ref,
    ) = more[:7]
    low_refs, more = more[7 : 7 + depth], more[7 + depth :]
    (
        nm, dy, w, grads, term, got, rows_sum, mine, branch, stage, down_own, down_near, down_far,
        l0, l1, l2, s1, r1, s2, r2, s3, r3, s4, r4, *refs,
    ) = more
    c, s, f = here()
    n, width = mid_ref.shape
    fw = w.shape[1] // 3
    pairs = PairSum(refs)
    loads = []
    w_loads = [
        pltpu.make_async_copy(early_ref, w.at[:, pl.ds(0, EARLY)], l2.at[11]),
    ]
    shard = w_refs[0].shape[0]
    for k, ref in enumerate(w_refs):
        rows = pl.ds(pl.multiple_of(lax.rem(f + depth - k, depth) * shard, shard), shard)
        w_loads.append(
            pltpu.make_async_copy(ref, w.at[rows, pl.ds(EARLY, 3 * fw - EARLY)], l2.at[12 + k])
        )
    for made in w_loads:
        made.start()
    for i, block in enumerate(PairSum.blocks(c, s)):
        src, dst = pl.ds(pl.multiple_of(block * n, n), n), pl.ds(i * n, n)
        made = [
            pltpu.make_async_copy(nm_ref.at[src], nm.at[dst], l0.at[i]),
            pltpu.make_async_copy(dy_all_ref.at[src], dy.at[dst], l1.at[i]),
        ]
        for one in made:
            one.start()
        if i % 2:
            loads[-1] += made
        else:
            loads.append(made)
    greeted = signal_line([p[:3] for p in plane_peers()], depth)
    pl.semaphore_wait(pltpu.get_barrier_semaphore(), greeted)
    for made in w_loads:
        made.wait()

    def one_pair(i, unused):
        rows = rows_of(i, 2 * n)
        wait_for(i, loads)
        for t in range(fw // TILE):
            cols = pl.ds(t * TILE, TILE)
            ups = pl.ds(fw + t * TILE, TILE)
            downs = pl.ds(2 * fw + t * TILE, TILE)
            gate_lin = dot(nm[rows, :], w[:, cols], 1, 0)
            up_lin = dot(nm[rows, :], w[:, ups], 1, 0)
            grad_hidden = dot(dy[rows, :], w[:, downs], 1, 0)
            sig = jax.nn.sigmoid(gate_lin)
            active = gate_lin * sig
            grads[rows, downs] = (active * up_lin).astype(BF)
            grads[rows, cols] = (
                grad_hidden * up_lin * sig * (1.0 + gate_lin * (1.0 - sig))
            ).astype(BF)
            grads[rows, ups] = (grad_hidden * active).astype(BF)
        pairs.between(i)
        for t in range(width // TILE):
            feats = pl.ds(t * TILE, TILE)
            part = dot(grads[rows, 0 : 2 * fw], w[feats, 0 : 2 * fw], 1, 1).astype(BF)
            pairs.put(i, feats, part)
        pairs.to_sibling(i).start()
        return unused

    lax.fori_loop(0, 4, one_pair, 0)
    pairs.relay()

    line = LineSum(term, got, s2, r2, depth)
    deep = width // TERM_PIECES
    per = term.shape[0] // TERM_PIECES

    def weight_tile(i, unused):
        tile = dot(nm[:, rows_of(i, deep)], grads[:, 0 : 2 * fw], 0, 0).astype(BF)
        term[pl.ds(i * per, per)] = tile.reshape((per,) + term.shape[1:])
        line.start_piece(i, 0)
        return unused

    lax.fori_loop(0, TERM_PIECES, weight_tile, 0)
    for k in range(1, depth - 1):
        for i in range(TERM_PIECES):
            line.start_piece(i, k)
    hw = gated_ref.shape[0]
    w_out, out_term = nm.at[pl.ds(0, hw)], nm.at[pl.ds(hw, hw)]
    w_out_load = pltpu.make_async_copy(w_out_ref, w_out, l2.at[9])
    w_out_load.start()
    todo = line.steps()
    pairs.arrive()

    def body(j, carry):
        r = rows_of(j, STEP)
        grad = pairs.total(j, STEP)
        mid = mid_ref[r, :]
        inverse = mean_square_inverse(mid)
        weighted = grad * gain_row(gain_ref)
        back = inverse * weighted - mid * inverse**3 * jnp.mean(
            weighted * mid, axis=1, keepdims=True
        )
        own_dy = dy[pl.ds(pl.multiple_of(7 * n + j * STEP, STEP), STEP), :]
        grad_mid = own_dy.astype(F32) + back
        grad_mid_ref[r, :] = grad_mid
        mine[r, :] = grad_mid.astype(BF)
        return carry + jnp.sum(grad * mid * inverse, axis=0, keepdims=True)

    gain_term_ref[...] = lax.fori_loop(0, n // STEP, body, jnp.zeros((1, width), F32))
    gather = Gather(mine, branch, s1, r1)
    gather.start()
    keep = pltpu.make_async_copy(mine, gather.block(0), l0.at[8])
    keep.start()

    def low_tile(i, unused):
        tile = dot(dy[:, rows_of(i, deep)], grads[:, 2 * fw :], 0, 0).astype(BF)
        tile = tile.reshape((per, depth, term.shape[2], fw))
        for g in range(depth):
            for k in range(depth):

                @pl.when(lax.rem(g + depth - f, depth) == k)
                def _(g=g, k=k):
                    low_refs[k][pl.ds(i * per, per)] = tile[:, g]

        for at in range(TERM_PIECES):

            @pl.when(i == at)
            def _(at=at):
                for step in todo[at * 2 : at * 2 + 2]:
                    line.pass_on(*step)

        return unused

    lax.fori_loop(0, TERM_PIECES, low_tile, 0)

    def down_copy(i):
        return REMOTE(
            pairs.out.at[lax.rem(i, 2)], down_near.at[i], s3.at[i], r3.at[i], pairs.sib, MESH
        )

    for i in (2, 3):
        pairs.to_sibling(i).wait_send()

    def down_pair(i, unused):
        rows = rows_of(i, 2 * n)

        @pl.when(i >= 2)
        def _():
            down_copy(i - 2).wait_send()

        for t in range(width // TILE):
            feats = pl.ds(t * TILE, TILE)
            part = dot(grads[rows, 2 * fw :], w[feats, 2 * fw :], 1, 1).astype(BF)
            pairs.out[lax.rem(i, 2), :, feats] = part[:n]
            down_own[i, :, feats] = part[n:]
        down_copy(i).start()
        return unused

    lax.fori_loop(0, 4, down_pair, 0)
    gather.relay()
    for step in todo[2 * TERM_PIECES :]:
        line.pass_on(*step)

    def down_sum(i, unused):
        down_copy(i).wait_recv()

        def body(j, carry):
            r = rows_of(j, 32)
            total = down_own[i, r, :].astype(F32) + down_near[i, r, :].astype(F32)
            down_own[i, r, :] = total.astype(BF)
            return carry

        return lax.fori_loop(0, n // 32, body, unused)

    lax.fori_loop(0, 4, down_sum, 0)
    down_fx = REMOTE(
        down_own.at[0, :, pairs.left], down_far.at[0], s3.at[4], r3.at[4], pairs.x, MESH
    )
    down_fy = REMOTE(
        down_own.at[0, :, pairs.right], down_far.at[1], s3.at[5], r3.at[5], pairs.y, MESH
    )
    down_fx.start()
    down_fy.start()
    gather.finish()
    keep.wait()

    def gg_copy(i):
        return pltpu.make_async_copy(
            stage.at[lax.rem(i, 2)], gg_ref.at[:, rows_of(i, stage.shape[2])], l2.at[lax.rem(i, 2)]
        )

    def gg_tile(i, unused):
        @pl.when(i >= 2)
        def _():
            gg_copy(i - 2).wait()

        stage[lax.rem(i, 2)] = dot(w_out[...], branch[rows_of(i, stage.shape[2]), :], 1, 1)
        gg_copy(i).start()
        return unused

    exchange = Exchange(rows_sum, gate_rows_ref, s4, r4, pl.ds(0, fw))

    def collect(i):
        line.collect(i, rows_sum)
        for j in range(i * per, (i + 1) * per):
            exchange.push(j)

    collect(0)
    collect(1)
    tiles = branch.shape[0] // stage.shape[2]
    w_out_load.wait()
    lax.fori_loop(0, tiles, gg_tile, 0)
    collect(2)
    out_term[...] = dot(gated_ref[...], branch[...], 1, 0).astype(BF)
    out_store = pltpu.make_async_copy(out_term, out_term_ref, l2.at[10])
    out_store.start()

    def down_add(at, cols, slot):
        def body(j, carry):
            r = rows_of(j, 32)
            total = down_own[at, r, cols].astype(F32) + down_far[slot, r, :].astype(F32)
            down_own[at, r, cols] = total.astype(BF)
            return carry

        lax.fori_loop(0, n // 32, body, 0)

    collect(3)
    down_fx.wait_recv()
    down_fy.wait_recv()
    down_add(2, pairs.left, 0)
    down_add(1, pairs.right, 1)
    stores = [
        pltpu.make_async_copy(down_own.at[i], down_ref.at[i - 1], l1.at[i]) for i in (1, 2, 3)
    ]
    for made in stores:
        made.start()
    up_own_ref[...] = rows_sum[:, :, fw:]
    exchange.finish()
    for made in stores:
        made.wait()
    for i in (2, 3):
        gg_copy(jnp.int32(tiles - 4 + i)).wait()
    out_store.wait()
    down_fx.wait_send()
    down_fy.wait_send()
    pairs.finish_plane()
    for i in (2, 3):
        down_copy(i).wait_send()
    line.finish()


def ffn(normed_all, cotangent_all, weights, early, mid, gain, gated, w_out, depth):
    n, width = mid.shape
    fw = (weights[0].shape[1] + EARLY) // 3
    r = width // (8 * depth)
    hw = gated.shape[0]
    dma = pltpu.SemaphoreType.DMA((16,))
    six = pltpu.SemaphoreType.DMA((6,))
    eight = pltpu.SemaphoreType.DMA((8,))
    line = pltpu.SemaphoreType.DMA((2, depth, TERM_PIECES))
    vmem = pl.BlockSpec(memory_space=pltpu.VMEM)
    anywhere = pl.BlockSpec(memory_space=pl.ANY)
    return pl.pallas_call(
        functools.partial(ffn_kernel, depth=depth),
        name="ffn",
        out_shape=(
            jax.ShapeDtypeStruct((n, width), F32),
            jax.ShapeDtypeStruct((1, width), F32),
            jax.ShapeDtypeStruct((hw, 8 * n), F32),
            jax.ShapeDtypeStruct((hw, width), BF),
            jax.ShapeDtypeStruct((3, n, width), BF),
            jax.ShapeDtypeStruct((8, r, fw), BF),
            jax.ShapeDtypeStruct((8, r, fw), BF),
        )
        + (jax.ShapeDtypeStruct((8, r, fw), BF),) * depth,
        in_specs=[anywhere] * 3 + [vmem] * 3 + [anywhere] * (1 + depth),
        out_specs=[vmem, vmem, anywhere, anywhere, anywhere, vmem, vmem] + [vmem] * depth,
        scratch_shapes=[
            pltpu.VMEM((8 * n, width), BF),
            pltpu.VMEM((8 * n, width), BF),
            pltpu.VMEM((width, 3 * fw), BF),
            pltpu.VMEM((8 * n, 3 * fw), BF),
            pltpu.VMEM((8, depth, r, 2 * fw), BF),
            pltpu.VMEM((2, depth - 1, 8, r, 2 * fw), BF),
            pltpu.VMEM((8, r, 2 * fw), BF),
            pltpu.VMEM((n, width), BF),
            pltpu.VMEM((8 * n, width), BF),
            pltpu.VMEM((2, hw, 256), F32),
            pltpu.VMEM((4, n, width), BF),
            pltpu.VMEM((4, n, width), BF),
            pltpu.VMEM((2, n, width // 2), BF),
            dma, dma, dma, dma, dma, line, line, six, six, eight, eight,
        ]
        + PairSum.scratch(n, width),
        compiler_params=pltpu.CompilerParams(
            collective_id=3, has_side_effects=True, vmem_limit_bytes=67_043_328
        ),
        cost_estimate=pl.CostEstimate(
            flops=2 * 8 * n * width * fw * 9, bytes_accessed=4 * 8 * n * width * 2,
            transcendentals=0,
        ),
    )(normed_all, cotangent_all, early, mid, gain, gated, w_out, *weights)


def leave_kernel(
    normed_ref, cat_ref, w_ref, down_ref, tok_in, grad_mid_in, mid_in, gain_ref,
    mlp_term_ref, bias_grad_ref, up_ref, wide_ref, *more, depth, heads,
):
    low_refs, more = more[:depth], more[depth:]
    (
        grad_ref, small_sum_ref, out_ref, attn_rows_ref, low_rows_ref, up_rows_ref, wide_rows_ref,
        normed, cat, turned, w, small, plane_small, line_small, term, got, rows, wide_got, low_sum,
        tok_ref, grad_mid_ref, mid_ref, l0, l1, s2, r2, s3, r3, s5, r5, s6, r6, s7, r7, s8, r8, *refs,
    ) = more
    c, s, f = here()
    n, width = tok_ref.shape
    pairs = PairSum(refs[:7])
    down = PairTail(refs[7:])
    down_loads = [pltpu.make_async_copy(down_ref, down.own, l0.at[9])]
    loads = []
    for i, block in enumerate(PairSum.blocks(c, s)):
        src, dst = pl.ds(pl.multiple_of(block * n, n), n), pl.ds(i * n, n)
        loads.append(pltpu.make_async_copy(cat_ref.at[:, src], cat.at[:, dst], l0.at[i]))
        loads.append(pltpu.make_async_copy(normed_ref.at[src], normed.at[dst], l1.at[i]))
    w_load = pltpu.make_async_copy(w_ref, w, l0.at[8])
    late = [
        pltpu.make_async_copy(src, dst, l0.at[10 + i])
        for i, (src, dst) in enumerate(
            ((tok_in, tok_ref), (grad_mid_in, grad_mid_ref), (mid_in, mid_ref))
        )
    ]
    for made in down_loads + loads:
        made.start()
    w_load.start()
    for made in late:
        made.start()
    peers = plane_peers()
    line_peers = [(c, s, lax.rem(f + k, depth), k) for k in range(1, depth)]
    greet([p[:3] for p in peers + line_peers])
    wide = LineSum(wide_ref, wide_got, s7, r7, depth, 1)
    for k in range(depth - 1):
        wide.start_piece(0, k)
    line = LineSum(term, got, s3, r3, depth)
    low_total = low_refs[0][...].astype(F32)
    for ref in low_refs[1:]:
        low_total = low_total + ref[...].astype(F32)
    low_sum[...] = low_total.astype(BF)
    low_rows = Exchange(low_sum, low_rows_ref, s6, r6)
    deep = width // TERM_PIECES
    per = term.shape[0] // TERM_PIECES
    low_rows.start()
    up_rows = Exchange(up_ref, up_rows_ref, s8, r8)
    up_rows.start()
    for made in down_loads:
        made.wait()
    down.start(0)
    for made in loads:
        made.wait()

    def weight_tile(i, unused):
        tile = dot(cat[...], normed[:, rows_of(i, deep)], 1, 0).T.astype(BF)
        term[pl.ds(i * per, per)] = tile.reshape((per,) + term.shape[1:])
        line.start_piece(i, 0)
        return unused

    lax.fori_loop(0, TERM_PIECES, weight_tile, 0)
    for k in range(1, depth - 1):
        for i in range(TERM_PIECES):
            line.start_piece(i, k)
    w_load.wait()

    def one_pair(i, unused):
        pairs.between(i)
        turned[...] = cat[:, rows_of(i, 2 * n)].T
        for t in range(width // TILE):
            feats = pl.ds(t * TILE, TILE)
            pairs.put(i, feats, dot(turned[...], w[feats, :], 1, 1).astype(BF))
        pairs.to_sibling(i).start()
        for at in range(4):

            @pl.when(i == at)
            def _(at=at):
                for step in todo[at : at + 1]:
                    line.pass_on(*step)

        return unused

    todo = line.steps()
    for step in wide.steps():
        wide.pass_on(*step)
    lax.fori_loop(0, 4, one_pair, 0)
    for step in todo[4:6]:
        line.pass_on(*step)
    pairs.relay()
    down.start(1)
    for step in todo[6:]:
        line.pass_on(*step)
    attn_rows = Exchange(rows, attn_rows_ref, s5, r5)

    def collect(i):
        line.collect(i, rows)
        for j in range(i * per, (i + 1) * per):
            attn_rows.push(j)

    pairs.arrive()

    def body(i, carry):
        r = rows_of(i, STEP)
        grad = pairs.total(i, STEP)
        tok = tok_ref[r, :].astype(F32)
        inverse = mean_square_inverse(tok)
        weighted = grad * gain_row(gain_ref)
        back = inverse * weighted - tok * inverse**3 * jnp.mean(
            weighted * tok, axis=1, keepdims=True
        )
        grad_ref[r, :] = grad_mid_ref[r, :] + back
        return carry + jnp.sum(grad * tok * inverse, axis=0, keepdims=True)

    for made in late:
        made.wait()
    gain_term = lax.fori_loop(0, n // STEP, body, jnp.zeros((1, width), F32))
    lane = small.shape[1]
    place = c * 4 + s
    for k in range(3):
        small[k : k + 1, :] = gain_term[:, k * lane : (k + 1) * lane]
        small[3 + k : 4 + k, :] = mlp_term_ref[:, k * lane : (k + 1) * lane]
    at = lax.broadcasted_iota(jnp.int32, (1, lane), 1)
    bias_row = jnp.zeros((1, lane), F32)
    for h in range(heads):
        bias_row = jnp.where(at == place * heads + h, bias_grad_ref[h : h + 1, 0:1], bias_row)
    small[6:7, :] = bias_row
    small[7:8, :] = jnp.zeros((1, lane), F32)
    plane_small[pl.ds(place, 1)] = small[...][None]
    sent = []
    for core, other_s, other_f, k in peers:
        made = REMOTE(
            small, plane_small.at[place], s2.at[k - 1], r2.at[k - 1], (core, other_s, other_f), MESH
        )
        made.start()
        sent.append(made)
    wide.collect(0, wide_rows_ref)
    collect(0)
    collect(1)
    for made in sent:
        made.wait()
    total = plane_small[0]
    for i in range(1, 8):
        total = total + plane_small[i]
    small[...] = total
    line_small[pl.ds(f, 1)] = total[None]
    sent = []
    for core, other_s, other_f, k in line_peers:
        made = REMOTE(
            small, line_small.at[f], s2.at[6 + k], r2.at[6 + k], (core, other_s, other_f), MESH
        )
        made.start()
        sent.append(made)
    collect(2)
    collect(3)
    down.arrive()

    def body2(i, carry):
        r = rows_of(i, STEP)
        out_ref[r, :] = (mid_ref[r, :] + down.total(i, STEP)).astype(BF)
        return carry

    lax.fori_loop(0, n // STEP, body2, 0)
    for made in sent:
        made.wait()
    total = line_small[0]
    for i in range(1, depth):
        total = total + line_small[i]
    small_sum_ref[...] = total
    pairs.finish()
    down.finish()
    line.finish()
    wide.finish()
    low_rows.finish()
    up_rows.finish()
    attn_rows.finish()


def leave(
    normed, cat, w_attn, down_sum, tokens, grad_mid, mid, gain, mlp_term, bias_grad, low, up_own,
    wide, depth, heads,
):
    n, w = grad_mid.shape
    plane = 8
    cols = w_attn.shape[1]
    r = w // (plane * depth)
    sems = pltpu.SemaphoreType.DMA((6 + depth,))
    dma = pltpu.SemaphoreType.DMA((16,))
    eight = pltpu.SemaphoreType.DMA((8,))
    line = pltpu.SemaphoreType.DMA((2, depth, TERM_PIECES))
    one = pltpu.SemaphoreType.DMA((2, depth, 1))
    vmem = pl.BlockSpec(memory_space=pltpu.VMEM)
    anywhere = pl.BlockSpec(memory_space=pl.ANY)
    return pl.pallas_call(
        functools.partial(leave_kernel, depth=depth, heads=heads),
        name="leave",
        out_shape=(
            jax.ShapeDtypeStruct((n, w), F32),
            jax.ShapeDtypeStruct((8, w // 3), F32),
            jax.ShapeDtypeStruct((n, w), BF),
            jax.ShapeDtypeStruct((plane, r, cols), BF),
            jax.ShapeDtypeStruct(low[0].shape, BF),
            jax.ShapeDtypeStruct(up_own.shape, BF),
            jax.ShapeDtypeStruct((1,) + wide.shape[2:], BF),
        ),
        in_specs=[anywhere] * 7 + [vmem] * (5 + depth),
        out_specs=[vmem] * 7,
        scratch_shapes=[
            pltpu.VMEM(normed.shape, BF),
            pltpu.VMEM(cat.shape, BF),
            pltpu.VMEM((2 * n, cols), BF),
            pltpu.VMEM(w_attn.shape, BF),
            pltpu.VMEM((8, w // 3), F32),
            pltpu.VMEM((8, 8, w // 3), F32),
            pltpu.VMEM((depth, 8, w // 3), F32),
            pltpu.VMEM((plane, depth, r, cols), BF),
            pltpu.VMEM((2, depth - 1, plane, r, cols), BF),
            pltpu.VMEM((plane, r, cols), BF),
            pltpu.VMEM((2, depth - 1, 1) + wide.shape[2:], BF),
            pltpu.VMEM(low[0].shape, BF),
            pltpu.VMEM((n, w), BF),
            pltpu.VMEM((n, w), F32),
            pltpu.VMEM((n, w), F32),
            dma, dma, sems, sems, line, line, eight, eight, eight, eight, one, one, eight, eight,
        ]
        + PairSum.scratch(n, w)
        + PairTail.scratch(n, w),
        compiler_params=pltpu.CompilerParams(
            collective_id=4, has_side_effects=True, vmem_limit_bytes=VMEM_BYTES
        ),
        cost_estimate=pl.CostEstimate(
            flops=4 * 8 * n * w * cols, bytes_accessed=4 * 8 * n * w * 2, transcendentals=0
        ),
    )(
        normed, cat, w_attn, down_sum, tokens, grad_mid, mid, gain, mlp_term, bias_grad, up_own,
        wide, *low,
    )


def finish_kernel(
    attn_ref, gate_rows_ref, up_rows_ref, low_ref, small_ref, out_w_ref, block_ref, tok_grad_ref,
    q_ref, k_ref, v_ref, g_ref, f_ref, o_ref, gate_ref, up_ref, down_ref,
    gain1_ref, gain2_ref, bias_ref, out_ref, tokens_ref, *, hw, heads,
):
    plane = attn_ref.shape[0]
    fw = low_ref.shape[2]
    for i, ref in enumerate((q_ref, k_ref, v_ref, g_ref)):
        ref[...] = jnp.concatenate(
            [attn_ref[t, :, i * hw : (i + 1) * hw].astype(F32) for t in range(plane)], axis=1
        )
    a = lax.broadcasted_iota(jnp.int32, (128, 128), 0)
    b = lax.broadcasted_iota(jnp.int32, (128, 128), 1)
    total = jnp.zeros((attn_ref.shape[1], 128), F32)
    for t in range(plane):
        pick = jnp.where((a + t * heads == b) & (a < heads), 1.0, 0.0).astype(BF)
        total = total + dot(attn_ref[t, :, 4 * hw : 4 * hw + 128], pick, 1, 0)
    f_ref[...] = total.T[: f_ref.shape[0]]
    o_ref[...] = out_w_ref[0].astype(F32)
    for t in range(plane):
        cols = slice(t * fw, (t + 1) * fw)
        gate_ref[:, cols] = gate_rows_ref[t].astype(F32)
        up_ref[:, cols] = up_rows_ref[t].astype(F32)
        down_ref[:, cols] = low_ref[t].astype(F32)
    lane = small_ref.shape[1]
    count = gain1_ref.shape[0] // lane
    for k in range(count):
        gain1_ref[k * lane : (k + 1) * lane] = small_ref[k, :]
        gain2_ref[k * lane : (k + 1) * lane] = small_ref[count + k, :]
    bias_ref[...] = small_ref[2 * count : 2 * count + 1, 0 : bias_ref.shape[1]]
    out_ref[...] = block_ref[...]
    tokens_ref[...] = tok_grad_ref[...]


def finish(
    attn_rows, gate_rows, up_rows, low_rows, small, out_w, block_out, tokens_grad, hw, heads
):
    plane, r, _ = attn_rows.shape
    n, w = tokens_grad.shape
    fw = low_rows.shape[2]
    vmem = pl.BlockSpec(memory_space=pltpu.VMEM)
    square = jax.ShapeDtypeStruct((r, plane * hw), F32)
    wide = jax.ShapeDtypeStruct((r, plane * fw), F32)
    row = jax.ShapeDtypeStruct((w,), F32)
    return pl.pallas_call(
        functools.partial(finish_kernel, hw=hw, heads=heads),
        name="finish",
        out_shape=(
            square, square, square, square,
            jax.ShapeDtypeStruct((plane * heads, r), F32),
            jax.ShapeDtypeStruct(out_w.shape[1:], F32),
            wide, wide, wide, row, row,
            jax.ShapeDtypeStruct((1, plane * heads), F32),
            jax.ShapeDtypeStruct((n, w), BF),
            jax.ShapeDtypeStruct((n, w), F32),
        ),
        in_specs=[vmem] * 8,
        out_specs=[vmem] * 14,
        compiler_params=pltpu.CompilerParams(vmem_limit_bytes=VMEM_BYTES),
    )(attn_rows, gate_rows, up_rows, low_rows, small, out_w, block_out, tokens_grad)


BQ = 512
BK = 512
AUG = 128


def dot(a, b, ca, cb):
    return lax.dot_general(a, b, (((ca,), (cb,)), ((), ())), preferred_element_type=F32)


def three_parts(v):
    hi = v.astype(BF).astype(F32)
    mid = (v - hi).astype(BF).astype(F32)
    low = (v - hi - mid).astype(BF).astype(F32)
    return hi, mid, low


def triangle(n, suffix):
    a = lax.broadcasted_iota(jnp.int32, (n, n), 0)
    b = lax.broadcasted_iota(jnp.int32, (n, n), 1)
    return jnp.where(a >= b if suffix else a <= b, 1.0, 0.0).astype(BF)


def log_sigmoid(v):
    return jnp.minimum(v, 0.0) - jnp.log1p(jnp.exp(-jnp.abs(v)))


def doc_starts(lens_ref, pos):
    start, end = jnp.zeros_like(pos), jnp.int32(0)
    for n in range(lens_ref.shape[1]):
        end = end + lens_ref[0, n]
        start = jnp.where(pos >= end, end, start)
    return start


def storage_of(place_ref, p):
    found = jnp.int32(0)
    for n in range(place_ref.shape[1]):
        found = jnp.where(place_ref[0, n] == p, n, found)
    return found


def extend(prefix_row, sign_first):
    hi, mid, low = three_parts(prefix_row)
    r = lax.broadcasted_iota(jnp.int32, (16, prefix_row.shape[1]), 0)
    base = 0 if sign_first else 3
    sign = 1.0 if sign_first else -1.0
    ones = (r >= 3) & (r < 6) if sign_first else r < 3
    out = jnp.where(ones, 1.0, 0.0)
    out = jnp.where(r == base, sign * hi, out)
    out = jnp.where(r == base + 1, sign * mid, out)
    return jnp.where(r == base + 2, sign * low, out)


def lay_out(place_ref, cat_ref, prefix_ref, heads, hd, slab, qa, ka, kta):
    hw = heads * hd
    slabs = cat_ref.shape[1] // slab
    for p in range(slabs):
        src = pl.ds(pl.multiple_of(storage_of(place_ref, p) * slab, slab), slab)
        dst = pl.ds(p * slab, slab)
        for h in range(heads):
            q = cat_ref[h * hd : (h + 1) * hd, src].astype(BF).astype(F32)
            row = prefix_ref[h : h + 1, dst]
            rest = jnp.zeros((AUG - hd - 16, slab), F32)
            qe = jnp.concatenate([q * hd**-0.5, extend(row, True), rest], axis=0)
            qa[h, :, dst] = qe.astype(BF)
            k = cat_ref[hw + h * hd : hw + (h + 1) * hd, src].astype(BF).astype(F32)
            ke = jnp.concatenate([k, extend(row, False), rest], axis=0)
            if kta is not None:
                kta[h, :, dst] = ke.astype(BF)
            ka[h, dst, :] = ke.T.astype(BF)


def attention_kernel(
    place_ref, lens_ref, cat_ref,
    gated_ref, att_ref, exact_ref, lse_ref, prefix_ref,
    qa, ka, va, *, heads, hd, slab,
):
    hw = heads * hd
    tokens = cat_ref.shape[1]
    slabs = tokens // slab
    tri = triangle(slab, False)
    carry = jnp.zeros((16, 1), F32)
    for p in range(slabs):
        src = pl.ds(pl.multiple_of(storage_of(place_ref, p) * slab, slab), slab)
        pre = cat_ref[4 * hw : 4 * hw + 16, src]
        steps = log_sigmoid(pre).astype(BF)
        part = dot(steps, tri, 1, 0) + carry
        prefix_ref[:, p * slab : (p + 1) * slab] = part
        carry = part[:, slab - 1 : slab]
        for h in range(heads):
            va[h, :, p * slab : (p + 1) * slab] = cat_ref[
                2 * hw + h * hd : 2 * hw + (h + 1) * hd, src
            ].astype(BF)
    lay_out(place_ref, cat_ref, prefix_ref, heads, hd, slab, qa, ka, None)
    per = slab // BQ

    def one_query_block(qb, unused):
        q0 = pl.multiple_of(qb * BQ, BQ)
        pos = q0 + lax.broadcasted_iota(jnp.int32, (1, BQ), 1)
        start = doc_starts(lens_ref, pos)
        low = doc_starts(lens_ref, q0) // BK
        inside = lax.broadcasted_iota(jnp.int32, (BK, BQ), 0)

        def one_key_block(kb, held):
            k0 = pl.multiple_of(kb * BK, BK)
            allowed = (inside <= pos - k0) & (inside >= start - k0)
            out = []
            for h in range(heads):
                m, l, acc = held[h]
                st = dot(ka[h, pl.ds(k0, BK), :], qa[h, :, pl.ds(q0, BQ)], 1, 0)
                st = jnp.where(allowed, st, very_low)
                new = jnp.maximum(m, jnp.max(st, axis=0, keepdims=True))
                p = jnp.exp(st - new)
                scale = jnp.exp(m - new)
                l = l * scale + jnp.sum(p, axis=0, keepdims=True)
                acc = acc * scale + dot(va[h, :, pl.ds(k0, BK)], p.astype(BF), 1, 0)
                out.append((new, l, acc))
            return tuple(out)

        begin = tuple(
            (jnp.full((1, BQ), very_low, F32), jnp.zeros((1, BQ), F32), jnp.zeros((hd, BQ), F32))
            for _ in range(heads)
        )
        done = lax.fori_loop(low, (q0 + BQ + BK - 1) // BK, one_key_block, begin)
        dst = pl.ds(pl.multiple_of(storage_of(place_ref, qb // per) * slab + lax.rem(qb, per) * BQ, BQ), BQ)
        for h in range(heads):
            m, l, acc = done[h]
            lse_ref[h : h + 1, pl.ds(q0, BQ)] = m + jnp.log(l)
            exact = acc / l
            rounded = exact.astype(BF)
            exact_ref[h * hd : (h + 1) * hd, dst] = exact
            att_ref[h * hd : (h + 1) * hd, dst] = rounded
            gate = jax.nn.sigmoid(cat_ref[3 * hw + h * hd : 3 * hw + (h + 1) * hd, dst])
            gated_ref[h * hd : (h + 1) * hd, dst] = (rounded.astype(F32) * gate).astype(BF)
        return unused

    lse_ref[...] = jnp.zeros_like(lse_ref)
    lax.fori_loop(0, tokens // BQ, one_query_block, 0)


def attention(place, lens, cat, heads, hd, slab):
    tokens = cat.shape[1]
    hw = heads * hd
    vmem = pl.BlockSpec(memory_space=pltpu.VMEM)
    smem = pl.BlockSpec(memory_space=pltpu.SMEM)
    return pl.pallas_call(
        functools.partial(attention_kernel, heads=heads, hd=hd, slab=slab),
        name="attention",
        out_shape=(
            jax.ShapeDtypeStruct((hw, tokens), BF),
            jax.ShapeDtypeStruct((hw, tokens), BF),
            jax.ShapeDtypeStruct((hw, tokens), F32),
            jax.ShapeDtypeStruct((8, tokens), F32),
            jax.ShapeDtypeStruct((16, tokens), F32),
        ),
        in_specs=[smem, smem, vmem],
        out_specs=[vmem] * 5,
        scratch_shapes=[
            pltpu.VMEM((heads, AUG, tokens), BF),
            pltpu.VMEM((heads, tokens, AUG), BF),
            pltpu.VMEM((heads, hd, tokens), BF),
        ],
        compiler_params=pltpu.CompilerParams(vmem_limit_bytes=VMEM_BYTES),
        cost_estimate=pl.CostEstimate(
            flops=8 * heads * tokens * tokens * hd, bytes_accessed=cat.size * 4,
            transcendentals=heads * tokens * tokens // 2,
        ),
    )(place, lens, cat)


def attention_back_kernel(
    place_ref, lens_ref, cat_ref, gg_ref, att_ref, exact_ref, lse_ref, prefix_ref,
    out_ref, bias_grad_ref,
    qa, ka, kta, va, do, delta_ref, dk, dv, gp, *, heads, hd, slab,
):
    hw = heads * hd
    tokens = cat_ref.shape[1]
    slabs = tokens // slab
    per = slab // BQ
    lay_out(place_ref, cat_ref, prefix_ref, heads, hd, slab, qa, ka, kta)
    delta_ref[...] = jnp.zeros_like(delta_ref)
    gp[...] = jnp.zeros_like(gp)
    dk[...] = jnp.zeros_like(dk)
    dv[...] = jnp.zeros_like(dv)
    out_ref[4 * hw :, :] = jnp.zeros((out_ref.shape[0] - 4 * hw, tokens), BF)
    for p in range(slabs):
        src = pl.ds(pl.multiple_of(storage_of(place_ref, p) * slab, slab), slab)
        dst = pl.ds(p * slab, slab)
        for h in range(heads):
            rows = slice(h * hd, (h + 1) * hd)
            gate = jax.nn.sigmoid(cat_ref[3 * hw + h * hd : 3 * hw + (h + 1) * hd, src])
            gg = gg_ref[rows, src]
            low = (gg * gate).astype(BF)
            do[h, :, dst] = low
            delta_ref[h : h + 1, dst] = jnp.sum(
                low.astype(F32) * exact_ref[rows, src], axis=0, keepdims=True
            )
            gate_grad = gg * att_ref[rows, src].astype(F32) * gate * (1.0 - gate)
            out_ref[3 * hw + h * hd : 3 * hw + (h + 1) * hd, src] = gate_grad.astype(BF)
            v = cat_ref[2 * hw + h * hd : 2 * hw + (h + 1) * hd, src]
            va[h, dst, :] = v.T.astype(BF)

    def one_query_block(qb, unused):
        q0 = pl.multiple_of(qb * BQ, BQ)
        pos = q0 + lax.broadcasted_iota(jnp.int32, (1, BQ), 1)
        start = doc_starts(lens_ref, pos)
        low = doc_starts(lens_ref, q0) // BK
        inside = lax.broadcasted_iota(jnp.int32, (BK, BQ), 0)

        def one_key_block(kb, held):
            k0 = pl.multiple_of(kb * BK, BK)
            keys = pl.ds(k0, BK)
            allowed = (inside <= pos - k0) & (inside >= start - k0)
            out = []
            for h in range(heads):
                queries = qa[h, :, pl.ds(q0, BQ)]
                grads = do[h, :, pl.ds(q0, BQ)]
                st = dot(ka[h, keys, :], queries, 1, 0) - lse_ref[h : h + 1, pl.ds(q0, BQ)]
                p = jnp.exp(jnp.where(allowed, st, very_low))
                dp = dot(va[h, keys, :], grads, 1, 0) - delta_ref[h : h + 1, pl.ds(q0, BQ)]
                ds = (p * dp).astype(BF)
                out.append(held[h] + dot(kta[h, :, keys], ds, 1, 0))
                dk[h, :, keys] += dot(queries, ds, 1, 1)
                dv[h, :, keys] += dot(grads, p.astype(BF), 1, 1)
            return tuple(out)

        begin = tuple(jnp.zeros((AUG, BQ), F32) for _ in range(heads))
        done = lax.fori_loop(low, (q0 + BQ + BK - 1) // BK, one_key_block, begin)
        dst = pl.ds(pl.multiple_of(storage_of(place_ref, qb // per) * slab + lax.rem(qb, per) * BQ, BQ), BQ)
        for h in range(heads):
            out_ref[h * hd : (h + 1) * hd, dst] = (done[h][0:hd, :] * hd**-0.5).astype(BF)
            gp[h : h + 1, pl.ds(q0, BQ)] = done[h][hd : hd + 1, :]
        return unused

    lax.fori_loop(0, tokens // BQ, one_query_block, 0)
    tri = triangle(slab, True)
    carry = jnp.zeros((16, 1), F32)
    bias_grad = jnp.zeros((16, 1), F32)
    for p in reversed(range(slabs)):
        src = pl.ds(pl.multiple_of(storage_of(place_ref, p) * slab, slab), slab)
        dst = pl.ds(p * slab, slab)
        for h in range(heads):
            out_ref[hw + h * hd : hw + (h + 1) * hd, src] = dk[h, 0:hd, dst].astype(BF)
            out_ref[2 * hw + h * hd : 2 * hw + (h + 1) * hd, src] = dv[h, :, dst].astype(BF)
            gp[h : h + 1, dst] = gp[h : h + 1, dst] - dk[h, hd + 3 : hd + 4, dst]
        grad = gp[:, dst]
        total = carry
        for piece in three_parts(grad):
            total = total + dot(piece.astype(BF), tri, 1, 0)
        carry = total[:, 0:1]
        pre = cat_ref[4 * hw : 4 * hw + 16, src]
        low = (total.astype(BF).astype(F32) * jax.nn.sigmoid(-pre)).astype(BF)
        out_ref[4 * hw : 4 * hw + 16, src] = low
        bias_grad = bias_grad + jnp.sum(low.astype(F32), axis=1, keepdims=True)
    bias_grad_ref[...] = jnp.broadcast_to(bias_grad, bias_grad_ref.shape)


def attention_back(place, lens, cat, gg, att, exact, lse, prefix, heads, hd, slab):
    tokens = cat.shape[1]
    vmem = pl.BlockSpec(memory_space=pltpu.VMEM)
    smem = pl.BlockSpec(memory_space=pltpu.SMEM)
    return pl.pallas_call(
        functools.partial(attention_back_kernel, heads=heads, hd=hd, slab=slab),
        name="attention_back",
        out_shape=(
            jax.ShapeDtypeStruct(cat.shape, BF),
            jax.ShapeDtypeStruct((16, 128), F32),
        ),
        in_specs=[smem, smem] + [vmem] * 6,
        out_specs=[vmem] * 2,
        scratch_shapes=[
            pltpu.VMEM((heads, AUG, tokens), BF),
            pltpu.VMEM((heads, tokens, AUG), BF),
            pltpu.VMEM((heads, AUG, tokens), BF),
            pltpu.VMEM((heads, tokens, hd), BF),
            pltpu.VMEM((heads, hd, tokens), BF),
            pltpu.VMEM((8, tokens), F32),
            pltpu.VMEM((heads, AUG, tokens), F32),
            pltpu.VMEM((heads, hd, tokens), F32),
            pltpu.VMEM((16, tokens), F32),
        ],
        compiler_params=pltpu.CompilerParams(vmem_limit_bytes=VMEM_BYTES),
        cost_estimate=pl.CostEstimate(
            flops=20 * heads * tokens * tokens * hd, bytes_accessed=cat.size * 8,
            transcendentals=heads * tokens * tokens // 2,
        ),
    )(place, lens, cat, gg, att, exact, lse, prefix)


def local_plane(
    tokens, out_cotangent, seq_lengths, slab_place, attn_gain, query_weight, key_weight,
    value_weight, outgate_weight, forget_weight, forget_bias, output_weight, mlp_gain,
    gate_weight, up_weight, down_weight,
):
    plane_axes = ("cp", "sp")
    plane = lax.axis_size("cp") * lax.axis_size("sp")
    depth = lax.axis_size("fsdp")
    place = lax.axis_index("cp") * lax.axis_size("sp") + lax.axis_index("sp")
    head_count = forget_weight.shape[1]
    width = tokens.shape[2]
    hd = width // head_count
    heads = head_count // plane
    hw = heads * hd
    fw = gate_weight.shape[1] // plane
    shard = query_weight.shape[0]
    group_rows = tokens.shape[1] * plane
    slab = group_rows // slab_place.shape[1]

    def shift(value, k):
        return lax.ppermute(value, "fsdp", [(j, (j + k) % depth) for j in range(depth)])

    inputs, cotangent = tokens[0], out_cotangent[0]
    normed, cotangent_all, w_attn, w_out, cat, own_mlp, early = enter(
        inputs, cotangent, attn_gain, forget_bias, forget_weight,
        (query_weight, key_weight, value_weight, outgate_weight),
        (gate_weight, up_weight, down_weight), output_weight, depth,
    )
    w_mlp = [own_mlp] + [shift(own_mlp, k) for k in range(1, depth)]
    gated, att, exact, lse, prefix = attention(slab_place, seq_lengths, cat, heads, hd, slab)
    mid, normed_mlp = middle(gated, w_out, inputs, mlp_gain)

    grad_mid, mlp_gain_term, grad_gated, out_term, down_sum, gate_rows, up_own, *low_terms = ffn(
        normed_mlp, cotangent_all, w_mlp, early, mid, mlp_gain, gated, w_out, depth
    )
    low = [low_terms[0]] + [shift(low_terms[k], k) for k in range(1, depth)]

    grad_cat, bias_grad = attention_back(
        slab_place, seq_lengths, cat, grad_gated, att, exact, lse, prefix, heads, hd, slab
    )
    part = width // (plane * depth)
    tokens_grad, small_sum, block_out, attn_rows, low_rows, up_rows, wide_rows = leave(
        normed, grad_cat, w_attn, down_sum, inputs, grad_mid, mid, attn_gain, mlp_gain_term,
        bias_grad, low, up_own,
        out_term.reshape(1, depth, part, width), depth, heads,
    )
    (
        query_grad, key_grad, value_grad, outgate_grad, forget_grad, out_grad, gate_grad, up_grad,
        down_grad, attn_gain_grad, mlp_gain_grad, forget_bias_grad, block_out, tokens_grad,
    ) = finish(
        attn_rows, gate_rows, up_rows, low_rows, small_sum, wide_rows, block_out, tokens_grad,
        hw, heads,
    )
    return (
        block_out[None],
        tokens_grad[None],
        attn_gain_grad,
        query_grad,
        key_grad,
        value_grad,
        outgate_grad,
        forget_grad.T,
        forget_bias_grad[0],
        out_grad,
        mlp_gain_grad,
        gate_grad,
        up_grad,
        down_grad,
    )


def fits_plane(mesh, tokens, slab_place, forget_weight, gate_weight):
    sizes = dict(mesh.shape)
    if (sizes["cp"], sizes["sp"]) != (2, 4):
        return False
    plane = sizes["cp"] * sizes["sp"]
    width = tokens.shape[2]
    head_count = forget_weight.shape[1]
    group_rows = tokens.shape[1]
    slab = group_rows // slab_place.shape[1]
    heads = head_count // plane
    return (
        head_count % plane == 0
        and heads <= 8
        and width // head_count == 64
        and heads % 2 == 1
        and width == 8 * heads * 64
        and slab % 512 == 0
        and group_rows <= 2048
        and width % 768 == 0
        and gate_weight.shape[1] % (128 * plane) == 0
        and width % (16 * plane * sizes["fsdp"]) == 0
        and (group_rows // plane) % 64 == 0
    )


def shard(mesh, fn):
    return jax.shard_map(
        fn,
        mesh=mesh,
        in_specs=(
            P("fsdp", ("cp", "sp"), None),
            P("fsdp", ("cp", "sp"), None),
            P("fsdp", None),
            P("fsdp", None),
            P(),
            P("fsdp", None),
            P("fsdp", None),
            P("fsdp", None),
            P("fsdp", None),
            P("fsdp", None),
            P(),
            P("fsdp", None),
            P(),
            P("fsdp", None),
            P("fsdp", None),
            P("fsdp", None),
        ),
        out_specs=(
            P("fsdp", ("cp", "sp"), None),
            P("fsdp", ("cp", "sp"), None),
            P(),
            P(("cp", "sp", "fsdp"), None),
            P(("cp", "sp", "fsdp"), None),
            P(("cp", "sp", "fsdp"), None),
            P(("cp", "sp", "fsdp"), None),
            P(("cp", "sp", "fsdp"), None),
            P(),
            P(("cp", "sp", "fsdp"), None),
            P(),
            P(("cp", "sp", "fsdp"), None),
            P(("cp", "sp", "fsdp"), None),
            P(("cp", "sp", "fsdp"), None),
        ),
        check_vma=False,
    )


def solution(mesh):
    def run(*args):
        fast = fits_plane(mesh, args[0], args[3], args[9], args[13])
        return shard(mesh, local_plane if fast else local)(*args)

    return run
```

```python
import functools

import jax
import jax.numpy as jnp
from jax import lax
from jax.experimental import pallas as pl
from jax.experimental.pallas import tpu as pltpu
from jax.sharding import PartitionSpec as P

epsilon = 1e-06
very_low = -1e30
MESH = pl.DeviceIdType.MESH
BF = jnp.bfloat16
F32 = jnp.float32
REMOTE = pltpu.make_async_remote_copy
VMEM_BYTES = 60 * 1024 * 1024


def matmul(left, right):
    return jnp.dot(left, right, preferred_element_type=jnp.float32)


def matmul_right_t(left, right):
    return lax.dot_general(
        left, right, (((1,), (1,)), ((), ())), preferred_element_type=jnp.float32
    )


def matmul_left_t(left, right):
    return lax.dot_general(
        left, right, (((0,), (0,)), ((), ())), preferred_element_type=jnp.float32
    )


def rms_inverse(values):
    return lax.rsqrt(jnp.mean(values * values, axis=1, keepdims=True) + epsilon)


def norm_back(upstream, values, inverse, gain):
    weighted = upstream * gain
    return inverse * weighted - values * inverse**3 * jnp.mean(
        weighted * values, axis=1, keepdims=True
    )


def row_layout(place_row, lens_row, count, slab_rows):
    rows = jnp.arange(count, dtype=jnp.int32)
    slab_index = rows // slab_rows
    table = (
        slab_index[:, None] == jnp.arange(place_row.shape[0], dtype=jnp.int32)[None, :]
    ).astype(jnp.int32)
    position = jnp.sum(table * place_row[None, :], axis=1) * slab_rows + rows % slab_rows
    ends = jnp.cumsum(lens_row)
    segment = jnp.sum((position[:, None] >= ends[None, :]).astype(jnp.int32), axis=1)
    return (position, segment)


def forget_prefix(log_all, place_row, slab_rows):
    slabs = place_row.shape[0]
    steps = log_all.astype(jnp.float32).reshape(slabs, slab_rows, -1)
    inside = jnp.cumsum(steps, axis=1)
    totals = inside[:, -1, :]
    earlier = (place_row[None, :] < place_row[:, None]).astype(jnp.float32)
    offsets = jnp.dot(earlier, totals, precision=lax.Precision.HIGHEST)
    return (inside + offsets[:, None, :]).reshape(slabs * slab_rows, -1)


def prefix_back(grad_prefix, place_row, slab_rows):
    slabs = place_row.shape[0]
    steps = grad_prefix.reshape(slabs, slab_rows, -1)
    inside = jnp.flip(jnp.cumsum(jnp.flip(steps, 1), axis=1), 1)
    totals = inside[:, 0, :]
    later = (place_row[None, :] > place_row[:, None]).astype(jnp.float32)
    offsets = jnp.dot(later, totals, precision=lax.Precision.HIGHEST)
    return (inside + offsets[:, None, :]).reshape(slabs * slab_rows, -1)


def local(
    tokens,
    out_cotangent,
    seq_lengths,
    slab_place,
    attn_gain,
    query_weight,
    key_weight,
    value_weight,
    outgate_weight,
    forget_weight,
    forget_bias,
    output_weight,
    mlp_gain,
    gate_weight,
    up_weight,
    down_weight,
):
    seq_devices = lax.axis_size("sp")
    ctx_devices = lax.axis_size("cp")
    ctx_index = lax.axis_index("cp")
    tok_rows = tokens.shape[1]
    model_width = tokens.shape[2]
    head_count = forget_weight.shape[1]
    local_heads = head_count // seq_devices
    head_size = model_width // head_count
    ctx_rows = tok_rows * seq_devices
    group_rows = ctx_rows * ctx_devices
    slab_rows = ctx_rows // 2
    key_block = min(512, group_rows)
    key_blocks = group_rows // key_block
    score_scale = head_size ** (-0.5)
    place_row = slab_place[0]
    lens_row = seq_lengths[0]
    ctx_start = ctx_index * ctx_rows
    inputs = tokens[0]
    input_f = inputs.astype(jnp.float32)
    weights_attn = (
        lax.all_gather(query_weight, "fsdp", axis=0, tiled=True),
        lax.all_gather(key_weight, "fsdp", axis=0, tiled=True),
        lax.all_gather(value_weight, "fsdp", axis=0, tiled=True),
        lax.all_gather(outgate_weight, "fsdp", axis=0, tiled=True),
        lax.all_gather(forget_weight, "fsdp", axis=0, tiled=True),
        lax.all_gather(output_weight, "fsdp", axis=0, tiled=True),
    )
    full_query, full_key, full_value, full_outgate, full_forget, full_output = weights_attn
    inv_first = rms_inverse(input_f)
    normed = (input_f * inv_first * attn_gain).astype(jnp.bfloat16)
    queries = matmul(normed, full_query).astype(jnp.bfloat16)
    keys = matmul(normed, full_key).astype(jnp.bfloat16)
    values = matmul(normed, full_value).astype(jnp.bfloat16)
    out_gate = jax.nn.sigmoid(matmul(normed, full_outgate))
    forget_pre = matmul(normed, full_forget) + forget_bias
    log_forget = jax.nn.log_sigmoid(forget_pre).astype(jnp.bfloat16)
    head_query, head_key, head_value, head_forget = (
        lax.all_to_all(queries, "sp", split_axis=1, concat_axis=0, tiled=True),
        lax.all_to_all(keys, "sp", split_axis=1, concat_axis=0, tiled=True),
        lax.all_to_all(values, "sp", split_axis=1, concat_axis=0, tiled=True),
        lax.all_to_all(log_forget, "sp", split_axis=1, concat_axis=0, tiled=True),
    )
    keys_all, values_all, forget_all = (
        lax.all_gather(head_key, "cp", axis=0, tiled=True),
        lax.all_gather(head_value, "cp", axis=0, tiled=True),
        lax.all_gather(head_forget, "cp", axis=0, tiled=True),
    )
    prefix_all = forget_prefix(forget_all, place_row, slab_rows)
    pos_all, seg_all = row_layout(place_row, lens_row, group_rows, slab_rows)
    query_pos = lax.dynamic_slice_in_dim(pos_all, ctx_start, ctx_rows, 0)
    query_seg = lax.dynamic_slice_in_dim(seg_all, ctx_start, ctx_rows, 0)
    query_prefix = lax.dynamic_slice_in_dim(prefix_all, ctx_start, ctx_rows, 0)
    query_three = head_query.reshape(ctx_rows, local_heads, head_size)
    query_pos_top = jnp.max(query_pos)
    query_seg_low = jnp.min(query_seg)
    query_seg_top = jnp.max(query_seg)
    key_pieces = (
        keys_all.reshape(key_blocks, key_block, local_heads, head_size),
        values_all.reshape(key_blocks, key_block, local_heads, head_size),
        prefix_all.reshape(key_blocks, key_block, local_heads),
        pos_all.reshape(key_blocks, key_block),
        seg_all.reshape(key_blocks, key_block),
    )

    def block_live(key_pos, key_seg):
        return (
            (query_pos_top >= jnp.min(key_pos))
            & (query_seg_top >= jnp.min(key_seg))
            & (jnp.max(key_seg) >= query_seg_low)
        )

    def block_scores(key_piece, key_prefix, key_pos, key_seg):
        raw = (
            jnp.einsum("qhd,khd->hqk", query_three, key_piece, preferred_element_type=jnp.float32)
            * score_scale
        )
        raw = raw + query_prefix.T[:, :, None] - key_prefix.T[:, None, :]
        allowed = (query_pos[:, None] >= key_pos[None, :]) & (
            query_seg[:, None] == key_seg[None, :]
        )
        return (raw, allowed[None, :, :])

    def total_work(carry, piece):
        running_max, running_sum = carry
        key_piece, value_piece, key_prefix, key_pos, key_seg = piece
        raw, allowed = block_scores(key_piece, key_prefix, key_pos, key_seg)
        new_max = jnp.maximum(running_max, jnp.max(jnp.where(allowed, raw, very_low), axis=2))
        terms = jnp.where(allowed, jnp.exp(raw - new_max[:, :, None]), 0.0)
        new_sum = running_sum * jnp.exp(running_max - new_max) + jnp.sum(terms, axis=2)
        return (new_max, new_sum)

    def total_step(carry, piece):
        live = block_live(piece[3], piece[4])
        return (lax.cond(live, total_work, lambda held, unused: held, carry, piece), None)

    start_max = jnp.full((local_heads, ctx_rows), very_low, jnp.float32)
    start_sum = jnp.zeros((local_heads, ctx_rows), jnp.float32)
    (final_max, final_sum), _ = lax.scan(total_step, (start_max, start_sum), key_pieces)
    log_total = final_max + jnp.log(final_sum)

    def output_work(carry, piece):
        coarse, fine = carry
        key_piece, value_piece, key_prefix, key_pos, key_seg = piece
        raw, allowed = block_scores(key_piece, key_prefix, key_pos, key_seg)
        probs = jnp.where(allowed, jnp.exp(raw - log_total[:, :, None]), 0.0)
        rounded = probs.astype(jnp.bfloat16)
        rest = (probs - rounded.astype(jnp.float32)).astype(jnp.bfloat16)
        coarse = coarse + jnp.einsum(
            "hqk,khd->qhd", rounded, value_piece, preferred_element_type=jnp.float32
        )
        fine = fine + jnp.einsum(
            "hqk,khd->qhd", rest, value_piece, preferred_element_type=jnp.float32
        )
        return (coarse, fine)

    def output_step(carry, piece):
        live = block_live(piece[3], piece[4])
        return (lax.cond(live, output_work, lambda held, unused: held, carry, piece), None)

    zero_out = jnp.zeros((ctx_rows, local_heads, head_size), jnp.float32)
    (coarse_out, fine_out), _ = lax.scan(output_step, (zero_out, zero_out), key_pieces)
    exact_out = coarse_out + fine_out
    head_out = coarse_out.reshape(ctx_rows, local_heads * head_size).astype(jnp.bfloat16)
    token_out = lax.all_to_all(head_out, "sp", split_axis=0, concat_axis=1, tiled=True)
    token_out_f = token_out.astype(jnp.float32)
    gated = (token_out_f * out_gate).astype(jnp.bfloat16)
    mid = input_f + matmul(gated, full_output)
    weights_mlp = (
        lax.all_gather(gate_weight, "fsdp", axis=0, tiled=True),
        lax.all_gather(up_weight, "fsdp", axis=0, tiled=True),
        lax.all_gather(down_weight, "fsdp", axis=0, tiled=True),
    )
    full_gate, full_up, full_down = weights_mlp
    inv_second = rms_inverse(mid)
    normed_mlp = (mid * inv_second * mlp_gain).astype(jnp.bfloat16)
    gate_lin = matmul(normed_mlp, full_gate)
    up_lin = matmul(normed_mlp, full_up)
    gate_sig = jax.nn.sigmoid(gate_lin)
    activated = gate_lin * gate_sig
    hidden = (activated * up_lin).astype(jnp.bfloat16)
    block_out = (mid + matmul_right_t(hidden, full_down)).astype(jnp.bfloat16)
    cotangent = out_cotangent[0]
    grad_hidden = matmul(cotangent, full_down)
    grad_gate_lin = (grad_hidden * up_lin * gate_sig * (1.0 + gate_lin * (1.0 - gate_sig))).astype(
        jnp.bfloat16
    )
    grad_up_lin = (grad_hidden * activated).astype(jnp.bfloat16)
    grad_normed_mlp = matmul_right_t(grad_gate_lin, full_gate) + matmul_right_t(
        grad_up_lin, full_up
    )
    mlp_gain_term = jnp.sum(grad_normed_mlp * mid * inv_second, axis=0)
    grad_mid = cotangent.astype(jnp.float32) + norm_back(grad_normed_mlp, mid, inv_second, mlp_gain)
    gate_term = matmul_left_t(normed_mlp, grad_gate_lin)
    up_term = matmul_left_t(normed_mlp, grad_up_lin)
    down_term = matmul_left_t(cotangent, hidden)
    grad_branch = grad_mid.astype(jnp.bfloat16)
    grad_gated = matmul_right_t(grad_branch, full_output)
    grad_attended = (grad_gated * out_gate).astype(jnp.bfloat16)
    grad_gate_pre = (grad_gated * token_out_f * out_gate * (1.0 - out_gate)).astype(jnp.bfloat16)
    head_grad = lax.all_to_all(grad_attended, "sp", split_axis=1, concat_axis=0, tiled=True)
    grad_three = head_grad.reshape(ctx_rows, local_heads, head_size)
    delta = jnp.sum(grad_three.astype(jnp.float32) * exact_out, axis=2).T

    def back_work(carry, piece):
        grad_query_acc, grad_prefix_acc = carry
        key_piece, value_piece, key_prefix, key_pos, key_seg = piece
        raw, allowed = block_scores(key_piece, key_prefix, key_pos, key_seg)
        probs = jnp.where(allowed, jnp.exp(raw - log_total[:, :, None]), 0.0)
        rounded = probs.astype(jnp.bfloat16)
        grad_probs = jnp.einsum(
            "qhd,khd->hqk", grad_three, value_piece, preferred_element_type=jnp.float32
        )
        grad_scores = (probs * (grad_probs - delta[:, :, None])).astype(jnp.bfloat16)
        grad_query_acc = (
            grad_query_acc
            + jnp.einsum("hqk,khd->qhd", grad_scores, key_piece, preferred_element_type=jnp.float32)
            * score_scale
        )
        key_term = (
            jnp.einsum("hqk,qhd->khd", grad_scores, query_three, preferred_element_type=jnp.float32)
            * score_scale
        )
        value_term = jnp.einsum(
            "hqk,qhd->khd", rounded, grad_three, preferred_element_type=jnp.float32
        )
        score_f = grad_scores.astype(jnp.float32)
        grad_prefix_acc = grad_prefix_acc + jnp.sum(score_f, axis=2)
        prefix_term = -jnp.sum(score_f, axis=1)
        return ((grad_query_acc, grad_prefix_acc), (key_term, value_term, prefix_term))

    def back_skip(carry, piece):
        empty_kv = jnp.zeros((key_block, local_heads, head_size), jnp.float32)
        empty_prefix = jnp.zeros((local_heads, key_block), jnp.float32)
        return (carry, (empty_kv, empty_kv, empty_prefix))

    def back_step(carry, piece):
        live = block_live(piece[3], piece[4])
        return lax.cond(live, back_work, back_skip, carry, piece)

    start_prefix = jnp.zeros((local_heads, ctx_rows), jnp.float32)
    (grad_query_acc, grad_prefix_q), (key_terms, value_terms, prefix_terms) = lax.scan(
        back_step, (zero_out, start_prefix), key_pieces
    )
    keys_grad_all = key_terms.reshape(group_rows, local_heads * head_size)
    values_grad_all = value_terms.reshape(group_rows, local_heads * head_size)
    prefix_grad_all = jnp.transpose(prefix_terms, (0, 2, 1)).reshape(group_rows, local_heads)
    own_prefix = lax.dynamic_slice_in_dim(prefix_grad_all, ctx_start, ctx_rows, 0)
    prefix_grad_all = lax.dynamic_update_slice_in_dim(
        prefix_grad_all, own_prefix + grad_prefix_q.T, ctx_start, 0
    )
    forget_grad_term = prefix_back(prefix_grad_all, place_row, slab_rows)
    key_sum, value_sum, forget_sum = (
        lax.psum_scatter(keys_grad_all, "cp", scatter_dimension=0, tiled=True),
        lax.psum_scatter(values_grad_all, "cp", scatter_dimension=0, tiled=True),
        lax.psum_scatter(forget_grad_term, "cp", scatter_dimension=0, tiled=True),
    )
    grad_query_head = grad_query_acc.reshape(ctx_rows, local_heads * head_size).astype(jnp.bfloat16)
    grad_query_tok, grad_key_tok, grad_value_tok, grad_forget_tok = (
        lax.all_to_all(grad_query_head, "sp", split_axis=0, concat_axis=1, tiled=True),
        lax.all_to_all(key_sum.astype(jnp.bfloat16), "sp", split_axis=0, concat_axis=1, tiled=True),
        lax.all_to_all(
            value_sum.astype(jnp.bfloat16), "sp", split_axis=0, concat_axis=1, tiled=True
        ),
        lax.all_to_all(
            forget_sum.astype(jnp.bfloat16), "sp", split_axis=0, concat_axis=1, tiled=True
        ),
    )
    grad_forget_pre = (grad_forget_tok.astype(jnp.float32) * jax.nn.sigmoid(-forget_pre)).astype(
        jnp.bfloat16
    )
    grad_normed = (
        matmul_right_t(grad_query_tok, full_query)
        + matmul_right_t(grad_key_tok, full_key)
        + matmul_right_t(grad_value_tok, full_value)
        + matmul_right_t(grad_gate_pre, full_outgate)
        + matmul_right_t(grad_forget_pre, full_forget)
    )
    attn_gain_term = jnp.sum(grad_normed * input_f * inv_first, axis=0)
    bias_term = jnp.sum(grad_forget_pre.astype(jnp.float32), axis=0)
    tokens_grad = grad_mid + norm_back(grad_normed, input_f, inv_first, attn_gain)
    query_term = matmul_left_t(normed, grad_query_tok)
    key_term_w = matmul_left_t(normed, grad_key_tok)
    value_term_w = matmul_left_t(normed, grad_value_tok)
    outgate_term = matmul_left_t(normed, grad_gate_pre)
    forget_term = matmul_left_t(normed, grad_forget_pre)
    output_term = matmul_left_t(gated, grad_branch)
    (
        query_grad,
        key_grad,
        value_grad,
        outgate_grad,
        forget_grad,
        output_weight_grad,
        gate_grad,
        up_grad,
        down_grad,
    ) = (
        lax.psum_scatter(query_term, ("cp", "sp", "fsdp"), scatter_dimension=0, tiled=True),
        lax.psum_scatter(key_term_w, ("cp", "sp", "fsdp"), scatter_dimension=0, tiled=True),
        lax.psum_scatter(value_term_w, ("cp", "sp", "fsdp"), scatter_dimension=0, tiled=True),
        lax.psum_scatter(outgate_term, ("cp", "sp", "fsdp"), scatter_dimension=0, tiled=True),
        lax.psum_scatter(forget_term, ("cp", "sp", "fsdp"), scatter_dimension=0, tiled=True),
        lax.psum_scatter(output_term, ("cp", "sp", "fsdp"), scatter_dimension=0, tiled=True),
        lax.psum_scatter(gate_term, ("cp", "sp", "fsdp"), scatter_dimension=0, tiled=True),
        lax.psum_scatter(up_term, ("cp", "sp", "fsdp"), scatter_dimension=0, tiled=True),
        lax.psum_scatter(down_term, ("cp", "sp", "fsdp"), scatter_dimension=0, tiled=True),
    )
    attn_gain_grad, mlp_gain_grad, forget_bias_grad = lax.psum(
        (attn_gain_term, mlp_gain_term, bias_term), ("cp", "sp", "fsdp")
    )
    return (
        block_out[None],
        tokens_grad[None],
        attn_gain_grad,
        query_grad,
        key_grad,
        value_grad,
        outgate_grad,
        forget_grad,
        forget_bias_grad,
        output_weight_grad,
        mlp_gain_grad,
        gate_grad,
        up_grad,
        down_grad,
    )


def here():
    return (lax.axis_index("cp"), lax.axis_index("sp"), lax.axis_index("fsdp"))


def flip(s, k):
    if k == 1:
        return s + 1 - 2 * lax.rem(s, 2)
    if k == 2:
        return lax.rem(s + 2, 4)
    return 3 - s


def greet(devices):
    sem = pltpu.get_barrier_semaphore()
    for device in devices:
        pl.semaphore_signal(sem, inc=1, device_id=device, device_id_type=MESH)
    pl.semaphore_wait(sem, len(devices))


def signal_line(devices, depth):
    c, s, f = here()
    sem = pltpu.get_barrier_semaphore()
    for device in devices:
        pl.semaphore_signal(sem, inc=1, device_id=device, device_id_type=MESH)

    @pl.when(f < depth - 1)
    def _():
        up = (c, s, lax.rem(f + 1, depth))
        pl.semaphore_signal(sem, inc=1, device_id=up, device_id_type=MESH)

    @pl.when(f > 0)
    def _():
        down = (c, s, lax.rem(f + depth - 1, depth))
        pl.semaphore_signal(sem, inc=1, device_id=down, device_id_type=MESH)

    neighbours = lax.div(f + depth - 1, depth) + lax.div(2 * depth - 2 - f, depth)
    return len(devices) + neighbours


def rows_of(index, count):
    return pl.ds(pl.multiple_of(index * count, count), count)


def row_loop(total, step, body):
    def one(i, carry):
        return body(rows_of(i, step), carry)

    return one, total // step


class Gather:
    sems = 13

    def __init__(self, src, out, send, recv, stride=None, offset=0):
        c, s, f = here()
        self.src, self.out, self.send, self.recv = src, out, send, recv
        self.c, self.s, self.rows = c, s, src.shape[0]
        self.stride, self.offset = stride or self.rows, offset
        self.x, self.y, self.sib = (c, flip(s, 1), f), (c, flip(s, 2), f), (1 - c, s, f)
        self.made = []

    def block(self, k, half=None):
        index = self.c * 4 + (self.s if k == 0 else flip(self.s, k))
        n = self.rows
        begin = index * self.stride + self.offset
        if half is None:
            return self.out.at[pl.ds(pl.multiple_of(begin, n), n)]
        return self.out.at[pl.ds(pl.multiple_of(begin + half * (n // 2), n // 2), n // 2)]

    def copy(self, src, dst, k, device):
        made = REMOTE(src, dst, self.send.at[k], self.recv.at[k], device, MESH)
        made.start()
        self.made.append(made)
        return made

    def start(self):
        half = self.rows // 2
        low, high = self.src.at[pl.ds(0, half)], self.src.at[pl.ds(half, half)]
        self.a = [
            self.copy(low, self.block(0, 0), 0, self.x),
            self.copy(high, self.block(0, 1), 1, self.y),
            self.copy(high, self.block(0, 1), 2, self.x),
            self.copy(low, self.block(0, 0), 3, self.y),
        ]
        self.g = [self.copy(self.src, self.block(0), 4, self.sib)]

    def pass_on(self, ref, k):
        self.g.append(self.copy(ref, ref, k, self.sib))

    def relay(self):
        self.a[0].wait_recv()
        self.b0 = self.copy(self.block(1, 0), self.block(1, 0), 5, self.y)
        self.a[1].wait_recv()
        self.b1 = self.copy(self.block(2, 1), self.block(2, 1), 6, self.x)
        self.pass_on(self.block(1, 0), 7)
        self.pass_on(self.block(2, 1), 8)
        self.a[2].wait_recv()
        self.pass_on(self.block(1, 1), 9)
        self.a[3].wait_recv()
        self.pass_on(self.block(2, 0), 10)

    def finish(self):
        self.b0.wait_recv()
        self.pass_on(self.block(3, 0), 11)
        self.b1.wait_recv()
        self.pass_on(self.block(3, 1), 12)
        for made in self.g:
            made.wait_recv()
        for made in self.made:
            made.wait_send()


class PairSum:
    order = (3, 1, 2, 0)

    @staticmethod
    def scratch(n, w):
        return [
            pltpu.VMEM((4, n, w), BF),
            pltpu.VMEM((4, n, w), BF),
            pltpu.VMEM((2, n, w), BF),
            pltpu.VMEM((4, n, w // 2), BF),
            pltpu.VMEM((2, n, w // 2), BF),
            pltpu.SemaphoreType.DMA((10,)),
            pltpu.SemaphoreType.DMA((10,)),
        ]

    def __init__(self, refs):
        self.own, self.near, self.out, self.far, self.last, self.send, self.recv = refs
        self.x, self.y, self.sib = partners()
        self.n, w = self.own.shape[1], self.own.shape[2]
        self.left, self.right = pl.ds(0, w // 2), pl.ds(w // 2, w // 2)
        self.fx = self.copy(self.own.at[0, :, self.left], self.far.at[1], 4, self.x)
        self.fy = self.copy(self.own.at[0, :, self.right], self.far.at[3], 5, self.y)
        self.nx = self.copy(self.own.at[1, :, self.left], self.far.at[0], 6, self.x)
        self.ny = self.copy(self.own.at[2, :, self.right], self.far.at[2], 7, self.y)
        self.by = self.copy(self.own.at[2, :, self.left], self.last.at[0], 8, self.y)
        self.bx = self.copy(self.own.at[1, :, self.right], self.last.at[1], 9, self.x)

    @staticmethod
    def blocks(c, s):
        return [
            core * 4 + (flip(s, k) if k else s) for k in PairSum.order for core in (1 - c, c)
        ]

    def copy(self, src, dst, k, device):
        return REMOTE(src, dst, self.send.at[k], self.recv.at[k], device, MESH)

    def to_sibling(self, i):
        return self.copy(self.out.at[lax.rem(i, 2)], self.near.at[i], i, self.sib)

    def combine(self, i):
        self.to_sibling(i).wait_recv()

        def body(j, carry):
            r = rows_of(j, 32)
            total = self.own[i, r, :].astype(F32) + self.near[i, r, :].astype(F32)
            self.own[i, r, :] = total.astype(BF)
            return carry

        lax.fori_loop(0, self.n // 32, body, 0)

    def between(self, i):
        @pl.when(i >= 1)
        def _():
            self.combine(i - 1)

        @pl.when(i == 1)
        def _():
            self.fx.start()
            self.fy.start()

        pl.when(i == 2)(self.nx.start)
        pl.when(i == 3)(self.ny.start)

        @pl.when(i >= 2)
        def _():
            self.to_sibling(i - 2).wait_send()

    def put(self, i, cols, part):
        self.out[lax.rem(i, 2), :, cols] = part[: self.n]
        self.own[i, :, cols] = part[self.n :]

    def add(self, at, cols, slot):
        def body(j, carry):
            r = rows_of(j, 32)
            total = self.own[at, r, cols].astype(F32) + self.far[slot, r, :].astype(F32)
            self.own[at, r, cols] = total.astype(BF)
            return carry

        lax.fori_loop(0, self.n // 32, body, 0)

    def relay(self):
        self.fx.wait_recv()
        self.add(2, self.left, 1)
        self.by.start()
        self.fy.wait_recv()
        self.add(1, self.right, 3)
        self.bx.start()

    def arrive(self):
        self.to_sibling(3).wait_recv()
        for made in (self.nx, self.ny, self.by, self.bx):
            made.wait_recv()

    def total(self, j, step):
        r = rows_of(j, step)
        total = self.own[3, r, :].astype(F32) + self.near[3, r, :].astype(F32)
        a = jnp.concatenate([self.far[0, r, :], self.far[2, r, :]], axis=1).astype(F32)
        b = jnp.concatenate([self.last[0, r, :], self.last[1, r, :]], axis=1).astype(F32)
        return total + a + b

    def finish_plane(self):
        for made in (self.fx, self.fy, self.nx, self.ny, self.by, self.bx):
            made.wait_send()

    def finish(self):
        self.finish_plane()
        for i in (2, 3):
            self.to_sibling(i).wait_send()


class PairTail:
    @staticmethod
    def scratch(n, w):
        return [
            pltpu.VMEM((3, n, w), BF),
            pltpu.VMEM((4, n, w // 2), BF),
            pltpu.SemaphoreType.DMA((4,)),
            pltpu.SemaphoreType.DMA((4,)),
        ]

    def __init__(self, refs):
        self.own, self.far, send, recv = refs
        x, y, sib = partners()
        w = self.own.shape[2]
        left, right = pl.ds(0, w // 2), pl.ds(w // 2, w // 2)
        self.made = [
            REMOTE(src, self.far.at[i], send.at[i], recv.at[i], device, MESH)
            for i, (src, device) in enumerate((
                (self.own.at[0, :, left], x),
                (self.own.at[0, :, right], x),
                (self.own.at[1, :, left], y),
                (self.own.at[1, :, right], y),
            ))
        ]

    def start(self, part):
        for made in self.made[part::2]:
            made.start()

    def arrive(self):
        for made in self.made:
            made.wait_recv()

    def total(self, j, step):
        r = rows_of(j, step)
        total = self.own[2, r, :].astype(F32)
        a = jnp.concatenate([self.far[0, r, :], self.far[1, r, :]], axis=1).astype(F32)
        b = jnp.concatenate([self.far[2, r, :], self.far[3, r, :]], axis=1).astype(F32)
        return total + a + b

    def finish(self):
        for made in self.made:
            made.wait_send()


def wait_for(i, loads):
    for at, pair in enumerate(loads):

        @pl.when(i == at)
        def _(pair=pair):
            for made in pair:
                made.wait()


def partners():
    c, s, f = here()
    return [(c, flip(s, 1), f), (c, flip(s, 2), f), (1 - c, s, f)]


STEP = 32


def gain_row(ref):
    return ref[...].reshape(1, ref.shape[0])


def mean_square_inverse(values):
    return lax.rsqrt(jnp.mean(values * values, axis=1, keepdims=True) + epsilon)


class Line:
    def __init__(self, own, slot, send, recv, depth):
        self.own, self.slot, self.send, self.recv, self.depth = own, slot, send, recv, depth
        self.c, self.s, self.f = here()

    def copy(self, i, distance, up):
        owner = self.owner(distance - 1, up)
        to = lax.rem(self.f + (1 if up else self.depth - 1), self.depth)
        src = self.own[i] if distance == 1 else self.slot(i, owner)
        k = 0 if up else 1
        return REMOTE(
            src,
            self.slot(i, owner),
            self.send.at[k, distance - 1, i],
            self.recv.at[k, distance - 1, i],
            (self.c, self.s, to),
            MESH,
        )

    def owner(self, distance, up):
        return lax.rem(self.f + (self.depth - distance if up else distance), self.depth)

    def may_send(self, distance, up):
        if up:
            return (self.f < self.depth - 1) & (self.f >= distance - 1)
        return (self.f > 0) & (self.f + distance <= self.depth)

    def gets(self, distance, up):
        return self.f >= distance if up else self.f + distance < self.depth

    def start(self, i):
        for up in (True, False):
            pl.when(self.may_send(1, up))(self.copy(i, 1, up).start)

    def pass_on(self, distance):
        for i in range(len(self.own)):
            for up in (True, False):
                pl.when(self.gets(distance, up))(self.got(i, distance, up).wait_recv)
                if distance < self.depth - 1:
                    pl.when(self.may_send(distance + 1, up))(self.copy(i, distance + 1, up).start)

    def got(self, i, distance, up):
        owner = self.owner(distance, up)
        k = 0 if up else 1
        place = self.slot(i, owner)
        return REMOTE(
            place,
            place,
            self.send.at[k, distance - 1, i],
            self.recv.at[k, distance - 1, i],
            (self.c, self.s, lax.rem(self.f + (self.depth - 1 if up else 1), self.depth)),
            MESH,
        )

    def finish(self):
        for distance in range(1, self.depth):
            for i in range(len(self.own)):
                for up in (True, False):
                    pl.when(self.may_send(distance, up))(self.copy(i, distance, up).wait_send)


class Spread:
    def __init__(self, src, dst, origin, send, recv, depth, pieces):
        self.c, self.s, self.f = here()
        self.src, self.dst, self.origin, self.depth = src, dst, origin, depth
        self.send, self.recv, self.pieces = send, recv, pieces
        self.n = dst.shape[0] // pieces

    def part(self, ref, i):
        return ref.at[pl.ds(i * self.n, self.n)]

    def copy(self, i, up, first):
        k = 0 if up else 1
        return REMOTE(
            self.part(self.src if first else self.dst, i),
            self.part(self.dst, i),
            self.send.at[k, i],
            self.recv.at[i],
            (self.c, self.s, lax.rem(self.f + (1 if up else self.depth - 1), self.depth)),
            MESH,
        )

    def above(self):
        return (self.f > self.origin) & (self.f < self.depth - 1)

    def below(self):
        return (self.f < self.origin) & (self.f > 0)

    def start(self, local):
        first = self.f == self.origin

        @pl.when(first)
        def _():
            pltpu.make_async_copy(self.src, self.dst, local).start()

        for i in range(self.pieces):
            pl.when(first & (self.f < self.depth - 1))(self.copy(i, True, True).start)
            pl.when(first & (self.f > 0))(self.copy(i, False, True).start)

    def pass_on(self):
        for i in range(self.pieces):
            pl.when(self.f != self.origin)(self.copy(i, True, False).wait_recv)
            pl.when(self.above())(self.copy(i, True, False).start)
            pl.when(self.below())(self.copy(i, False, False).start)

    def finish(self, local):
        first = self.f == self.origin

        @pl.when(first)
        def _():
            pltpu.make_async_copy(self.src, self.dst, local).wait()

        for i in range(self.pieces):
            pl.when((first & (self.f < self.depth - 1)) | self.above())(
                self.copy(i, True, False).wait_send
            )
            pl.when((first & (self.f > 0)) | self.below())(self.copy(i, False, False).wait_send)


WEIGHT_PIECES = 4
OUT_PIECES = 2
EARLY = 128


def enter_kernel(
    tok_ref, dy_ref, gain_ref, bias_ref, forget_ref,
    query_ref, key_ref, value_ref, outgate_ref, gate_ref, up_ref, down_ref, out_w_ref,
    normed_ref, dy_all_ref, w_attn_ref, w_out_ref, cat_ref, mlp_ref, early_ref,
    mine, windows, attn, own_forget, forget_all, mlp, normed, turned, cat,
    s0, r0, s1, r1, sz, rz, se, re, so, ro, l0, l1, l2, *, depth, heads,
):
    c, s, f = here()
    t = c * 4 + s
    n = tok_ref.shape[0]
    shard, cols = attn.shape
    hw = cols // 4
    fw = mlp.shape[1] // 3
    base = ((t * hw) // 128) * 128
    window = pl.ds(pl.multiple_of(base, 128), windows.shape[2])
    slices = [
        pltpu.make_async_copy(ref.at[:, window], windows.at[i], l2.at[i])
        for i, ref in enumerate((query_ref, key_ref, value_ref, outgate_ref))
    ]
    hidden = pl.ds(pl.multiple_of(t * fw, fw), fw)
    mlp_loads = [
        pltpu.make_async_copy(ref.at[:, hidden], mlp.at[:, pl.ds(i * fw, fw)], l2.at[4 + i])
        for i, ref in enumerate((gate_ref, up_ref, down_ref))
    ]
    for made in slices + mlp_loads:
        made.start()
    greeted = signal_line(partners(), depth)
    gain = gain_ref[...].reshape(1, gain_ref.shape[0])

    def body(i, carry):
        r = rows_of(i, STEP)
        v = tok_ref[r, :].astype(F32)
        mine[r, :] = (v * mean_square_inverse(v) * gain).astype(BF)
        return carry

    lax.fori_loop(0, n // STEP, body, 0)
    a = lax.broadcasted_iota(jnp.int32, (own_forget.shape[0], forget_ref.shape[0]), 0)
    b = lax.broadcasted_iota(jnp.int32, (own_forget.shape[0], forget_ref.shape[0]), 1)
    pick = jnp.where((b == a + t * heads) & (a < heads), 1.0, 0.0).astype(BF)
    own_forget[...] = dot(pick, forget_ref[...], 1, 0).astype(BF)
    for made in slices:
        made.wait()

    step = shard // WEIGHT_PIECES
    own = [attn.at[pl.ds(i * step, step)] for i in range(WEIGHT_PIECES)] + [own_forget]

    def slot(i, owner):
        if i == WEIGHT_PIECES:
            return forget_all.at[owner]
        rows = pl.ds(pl.multiple_of(owner * shard + i * step, step), step)
        return w_attn_ref.at[rows, pl.ds(0, cols)]

    line = Line(own, slot, sz, rz, depth)
    pl.semaphore_wait(pltpu.get_barrier_semaphore(), greeted)
    first = Gather(mine, normed_ref, s0, r0)
    second = Gather(dy_ref, dy_all_ref, s1, r1)
    first.start()
    for i in range(WEIGHT_PIECES):
        rows = slice(i * step, (i + 1) * step)
        for begin in (0, 64):

            @pl.when(t * hw - base == begin)
            def _(rows=rows, begin=begin):
                attn[rows, :] = jnp.concatenate(
                    [windows[k, rows, begin : begin + hw].astype(F32) for k in range(4)], axis=1
                ).astype(BF)

        line.start(i)
    line.start(WEIGHT_PIECES)
    heads_rows = w_out_ref.shape[0]
    origin = (t * heads_rows) // shard
    spread = Spread(
        out_w_ref.at[pl.ds(pl.multiple_of(t * heads_rows - origin * shard, heads_rows), heads_rows)],
        w_out_ref, origin, so, ro, depth, OUT_PIECES,
    )
    keep = [
        pltpu.make_async_copy(
            attn,
            w_attn_ref.at[pl.ds(pl.multiple_of(f * shard, shard), shard), pl.ds(0, cols)],
            l0.at[2],
        ),
        pltpu.make_async_copy(own_forget, forget_all.at[f], l0.at[3]),
        pltpu.make_async_copy(mine, first.block(0), l0.at[0]),
        pltpu.make_async_copy(dy_ref, second.block(0), l0.at[1]),
    ]
    for made in keep:
        made.start()
    for made in mlp_loads:
        made.wait()
    mlp_store = pltpu.make_async_copy(mlp.at[:, pl.ds(EARLY, 3 * fw - EARLY)], mlp_ref, l2.at[7])
    mlp_store.start()
    first_columns = mlp.at[:, pl.ds(0, EARLY)]

    def early_slot(i, owner):
        return early_ref.at[pl.ds(pl.multiple_of(owner * shard, shard), shard)]

    early = Line([first_columns], early_slot, se, re, depth)
    early_keep = pltpu.make_async_copy(first_columns, early_slot(0, f), l2.at[8])
    early_keep.start()
    line.pass_on(1)
    spread.start(l0.at[4])
    early.start(0)
    first.relay()
    second.start()
    line.pass_on(2)
    first.finish()
    for made in keep[2:3]:
        made.wait()
    load = pltpu.make_async_copy(normed_ref, normed, l0.at[5])
    load.start()
    keep[0].wait()
    keep[1].wait()
    r = lax.broadcasted_iota(jnp.int32, (16, 1), 0)
    bias = jnp.zeros((16, 1), F32)
    for h in range(heads):
        bias = jnp.where(r == h, bias_ref[t * heads + h], bias)

    def store(i):
        tokens = rows_of(i, 512)
        return pltpu.make_async_copy(cat.at[:, tokens], cat_ref.at[:, tokens], l1.at[i])

    def add_shard(owner, begin, end):
        small = forget_all[owner].astype(F32)
        tall = jnp.concatenate([small, jnp.zeros((128 - small.shape[0], shard), F32)], axis=0)
        rows = rows_of(owner, shard)
        w_attn_ref[rows, cols:] = tall.T.astype(BF)
        turned[...] = w_attn_ref[rows, :].T

        def tile(i, unused):
            tokens = rows_of(i, 512)
            part = dot(turned[...], normed[tokens, rows], 1, 1)
            if begin:
                cat[:, tokens] = part
            else:
                cat[:, tokens] += part
            if end:
                cat[4 * hw : 4 * hw + 16, tokens] += bias
                store(i).start()
            return unused

        lax.fori_loop(0, normed.shape[0] // 512, tile, 0)

    half = depth // 2
    upper = lax.div(f, half)
    load.wait()
    for k in range(1, depth - 1):
        add_shard(jnp.int32(k), k == 1, False)
    add_shard(upper * (depth - 1), False, False)
    early.pass_on(1)
    second.relay()
    spread.pass_on()
    early.pass_on(2)
    line.pass_on(3)
    add_shard((1 - upper) * (depth - 1), False, True)
    early.pass_on(3)
    second.finish()
    line.finish()
    early.finish()
    early_keep.wait()
    keep[3].wait()
    spread.finish(l0.at[4])
    mlp_store.wait()
    for i in range(normed.shape[0] // 512):
        store(i).wait()


def enter(tokens, cotangent, gain, bias, forget_weight, attn_weights, mlp_weights, out_weight, depth):
    n, w = tokens.shape
    shard, head_count = forget_weight.shape
    heads = head_count // 8
    hw = w // 8
    cols, fw = 4 * hw, mlp_weights[0].shape[1] // 8
    whole = jax.ShapeDtypeStruct((8 * n, w), BF)
    dma = pltpu.SemaphoreType.DMA((Gather.sems,))
    line = pltpu.SemaphoreType.DMA((2, depth - 1, WEIGHT_PIECES + 1))
    early = pltpu.SemaphoreType.DMA((2, depth - 1, 1))
    vmem = pl.BlockSpec(memory_space=pltpu.VMEM)
    smem = pl.BlockSpec(memory_space=pltpu.SMEM)
    anywhere = pl.BlockSpec(memory_space=pl.ANY)
    return pl.pallas_call(
        functools.partial(enter_kernel, depth=depth, heads=heads),
        name="enter",
        out_shape=(
            whole,
            whole,
            jax.ShapeDtypeStruct((depth * shard, cols + 128), BF),
            jax.ShapeDtypeStruct((hw, w), BF),
            jax.ShapeDtypeStruct((cols + 128, 8 * n), F32),
            jax.ShapeDtypeStruct((shard, 3 * fw - EARLY), BF),
            jax.ShapeDtypeStruct((depth * shard, EARLY), BF),
        ),
        in_specs=[vmem, vmem, vmem, smem, vmem] + [anywhere] * 8,
        out_specs=[anywhere, anywhere, vmem, anywhere, anywhere, anywhere, anywhere],
        scratch_shapes=[
            pltpu.VMEM((n, w), BF),
            pltpu.VMEM((4, shard, hw + 64), BF),
            pltpu.VMEM((shard, cols), BF),
            pltpu.VMEM((16, shard), BF),
            pltpu.VMEM((depth, 16, shard), BF),
            pltpu.VMEM((shard, 3 * fw), BF),
            pltpu.VMEM((8 * n, w), BF),
            pltpu.VMEM((cols + 128, shard), BF),
            pltpu.VMEM((cols + 128, 8 * n), F32),
            dma, dma, dma, dma, line, line, early, early,
            pltpu.SemaphoreType.DMA((2, OUT_PIECES)),
            pltpu.SemaphoreType.DMA((OUT_PIECES,)),
            pltpu.SemaphoreType.DMA((6,)),
            pltpu.SemaphoreType.DMA((8 * n // 512,)),
            pltpu.SemaphoreType.DMA((9,)),
        ],
        compiler_params=pltpu.CompilerParams(
            collective_id=1, has_side_effects=True, vmem_limit_bytes=VMEM_BYTES
        ),
        cost_estimate=pl.CostEstimate(
            flops=2 * 8 * n * w * cols, bytes_accessed=4 * 8 * n * w * 2, transcendentals=0
        ),
    )(tokens, cotangent, gain, bias, forget_weight.T, *attn_weights, *mlp_weights, out_weight)


TILE = 256


def middle_kernel(
    gated_ref, w_ref, tok_ref, gain_ref, mid_ref, normed_ref,
    gated, turned, mine, s0, r0, s1, r1, l0, *refs,
):
    c, s, f = here()
    n, width = mine.shape
    h = n // 2
    count = len(refs) // 2
    halves = [PairSum(refs[:count]), PairSum(refs[count:])]
    loads = [
        pltpu.make_async_copy(
            gated_ref.at[:, pl.ds(pl.multiple_of(block * n, n), n)],
            gated.at[:, pl.ds(i * n, n)],
            l0.at[i],
        )
        for i, block in enumerate(PairSum.blocks(c, s))
    ]
    for made in loads:
        made.start()
    greet(partners())
    for made in loads:
        made.wait()
    for q, pairs in enumerate(halves):

        def one_pair(i, unused, q=q, pairs=pairs):
            pairs.between(i)
            for core in (0, 1):
                tokens = pl.ds(pl.multiple_of((2 * i + core) * n + q * h, h), h)
                turned[core * h : (core + 1) * h, :] = gated[:, tokens].T
            for t in range(width // TILE):
                feats = pl.ds(t * TILE, TILE)
                pairs.put(i, feats, dot(turned[...], w_ref[:, feats], 1, 0).astype(BF))
            pairs.to_sibling(i).start()
            return unused

        lax.fori_loop(0, 4, one_pair, 0)
    for pairs in halves:
        pairs.relay()
    gathers = [
        Gather(mine.at[pl.ds(q * h, h)], normed_ref, send, recv, n, q * h)
        for q, (send, recv) in enumerate(((s0, r0), (s1, r1)))
    ]
    keep = []
    for q, pairs in enumerate(halves):
        pairs.arrive()

        def body(i, carry, q=q, pairs=pairs):
            r = pl.ds(pl.multiple_of(q * h + i * STEP, STEP), STEP)
            mid = tok_ref[r, :].astype(F32) + pairs.total(i, STEP)
            mid_ref[r, :] = mid
            mine[r, :] = (mid * mean_square_inverse(mid) * gain_row(gain_ref)).astype(BF)
            return carry

        lax.fori_loop(0, h // STEP, body, 0)
        gathers[q].start()
        keep.append(pltpu.make_async_copy(gathers[q].src, gathers[q].block(0), l0.at[8 + q]))
        keep[q].start()
    for gather in gathers:
        gather.relay()
        gather.finish()
    for pairs in halves:
        pairs.finish()
    for made in keep:
        made.wait()


def middle(gated, w_out, tokens, gain):
    n, w = tokens.shape
    dma = pltpu.SemaphoreType.DMA((16,))
    vmem = pl.BlockSpec(memory_space=pltpu.VMEM)
    anywhere = pl.BlockSpec(memory_space=pl.ANY)
    return pl.pallas_call(
        middle_kernel,
        name="middle",
        out_shape=(jax.ShapeDtypeStruct((n, w), F32), jax.ShapeDtypeStruct((8 * n, w), BF)),
        in_specs=[anywhere, vmem, vmem, vmem],
        out_specs=[vmem, anywhere],
        scratch_shapes=[
            pltpu.VMEM(gated.shape, BF),
            pltpu.VMEM((n, gated.shape[0]), BF),
            pltpu.VMEM((n, w), BF),
            dma, dma, dma, dma, dma,
        ]
        + PairSum.scratch(n // 2, w)
        + PairSum.scratch(n // 2, w),
        compiler_params=pltpu.CompilerParams(
            collective_id=2, has_side_effects=True, vmem_limit_bytes=VMEM_BYTES
        ),
        cost_estimate=pl.CostEstimate(
            flops=2 * 8 * n * w * gated.shape[0], bytes_accessed=4 * 8 * n * w * 2,
            transcendentals=0,
        ),
    )(gated, w_out, tokens, gain)


TERM_PIECES = 4


class LineSum:
    def __init__(self, term, got, send, recv, depth, pieces=TERM_PIECES):
        self.term, self.got, self.send, self.recv, self.depth = term, got, send, recv, depth
        self.c, self.s, self.f = here()
        self.pieces = pieces
        self.n = term.shape[0] // pieces

    def source(self, i, g):
        return self.term.at[pl.ds(i * self.n, self.n), g]

    def copy(self, k, g, i, src):
        to = lax.rem(self.f + (1 if k == 0 else self.depth - 1), self.depth)
        return REMOTE(
            src,
            self.got.at[k, g + k - 1, pl.ds(i * self.n, self.n)],
            self.send.at[k, g, i],
            self.recv.at[k, g, i],
            (self.c, self.s, to),
            MESH,
        )

    def targets(self, k):
        return range(self.depth - 1, 0, -1) if k == 0 else range(self.depth - 1)

    def is_end(self, k):
        return self.f == (0 if k == 0 else self.depth - 1)

    def start_piece(self, i, n):
        for k in (0, 1):
            g = self.targets(k)[n]
            pl.when(self.is_end(k))(self.copy(k, g, i, self.source(i, g)).start)

    def add(self, k, g, i):
        rows = pl.ds(i * self.n, self.n)
        total = self.got[k, g + k - 1, rows].astype(F32) + self.term[rows, g].astype(F32)
        self.got[k, g + k - 1, rows] = total.astype(BF)

    def pass_on(self, i, n, hop):
        for k in (0, 1):
            g = self.targets(k)[n]
            at = hop if k == 0 else self.depth - 1 - hop

            @pl.when(self.f == at)
            def _(k=k, g=g):
                made = self.copy(k, g, i, self.got.at[k, g + k - 1, pl.ds(i * self.n, self.n)])
                made.wait_recv()
                self.add(k, g, i)
                made.start()

    def steps(self):
        todo = [
            (n * self.pieces + i + 2 * (hop - 1), -hop, i, n, hop)
            for n in range(self.depth - 2)
            for hop in range(1, self.depth - 1 - n)
            for i in range(self.pieces)
        ]
        return [step[2:] for step in sorted(todo)]

    def collect(self, i, out):
        rows = pl.ds(i * self.n, self.n)
        for g in range(self.depth):

            @pl.when(self.f == g)
            def _(g=g):
                total = self.term[rows, g].astype(F32)
                for k in (0, 1):
                    if g != (0 if k == 0 else self.depth - 1):
                        self.copy(k, g, i, self.source(i, g)).wait_recv()
                        total = total + self.got[k, g + k - 1, rows].astype(F32)
                out[rows] = total.astype(BF)

    def finish(self):
        for k in (0, 1):
            for g in self.targets(k):
                beyond = self.f < g if k == 0 else self.f > g
                for i in range(self.pieces):
                    pl.when(beyond)(self.copy(k, g, i, self.source(i, g)).wait_send)


class Exchange:
    def __init__(self, rows, out, send, recv, cols=None):
        self.c, self.s, self.f = here()
        self.place = self.c * 4 + self.s
        self.rows, self.out, self.send, self.recv, self.cols = rows, out, send, recv, cols

    def mine(self, j):
        return self.rows.at[j] if self.cols is None else self.rows.at[j, :, self.cols]

    def remote(self, j):
        return REMOTE(
            self.mine(j), self.out.at[self.place], self.send.at[j], self.recv.at[self.place],
            (j // 4, j % 4, self.f), MESH,
        )

    def local(self, j):
        return pltpu.make_async_copy(self.mine(j), self.out.at[j], self.send.at[j])

    def push(self, j):
        pl.when(self.place != j)(self.remote(j).start)
        pl.when(self.place == j)(self.local(j).start)

    def start(self):
        for j in range(8):
            self.push(j)

    def finish(self):
        for j in range(8):
            got = REMOTE(
                self.mine(j), self.out.at[j], self.send.at[j], self.recv.at[j],
                (j // 4, j % 4, self.f), MESH,
            )
            pl.when(self.place != j)(got.wait_recv)
            pl.when(self.place != j)(self.remote(j).wait_send)
            pl.when(self.place == j)(self.local(j).wait)


def plane_peers():
    c, s, f = here()
    return [
        (core, flip(s, k) if k else s, f, k + 4 * i)
        for i, core in enumerate((c, 1 - c))
        for k in range(4)
        if i or k
    ]


def ffn_kernel(
    nm_ref, dy_all_ref, early_ref, mid_ref, gain_ref, gated_ref, w_out_ref, *more, depth,
):
    w_refs, more = more[:depth], more[depth:]
    (
        grad_mid_ref, gain_term_ref, gg_ref, out_term_ref, down_ref, gate_rows_ref, up_own_ref,
    ) = more[:7]
    low_refs, more = more[7 : 7 + depth], more[7 + depth :]
    (
        nm, dy, w, grads, term, got, rows_sum, mine, branch, stage, down_own, down_near, down_far,
        l0, l1, l2, s1, r1, s2, r2, s3, r3, s4, r4, *refs,
    ) = more
    c, s, f = here()
    n, width = mid_ref.shape
    fw = w.shape[1] // 3
    pairs = PairSum(refs)
    loads = []
    w_loads = [
        pltpu.make_async_copy(early_ref, w.at[:, pl.ds(0, EARLY)], l2.at[11]),
    ]
    shard = w_refs[0].shape[0]
    for k, ref in enumerate(w_refs):
        rows = pl.ds(pl.multiple_of(lax.rem(f + depth - k, depth) * shard, shard), shard)
        w_loads.append(
            pltpu.make_async_copy(ref, w.at[rows, pl.ds(EARLY, 3 * fw - EARLY)], l2.at[12 + k])
        )
    for made in w_loads:
        made.start()
    for i, block in enumerate(PairSum.blocks(c, s)):
        src, dst = pl.ds(pl.multiple_of(block * n, n), n), pl.ds(i * n, n)
        made = [
            pltpu.make_async_copy(nm_ref.at[src], nm.at[dst], l0.at[i]),
            pltpu.make_async_copy(dy_all_ref.at[src], dy.at[dst], l1.at[i]),
        ]
        for one in made:
            one.start()
        if i % 2:
            loads[-1] += made
        else:
            loads.append(made)
    greeted = signal_line([p[:3] for p in plane_peers()], depth)
    pl.semaphore_wait(pltpu.get_barrier_semaphore(), greeted)
    for made in w_loads:
        made.wait()

    def one_pair(i, unused):
        rows = rows_of(i, 2 * n)
        wait_for(i, loads)
        for t in range(fw // TILE):
            cols = pl.ds(t * TILE, TILE)
            ups = pl.ds(fw + t * TILE, TILE)
            downs = pl.ds(2 * fw + t * TILE, TILE)
            gate_lin = dot(nm[rows, :], w[:, cols], 1, 0)
            up_lin = dot(nm[rows, :], w[:, ups], 1, 0)
            grad_hidden = dot(dy[rows, :], w[:, downs], 1, 0)
            sig = jax.nn.sigmoid(gate_lin)
            active = gate_lin * sig
            grads[rows, downs] = (active * up_lin).astype(BF)
            grads[rows, cols] = (
                grad_hidden * up_lin * sig * (1.0 + gate_lin * (1.0 - sig))
            ).astype(BF)
            grads[rows, ups] = (grad_hidden * active).astype(BF)
        pairs.between(i)
        for t in range(width // TILE):
            feats = pl.ds(t * TILE, TILE)
            part = dot(grads[rows, 0 : 2 * fw], w[feats, 0 : 2 * fw], 1, 1).astype(BF)
            pairs.put(i, feats, part)
        pairs.to_sibling(i).start()
        return unused

    lax.fori_loop(0, 4, one_pair, 0)
    pairs.relay()

    line = LineSum(term, got, s2, r2, depth)
    deep = width // TERM_PIECES
    per = term.shape[0] // TERM_PIECES

    def weight_tile(i, unused):
        tile = dot(nm[:, rows_of(i, deep)], grads[:, 0 : 2 * fw], 0, 0).astype(BF)
        term[pl.ds(i * per, per)] = tile.reshape((per,) + term.shape[1:])
        line.start_piece(i, 0)
        return unused

    lax.fori_loop(0, TERM_PIECES, weight_tile, 0)
    for k in range(1, depth - 1):
        for i in range(TERM_PIECES):
            line.start_piece(i, k)
    hw = gated_ref.shape[0]
    w_out, out_term = nm.at[pl.ds(0, hw)], nm.at[pl.ds(hw, hw)]
    w_out_load = pltpu.make_async_copy(w_out_ref, w_out, l2.at[9])
    w_out_load.start()
    todo = line.steps()
    pairs.arrive()

    def body(j, carry):
        r = rows_of(j, STEP)
        grad = pairs.total(j, STEP)
        mid = mid_ref[r, :]
        inverse = mean_square_inverse(mid)
        weighted = grad * gain_row(gain_ref)
        back = inverse * weighted - mid * inverse**3 * jnp.mean(
            weighted * mid, axis=1, keepdims=True
        )
        own_dy = dy[pl.ds(pl.multiple_of(7 * n + j * STEP, STEP), STEP), :]
        grad_mid = own_dy.astype(F32) + back
        grad_mid_ref[r, :] = grad_mid
        mine[r, :] = grad_mid.astype(BF)
        return carry + jnp.sum(grad * mid * inverse, axis=0, keepdims=True)

    gain_term_ref[...] = lax.fori_loop(0, n // STEP, body, jnp.zeros((1, width), F32))
    gather = Gather(mine, branch, s1, r1)
    gather.start()
    keep = pltpu.make_async_copy(mine, gather.block(0), l0.at[8])
    keep.start()

    def low_tile(i, unused):
        tile = dot(dy[:, rows_of(i, deep)], grads[:, 2 * fw :], 0, 0).astype(BF)
        tile = tile.reshape((per, depth, term.shape[2], fw))
        for g in range(depth):
            for k in range(depth):

                @pl.when(lax.rem(g + depth - f, depth) == k)
                def _(g=g, k=k):
                    low_refs[k][pl.ds(i * per, per)] = tile[:, g]

        for at in range(TERM_PIECES):

            @pl.when(i == at)
            def _(at=at):
                for step in todo[at * 2 : at * 2 + 2]:
                    line.pass_on(*step)

        return unused

    lax.fori_loop(0, TERM_PIECES, low_tile, 0)

    def down_copy(i):
        return REMOTE(
            pairs.out.at[lax.rem(i, 2)], down_near.at[i], s3.at[i], r3.at[i], pairs.sib, MESH
        )

    for i in (2, 3):
        pairs.to_sibling(i).wait_send()

    def down_pair(i, unused):
        rows = rows_of(i, 2 * n)

        @pl.when(i >= 2)
        def _():
            down_copy(i - 2).wait_send()

        for t in range(width // TILE):
            feats = pl.ds(t * TILE, TILE)
            part = dot(grads[rows, 2 * fw :], w[feats, 2 * fw :], 1, 1).astype(BF)
            pairs.out[lax.rem(i, 2), :, feats] = part[:n]
            down_own[i, :, feats] = part[n:]
        down_copy(i).start()
        return unused

    lax.fori_loop(0, 4, down_pair, 0)
    gather.relay()
    for step in todo[2 * TERM_PIECES :]:
        line.pass_on(*step)

    def down_sum(i, unused):
        down_copy(i).wait_recv()

        def body(j, carry):
            r = rows_of(j, 32)
            total = down_own[i, r, :].astype(F32) + down_near[i, r, :].astype(F32)
            down_own[i, r, :] = total.astype(BF)
            return carry

        return lax.fori_loop(0, n // 32, body, unused)

    lax.fori_loop(0, 4, down_sum, 0)
    down_fx = REMOTE(
        down_own.at[0, :, pairs.left], down_far.at[0], s3.at[4], r3.at[4], pairs.x, MESH
    )
    down_fy = REMOTE(
        down_own.at[0, :, pairs.right], down_far.at[1], s3.at[5], r3.at[5], pairs.y, MESH
    )
    down_fx.start()
    down_fy.start()
    gather.finish()
    keep.wait()

    def gg_copy(i):
        return pltpu.make_async_copy(
            stage.at[lax.rem(i, 2)], gg_ref.at[:, rows_of(i, stage.shape[2])], l2.at[lax.rem(i, 2)]
        )

    def gg_tile(i, unused):
        @pl.when(i >= 2)
        def _():
            gg_copy(i - 2).wait()

        stage[lax.rem(i, 2)] = dot(w_out[...], branch[rows_of(i, stage.shape[2]), :], 1, 1)
        gg_copy(i).start()
        return unused

    exchange = Exchange(rows_sum, gate_rows_ref, s4, r4, pl.ds(0, fw))

    def collect(i):
        line.collect(i, rows_sum)
        for j in range(i * per, (i + 1) * per):
            exchange.push(j)

    collect(0)
    collect(1)
    tiles = branch.shape[0] // stage.shape[2]
    w_out_load.wait()
    lax.fori_loop(0, tiles, gg_tile, 0)
    collect(2)
    out_term[...] = dot(gated_ref[...], branch[...], 1, 0).astype(BF)
    out_store = pltpu.make_async_copy(out_term, out_term_ref, l2.at[10])
    out_store.start()

    def down_add(at, cols, slot):
        def body(j, carry):
            r = rows_of(j, 32)
            total = down_own[at, r, cols].astype(F32) + down_far[slot, r, :].astype(F32)
            down_own[at, r, cols] = total.astype(BF)
            return carry

        lax.fori_loop(0, n // 32, body, 0)

    collect(3)
    down_fx.wait_recv()
    down_fy.wait_recv()
    down_add(2, pairs.left, 0)
    down_add(1, pairs.right, 1)
    stores = [
        pltpu.make_async_copy(down_own.at[i], down_ref.at[i - 1], l1.at[i]) for i in (1, 2, 3)
    ]
    for made in stores:
        made.start()
    up_own_ref[...] = rows_sum[:, :, fw:]
    exchange.finish()
    for made in stores:
        made.wait()
    for i in (2, 3):
        gg_copy(jnp.int32(tiles - 4 + i)).wait()
    out_store.wait()
    down_fx.wait_send()
    down_fy.wait_send()
    pairs.finish_plane()
    for i in (2, 3):
        down_copy(i).wait_send()
    line.finish()


def ffn(normed_all, cotangent_all, weights, early, mid, gain, gated, w_out, depth):
    n, width = mid.shape
    fw = (weights[0].shape[1] + EARLY) // 3
    r = width // (8 * depth)
    hw = gated.shape[0]
    dma = pltpu.SemaphoreType.DMA((16,))
    six = pltpu.SemaphoreType.DMA((6,))
    eight = pltpu.SemaphoreType.DMA((8,))
    line = pltpu.SemaphoreType.DMA((2, depth, TERM_PIECES))
    vmem = pl.BlockSpec(memory_space=pltpu.VMEM)
    anywhere = pl.BlockSpec(memory_space=pl.ANY)
    return pl.pallas_call(
        functools.partial(ffn_kernel, depth=depth),
        name="ffn",
        out_shape=(
            jax.ShapeDtypeStruct((n, width), F32),
            jax.ShapeDtypeStruct((1, width), F32),
            jax.ShapeDtypeStruct((hw, 8 * n), F32),
            jax.ShapeDtypeStruct((hw, width), BF),
            jax.ShapeDtypeStruct((3, n, width), BF),
            jax.ShapeDtypeStruct((8, r, fw), BF),
            jax.ShapeDtypeStruct((8, r, fw), BF),
        )
        + (jax.ShapeDtypeStruct((8, r, fw), BF),) * depth,
        in_specs=[anywhere] * 3 + [vmem] * 3 + [anywhere] * (1 + depth),
        out_specs=[vmem, vmem, anywhere, anywhere, anywhere, vmem, vmem] + [vmem] * depth,
        scratch_shapes=[
            pltpu.VMEM((8 * n, width), BF),
            pltpu.VMEM((8 * n, width), BF),
            pltpu.VMEM((width, 3 * fw), BF),
            pltpu.VMEM((8 * n, 3 * fw), BF),
            pltpu.VMEM((8, depth, r, 2 * fw), BF),
            pltpu.VMEM((2, depth - 1, 8, r, 2 * fw), BF),
            pltpu.VMEM((8, r, 2 * fw), BF),
            pltpu.VMEM((n, width), BF),
            pltpu.VMEM((8 * n, width), BF),
            pltpu.VMEM((2, hw, 256), F32),
            pltpu.VMEM((4, n, width), BF),
            pltpu.VMEM((4, n, width), BF),
            pltpu.VMEM((2, n, width // 2), BF),
            dma, dma, dma, dma, dma, line, line, six, six, eight, eight,
        ]
        + PairSum.scratch(n, width),
        compiler_params=pltpu.CompilerParams(
            collective_id=3, has_side_effects=True, vmem_limit_bytes=67_043_328
        ),
        cost_estimate=pl.CostEstimate(
            flops=2 * 8 * n * width * fw * 9, bytes_accessed=4 * 8 * n * width * 2,
            transcendentals=0,
        ),
    )(normed_all, cotangent_all, early, mid, gain, gated, w_out, *weights)


def leave_kernel(
    normed_ref, cat_ref, w_ref, down_ref, tok_in, grad_mid_in, mid_in, gain_ref,
    mlp_term_ref, bias_grad_ref, up_ref, wide_ref, *more, depth, heads,
):
    low_refs, more = more[:depth], more[depth:]
    (
        grad_ref, small_sum_ref, out_ref, attn_rows_ref, low_rows_ref, up_rows_ref, wide_rows_ref,
        normed, cat, turned, w, small, plane_small, line_small, term, got, rows, wide_got, low_sum,
        tok_ref, grad_mid_ref, mid_ref, l0, l1, s2, r2, s3, r3, s5, r5, s6, r6, s7, r7, s8, r8, *refs,
    ) = more
    c, s, f = here()
    n, width = tok_ref.shape
    pairs = PairSum(refs[:7])
    down = PairTail(refs[7:])
    down_loads = [pltpu.make_async_copy(down_ref, down.own, l0.at[9])]
    loads = []
    for i, block in enumerate(PairSum.blocks(c, s)):
        src, dst = pl.ds(pl.multiple_of(block * n, n), n), pl.ds(i * n, n)
        loads.append(pltpu.make_async_copy(cat_ref.at[:, src], cat.at[:, dst], l0.at[i]))
        loads.append(pltpu.make_async_copy(normed_ref.at[src], normed.at[dst], l1.at[i]))
    w_load = pltpu.make_async_copy(w_ref, w, l0.at[8])
    late = [
        pltpu.make_async_copy(src, dst, l0.at[10 + i])
        for i, (src, dst) in enumerate(
            ((tok_in, tok_ref), (grad_mid_in, grad_mid_ref), (mid_in, mid_ref))
        )
    ]
    for made in down_loads + loads:
        made.start()
    w_load.start()
    for made in late:
        made.start()
    peers = plane_peers()
    line_peers = [(c, s, lax.rem(f + k, depth), k) for k in range(1, depth)]
    greet([p[:3] for p in peers + line_peers])
    wide = LineSum(wide_ref, wide_got, s7, r7, depth, 1)
    for k in range(depth - 1):
        wide.start_piece(0, k)
    line = LineSum(term, got, s3, r3, depth)
    low_total = low_refs[0][...].astype(F32)
    for ref in low_refs[1:]:
        low_total = low_total + ref[...].astype(F32)
    low_sum[...] = low_total.astype(BF)
    low_rows = Exchange(low_sum, low_rows_ref, s6, r6)
    deep = width // TERM_PIECES
    per = term.shape[0] // TERM_PIECES
    low_rows.start()
    up_rows = Exchange(up_ref, up_rows_ref, s8, r8)
    up_rows.start()
    for made in down_loads:
        made.wait()
    down.start(0)
    for made in loads:
        made.wait()

    def weight_tile(i, unused):
        tile = dot(cat[...], normed[:, rows_of(i, deep)], 1, 0).T.astype(BF)
        term[pl.ds(i * per, per)] = tile.reshape((per,) + term.shape[1:])
        line.start_piece(i, 0)
        return unused

    lax.fori_loop(0, TERM_PIECES, weight_tile, 0)
    for k in range(1, depth - 1):
        for i in range(TERM_PIECES):
            line.start_piece(i, k)
    w_load.wait()

    def one_pair(i, unused):
        pairs.between(i)
        turned[...] = cat[:, rows_of(i, 2 * n)].T
        for t in range(width // TILE):
            feats = pl.ds(t * TILE, TILE)
            pairs.put(i, feats, dot(turned[...], w[feats, :], 1, 1).astype(BF))
        pairs.to_sibling(i).start()
        for at in range(4):

            @pl.when(i == at)
            def _(at=at):
                for step in todo[at : at + 1]:
                    line.pass_on(*step)

        return unused

    todo = line.steps()
    for step in wide.steps():
        wide.pass_on(*step)
    lax.fori_loop(0, 4, one_pair, 0)
    for step in todo[4:6]:
        line.pass_on(*step)
    pairs.relay()
    down.start(1)
    for step in todo[6:]:
        line.pass_on(*step)
    attn_rows = Exchange(rows, attn_rows_ref, s5, r5)

    def collect(i):
        line.collect(i, rows)
        for j in range(i * per, (i + 1) * per):
            attn_rows.push(j)

    pairs.arrive()

    def body(i, carry):
        r = rows_of(i, STEP)
        grad = pairs.total(i, STEP)
        tok = tok_ref[r, :].astype(F32)
        inverse = mean_square_inverse(tok)
        weighted = grad * gain_row(gain_ref)
        back = inverse * weighted - tok * inverse**3 * jnp.mean(
            weighted * tok, axis=1, keepdims=True
        )
        grad_ref[r, :] = grad_mid_ref[r, :] + back
        return carry + jnp.sum(grad * tok * inverse, axis=0, keepdims=True)

    for made in late:
        made.wait()
    gain_term = lax.fori_loop(0, n // STEP, body, jnp.zeros((1, width), F32))
    lane = small.shape[1]
    place = c * 4 + s
    for k in range(3):
        small[k : k + 1, :] = gain_term[:, k * lane : (k + 1) * lane]
        small[3 + k : 4 + k, :] = mlp_term_ref[:, k * lane : (k + 1) * lane]
    at = lax.broadcasted_iota(jnp.int32, (1, lane), 1)
    bias_row = jnp.zeros((1, lane), F32)
    for h in range(heads):
        bias_row = jnp.where(at == place * heads + h, bias_grad_ref[h : h + 1, 0:1], bias_row)
    small[6:7, :] = bias_row
    small[7:8, :] = jnp.zeros((1, lane), F32)
    plane_small[pl.ds(place, 1)] = small[...][None]
    sent = []
    for core, other_s, other_f, k in peers:
        made = REMOTE(
            small, plane_small.at[place], s2.at[k - 1], r2.at[k - 1], (core, other_s, other_f), MESH
        )
        made.start()
        sent.append(made)
    wide.collect(0, wide_rows_ref)
    collect(0)
    collect(1)
    for made in sent:
        made.wait()
    total = plane_small[0]
    for i in range(1, 8):
        total = total + plane_small[i]
    small[...] = total
    line_small[pl.ds(f, 1)] = total[None]
    sent = []
    for core, other_s, other_f, k in line_peers:
        made = REMOTE(
            small, line_small.at[f], s2.at[6 + k], r2.at[6 + k], (core, other_s, other_f), MESH
        )
        made.start()
        sent.append(made)
    collect(2)
    collect(3)
    down.arrive()

    def body2(i, carry):
        r = rows_of(i, STEP)
        out_ref[r, :] = (mid_ref[r, :] + down.total(i, STEP)).astype(BF)
        return carry

    lax.fori_loop(0, n // STEP, body2, 0)
    for made in sent:
        made.wait()
    total = line_small[0]
    for i in range(1, depth):
        total = total + line_small[i]
    small_sum_ref[...] = total
    pairs.finish()
    down.finish()
    line.finish()
    wide.finish()
    low_rows.finish()
    up_rows.finish()
    attn_rows.finish()


def leave(
    normed, cat, w_attn, down_sum, tokens, grad_mid, mid, gain, mlp_term, bias_grad, low, up_own,
    wide, depth, heads,
):
    n, w = grad_mid.shape
    plane = 8
    cols = w_attn.shape[1]
    r = w // (plane * depth)
    sems = pltpu.SemaphoreType.DMA((6 + depth,))
    dma = pltpu.SemaphoreType.DMA((16,))
    eight = pltpu.SemaphoreType.DMA((8,))
    line = pltpu.SemaphoreType.DMA((2, depth, TERM_PIECES))
    one = pltpu.SemaphoreType.DMA((2, depth, 1))
    vmem = pl.BlockSpec(memory_space=pltpu.VMEM)
    anywhere = pl.BlockSpec(memory_space=pl.ANY)
    return pl.pallas_call(
        functools.partial(leave_kernel, depth=depth, heads=heads),
        name="leave",
        out_shape=(
            jax.ShapeDtypeStruct((n, w), F32),
            jax.ShapeDtypeStruct((8, w // 3), F32),
            jax.ShapeDtypeStruct((n, w), BF),
            jax.ShapeDtypeStruct((plane, r, cols), BF),
            jax.ShapeDtypeStruct(low[0].shape, BF),
            jax.ShapeDtypeStruct(up_own.shape, BF),
            jax.ShapeDtypeStruct((1,) + wide.shape[2:], BF),
        ),
        in_specs=[anywhere] * 7 + [vmem] * (5 + depth),
        out_specs=[vmem] * 7,
        scratch_shapes=[
            pltpu.VMEM(normed.shape, BF),
            pltpu.VMEM(cat.shape, BF),
            pltpu.VMEM((2 * n, cols), BF),
            pltpu.VMEM(w_attn.shape, BF),
            pltpu.VMEM((8, w // 3), F32),
            pltpu.VMEM((8, 8, w // 3), F32),
            pltpu.VMEM((depth, 8, w // 3), F32),
            pltpu.VMEM((plane, depth, r, cols), BF),
            pltpu.VMEM((2, depth - 1, plane, r, cols), BF),
            pltpu.VMEM((plane, r, cols), BF),
            pltpu.VMEM((2, depth - 1, 1) + wide.shape[2:], BF),
            pltpu.VMEM(low[0].shape, BF),
            pltpu.VMEM((n, w), BF),
            pltpu.VMEM((n, w), F32),
            pltpu.VMEM((n, w), F32),
            dma, dma, sems, sems, line, line, eight, eight, eight, eight, one, one, eight, eight,
        ]
        + PairSum.scratch(n, w)
        + PairTail.scratch(n, w),
        compiler_params=pltpu.CompilerParams(
            collective_id=4, has_side_effects=True, vmem_limit_bytes=VMEM_BYTES
        ),
        cost_estimate=pl.CostEstimate(
            flops=4 * 8 * n * w * cols, bytes_accessed=4 * 8 * n * w * 2, transcendentals=0
        ),
    )(
        normed, cat, w_attn, down_sum, tokens, grad_mid, mid, gain, mlp_term, bias_grad, up_own,
        wide, *low,
    )


def finish_kernel(
    attn_ref, gate_rows_ref, up_rows_ref, low_ref, small_ref, out_w_ref, block_ref, tok_grad_ref,
    q_ref, k_ref, v_ref, g_ref, f_ref, o_ref, gate_ref, up_ref, down_ref,
    gain1_ref, gain2_ref, bias_ref, out_ref, tokens_ref, *, hw, heads,
):
    plane = attn_ref.shape[0]
    fw = low_ref.shape[2]
    for i, ref in enumerate((q_ref, k_ref, v_ref, g_ref)):
        ref[...] = jnp.concatenate(
            [attn_ref[t, :, i * hw : (i + 1) * hw].astype(F32) for t in range(plane)], axis=1
        )
    a = lax.broadcasted_iota(jnp.int32, (128, 128), 0)
    b = lax.broadcasted_iota(jnp.int32, (128, 128), 1)
    total = jnp.zeros((attn_ref.shape[1], 128), F32)
    for t in range(plane):
        pick = jnp.where((a + t * heads == b) & (a < heads), 1.0, 0.0).astype(BF)
        total = total + dot(attn_ref[t, :, 4 * hw : 4 * hw + 128], pick, 1, 0)
    f_ref[...] = total.T[: f_ref.shape[0]]
    o_ref[...] = out_w_ref[0].astype(F32)
    for t in range(plane):
        cols = slice(t * fw, (t + 1) * fw)
        gate_ref[:, cols] = gate_rows_ref[t].astype(F32)
        up_ref[:, cols] = up_rows_ref[t].astype(F32)
        down_ref[:, cols] = low_ref[t].astype(F32)
    lane = small_ref.shape[1]
    count = gain1_ref.shape[0] // lane
    for k in range(count):
        gain1_ref[k * lane : (k + 1) * lane] = small_ref[k, :]
        gain2_ref[k * lane : (k + 1) * lane] = small_ref[count + k, :]
    bias_ref[...] = small_ref[2 * count : 2 * count + 1, 0 : bias_ref.shape[1]]
    out_ref[...] = block_ref[...]
    tokens_ref[...] = tok_grad_ref[...]


def finish(
    attn_rows, gate_rows, up_rows, low_rows, small, out_w, block_out, tokens_grad, hw, heads
):
    plane, r, _ = attn_rows.shape
    n, w = tokens_grad.shape
    fw = low_rows.shape[2]
    vmem = pl.BlockSpec(memory_space=pltpu.VMEM)
    square = jax.ShapeDtypeStruct((r, plane * hw), F32)
    wide = jax.ShapeDtypeStruct((r, plane * fw), F32)
    row = jax.ShapeDtypeStruct((w,), F32)
    return pl.pallas_call(
        functools.partial(finish_kernel, hw=hw, heads=heads),
        name="finish",
        out_shape=(
            square, square, square, square,
            jax.ShapeDtypeStruct((plane * heads, r), F32),
            jax.ShapeDtypeStruct(out_w.shape[1:], F32),
            wide, wide, wide, row, row,
            jax.ShapeDtypeStruct((1, plane * heads), F32),
            jax.ShapeDtypeStruct((n, w), BF),
            jax.ShapeDtypeStruct((n, w), F32),
        ),
        in_specs=[vmem] * 8,
        out_specs=[vmem] * 14,
        compiler_params=pltpu.CompilerParams(vmem_limit_bytes=VMEM_BYTES),
    )(attn_rows, gate_rows, up_rows, low_rows, small, out_w, block_out, tokens_grad)


BQ = 512
BK = 512
AUG = 128


def dot(a, b, ca, cb):
    return lax.dot_general(a, b, (((ca,), (cb,)), ((), ())), preferred_element_type=F32)


def three_parts(v):
    hi = v.astype(BF).astype(F32)
    mid = (v - hi).astype(BF).astype(F32)
    low = (v - hi - mid).astype(BF).astype(F32)
    return hi, mid, low


def triangle(n, suffix):
    a = lax.broadcasted_iota(jnp.int32, (n, n), 0)
    b = lax.broadcasted_iota(jnp.int32, (n, n), 1)
    return jnp.where(a >= b if suffix else a <= b, 1.0, 0.0).astype(BF)


def log_sigmoid(v):
    return jnp.minimum(v, 0.0) - jnp.log1p(jnp.exp(-jnp.abs(v)))


def doc_starts(lens_ref, pos):
    start, end = jnp.zeros_like(pos), jnp.int32(0)
    for n in range(lens_ref.shape[1]):
        end = end + lens_ref[0, n]
        start = jnp.where(pos >= end, end, start)
    return start


def storage_of(place_ref, p):
    found = jnp.int32(0)
    for n in range(place_ref.shape[1]):
        found = jnp.where(place_ref[0, n] == p, n, found)
    return found


def extend(prefix_row, sign_first):
    hi, mid, low = three_parts(prefix_row)
    r = lax.broadcasted_iota(jnp.int32, (16, prefix_row.shape[1]), 0)
    base = 0 if sign_first else 3
    sign = 1.0 if sign_first else -1.0
    ones = (r >= 3) & (r < 6) if sign_first else r < 3
    out = jnp.where(ones, 1.0, 0.0)
    out = jnp.where(r == base, sign * hi, out)
    out = jnp.where(r == base + 1, sign * mid, out)
    return jnp.where(r == base + 2, sign * low, out)


def lay_out(place_ref, cat_ref, prefix_ref, heads, hd, slab, qa, ka, kta):
    hw = heads * hd
    slabs = cat_ref.shape[1] // slab
    for p in range(slabs):
        src = pl.ds(pl.multiple_of(storage_of(place_ref, p) * slab, slab), slab)
        dst = pl.ds(p * slab, slab)
        for h in range(heads):
            q = cat_ref[h * hd : (h + 1) * hd, src].astype(BF).astype(F32)
            row = prefix_ref[h : h + 1, dst]
            rest = jnp.zeros((AUG - hd - 16, slab), F32)
            qe = jnp.concatenate([q * hd**-0.5, extend(row, True), rest], axis=0)
            qa[h, :, dst] = qe.astype(BF)
            k = cat_ref[hw + h * hd : hw + (h + 1) * hd, src].astype(BF).astype(F32)
            ke = jnp.concatenate([k, extend(row, False), rest], axis=0)
            if kta is not None:
                kta[h, :, dst] = ke.astype(BF)
            ka[h, dst, :] = ke.T.astype(BF)


def attention_kernel(
    place_ref, lens_ref, cat_ref,
    gated_ref, att_ref, exact_ref, lse_ref, prefix_ref,
    qa, ka, va, *, heads, hd, slab,
):
    hw = heads * hd
    tokens = cat_ref.shape[1]
    slabs = tokens // slab
    tri = triangle(slab, False)
    carry = jnp.zeros((16, 1), F32)
    for p in range(slabs):
        src = pl.ds(pl.multiple_of(storage_of(place_ref, p) * slab, slab), slab)
        pre = cat_ref[4 * hw : 4 * hw + 16, src]
        steps = log_sigmoid(pre).astype(BF)
        part = dot(steps, tri, 1, 0) + carry
        prefix_ref[:, p * slab : (p + 1) * slab] = part
        carry = part[:, slab - 1 : slab]
        for h in range(heads):
            va[h, :, p * slab : (p + 1) * slab] = cat_ref[
                2 * hw + h * hd : 2 * hw + (h + 1) * hd, src
            ].astype(BF)
    lay_out(place_ref, cat_ref, prefix_ref, heads, hd, slab, qa, ka, None)
    per = slab // BQ

    def one_query_block(qb, unused):
        q0 = pl.multiple_of(qb * BQ, BQ)
        pos = q0 + lax.broadcasted_iota(jnp.int32, (1, BQ), 1)
        start = doc_starts(lens_ref, pos)
        low = doc_starts(lens_ref, q0) // BK
        inside = lax.broadcasted_iota(jnp.int32, (BK, BQ), 0)

        def one_key_block(kb, held):
            k0 = pl.multiple_of(kb * BK, BK)
            allowed = (inside <= pos - k0) & (inside >= start - k0)
            out = []
            for h in range(heads):
                m, l, acc = held[h]
                st = dot(ka[h, pl.ds(k0, BK), :], qa[h, :, pl.ds(q0, BQ)], 1, 0)
                st = jnp.where(allowed, st, very_low)
                new = jnp.maximum(m, jnp.max(st, axis=0, keepdims=True))
                p = jnp.exp(st - new)
                scale = jnp.exp(m - new)
                l = l * scale + jnp.sum(p, axis=0, keepdims=True)
                acc = acc * scale + dot(va[h, :, pl.ds(k0, BK)], p.astype(BF), 1, 0)
                out.append((new, l, acc))
            return tuple(out)

        begin = tuple(
            (jnp.full((1, BQ), very_low, F32), jnp.zeros((1, BQ), F32), jnp.zeros((hd, BQ), F32))
            for _ in range(heads)
        )
        done = lax.fori_loop(low, (q0 + BQ + BK - 1) // BK, one_key_block, begin)
        dst = pl.ds(pl.multiple_of(storage_of(place_ref, qb // per) * slab + lax.rem(qb, per) * BQ, BQ), BQ)
        for h in range(heads):
            m, l, acc = done[h]
            lse_ref[h : h + 1, pl.ds(q0, BQ)] = m + jnp.log(l)
            exact = acc / l
            rounded = exact.astype(BF)
            exact_ref[h * hd : (h + 1) * hd, dst] = exact
            att_ref[h * hd : (h + 1) * hd, dst] = rounded
            gate = jax.nn.sigmoid(cat_ref[3 * hw + h * hd : 3 * hw + (h + 1) * hd, dst])
            gated_ref[h * hd : (h + 1) * hd, dst] = (rounded.astype(F32) * gate).astype(BF)
        return unused

    lse_ref[...] = jnp.zeros_like(lse_ref)
    lax.fori_loop(0, tokens // BQ, one_query_block, 0)


def attention(place, lens, cat, heads, hd, slab):
    tokens = cat.shape[1]
    hw = heads * hd
    vmem = pl.BlockSpec(memory_space=pltpu.VMEM)
    smem = pl.BlockSpec(memory_space=pltpu.SMEM)
    return pl.pallas_call(
        functools.partial(attention_kernel, heads=heads, hd=hd, slab=slab),
        name="attention",
        out_shape=(
            jax.ShapeDtypeStruct((hw, tokens), BF),
            jax.ShapeDtypeStruct((hw, tokens), BF),
            jax.ShapeDtypeStruct((hw, tokens), F32),
            jax.ShapeDtypeStruct((8, tokens), F32),
            jax.ShapeDtypeStruct((16, tokens), F32),
        ),
        in_specs=[smem, smem, vmem],
        out_specs=[vmem] * 5,
        scratch_shapes=[
            pltpu.VMEM((heads, AUG, tokens), BF),
            pltpu.VMEM((heads, tokens, AUG), BF),
            pltpu.VMEM((heads, hd, tokens), BF),
        ],
        compiler_params=pltpu.CompilerParams(vmem_limit_bytes=VMEM_BYTES),
        cost_estimate=pl.CostEstimate(
            flops=8 * heads * tokens * tokens * hd, bytes_accessed=cat.size * 4,
            transcendentals=heads * tokens * tokens // 2,
        ),
    )(place, lens, cat)


def attention_back_kernel(
    place_ref, lens_ref, cat_ref, gg_ref, att_ref, exact_ref, lse_ref, prefix_ref,
    out_ref, bias_grad_ref,
    qa, ka, kta, va, do, delta_ref, dk, dv, gp, *, heads, hd, slab,
):
    hw = heads * hd
    tokens = cat_ref.shape[1]
    slabs = tokens // slab
    per = slab // BQ
    lay_out(place_ref, cat_ref, prefix_ref, heads, hd, slab, qa, ka, kta)
    delta_ref[...] = jnp.zeros_like(delta_ref)
    gp[...] = jnp.zeros_like(gp)
    dk[...] = jnp.zeros_like(dk)
    dv[...] = jnp.zeros_like(dv)
    out_ref[4 * hw :, :] = jnp.zeros((out_ref.shape[0] - 4 * hw, tokens), BF)
    for p in range(slabs):
        src = pl.ds(pl.multiple_of(storage_of(place_ref, p) * slab, slab), slab)
        dst = pl.ds(p * slab, slab)
        for h in range(heads):
            rows = slice(h * hd, (h + 1) * hd)
            gate = jax.nn.sigmoid(cat_ref[3 * hw + h * hd : 3 * hw + (h + 1) * hd, src])
            gg = gg_ref[rows, src]
            low = (gg * gate).astype(BF)
            do[h, :, dst] = low
            delta_ref[h : h + 1, dst] = jnp.sum(
                low.astype(F32) * exact_ref[rows, src], axis=0, keepdims=True
            )
            gate_grad = gg * att_ref[rows, src].astype(F32) * gate * (1.0 - gate)
            out_ref[3 * hw + h * hd : 3 * hw + (h + 1) * hd, src] = gate_grad.astype(BF)
            v = cat_ref[2 * hw + h * hd : 2 * hw + (h + 1) * hd, src]
            va[h, dst, :] = v.T.astype(BF)

    def one_query_block(qb, unused):
        q0 = pl.multiple_of(qb * BQ, BQ)
        pos = q0 + lax.broadcasted_iota(jnp.int32, (1, BQ), 1)
        start = doc_starts(lens_ref, pos)
        low = doc_starts(lens_ref, q0) // BK
        inside = lax.broadcasted_iota(jnp.int32, (BK, BQ), 0)

        def one_key_block(kb, held):
            k0 = pl.multiple_of(kb * BK, BK)
            keys = pl.ds(k0, BK)
            allowed = (inside <= pos - k0) & (inside >= start - k0)
            out = []
            for h in range(heads):
                queries = qa[h, :, pl.ds(q0, BQ)]
                grads = do[h, :, pl.ds(q0, BQ)]
                st = dot(ka[h, keys, :], queries, 1, 0) - lse_ref[h : h + 1, pl.ds(q0, BQ)]
                p = jnp.exp(jnp.where(allowed, st, very_low))
                dp = dot(va[h, keys, :], grads, 1, 0) - delta_ref[h : h + 1, pl.ds(q0, BQ)]
                ds = (p * dp).astype(BF)
                out.append(held[h] + dot(kta[h, :, keys], ds, 1, 0))
                dk[h, :, keys] += dot(queries, ds, 1, 1)
                dv[h, :, keys] += dot(grads, p.astype(BF), 1, 1)
            return tuple(out)

        begin = tuple(jnp.zeros((AUG, BQ), F32) for _ in range(heads))
        done = lax.fori_loop(low, (q0 + BQ + BK - 1) // BK, one_key_block, begin)
        dst = pl.ds(pl.multiple_of(storage_of(place_ref, qb // per) * slab + lax.rem(qb, per) * BQ, BQ), BQ)
        for h in range(heads):
            out_ref[h * hd : (h + 1) * hd, dst] = (done[h][0:hd, :] * hd**-0.5).astype(BF)
            gp[h : h + 1, pl.ds(q0, BQ)] = done[h][hd : hd + 1, :]
        return unused

    lax.fori_loop(0, tokens // BQ, one_query_block, 0)
    tri = triangle(slab, True)
    carry = jnp.zeros((16, 1), F32)
    bias_grad = jnp.zeros((16, 1), F32)
    for p in reversed(range(slabs)):
        src = pl.ds(pl.multiple_of(storage_of(place_ref, p) * slab, slab), slab)
        dst = pl.ds(p * slab, slab)
        for h in range(heads):
            out_ref[hw + h * hd : hw + (h + 1) * hd, src] = dk[h, 0:hd, dst].astype(BF)
            out_ref[2 * hw + h * hd : 2 * hw + (h + 1) * hd, src] = dv[h, :, dst].astype(BF)
            gp[h : h + 1, dst] = gp[h : h + 1, dst] - dk[h, hd + 3 : hd + 4, dst]
        grad = gp[:, dst]
        total = carry
        for piece in three_parts(grad):
            total = total + dot(piece.astype(BF), tri, 1, 0)
        carry = total[:, 0:1]
        pre = cat_ref[4 * hw : 4 * hw + 16, src]
        low = (total.astype(BF).astype(F32) * jax.nn.sigmoid(-pre)).astype(BF)
        out_ref[4 * hw : 4 * hw + 16, src] = low
        bias_grad = bias_grad + jnp.sum(low.astype(F32), axis=1, keepdims=True)
    bias_grad_ref[...] = jnp.broadcast_to(bias_grad, bias_grad_ref.shape)


def attention_back(place, lens, cat, gg, att, exact, lse, prefix, heads, hd, slab):
    tokens = cat.shape[1]
    vmem = pl.BlockSpec(memory_space=pltpu.VMEM)
    smem = pl.BlockSpec(memory_space=pltpu.SMEM)
    return pl.pallas_call(
        functools.partial(attention_back_kernel, heads=heads, hd=hd, slab=slab),
        name="attention_back",
        out_shape=(
            jax.ShapeDtypeStruct(cat.shape, BF),
            jax.ShapeDtypeStruct((16, 128), F32),
        ),
        in_specs=[smem, smem] + [vmem] * 6,
        out_specs=[vmem] * 2,
        scratch_shapes=[
            pltpu.VMEM((heads, AUG, tokens), BF),
            pltpu.VMEM((heads, tokens, AUG), BF),
            pltpu.VMEM((heads, AUG, tokens), BF),
            pltpu.VMEM((heads, tokens, hd), BF),
            pltpu.VMEM((heads, hd, tokens), BF),
            pltpu.VMEM((8, tokens), F32),
            pltpu.VMEM((heads, AUG, tokens), F32),
            pltpu.VMEM((heads, hd, tokens), F32),
            pltpu.VMEM((16, tokens), F32),
        ],
        compiler_params=pltpu.CompilerParams(vmem_limit_bytes=VMEM_BYTES),
        cost_estimate=pl.CostEstimate(
            flops=20 * heads * tokens * tokens * hd, bytes_accessed=cat.size * 8,
            transcendentals=heads * tokens * tokens // 2,
        ),
    )(place, lens, cat, gg, att, exact, lse, prefix)


def local_plane(
    tokens, out_cotangent, seq_lengths, slab_place, attn_gain, query_weight, key_weight,
    value_weight, outgate_weight, forget_weight, forget_bias, output_weight, mlp_gain,
    gate_weight, up_weight, down_weight,
):
    plane_axes = ("cp", "sp")
    plane = lax.axis_size("cp") * lax.axis_size("sp")
    depth = lax.axis_size("fsdp")
    place = lax.axis_index("cp") * lax.axis_size("sp") + lax.axis_index("sp")
    head_count = forget_weight.shape[1]
    width = tokens.shape[2]
    hd = width // head_count
    heads = head_count // plane
    hw = heads * hd
    fw = gate_weight.shape[1] // plane
    shard = query_weight.shape[0]
    group_rows = tokens.shape[1] * plane
    slab = group_rows // slab_place.shape[1]

    def shift(value, k):
        return lax.ppermute(value, "fsdp", [(j, (j + k) % depth) for j in range(depth)])

    inputs, cotangent = tokens[0], out_cotangent[0]
    normed, cotangent_all, w_attn, w_out, cat, own_mlp, early = enter(
        inputs, cotangent, attn_gain, forget_bias, forget_weight,
        (query_weight, key_weight, value_weight, outgate_weight),
        (gate_weight, up_weight, down_weight), output_weight, depth,
    )
    w_mlp = [own_mlp] + [shift(own_mlp, k) for k in range(1, depth)]
    gated, att, exact, lse, prefix = attention(slab_place, seq_lengths, cat, heads, hd, slab)
    mid, normed_mlp = middle(gated, w_out, inputs, mlp_gain)

    grad_mid, mlp_gain_term, grad_gated, out_term, down_sum, gate_rows, up_own, *low_terms = ffn(
        normed_mlp, cotangent_all, w_mlp, early, mid, mlp_gain, gated, w_out, depth
    )
    low = [low_terms[0]] + [shift(low_terms[k], k) for k in range(1, depth)]

    grad_cat, bias_grad = attention_back(
        slab_place, seq_lengths, cat, grad_gated, att, exact, lse, prefix, heads, hd, slab
    )
    part = width // (plane * depth)
    tokens_grad, small_sum, block_out, attn_rows, low_rows, up_rows, wide_rows = leave(
        normed, grad_cat, w_attn, down_sum, inputs, grad_mid, mid, attn_gain, mlp_gain_term,
        bias_grad, low, up_own,
        out_term.reshape(1, depth, part, width), depth, heads,
    )
    (
        query_grad, key_grad, value_grad, outgate_grad, forget_grad, out_grad, gate_grad, up_grad,
        down_grad, attn_gain_grad, mlp_gain_grad, forget_bias_grad, block_out, tokens_grad,
    ) = finish(
        attn_rows, gate_rows, up_rows, low_rows, small_sum, wide_rows, block_out, tokens_grad,
        hw, heads,
    )
    return (
        block_out[None],
        tokens_grad[None],
        attn_gain_grad,
        query_grad,
        key_grad,
        value_grad,
        outgate_grad,
        forget_grad.T,
        forget_bias_grad[0],
        out_grad,
        mlp_gain_grad,
        gate_grad,
        up_grad,
        down_grad,
    )


def fits_plane(mesh, tokens, slab_place, forget_weight, gate_weight):
    sizes = dict(mesh.shape)
    if (sizes["cp"], sizes["sp"]) != (2, 4):
        return False
    plane = sizes["cp"] * sizes["sp"]
    width = tokens.shape[2]
    head_count = forget_weight.shape[1]
    group_rows = tokens.shape[1]
    slab = group_rows // slab_place.shape[1]
    heads = head_count // plane
    return (
        head_count % plane == 0
        and heads <= 8
        and width // head_count == 64
        and heads % 2 == 1
        and width == 8 * heads * 64
        and slab % 512 == 0
        and group_rows <= 2048
        and width % 768 == 0
        and gate_weight.shape[1] % (128 * plane) == 0
        and width % (16 * plane * sizes["fsdp"]) == 0
        and (group_rows // plane) % 64 == 0
    )


def shard(mesh, fn):
    return jax.shard_map(
        fn,
        mesh=mesh,
        in_specs=(
            P("fsdp", ("cp", "sp"), None),
            P("fsdp", ("cp", "sp"), None),
            P("fsdp", None),
            P("fsdp", None),
            P(),
            P("fsdp", None),
            P("fsdp", None),
            P("fsdp", None),
            P("fsdp", None),
            P("fsdp", None),
            P(),
            P("fsdp", None),
            P(),
            P("fsdp", None),
            P("fsdp", None),
            P("fsdp", None),
        ),
        out_specs=(
            P("fsdp", ("cp", "sp"), None),
            P("fsdp", ("cp", "sp"), None),
            P(),
            P(("cp", "sp", "fsdp"), None),
            P(("cp", "sp", "fsdp"), None),
            P(("cp", "sp", "fsdp"), None),
            P(("cp", "sp", "fsdp"), None),
            P(("cp", "sp", "fsdp"), None),
            P(),
            P(("cp", "sp", "fsdp"), None),
            P(),
            P(("cp", "sp", "fsdp"), None),
            P(("cp", "sp", "fsdp"), None),
            P(("cp", "sp", "fsdp"), None),
        ),
        check_vma=False,
    )


def solution(mesh):
    def run(*args):
        fast = fits_plane(mesh, args[0], args[3], args[9], args[13])
        return shard(mesh, local_plane if fast else local)(*args)

    return run
```
